32 devices in a mesh: dp: 4 (over y, x), seq: 8 (over z, core).
Axes of the slice: x: 2, y: 2, z: 4, core: 2. Of those that a mesh axis runs over, the one named last changes fastest.
Arguments:
- inputs: bfloat16 [4, 4096, 1024], P('dp', 'seq'), may hold values from -6 to 6
- skip_input: bfloat16 [4, 4096, 1024], P('dp', 'seq'), may hold values from -6 to 6
- time_embed: bfloat16 [4, 1024], P('dp'), may hold values from -6 to 6
- segment_ids: int32 [4, 4096], P('dp'), may hold values from 0 to 2, as said below
- span_start: int32 [4, 3], P('dp'), may hold values from 0 to 768, as said below
- span_length: int32 [4, 3], P('dp'), may hold values from 359 to 2560, as said below
- cotangent: bfloat16 [4, 4096, 1024], P('dp', 'seq'), may hold values from -6 to 6
- skip_weight: bfloat16 [2048, 1024], P('dp', 'seq'), may hold values from -0.125 to 0.125
- ada_weight: bfloat16 [1024, 4096], P('dp', 'seq'), may hold values from -0.09375 to 0.09375
- qkv_weight: bfloat16 [1024, 3072], P('dp', 'seq'), may hold values from -0.1875 to 0.1875
- out_weight: bfloat16 [1024, 1024], P('dp', 'seq'), may hold values from -1 to 1
- up_weight: bfloat16 [1024, 4096], P('dp', 'seq'), may hold values from -0.1875 to 0.1875
- down_weight: bfloat16 [4096, 1024], P('dp', 'seq'), may hold values from -0.09375 to 0.09375
Outputs:
- layer_output: bfloat16 [4, 4096, 1024], P('dp', 'seq')
- grad_inputs: float32 [4, 4096, 1024], P('dp', 'seq')
- grad_skip: float32 [4, 4096, 1024], P('dp', 'seq')
- grad_skip_weight: float32 [2048, 1024], P('dp', 'seq')
- grad_ada_weight: float32 [1024, 4096], P('dp', 'seq')
- grad_qkv_weight: float32 [1024, 3072], P('dp', 'seq')
- grad_out_weight: float32 [1024, 1024], P('dp', 'seq')
- grad_up_weight: float32 [1024, 4096], P('dp', 'seq')
- grad_down_weight: float32 [4096, 1024], P('dp', 'seq')
The draws below stay inside these ranges and needn't reach their ends.
Inputs may be any that keep to these rules, and one draw needn't show every extreme that they name: `segment_ids`: each row holds 3 utterances in order, ids never falling; each utterance has 512 to 2560 frames. `span_start`: the span of each utterance lies inside it and covers 70 to 100 percent of its frames. `span_length`: see span_start.
All inputs are finite; a program needn't handle non-finite values.
Results may differ from the reference program's by a relative error of at most 0.022.
Values may be sent and summed in bfloat16 or wider, within the bound.
No kernel may reach another device: no remote copies, remote signals or barrier semaphores. Data moves between devices by JAX's collectives and lax.ppermute only.
A program may use at most 512 MiB of HBM per device.

```python
import math
import jax
import jax.numpy as jnp
from jax import lax

D = 1024
H = 16
HD = 64
FF = 4096
L = 4096
UTT = 3
ROWS = 4


def utterance_plan(key):
    base_key = jax.random.fold_in(key, 7)
    size_key, length_key, offset_key = jax.random.split(base_key, 3)
    leading = jax.random.randint(size_key, (ROWS, UTT - 1), L // 4, 3 * L // 8 + 1)
    leading = leading.at[0, 0].set(5 * L // 8).at[0, 1].set(L // 4)
    leading = leading.at[ROWS - 1, 0].set(L // 4).at[ROWS - 1, 1].set(5 * L // 8)
    trailing = L - jnp.sum(leading, axis=1, keepdims=True)
    sizes = jnp.concatenate([leading, trailing], axis=1)
    least = (7 * sizes + 9) // 10
    spans = least + jax.random.randint(length_key, (ROWS, UTT), 0, sizes - least + 1)
    spans = spans.at[0, 0].set(least[0, 0]).at[0, UTT - 1].set(least[0, UTT - 1])
    spans = spans.at[ROWS - 1, 1].set(sizes[ROWS - 1, 1])
    offsets = jax.random.randint(offset_key, (ROWS, UTT), 0, sizes - spans + 1)
    offsets = offsets.at[0, 0].set(sizes[0, 0] - spans[0, 0])
    return (sizes, spans, offsets)


def draw_segment_ids(key, part):
    sizes, spans, offsets = utterance_plan(key)
    ends = jnp.cumsum(sizes, axis=1)
    frames = jnp.arange(L, dtype=jnp.int32)
    passed = frames[None, :, None] >= ends[:, None, :UTT - 1]
    return jnp.sum(passed.astype(jnp.int32), axis=2).astype(jnp.int32)


def draw_span_start(key, part):
    sizes, spans, offsets = utterance_plan(key)
    return offsets.astype(jnp.int32)


def draw_span_length(key, part):
    sizes, spans, offsets = utterance_plan(key)
    return spans.astype(jnp.int32)


def steps_of(rng, shape, cuts, smallest, largest):
    gain, own = 1.0, jax.random.fold_in(rng, 6)
    for axis_at, parts in cuts:
        steps = jnp.exp(jax.random.uniform(jax.random.fold_in(own, axis_at), (parts,), jnp.float32, smallest / len(cuts), largest / len(cuts)))
        gain = gain * jnp.repeat(steps, shape[axis_at] // parts).reshape([-1 if axis == axis_at else 1 for axis in range(len(shape))])
    return gain


def scatter_about(key, extent, scale, bound, cuts=(), kind=jnp.bfloat16):
    gain = steps_of(key, extent, cuts, -0.22, 0.18) if cuts else 1.0
    entries = jax.random.normal(key, extent, jnp.float32) * scale * gain
    return jnp.minimum(jnp.maximum(entries, -bound), bound).astype(kind)


def setup_inputs(seed: int = 0) -> dict:
    keys = jax.random.split(jax.random.key(seed), 14)
    return {
        "inputs": scatter_about(keys[0], (ROWS, L, D), 1.0, 6.0, ((0, 4), (1, 8))),
        "skip_input": scatter_about(keys[1], (ROWS, L, D), 1.0, 6.0, ((0, 4), (1, 8))),
        "time_embed": scatter_about(keys[2], (ROWS, D), 1.0, 6.0, ((0, 4),)),
        "segment_ids": draw_segment_ids(jax.random.fold_in(keys[13], 71), 0),
        "span_start": draw_span_start(jax.random.fold_in(keys[13], 71), 0),
        "span_length": draw_span_length(jax.random.fold_in(keys[13], 71), 0),
        "cotangent": scatter_about(keys[6], (ROWS, L, D), 1.0, 6.0, ((0, 4), (1, 8))),
        "skip_weight": scatter_about(keys[7], (2 * D, D), (2 * D) ** -0.5, 0.125, ((0, 4), (1, 8))),
        "ada_weight": scatter_about(keys[8], (D, 4 * D), (4 * D) ** -0.5, 0.09375, ((0, 4), (1, 8))),
        "qkv_weight": scatter_about(keys[9], (D, 3 * D), D ** -0.5, 0.1875, ((0, 4), (1, 8))),
        "out_weight": scatter_about(keys[10], (D, D), (D // 32) ** -0.5, 1.0, ((0, 4), (1, 8))),
        "up_weight": scatter_about(keys[11], (D, FF), D ** -0.5, 0.1875, ((0, 4), (1, 8))),
        "down_weight": scatter_about(keys[12], (FF, D), FF ** -0.5, 0.09375, ((0, 4), (1, 8))),
    }


@jax.custom_vjp
def low(v):
    return lax.optimization_barrier(v.astype(jnp.bfloat16)).astype(jnp.float32)

@jax.custom_vjp
def low_back(v):
    return v

def low_keep(v):
    return (low(v), None)

def low_pass(kept, grad):
    return (grad,)

def back_keep(v):
    return (v, None)

def back_low(kept, grad):
    return (low(grad),)
low.defvjp(low_keep, low_pass)
low_back.defvjp(back_keep, back_low)
epsilon = 1e-06
highest = lax.Precision.HIGHEST
masked_score = -1e+30

def ada_norm(stream, scale_part, shift_part):
    inverse = lax.rsqrt(lax.optimization_barrier(jnp.mean(stream * stream, axis=-1, keepdims=True)) + epsilon)
    return stream * inverse * (1.0 + scale_part) + shift_part

def rotate(tensor, cosine, sine_part):
    half_width = tensor.shape[-1] // 2
    lower_half = tensor[..., :half_width]
    upper_half = tensor[..., half_width:]
    cos_wide = cosine[..., None, :]
    sin_wide = sine_part[..., None, :]
    return jnp.concatenate([lower_half * cos_wide - upper_half * sin_wide, lower_half * sin_wide + upper_half * cos_wide], axis=-1)

def rotary_tables(position, half_width):
    frequency = jnp.exp(-math.log(10000.0) * jnp.arange(half_width, dtype=jnp.float32) / half_width)
    angles = position.astype(jnp.float32)[..., None] * frequency
    return (jnp.cos(angles), jnp.sin(angles))

def attend(queries, key_rows, value_rows, segments):
    block_rows = min(512, L)
    block_count = L // block_rows
    factor = HD ** (-0.5)
    query_blocks = queries.reshape(block_count, block_rows, H, HD)
    segment_blocks = segments.reshape(block_count, block_rows)

    @jax.checkpoint
    def one_block(block_pair):
        query_part, segment_part = block_pair
        scores = low_back(jnp.einsum('qhd,khd->hqk', query_part, key_rows, precision=highest) * factor)
        allowed = segment_part[:, None] == segments[None, :]
        scores = jnp.where(allowed[None], scores, masked_score)
        log_total = jax.nn.logsumexp(scores, axis=-1, keepdims=True)
        weights = low(jnp.exp(scores - log_total))
        return jnp.einsum('hqk,khd->qhd', weights, value_rows, precision=highest).reshape(block_rows, H * HD)
    return lax.map(one_block, (query_blocks, segment_blocks)).reshape(L, H * HD)

def row_forward(main_row, skip_row, embed_row, segments, cosine, sine_part, params):
    skip_w, ada_w, qkv_w, out_w, up_w, down_w = params
    model_width = main_row.shape[-1]
    joined = jnp.concatenate([main_row, skip_row], axis=-1)
    stream = low_back(jnp.dot(joined, skip_w, precision=highest))
    modulation = jnp.dot(embed_row, ada_w, precision=highest)
    scale_one = modulation[:model_width]
    shift_one = modulation[model_width:2 * model_width]
    scale_two = modulation[2 * model_width:3 * model_width]
    shift_two = modulation[3 * model_width:]
    normed_one = low(ada_norm(stream, scale_one, shift_one))
    projected = low_back(jnp.dot(normed_one, qkv_w, precision=highest))
    queries = low(rotate(projected[:, :model_width].reshape(L, H, HD), cosine, sine_part))
    key_rows = low(rotate(projected[:, model_width:2 * model_width].reshape(L, H, HD), cosine, sine_part))
    value_rows = low(projected[:, 2 * model_width:].reshape(L, H, HD))
    attended = low_back(low(attend(queries, key_rows, value_rows, segments)))
    middle = stream + low_back(jnp.dot(attended, out_w, precision=highest))
    normed_two = low(ada_norm(middle, scale_two, shift_two))
    up_proj = low_back(jnp.dot(normed_two, up_w, precision=highest))
    hidden = low(jax.nn.gelu(up_proj, approximate=True))
    return middle + low_back(jnp.dot(hidden, down_w, precision=highest))

def forward(main_all, skip_all, embed_all, segment_all, cosine_all, sine_all, params):

    def one_row(row_items):
        return jax.checkpoint(row_forward)(row_items[0], row_items[1], row_items[2], row_items[3], row_items[4], row_items[5], params)
    return lax.map(one_row, (main_all, skip_all, embed_all, segment_all, cosine_all, sine_all))

def reference(inputs, skip_input, time_embed, segment_ids, span_start, span_length, cotangent, skip_weight, ada_weight, qkv_weight, out_weight, up_weight, down_weight):
    utterance = jnp.arange(UTT, dtype=jnp.int32)
    member = (segment_ids[:, :, None] == utterance[None, None, :]).astype(jnp.int32)
    counts = lax.optimization_barrier(jnp.sum(member, axis=1))
    firsts = jnp.cumsum(counts, axis=1) - counts
    frames = jnp.arange(L, dtype=jnp.int32)
    position = frames[None, :] - lax.optimization_barrier(jnp.sum(member * firsts[:, None, :], axis=2))
    span_begin = lax.optimization_barrier(jnp.sum(member * span_start[:, None, :], axis=2))
    span_end = span_begin + lax.optimization_barrier(jnp.sum(member * span_length[:, None, :], axis=2))
    inside = jnp.logical_and(position >= span_begin, position < span_end)
    cosine, sine_part = rotary_tables(position, HD // 2)
    params = (skip_weight.astype(jnp.float32), ada_weight.astype(jnp.float32), qkv_weight.astype(jnp.float32), out_weight.astype(jnp.float32), up_weight.astype(jnp.float32), down_weight.astype(jnp.float32))
    embed_all = time_embed.astype(jnp.float32)

    def run(main_all, skip_all, weight_set):
        return forward(main_all, skip_all, embed_all, segment_ids, cosine, sine_part, weight_set)
    output, pullback = jax.vjp(run, inputs.astype(jnp.float32), skip_input.astype(jnp.float32), params)
    grad_out = cotangent.astype(jnp.float32) * inside[..., None].astype(jnp.float32)
    grad_main, grad_side, grad_params = pullback(grad_out)
    return (output.astype(jnp.bfloat16), grad_main, grad_side, grad_params[0], grad_params[1], grad_params[2], grad_params[3], grad_params[4], grad_params[5])
```

```python
from functools import partial
import math

import jax
import jax.numpy as jnp
from jax import lax
from jax.experimental import pallas as pl
from jax.experimental.pallas import tpu as pltpu
from jax.sharding import PartitionSpec as P

H = 16
HD = 64
UTT = 3
HG = 8


epsilon = 1e-06
masked_score = -1e30


def ada_norm(stream, scale_part, shift_part):
    inverse = lax.rsqrt(jnp.mean(stream * stream, axis=-1, keepdims=True) + epsilon)
    return stream * inverse * (1.0 + scale_part) + shift_part


def rotate(tensor, cosine, sine_part):
    half_width = tensor.shape[-1] // 2
    lower_half = tensor[..., :half_width]
    upper_half = tensor[..., half_width:]
    cos_wide = cosine[..., None, :]
    sin_wide = sine_part[..., None, :]
    return jnp.concatenate(
        [
            lower_half * cos_wide - upper_half * sin_wide,
            lower_half * sin_wide + upper_half * cos_wide,
        ],
        axis=-1,
    )


def rotary_tables(position, half_width):
    frequency = jnp.exp(-math.log(10000.0) * jnp.arange(half_width, dtype=jnp.float32) / half_width)
    angles = position.astype(jnp.float32)[..., None] * frequency
    return (jnp.cos(angles), jnp.sin(angles))


def gather_weights(skip_tile, ada_tile, qkv_tile, out_tile, up_tile, down_tile):
    row_full = (
        lax.all_gather(skip_tile, "dp", axis=0, tiled=True),
        lax.all_gather(ada_tile, "dp", axis=0, tiled=True),
        lax.all_gather(qkv_tile, "dp", axis=0, tiled=True),
        lax.all_gather(out_tile, "dp", axis=0, tiled=True),
        lax.all_gather(up_tile, "dp", axis=0, tiled=True),
        lax.all_gather(down_tile, "dp", axis=0, tiled=True),
    )
    return (
        lax.all_gather(row_full[0], "seq", axis=1, tiled=True),
        lax.all_gather(row_full[1], "seq", axis=1, tiled=True),
        lax.all_gather(row_full[2], "seq", axis=1, tiled=True),
        lax.all_gather(row_full[3], "seq", axis=1, tiled=True),
        lax.all_gather(row_full[4], "seq", axis=1, tiled=True),
        lax.all_gather(row_full[5], "seq", axis=1, tiled=True),
    )


def group_scores(query_part, key_part, allowed, factor):
    scores = (
        jnp.einsum("qhd,khd->hqk", query_part, key_part, preferred_element_type=jnp.float32)
        * factor
    )
    return jnp.where(allowed[None], scores, masked_score)


def attend_row(queries, key_rows, value_rows, segment_local, segment_full):
    factor = queries.shape[2] ** (-0.5)
    allowed = segment_local[:, None] == segment_full[None, :]
    outputs = []
    totals = []
    for head_start in range(0, H, HG):
        head_end = head_start + HG
        scores = group_scores(
            queries[:, head_start:head_end], key_rows[:, head_start:head_end], allowed, factor
        )
        log_total = jax.nn.logsumexp(scores, axis=-1)
        weights = jnp.exp(scores - log_total[..., None]).astype(jnp.bfloat16)
        outputs.append(
            jnp.einsum(
                "hqk,khd->qhd",
                weights,
                value_rows[:, head_start:head_end],
                preferred_element_type=jnp.float32,
            )
        )
        totals.append(log_total)
    return (jnp.concatenate(outputs, axis=1), jnp.concatenate(totals, axis=0))


def attend_back(
    queries, key_rows, value_rows, segment_local, segment_full, log_total, grad_attended, row_dot
):
    factor = queries.shape[2] ** (-0.5)
    allowed = segment_local[:, None] == segment_full[None, :]
    query_grads = []
    key_grads = []
    value_grads = []
    for head_start in range(0, H, HG):
        head_end = head_start + HG
        key_part = key_rows[:, head_start:head_end]
        query_part = queries[:, head_start:head_end]
        grad_part = grad_attended[:, head_start:head_end]
        scores = group_scores(query_part, key_part, allowed, factor)
        weights = jnp.exp(scores - log_total[head_start:head_end][..., None])
        weights_low = weights.astype(jnp.bfloat16)
        value_grads.append(
            jnp.einsum("hqk,qhd->khd", weights_low, grad_part, preferred_element_type=jnp.float32)
        )
        grad_weights = jnp.einsum(
            "qhd,khd->hqk",
            grad_part,
            value_rows[:, head_start:head_end],
            preferred_element_type=jnp.float32,
        )
        grad_scores = (weights * (grad_weights - row_dot[head_start:head_end][..., None])).astype(
            jnp.bfloat16
        )
        query_grads.append(
            jnp.einsum("hqk,khd->qhd", grad_scores, key_part, preferred_element_type=jnp.float32)
            * factor
        )
        key_grads.append(
            jnp.einsum("hqk,qhd->khd", grad_scores, query_part, preferred_element_type=jnp.float32)
            * factor
        )
    return (
        jnp.concatenate(query_grads, axis=1),
        jnp.concatenate(key_grads, axis=1),
        jnp.concatenate(value_grads, axis=1),
    )


def local_general(
    inputs,
    skip_input,
    time_embed,
    segment_ids,
    span_start,
    span_length,
    cotangent,
    skip_weight,
    ada_weight,
    qkv_weight,
    out_weight,
    up_weight,
    down_weight,
):
    row_count = inputs.shape[0]
    frames = inputs.shape[1]
    model_width = inputs.shape[2]
    row_length = segment_ids.shape[1]
    frame_base = lax.axis_index("seq") * frames
    utterance = jnp.arange(UTT, dtype=jnp.int32)
    member = (segment_ids[:, :, None] == utterance[None, None, :]).astype(jnp.int32)
    counts = jnp.sum(member, axis=1)
    firsts = jnp.cumsum(counts, axis=1) - counts
    local_member = lax.dynamic_slice_in_dim(member, frame_base, frames, 1)
    local_segments = lax.dynamic_slice_in_dim(segment_ids, frame_base, frames, 1)
    local_frames = frame_base + jnp.arange(frames, dtype=jnp.int32)
    position = local_frames[None, :] - jnp.sum(local_member * firsts[:, None, :], axis=2)
    span_begin = jnp.sum(local_member * span_start[:, None, :], axis=2)
    span_end = span_begin + jnp.sum(local_member * span_length[:, None, :], axis=2)
    inside = jnp.logical_and(position >= span_begin, position < span_end)
    cosine, sine_part = rotary_tables(position, HD // 2)
    skip_full, ada_full, qkv_full, out_full, up_full, down_full = gather_weights(
        skip_weight, ada_weight, qkv_weight, out_weight, up_weight, down_weight
    )
    joined = jnp.concatenate([inputs, skip_input], axis=-1)
    stream = jnp.einsum("rfc,cd->rfd", joined, skip_full, preferred_element_type=jnp.float32)
    modulation = jnp.dot(time_embed, ada_full, preferred_element_type=jnp.float32)[:, None, :]
    scale_one = modulation[..., :model_width]
    shift_one = modulation[..., model_width : 2 * model_width]
    scale_two = modulation[..., 2 * model_width : 3 * model_width]
    shift_two = modulation[..., 3 * model_width :]
    normed_one = ada_norm(stream, scale_one, shift_one).astype(jnp.bfloat16)
    projected = jnp.einsum("rfd,de->rfe", normed_one, qkv_full, preferred_element_type=jnp.float32)
    queries = rotate(
        projected[..., :model_width].reshape(row_count, frames, H, HD), cosine, sine_part
    ).astype(jnp.bfloat16)
    key_rotated = rotate(
        projected[..., model_width : 2 * model_width].reshape(row_count, frames, H, HD),
        cosine,
        sine_part,
    )
    key_local = key_rotated.reshape(row_count, frames, model_width).astype(jnp.bfloat16)
    value_local = projected[..., 2 * model_width :].astype(jnp.bfloat16)
    key_all, value_all = (
        lax.all_gather(key_local, "seq", axis=1, tiled=True),
        lax.all_gather(value_local, "seq", axis=1, tiled=True),
    )

    def forward_row(row_items):
        query_row, key_row, value_row, local_row, full_row = row_items
        return attend_row(
            query_row,
            key_row.reshape(row_length, H, HD),
            value_row.reshape(row_length, H, HD),
            local_row,
            full_row,
        )

    attended, log_total = lax.map(
        forward_row, (queries, key_all, value_all, local_segments, segment_ids)
    )
    attended = attended.reshape(row_count, frames, model_width)
    attended_low = attended.astype(jnp.bfloat16)
    middle = stream + jnp.einsum(
        "rfe,ed->rfd", attended_low, out_full, preferred_element_type=jnp.float32
    )
    normed_two = ada_norm(middle, scale_two, shift_two).astype(jnp.bfloat16)
    up_proj = jnp.einsum("rfd,di->rfi", normed_two, up_full, preferred_element_type=jnp.float32)
    hidden = jax.nn.gelu(up_proj, approximate=True).astype(jnp.bfloat16)
    down_proj = jnp.einsum("rfi,id->rfd", hidden, down_full, preferred_element_type=jnp.float32)
    layer_output = (middle + down_proj).astype(jnp.bfloat16)
    skip_full, ada_full, qkv_full, out_full, up_full, down_full = gather_weights(
        skip_weight, ada_weight, qkv_weight, out_weight, up_weight, down_weight
    )
    grad_out = cotangent.astype(jnp.float32) * inside[..., None].astype(jnp.float32)
    grad_low = grad_out.astype(jnp.bfloat16)
    grad_hidden = jnp.einsum("rfd,id->rfi", grad_low, down_full, preferred_element_type=jnp.float32)
    _, gelu_pull = jax.vjp(partial(jax.nn.gelu, approximate=True), up_proj)
    grad_up_act = gelu_pull(grad_hidden)[0].astype(jnp.bfloat16)
    grad_normed_two = jnp.einsum(
        "rfi,di->rfd", grad_up_act, up_full, preferred_element_type=jnp.float32
    )
    _, norm_pull_two = jax.vjp(ada_norm, middle, scale_two, shift_two)
    grad_middle_norm, grad_scale_two, grad_shift_two = norm_pull_two(grad_normed_two)
    grad_middle = grad_out + grad_middle_norm
    grad_middle_low = grad_middle.astype(jnp.bfloat16)
    grad_attended = jnp.einsum(
        "rfd,ed->rfe", grad_middle_low, out_full, preferred_element_type=jnp.float32
    ).astype(jnp.bfloat16)
    row_dot = jnp.sum(
        (grad_attended.astype(jnp.float32) * attended).reshape(row_count, frames, H, HD), axis=-1
    )
    row_dot = jnp.swapaxes(row_dot, 1, 2)
    grad_heads = grad_attended.reshape(row_count, frames, H, HD)

    def backward_row(row_items):
        query_row, key_row, value_row, local_row, full_row, total_row, grad_row, dot_row = row_items
        return attend_back(
            query_row,
            key_row.reshape(row_length, H, HD),
            value_row.reshape(row_length, H, HD),
            local_row,
            full_row,
            total_row,
            grad_row,
            dot_row,
        )

    grad_queries, grad_keys, grad_values = lax.map(
        backward_row,
        (queries, key_all, value_all, local_segments, segment_ids, log_total, grad_heads, row_dot),
    )
    key_share, value_share = (
        lax.psum_scatter(
            grad_keys.reshape(row_count, row_length, model_width).astype(jnp.bfloat16),
            "seq",
            scatter_dimension=1,
            tiled=True,
        ).astype(jnp.float32),
        lax.psum_scatter(
            grad_values.reshape(row_count, row_length, model_width).astype(jnp.bfloat16),
            "seq",
            scatter_dimension=1,
            tiled=True,
        ).astype(jnp.float32),
    )
    _, rotate_pull = jax.vjp(
        partial(rotate, cosine=cosine, sine_part=sine_part),
        jnp.zeros((row_count, frames, H, HD), jnp.float32),
    )
    grad_query_raw = rotate_pull(grad_queries)[0].reshape(row_count, frames, model_width)
    grad_key_raw = rotate_pull(key_share.reshape(row_count, frames, H, HD))[0].reshape(
        row_count, frames, model_width
    )
    grad_projected = jnp.concatenate([grad_query_raw, grad_key_raw, value_share], axis=-1).astype(
        jnp.bfloat16
    )
    grad_normed_one = jnp.einsum(
        "rfe,de->rfd", grad_projected, qkv_full, preferred_element_type=jnp.float32
    )
    _, norm_pull_one = jax.vjp(ada_norm, stream, scale_one, shift_one)
    grad_stream_norm, grad_scale_one, grad_shift_one = norm_pull_one(grad_normed_one)
    grad_stream = (grad_middle + grad_stream_norm).astype(jnp.bfloat16)
    grad_joined = jnp.einsum(
        "rfd,cd->rfc", grad_stream, skip_full, preferred_element_type=jnp.float32
    )
    grad_modulation = jnp.concatenate(
        [grad_scale_one, grad_shift_one, grad_scale_two, grad_shift_two], axis=-1
    )[:, 0, :]
    grad_down = jnp.einsum("rfi,rfd->id", hidden, grad_low, preferred_element_type=jnp.float32)
    grad_up = jnp.einsum("rfd,rfi->di", normed_two, grad_up_act, preferred_element_type=jnp.float32)
    grad_attn_out = jnp.einsum(
        "rfe,rfd->ed", attended_low, grad_middle_low, preferred_element_type=jnp.float32
    )
    grad_qkv = jnp.einsum(
        "rfd,rfe->de", normed_one, grad_projected, preferred_element_type=jnp.float32
    )
    grad_skip_w = jnp.einsum("rfc,rfd->cd", joined, grad_stream, preferred_element_type=jnp.float32)
    grad_ada = jnp.einsum(
        "rd,re->de",
        time_embed.astype(jnp.float32),
        grad_modulation,
        precision=lax.Precision.HIGHEST,
    )
    column_parts = (
        lax.psum_scatter(
            grad_skip_w.astype(jnp.bfloat16), "seq", scatter_dimension=1, tiled=True
        ).astype(jnp.float32),
        lax.psum_scatter(
            grad_ada.astype(jnp.bfloat16), "seq", scatter_dimension=1, tiled=True
        ).astype(jnp.float32),
        lax.psum_scatter(
            grad_qkv.astype(jnp.bfloat16), "seq", scatter_dimension=1, tiled=True
        ).astype(jnp.float32),
        lax.psum_scatter(
            grad_attn_out.astype(jnp.bfloat16), "seq", scatter_dimension=1, tiled=True
        ).astype(jnp.float32),
        lax.psum_scatter(
            grad_up.astype(jnp.bfloat16), "seq", scatter_dimension=1, tiled=True
        ).astype(jnp.float32),
        lax.psum_scatter(
            grad_down.astype(jnp.bfloat16), "seq", scatter_dimension=1, tiled=True
        ).astype(jnp.float32),
    )
    weight_tiles = (
        lax.psum_scatter(
            column_parts[0].astype(jnp.bfloat16), "dp", scatter_dimension=0, tiled=True
        ).astype(jnp.float32),
        lax.psum_scatter(
            column_parts[1].astype(jnp.bfloat16), "dp", scatter_dimension=0, tiled=True
        ).astype(jnp.float32),
        lax.psum_scatter(
            column_parts[2].astype(jnp.bfloat16), "dp", scatter_dimension=0, tiled=True
        ).astype(jnp.float32),
        lax.psum_scatter(
            column_parts[3].astype(jnp.bfloat16), "dp", scatter_dimension=0, tiled=True
        ).astype(jnp.float32),
        lax.psum_scatter(
            column_parts[4].astype(jnp.bfloat16), "dp", scatter_dimension=0, tiled=True
        ).astype(jnp.float32),
        lax.psum_scatter(
            column_parts[5].astype(jnp.bfloat16), "dp", scatter_dimension=0, tiled=True
        ).astype(jnp.float32),
    )
    skip_tile, ada_tile, qkv_tile, out_tile, up_tile, down_tile = weight_tiles
    return (
        layer_output,
        grad_joined[..., :model_width],
        grad_joined[..., model_width:],
        skip_tile,
        ada_tile,
        qkv_tile,
        out_tile,
        up_tile,
        down_tile,
    )


LOG2E = 1.4426950408889634
SCALE = HD**-0.5
PAIR = 2 * HD


def dot_nn(a, b):
    return lax.dot_general(a, b, (((1,), (0,)), ((), ())), preferred_element_type=jnp.float32)


def dot_nt(a, b):
    return lax.dot_general(a, b, (((1,), (1,)), ((), ())), preferred_element_type=jnp.float32)


def dot_tn(a, b):
    return lax.dot_general(a, b, (((0,), (0,)), ((), ())), preferred_element_type=jnp.float32)


def segment_of(index, ends_ref):
    return (index >= ends_ref[0]).astype(jnp.int32) + (index >= ends_ref[1]).astype(jnp.int32)


def segment_span(ends_ref, first, last, length):
    end_a, end_b = ends_ref[0], ends_ref[1]
    low = jnp.where(first < end_a, 0, jnp.where(first < end_b, end_a, end_b))
    high = jnp.where(last < end_a, end_a, jnp.where(last < end_b, end_b, length))
    return low, high


def key_blocks(ends_ref, start, size, length):
    low, high = segment_span(ends_ref, start, start + size - 1, length)
    low_last, _ = segment_span(ends_ref, start + size - 1, start, length)
    first = low // size
    last = (high + size - 1) // size
    whole_first = jnp.where(low == low_last, (low + size - 1) // size, last)
    whole_first = jnp.minimum(whole_first, last)
    whole_last = jnp.where(low == low_last, jnp.maximum(high // size, whole_first), last)
    return first, whole_first, whole_last, last


def turn(pair, cosine, sine_part):
    half = HD // 2
    rows = []
    for head in range(2):
        lower = pair[head * HD : head * HD + half]
        upper = pair[head * HD + half : (head + 1) * HD]
        rows += [lower * cosine - upper * sine_part, lower * sine_part + upper * cosine]
    return jnp.concatenate(rows, axis=0)


def project_kernel(normed_ref, weight_ref, cos_ref, sin_ref, qt_ref, kt_ref, vt_ref, k_ref, v_ref):
    projected = dot_nt(weight_ref[...], normed_ref[0])
    cosine, sine_part = cos_ref[...], sin_ref[...]
    queries = turn(projected[:PAIR], cosine, sine_part).astype(jnp.bfloat16)
    keys = turn(projected[PAIR : 2 * PAIR], cosine, sine_part)
    values = projected[2 * PAIR :]
    qt_ref[0] = (queries.astype(jnp.float32) * SCALE).astype(jnp.bfloat16)
    kt_ref[...] = keys.astype(jnp.bfloat16)
    vt_ref[...] = values.astype(jnp.bfloat16)
    k_ref[...] = keys.T.astype(jnp.bfloat16)
    v_ref[...] = values.T.astype(jnp.bfloat16)


def project_pair(normed_all, weight_rows, cos_all, sin_all):
    chunks, frames, width = normed_all.shape
    length = chunks * frames
    return pl.pallas_call(
        project_kernel,
        grid=(chunks,),
        in_specs=[
            pl.BlockSpec((1, frames, width), lambda i: (i, 0, 0)),
            pl.BlockSpec((3 * PAIR, width), lambda i: (0, 0)),
            pl.BlockSpec((HD // 2, frames), lambda i: (0, i)),
            pl.BlockSpec((HD // 2, frames), lambda i: (0, i)),
        ],
        out_specs=[
            pl.BlockSpec((1, PAIR, frames), lambda i: (i, 0, 0)),
            pl.BlockSpec((PAIR, frames), lambda i: (0, i)),
            pl.BlockSpec((PAIR, frames), lambda i: (0, i)),
            pl.BlockSpec((frames, PAIR), lambda i: (i, 0)),
            pl.BlockSpec((frames, PAIR), lambda i: (i, 0)),
        ],
        out_shape=[
            jax.ShapeDtypeStruct((chunks, PAIR, frames), jnp.bfloat16),
            jax.ShapeDtypeStruct((PAIR, length), jnp.bfloat16),
            jax.ShapeDtypeStruct((PAIR, length), jnp.bfloat16),
            jax.ShapeDtypeStruct((length, PAIR), jnp.bfloat16),
            jax.ShapeDtypeStruct((length, PAIR), jnp.bfloat16),
        ],
        compiler_params=pltpu.CompilerParams(vmem_limit_bytes=32 << 20),
        cost_estimate=pl.CostEstimate(
            flops=6 * length * width * PAIR, bytes_accessed=2 * length * (width + 5 * PAIR), transcendentals=0
        ),
        name="project_pair",
    )(normed_all, weight_rows, cos_all, sin_all)


def split_heads(block):
    row = lax.broadcasted_iota(jnp.int32, block.shape, 0)
    zero = jnp.zeros((), block.dtype)
    return jnp.where(row < HD, block, zero), jnp.where(row < HD, zero, block)


def attend_kernel(ends_ref, qt_ref, k_ref, vt_ref, low_ref, full_ref, total_ref, acc_ref, top_ref, *, size, length):
    start = pl.program_id(0) * size
    queries = split_heads(qt_ref[0])
    query_segment = segment_of(start + lax.broadcasted_iota(jnp.int32, (1, size), 1), ends_ref)
    first, whole_first, whole_last, last = key_blocks(ends_ref, start, size, length)
    acc_ref[...] = jnp.zeros_like(acc_ref)
    top_ref[...] = jnp.full_like(top_ref, masked_score)
    ones = jnp.ones((16, size), jnp.bfloat16)

    def step(masked):
        def run(block, carry):
            offset = pl.multiple_of(block * size, size)
            keys = k_ref[pl.ds(offset, size), :]
            scores = [dot_nn(keys, queries[head]) for head in range(2)]
            if masked:
                key_segment = segment_of(offset + lax.broadcasted_iota(jnp.int32, (size, 1), 0), ends_ref)
                same = key_segment == query_segment
                scores = [jnp.where(same, part, masked_score) for part in scores]
            old = [top_ref[head] for head in range(2)]
            new = [jnp.maximum(old[head], jnp.max(scores[head], axis=0, keepdims=True) * LOG2E) for head in range(2)]
            weights = [jnp.exp2(scores[head] * LOG2E - new[head]).astype(jnp.bfloat16) for head in range(2)]
            for head in range(2):
                values = jnp.concatenate([vt_ref[pl.ds(head * HD, HD), pl.ds(offset, size)], ones], axis=0)
                acc_ref[head] = acc_ref[head] * jnp.exp2(old[head] - new[head]) + dot_nn(values, weights[head])
                top_ref[head] = new[head]
            return carry

        return run

    lax.fori_loop(first, whole_first, step(True), 0)
    lax.fori_loop(whole_first, whole_last, step(False), 0)
    lax.fori_loop(whole_last, last, step(True), 0)
    for head in range(2):
        total = acc_ref[head, HD : HD + 1, :]
        attended = acc_ref[head, :HD, :] / total
        full_ref[0, head * HD : (head + 1) * HD, :] = attended
        low_ref[0, head * HD : (head + 1) * HD, :] = attended.astype(jnp.bfloat16)
        total_ref[0, head : head + 1, :] = jnp.log(total) * LOG2E + top_ref[head]


def attend_pair(ends, qt, k, vt):
    chunks, _, size = qt.shape
    length = k.shape[0]
    chunk = pl.BlockSpec((1, PAIR, size), lambda i, ends: (i, 0, 0))
    return pl.pallas_call(
        partial(attend_kernel, size=size, length=length),
        grid_spec=pltpu.PrefetchScalarGridSpec(
            num_scalar_prefetch=1,
            grid=(chunks,),
            in_specs=[
                chunk,
                pl.BlockSpec((length, PAIR), lambda i, ends: (0, 0)),
                pl.BlockSpec((PAIR, length), lambda i, ends: (0, 0)),
            ],
            out_specs=[chunk, chunk, pl.BlockSpec((1, 2, size), lambda i, ends: (i, 0, 0))],
            scratch_shapes=[pltpu.VMEM((2, HD + 16, size), jnp.float32), pltpu.VMEM((2, 1, size), jnp.float32)],
        ),
        out_shape=[
            jax.ShapeDtypeStruct((chunks, PAIR, size), jnp.bfloat16),
            jax.ShapeDtypeStruct((chunks, PAIR, size), jnp.float32),
            jax.ShapeDtypeStruct((chunks, 2, size), jnp.float32),
        ],
        compiler_params=pltpu.CompilerParams(vmem_limit_bytes=32 << 20),
        cost_estimate=pl.CostEstimate(
            flops=8 * length * length * HD, bytes_accessed=14 * length * PAIR, transcendentals=length * length
        ),
        name="attend_pair",
    )(ends, qt, k, vt)


def attend_back_kernel(
    ends_ref, qt_ref, gt_ref, full_ref, total_ref, k_ref, v_ref, kt_ref, cos_ref, sin_ref, out_ref,
    dk_ref, dv_ref, dq_ref, *, size, length, chunks,
):
    index = pl.program_id(0)
    start = index * size

    @pl.when(index == 0)
    def _():
        dk_ref[...] = jnp.zeros_like(dk_ref)
        dv_ref[...] = jnp.zeros_like(dv_ref)

    queries = split_heads(qt_ref[0])
    grads = split_heads(gt_ref[0])
    product = gt_ref[0].astype(jnp.float32) * full_ref[0]
    row_dot = [jnp.sum(product[head * HD : (head + 1) * HD], axis=0, keepdims=True) for head in range(2)]
    query_segment = segment_of(start + lax.broadcasted_iota(jnp.int32, (1, size), 1), ends_ref)
    first, whole_first, whole_last, last = key_blocks(ends_ref, start, size, length)
    dq_ref[...] = jnp.zeros_like(dq_ref)
    part = size // 2

    def step(masked):
        def run(block, carry):
            for piece in range(2):
                offset = pl.multiple_of(block * size + piece * part, part)
                rows = pl.ds(offset, part)
                keys, values = k_ref[rows, :], v_ref[rows, :]
                for head in range(2):
                    scores = dot_nn(keys, queries[head])
                    if masked:
                        key_segment = segment_of(offset + lax.broadcasted_iota(jnp.int32, (part, 1), 0), ends_ref)
                        scores = jnp.where(key_segment == query_segment, scores, masked_score)
                    weights = jnp.exp2(scores * LOG2E - total_ref[0, head : head + 1, :])
                    grad_weights = dot_nn(values, grads[head])
                    grad_scores = (weights * (grad_weights - row_dot[head])).astype(jnp.bfloat16)
                    dv_ref[rows, :] += dot_nt(weights.astype(jnp.bfloat16), grads[head])
                    dk_ref[rows, :] += dot_nt(grad_scores, queries[head])
                    dq_ref[head * HD : (head + 1) * HD, :] += dot_nn(
                        kt_ref[head * HD : (head + 1) * HD, rows], grad_scores
                    )
            return carry

        return run

    lax.fori_loop(first, whole_first, step(True), 0)
    lax.fori_loop(whole_first, whole_last, step(False), 0)
    lax.fori_loop(whole_last, last, step(True), 0)
    own = pl.ds(pl.multiple_of(start, size), size)
    out_ref[index, :PAIR, :] = turn(dq_ref[...] * SCALE, cos_ref[:, own], -sin_ref[:, own]).astype(jnp.bfloat16)

    @pl.when(index == chunks - 1)
    def _():
        for chunk in range(chunks):
            rows = pl.ds(chunk * size, size)
            turned = turn(dk_ref[rows, :].T, cos_ref[:, rows], -sin_ref[:, rows])
            out_ref[chunk, PAIR : 2 * PAIR, :] = turned.astype(jnp.bfloat16)
            out_ref[chunk, 2 * PAIR :, :] = dv_ref[rows, :].T.astype(jnp.bfloat16)


def attend_pair_back(ends, qt, gt, full, total, k, v, kt, cos_all, sin_all):
    chunks, _, size = qt.shape
    length = k.shape[0]
    chunk = pl.BlockSpec((1, PAIR, size), lambda i, ends: (i, 0, 0))

    def whole(shape):
        return pl.BlockSpec(shape, lambda i, ends: (0,) * len(shape))

    return pl.pallas_call(
        partial(attend_back_kernel, size=size, length=length, chunks=chunks),
        grid_spec=pltpu.PrefetchScalarGridSpec(
            num_scalar_prefetch=1,
            grid=(chunks,),
            in_specs=[
                chunk, chunk, chunk, pl.BlockSpec((1, 2, size), lambda i, ends: (i, 0, 0)),
                whole((length, PAIR)), whole((length, PAIR)), whole((PAIR, length)),
                whole((HD // 2, length)), whole((HD // 2, length)),
            ],
            out_specs=whole((chunks, 3 * PAIR, size)),
            scratch_shapes=[
                pltpu.VMEM((length, PAIR), jnp.float32),
                pltpu.VMEM((length, PAIR), jnp.float32),
                pltpu.VMEM((PAIR, size), jnp.float32),
            ],
        ),
        out_shape=jax.ShapeDtypeStruct((chunks, 3 * PAIR, size), jnp.bfloat16),
        compiler_params=pltpu.CompilerParams(vmem_limit_bytes=40 << 20),
        cost_estimate=pl.CostEstimate(
            flops=20 * length * length * HD, bytes_accessed=30 * length * PAIR, transcendentals=length * length
        ),
        name="attend_pair_back",
    )(ends, qt, gt, full, total, k, v, kt, cos_all, sin_all)


def pair_routes(count):
    routes = [[(source, (3 * source + piece) % count) for source in range(count)] for piece in range(3)]
    slots = [[0] * 3 for _ in range(count)]
    for piece in range(3):
        for source, target in routes[piece]:
            slots[target][piece] = (3 * source + piece) // count
    return routes, slots


def own_pair_columns(tile, count):
    routes, slots = pair_routes(count)
    width = tile.shape[1] // 3
    got = [lax.ppermute(tile[:, p * width : (p + 1) * width], "seq", routes[p]) for p in range(3)]
    slot_of = jnp.asarray(slots, jnp.int32)[lax.axis_index("seq")]
    columns = []
    for slot in range(3):
        columns.append(
            jnp.where(slot_of[0] == slot, got[0], jnp.where(slot_of[1] == slot, got[1], got[2]))
        )
    return jnp.concatenate(columns, axis=1)


def stored_columns(pair_tile, count):
    routes, slots = pair_routes(count)
    width = pair_tile.shape[1] // 3
    slot_of = jnp.asarray(slots, jnp.int32)[lax.axis_index("seq")]
    parts = [pair_tile[:, s * width : (s + 1) * width] for s in range(3)]
    back = []
    for piece in range(3):
        slot = slot_of[piece]
        chosen = jnp.where(slot == 0, parts[0], jnp.where(slot == 1, parts[1], parts[2]))
        back.append(lax.ppermute(chosen, "seq", [(target, source) for source, target in routes[piece]]))
    return jnp.concatenate(back, axis=1)


def gather_tiles(tile):
    rows, columns = tile.shape
    dp, seq = lax.axis_size("dp"), lax.axis_size("seq")
    pieces = lax.all_gather(tile, ("dp", "seq"), axis=0).reshape(dp, seq, rows, columns)
    return jnp.swapaxes(pieces, 1, 2).reshape(dp * rows, seq * columns)


def scatter_sum(partial_sum):
    rows, columns = partial_sum.shape
    dp, seq = lax.axis_size("dp"), lax.axis_size("seq")
    over_seq = lax.psum_scatter(
        partial_sum.astype(jnp.bfloat16), "seq", scatter_dimension=1, tiled=True
    ).astype(jnp.float32)
    return lax.psum_scatter(
        over_seq.astype(jnp.bfloat16), "dp", scatter_dimension=0, tiled=True
    ).astype(jnp.float32)


def norm_back(grad, stream, inverse, scale_part):
    unit = stream * inverse
    lifted = grad * (1.0 + scale_part)
    grad_stream = inverse * (lifted - unit * jnp.mean(lifted * unit, axis=-1, keepdims=True))
    return grad_stream, jnp.sum(grad * unit, axis=0), jnp.sum(grad, axis=0)


def local_paired(
    inputs, skip_input, time_embed, segment_ids, span_start, span_length, cotangent,
    skip_weight, ada_weight, qkv_weight, out_weight, up_weight, down_weight,
):
    seq = lax.axis_size("seq")
    dp = lax.axis_size("dp")
    frames, width = inputs.shape[1], inputs.shape[2]
    length = segment_ids.shape[1]
    segments = segment_ids[0]
    end_a = jnp.sum((segments < 1).astype(jnp.int32))
    end_b = jnp.sum((segments < 2).astype(jnp.int32))
    ends = jnp.stack([end_a, end_b])
    firsts = jnp.where(segments == 0, 0, jnp.where(segments == 1, end_a, end_b))
    position = jnp.arange(length, dtype=jnp.int32) - firsts
    half = HD // 2
    frequency = jnp.exp(-math.log(10000.0) * jnp.arange(half, dtype=jnp.float32) / half)
    angles = frequency[:, None] * position.astype(jnp.float32)[None, :]
    cos_all, sin_all = jnp.cos(angles), jnp.sin(angles)
    base = lax.axis_index("seq") * frames
    local_segments = lax.dynamic_slice_in_dim(segments, base, frames, 0)
    local_position = lax.dynamic_slice_in_dim(position, base, frames, 0)
    starts, lengths = span_start[0], span_length[0]

    def pick(table):
        return jnp.where(local_segments == 0, table[0], jnp.where(local_segments == 1, table[1], table[2]))

    span_begin = pick(starts)
    inside = jnp.logical_and(local_position >= span_begin, local_position < span_begin + pick(lengths))
    embed_all = lax.all_gather(time_embed, "dp", axis=0, tiled=True)
    embed_rows = width // dp
    embed_part = lax.dynamic_slice_in_dim(embed_all, lax.axis_index("dp") * embed_rows, embed_rows, 1)
    modulation_part = jnp.dot(embed_part, ada_weight, preferred_element_type=jnp.float32)
    modulation_part = lax.psum_scatter(modulation_part, "dp", scatter_dimension=0, tiled=True)
    modulation = lax.all_gather(modulation_part, "seq", axis=1, tiled=True)
    scale_one = modulation[:, :width]
    shift_one = modulation[:, width : 2 * width]
    scale_two = modulation[:, 2 * width : 3 * width]
    shift_two = modulation[:, 3 * width :]

    skip_full = gather_tiles(skip_weight)
    pair_tile = own_pair_columns(qkv_weight, seq)
    pair_weight = lax.all_gather(pair_tile, "dp", axis=0, tiled=True)
    joined = jnp.concatenate([inputs[0], skip_input[0]], axis=-1)
    stream = dot_nn(joined, skip_full)
    inverse_one = lax.rsqrt(jnp.mean(stream * stream, axis=-1, keepdims=True) + epsilon)
    normed_one = (stream * inverse_one * (1.0 + scale_one) + shift_one).astype(jnp.bfloat16)
    normed_all = lax.all_gather(normed_one, "seq", axis=0)
    qt, kt, vt, keys, values = project_pair(normed_all, pair_weight.T, cos_all, sin_all)
    attended_pair, attended_wide, total = attend_pair(ends, qt, keys, vt)
    attended = lax.all_to_all(attended_pair, "seq", 0, 0).reshape(width, frames)
    out_full = gather_tiles(out_weight)
    up_full = gather_tiles(up_weight)
    down_full = gather_tiles(down_weight)
    middle = stream + dot_tn(attended, out_full)
    inverse_two = lax.rsqrt(jnp.mean(middle * middle, axis=-1, keepdims=True) + epsilon)
    normed_two = (middle * inverse_two * (1.0 + scale_two) + shift_two).astype(jnp.bfloat16)
    up_proj = dot_nn(normed_two, up_full)
    hidden = jax.nn.gelu(up_proj, approximate=True).astype(jnp.bfloat16)
    layer_output = (middle + dot_nn(hidden, down_full)).astype(jnp.bfloat16)

    grad_out = cotangent[0].astype(jnp.float32) * inside[:, None].astype(jnp.float32)
    grad_low = grad_out.astype(jnp.bfloat16)
    grad_hidden = dot_nt(grad_low, down_full)
    _, gelu_pull = jax.vjp(partial(jax.nn.gelu, approximate=True), up_proj)
    grad_up_act = gelu_pull(grad_hidden)[0].astype(jnp.bfloat16)
    grad_normed_two = dot_nt(grad_up_act, up_full)
    grad_middle_norm, grad_scale_two, grad_shift_two = norm_back(grad_normed_two, middle, inverse_two, scale_two)
    grad_middle = grad_out + grad_middle_norm
    grad_middle_low = grad_middle.astype(jnp.bfloat16)
    grad_attended = dot_nt(out_full, grad_middle_low).astype(jnp.bfloat16)
    grad_pair = lax.all_to_all(grad_attended.reshape(seq, PAIR, frames), "seq", 0, 0)
    down_tile = scatter_sum(dot_tn(hidden, grad_low))
    up_tile = scatter_sum(dot_tn(normed_two, grad_up_act))
    out_tile = scatter_sum(dot_nn(attended, grad_middle_low))

    grad_projected = attend_pair_back(ends, qt, grad_pair, attended_wide, total, keys, values, kt, cos_all, sin_all)
    grad_local = lax.all_to_all(grad_projected, "seq", 0, 0)
    pair_all = lax.all_gather(pair_tile, ("dp", "seq"), axis=0).reshape(dp, seq, width // dp, 3 * PAIR)
    pair_all = pair_all.transpose(0, 2, 1, 3).reshape(width, 3 * width)
    grad_normed_one = lax.dot_general(
        grad_local.reshape(3 * width, frames), pair_all, (((0,), (1,)), ((), ())),
        preferred_element_type=jnp.float32,
    )
    grad_pair_weight = jnp.einsum(
        "icf,ifd->cd", grad_projected, normed_all, preferred_element_type=jnp.float32
    )
    grad_pair_tile = lax.psum_scatter(
        grad_pair_weight.astype(jnp.bfloat16), "dp", scatter_dimension=1, tiled=True
    )
    qkv_tile = stored_columns(grad_pair_tile.T, seq).astype(jnp.float32)
    grad_stream_norm, grad_scale_one, grad_shift_one = norm_back(grad_normed_one, stream, inverse_one, scale_one)
    grad_stream = (grad_middle + grad_stream_norm).astype(jnp.bfloat16)
    grad_joined = dot_nt(grad_stream, skip_full)
    skip_tile = scatter_sum(dot_tn(joined, grad_stream))
    grad_modulation = jnp.concatenate([grad_scale_one, grad_shift_one, grad_scale_two, grad_shift_two])
    grad_modulation = lax.psum_scatter(grad_modulation, "seq", scatter_dimension=0, tiled=True)
    grad_modulation = lax.all_gather(grad_modulation[None], "dp", axis=0, tiled=True)
    ada_tile = lax.dot_general(
        embed_part.astype(jnp.float32), grad_modulation, (((0,), (0,)), ((), ())),
        precision=lax.Precision.HIGHEST,
    )
    return (
        layer_output[None],
        grad_joined[None, :, :width],
        grad_joined[None, :, width:],
        skip_tile,
        ada_tile,
        qkv_tile,
        out_tile,
        up_tile,
        down_tile,
    )


def solution(mesh):
    in_specs = (
        P("dp", "seq", None),
        P("dp", "seq", None),
        P("dp", None),
        P("dp", None),
        P("dp", None),
        P("dp", None),
        P("dp", "seq", None),
        P("dp", "seq"),
        P("dp", "seq"),
        P("dp", "seq"),
        P("dp", "seq"),
        P("dp", "seq"),
        P("dp", "seq"),
    )
    out_specs = (
        P("dp", "seq", None),
        P("dp", "seq", None),
        P("dp", "seq", None),
        P("dp", "seq"),
        P("dp", "seq"),
        P("dp", "seq"),
        P("dp", "seq"),
        P("dp", "seq"),
        P("dp", "seq"),
    )
    seq_size = mesh.shape["seq"]
    paired = H == 2 * seq_size and seq_size % 3 != 0
    body = local_paired if paired else local_general
    return jax.shard_map(body, mesh=mesh, in_specs=in_specs, out_specs=out_specs, check_vma=False)
```

```python
from functools import partial
import math

import jax
import jax.numpy as jnp
from jax import lax
from jax.experimental import pallas as pl
from jax.experimental.pallas import tpu as pltpu
from jax.sharding import PartitionSpec as P

H = 16
HD = 64
UTT = 3
HG = 8


epsilon = 1e-06
masked_score = -1e30


def ada_norm(stream, scale_part, shift_part):
    inverse = lax.rsqrt(jnp.mean(stream * stream, axis=-1, keepdims=True) + epsilon)
    return stream * inverse * (1.0 + scale_part) + shift_part


def rotate(tensor, cosine, sine_part):
    half_width = tensor.shape[-1] // 2
    lower_half = tensor[..., :half_width]
    upper_half = tensor[..., half_width:]
    cos_wide = cosine[..., None, :]
    sin_wide = sine_part[..., None, :]
    return jnp.concatenate(
        [
            lower_half * cos_wide - upper_half * sin_wide,
            lower_half * sin_wide + upper_half * cos_wide,
        ],
        axis=-1,
    )


def rotary_tables(position, half_width):
    frequency = jnp.exp(-math.log(10000.0) * jnp.arange(half_width, dtype=jnp.float32) / half_width)
    angles = position.astype(jnp.float32)[..., None] * frequency
    return (jnp.cos(angles), jnp.sin(angles))


def gather_weights(skip_tile, ada_tile, qkv_tile, out_tile, up_tile, down_tile):
    row_full = (
        lax.all_gather(skip_tile, "dp", axis=0, tiled=True),
        lax.all_gather(ada_tile, "dp", axis=0, tiled=True),
        lax.all_gather(qkv_tile, "dp", axis=0, tiled=True),
        lax.all_gather(out_tile, "dp", axis=0, tiled=True),
        lax.all_gather(up_tile, "dp", axis=0, tiled=True),
        lax.all_gather(down_tile, "dp", axis=0, tiled=True),
    )
    return (
        lax.all_gather(row_full[0], "seq", axis=1, tiled=True),
        lax.all_gather(row_full[1], "seq", axis=1, tiled=True),
        lax.all_gather(row_full[2], "seq", axis=1, tiled=True),
        lax.all_gather(row_full[3], "seq", axis=1, tiled=True),
        lax.all_gather(row_full[4], "seq", axis=1, tiled=True),
        lax.all_gather(row_full[5], "seq", axis=1, tiled=True),
    )


def group_scores(query_part, key_part, allowed, factor):
    scores = (
        jnp.einsum("qhd,khd->hqk", query_part, key_part, preferred_element_type=jnp.float32)
        * factor
    )
    return jnp.where(allowed[None], scores, masked_score)


def attend_row(queries, key_rows, value_rows, segment_local, segment_full):
    factor = queries.shape[2] ** (-0.5)
    allowed = segment_local[:, None] == segment_full[None, :]
    outputs = []
    totals = []
    for head_start in range(0, H, HG):
        head_end = head_start + HG
        scores = group_scores(
            queries[:, head_start:head_end], key_rows[:, head_start:head_end], allowed, factor
        )
        log_total = jax.nn.logsumexp(scores, axis=-1)
        weights = jnp.exp(scores - log_total[..., None]).astype(jnp.bfloat16)
        outputs.append(
            jnp.einsum(
                "hqk,khd->qhd",
                weights,
                value_rows[:, head_start:head_end],
                preferred_element_type=jnp.float32,
            )
        )
        totals.append(log_total)
    return (jnp.concatenate(outputs, axis=1), jnp.concatenate(totals, axis=0))


def attend_back(
    queries, key_rows, value_rows, segment_local, segment_full, log_total, grad_attended, row_dot
):
    factor = queries.shape[2] ** (-0.5)
    allowed = segment_local[:, None] == segment_full[None, :]
    query_grads = []
    key_grads = []
    value_grads = []
    for head_start in range(0, H, HG):
        head_end = head_start + HG
        key_part = key_rows[:, head_start:head_end]
        query_part = queries[:, head_start:head_end]
        grad_part = grad_attended[:, head_start:head_end]
        scores = group_scores(query_part, key_part, allowed, factor)
        weights = jnp.exp(scores - log_total[head_start:head_end][..., None])
        weights_low = weights.astype(jnp.bfloat16)
        value_grads.append(
            jnp.einsum("hqk,qhd->khd", weights_low, grad_part, preferred_element_type=jnp.float32)
        )
        grad_weights = jnp.einsum(
            "qhd,khd->hqk",
            grad_part,
            value_rows[:, head_start:head_end],
            preferred_element_type=jnp.float32,
        )
        grad_scores = (weights * (grad_weights - row_dot[head_start:head_end][..., None])).astype(
            jnp.bfloat16
        )
        query_grads.append(
            jnp.einsum("hqk,khd->qhd", grad_scores, key_part, preferred_element_type=jnp.float32)
            * factor
        )
        key_grads.append(
            jnp.einsum("hqk,qhd->khd", grad_scores, query_part, preferred_element_type=jnp.float32)
            * factor
        )
    return (
        jnp.concatenate(query_grads, axis=1),
        jnp.concatenate(key_grads, axis=1),
        jnp.concatenate(value_grads, axis=1),
    )


def local_general(
    inputs,
    skip_input,
    time_embed,
    segment_ids,
    span_start,
    span_length,
    cotangent,
    skip_weight,
    ada_weight,
    qkv_weight,
    out_weight,
    up_weight,
    down_weight,
):
    row_count = inputs.shape[0]
    frames = inputs.shape[1]
    model_width = inputs.shape[2]
    row_length = segment_ids.shape[1]
    frame_base = lax.axis_index("seq") * frames
    utterance = jnp.arange(UTT, dtype=jnp.int32)
    member = (segment_ids[:, :, None] == utterance[None, None, :]).astype(jnp.int32)
    counts = jnp.sum(member, axis=1)
    firsts = jnp.cumsum(counts, axis=1) - counts
    local_member = lax.dynamic_slice_in_dim(member, frame_base, frames, 1)
    local_segments = lax.dynamic_slice_in_dim(segment_ids, frame_base, frames, 1)
    local_frames = frame_base + jnp.arange(frames, dtype=jnp.int32)
    position = local_frames[None, :] - jnp.sum(local_member * firsts[:, None, :], axis=2)
    span_begin = jnp.sum(local_member * span_start[:, None, :], axis=2)
    span_end = span_begin + jnp.sum(local_member * span_length[:, None, :], axis=2)
    inside = jnp.logical_and(position >= span_begin, position < span_end)
    cosine, sine_part = rotary_tables(position, HD // 2)
    skip_full, ada_full, qkv_full, out_full, up_full, down_full = gather_weights(
        skip_weight, ada_weight, qkv_weight, out_weight, up_weight, down_weight
    )
    joined = jnp.concatenate([inputs, skip_input], axis=-1)
    stream = jnp.einsum("rfc,cd->rfd", joined, skip_full, preferred_element_type=jnp.float32)
    modulation = jnp.dot(time_embed, ada_full, preferred_element_type=jnp.float32)[:, None, :]
    scale_one = modulation[..., :model_width]
    shift_one = modulation[..., model_width : 2 * model_width]
    scale_two = modulation[..., 2 * model_width : 3 * model_width]
    shift_two = modulation[..., 3 * model_width :]
    normed_one = ada_norm(stream, scale_one, shift_one).astype(jnp.bfloat16)
    projected = jnp.einsum("rfd,de->rfe", normed_one, qkv_full, preferred_element_type=jnp.float32)
    queries = rotate(
        projected[..., :model_width].reshape(row_count, frames, H, HD), cosine, sine_part
    ).astype(jnp.bfloat16)
    key_rotated = rotate(
        projected[..., model_width : 2 * model_width].reshape(row_count, frames, H, HD),
        cosine,
        sine_part,
    )
    key_local = key_rotated.reshape(row_count, frames, model_width).astype(jnp.bfloat16)
    value_local = projected[..., 2 * model_width :].astype(jnp.bfloat16)
    key_all, value_all = (
        lax.all_gather(key_local, "seq", axis=1, tiled=True),
        lax.all_gather(value_local, "seq", axis=1, tiled=True),
    )

    def forward_row(row_items):
        query_row, key_row, value_row, local_row, full_row = row_items
        return attend_row(
            query_row,
            key_row.reshape(row_length, H, HD),
            value_row.reshape(row_length, H, HD),
            local_row,
            full_row,
        )

    attended, log_total = lax.map(
        forward_row, (queries, key_all, value_all, local_segments, segment_ids)
    )
    attended = attended.reshape(row_count, frames, model_width)
    attended_low = attended.astype(jnp.bfloat16)
    middle = stream + jnp.einsum(
        "rfe,ed->rfd", attended_low, out_full, preferred_element_type=jnp.float32
    )
    normed_two = ada_norm(middle, scale_two, shift_two).astype(jnp.bfloat16)
    up_proj = jnp.einsum("rfd,di->rfi", normed_two, up_full, preferred_element_type=jnp.float32)
    hidden = jax.nn.gelu(up_proj, approximate=True).astype(jnp.bfloat16)
    down_proj = jnp.einsum("rfi,id->rfd", hidden, down_full, preferred_element_type=jnp.float32)
    layer_output = (middle + down_proj).astype(jnp.bfloat16)
    skip_full, ada_full, qkv_full, out_full, up_full, down_full = gather_weights(
        skip_weight, ada_weight, qkv_weight, out_weight, up_weight, down_weight
    )
    grad_out = cotangent.astype(jnp.float32) * inside[..., None].astype(jnp.float32)
    grad_low = grad_out.astype(jnp.bfloat16)
    grad_hidden = jnp.einsum("rfd,id->rfi", grad_low, down_full, preferred_element_type=jnp.float32)
    _, gelu_pull = jax.vjp(partial(jax.nn.gelu, approximate=True), up_proj)
    grad_up_act = gelu_pull(grad_hidden)[0].astype(jnp.bfloat16)
    grad_normed_two = jnp.einsum(
        "rfi,di->rfd", grad_up_act, up_full, preferred_element_type=jnp.float32
    )
    _, norm_pull_two = jax.vjp(ada_norm, middle, scale_two, shift_two)
    grad_middle_norm, grad_scale_two, grad_shift_two = norm_pull_two(grad_normed_two)
    grad_middle = grad_out + grad_middle_norm
    grad_middle_low = grad_middle.astype(jnp.bfloat16)
    grad_attended = jnp.einsum(
        "rfd,ed->rfe", grad_middle_low, out_full, preferred_element_type=jnp.float32
    ).astype(jnp.bfloat16)
    row_dot = jnp.sum(
        (grad_attended.astype(jnp.float32) * attended).reshape(row_count, frames, H, HD), axis=-1
    )
    row_dot = jnp.swapaxes(row_dot, 1, 2)
    grad_heads = grad_attended.reshape(row_count, frames, H, HD)

    def backward_row(row_items):
        query_row, key_row, value_row, local_row, full_row, total_row, grad_row, dot_row = row_items
        return attend_back(
            query_row,
            key_row.reshape(row_length, H, HD),
            value_row.reshape(row_length, H, HD),
            local_row,
            full_row,
            total_row,
            grad_row,
            dot_row,
        )

    grad_queries, grad_keys, grad_values = lax.map(
        backward_row,
        (queries, key_all, value_all, local_segments, segment_ids, log_total, grad_heads, row_dot),
    )
    key_share, value_share = (
        lax.psum_scatter(
            grad_keys.reshape(row_count, row_length, model_width).astype(jnp.bfloat16),
            "seq",
            scatter_dimension=1,
            tiled=True,
        ).astype(jnp.float32),
        lax.psum_scatter(
            grad_values.reshape(row_count, row_length, model_width).astype(jnp.bfloat16),
            "seq",
            scatter_dimension=1,
            tiled=True,
        ).astype(jnp.float32),
    )
    _, rotate_pull = jax.vjp(
        partial(rotate, cosine=cosine, sine_part=sine_part),
        jnp.zeros((row_count, frames, H, HD), jnp.float32),
    )
    grad_query_raw = rotate_pull(grad_queries)[0].reshape(row_count, frames, model_width)
    grad_key_raw = rotate_pull(key_share.reshape(row_count, frames, H, HD))[0].reshape(
        row_count, frames, model_width
    )
    grad_projected = jnp.concatenate([grad_query_raw, grad_key_raw, value_share], axis=-1).astype(
        jnp.bfloat16
    )
    grad_normed_one = jnp.einsum(
        "rfe,de->rfd", grad_projected, qkv_full, preferred_element_type=jnp.float32
    )
    _, norm_pull_one = jax.vjp(ada_norm, stream, scale_one, shift_one)
    grad_stream_norm, grad_scale_one, grad_shift_one = norm_pull_one(grad_normed_one)
    grad_stream = (grad_middle + grad_stream_norm).astype(jnp.bfloat16)
    grad_joined = jnp.einsum(
        "rfd,cd->rfc", grad_stream, skip_full, preferred_element_type=jnp.float32
    )
    grad_modulation = jnp.concatenate(
        [grad_scale_one, grad_shift_one, grad_scale_two, grad_shift_two], axis=-1
    )[:, 0, :]
    grad_down = jnp.einsum("rfi,rfd->id", hidden, grad_low, preferred_element_type=jnp.float32)
    grad_up = jnp.einsum("rfd,rfi->di", normed_two, grad_up_act, preferred_element_type=jnp.float32)
    grad_attn_out = jnp.einsum(
        "rfe,rfd->ed", attended_low, grad_middle_low, preferred_element_type=jnp.float32
    )
    grad_qkv = jnp.einsum(
        "rfd,rfe->de", normed_one, grad_projected, preferred_element_type=jnp.float32
    )
    grad_skip_w = jnp.einsum("rfc,rfd->cd", joined, grad_stream, preferred_element_type=jnp.float32)
    grad_ada = jnp.einsum(
        "rd,re->de",
        time_embed.astype(jnp.float32),
        grad_modulation,
        precision=lax.Precision.HIGHEST,
    )
    column_parts = (
        lax.psum_scatter(
            grad_skip_w.astype(jnp.bfloat16), "seq", scatter_dimension=1, tiled=True
        ).astype(jnp.float32),
        lax.psum_scatter(
            grad_ada.astype(jnp.bfloat16), "seq", scatter_dimension=1, tiled=True
        ).astype(jnp.float32),
        lax.psum_scatter(
            grad_qkv.astype(jnp.bfloat16), "seq", scatter_dimension=1, tiled=True
        ).astype(jnp.float32),
        lax.psum_scatter(
            grad_attn_out.astype(jnp.bfloat16), "seq", scatter_dimension=1, tiled=True
        ).astype(jnp.float32),
        lax.psum_scatter(
            grad_up.astype(jnp.bfloat16), "seq", scatter_dimension=1, tiled=True
        ).astype(jnp.float32),
        lax.psum_scatter(
            grad_down.astype(jnp.bfloat16), "seq", scatter_dimension=1, tiled=True
        ).astype(jnp.float32),
    )
    weight_tiles = (
        lax.psum_scatter(
            column_parts[0].astype(jnp.bfloat16), "dp", scatter_dimension=0, tiled=True
        ).astype(jnp.float32),
        lax.psum_scatter(
            column_parts[1].astype(jnp.bfloat16), "dp", scatter_dimension=0, tiled=True
        ).astype(jnp.float32),
        lax.psum_scatter(
            column_parts[2].astype(jnp.bfloat16), "dp", scatter_dimension=0, tiled=True
        ).astype(jnp.float32),
        lax.psum_scatter(
            column_parts[3].astype(jnp.bfloat16), "dp", scatter_dimension=0, tiled=True
        ).astype(jnp.float32),
        lax.psum_scatter(
            column_parts[4].astype(jnp.bfloat16), "dp", scatter_dimension=0, tiled=True
        ).astype(jnp.float32),
        lax.psum_scatter(
            column_parts[5].astype(jnp.bfloat16), "dp", scatter_dimension=0, tiled=True
        ).astype(jnp.float32),
    )
    skip_tile, ada_tile, qkv_tile, out_tile, up_tile, down_tile = weight_tiles
    return (
        layer_output,
        grad_joined[..., :model_width],
        grad_joined[..., model_width:],
        skip_tile,
        ada_tile,
        qkv_tile,
        out_tile,
        up_tile,
        down_tile,
    )


LOG2E = 1.4426950408889634
SCALE = HD**-0.5
PAIR = 2 * HD


def dot_nn(a, b):
    return lax.dot_general(a, b, (((1,), (0,)), ((), ())), preferred_element_type=jnp.float32)


def dot_nt(a, b):
    return lax.dot_general(a, b, (((1,), (1,)), ((), ())), preferred_element_type=jnp.float32)


def dot_tn(a, b):
    return lax.dot_general(a, b, (((0,), (0,)), ((), ())), preferred_element_type=jnp.float32)


def segment_of(index, ends_ref):
    return (index >= ends_ref[0]).astype(jnp.int32) + (index >= ends_ref[1]).astype(jnp.int32)


def segment_span(ends_ref, first, last, length):
    end_a, end_b = ends_ref[0], ends_ref[1]
    low = jnp.where(first < end_a, 0, jnp.where(first < end_b, end_a, end_b))
    high = jnp.where(last < end_a, end_a, jnp.where(last < end_b, end_b, length))
    return low, high


def key_blocks(ends_ref, start, size, length):
    low, high = segment_span(ends_ref, start, start + size - 1, length)
    low_last, _ = segment_span(ends_ref, start + size - 1, start, length)
    first = low // size
    last = (high + size - 1) // size
    whole_first = jnp.where(low == low_last, (low + size - 1) // size, last)
    whole_first = jnp.minimum(whole_first, last)
    whole_last = jnp.where(low == low_last, jnp.maximum(high // size, whole_first), last)
    return first, whole_first, whole_last, last


def turn(pair, cosine, sine_part):
    half = HD // 2
    rows = []
    for head in range(2):
        lower = pair[head * HD : head * HD + half]
        upper = pair[head * HD + half : (head + 1) * HD]
        rows += [lower * cosine - upper * sine_part, lower * sine_part + upper * cosine]
    return jnp.concatenate(rows, axis=0)


def project_kernel(normed_ref, weight_ref, cos_ref, sin_ref, qt_ref, kt_ref, vt_ref, k_ref, v_ref):
    projected = dot_nt(weight_ref[...], normed_ref[0])
    cosine, sine_part = cos_ref[...], sin_ref[...]
    queries = turn(projected[:PAIR], cosine, sine_part).astype(jnp.bfloat16)
    keys = turn(projected[PAIR : 2 * PAIR], cosine, sine_part)
    values = projected[2 * PAIR :]
    qt_ref[0] = (queries.astype(jnp.float32) * SCALE).astype(jnp.bfloat16)
    kt_ref[...] = keys.astype(jnp.bfloat16)
    vt_ref[...] = values.astype(jnp.bfloat16)
    k_ref[...] = keys.T.astype(jnp.bfloat16)
    v_ref[...] = values.T.astype(jnp.bfloat16)


def project_pair(normed_all, weight_rows, cos_all, sin_all):
    chunks, frames, width = normed_all.shape
    length = chunks * frames
    return pl.pallas_call(
        project_kernel,
        grid=(chunks,),
        in_specs=[
            pl.BlockSpec((1, frames, width), lambda i: (i, 0, 0)),
            pl.BlockSpec((3 * PAIR, width), lambda i: (0, 0)),
            pl.BlockSpec((HD // 2, frames), lambda i: (0, i)),
            pl.BlockSpec((HD // 2, frames), lambda i: (0, i)),
        ],
        out_specs=[
            pl.BlockSpec((1, PAIR, frames), lambda i: (i, 0, 0)),
            pl.BlockSpec((PAIR, frames), lambda i: (0, i)),
            pl.BlockSpec((PAIR, frames), lambda i: (0, i)),
            pl.BlockSpec((frames, PAIR), lambda i: (i, 0)),
            pl.BlockSpec((frames, PAIR), lambda i: (i, 0)),
        ],
        out_shape=[
            jax.ShapeDtypeStruct((chunks, PAIR, frames), jnp.bfloat16),
            jax.ShapeDtypeStruct((PAIR, length), jnp.bfloat16),
            jax.ShapeDtypeStruct((PAIR, length), jnp.bfloat16),
            jax.ShapeDtypeStruct((length, PAIR), jnp.bfloat16),
            jax.ShapeDtypeStruct((length, PAIR), jnp.bfloat16),
        ],
        compiler_params=pltpu.CompilerParams(vmem_limit_bytes=32 << 20),
        cost_estimate=pl.CostEstimate(
            flops=6 * length * width * PAIR, bytes_accessed=2 * length * (width + 5 * PAIR), transcendentals=0
        ),
        name="project_pair",
    )(normed_all, weight_rows, cos_all, sin_all)


def split_heads(block):
    row = lax.broadcasted_iota(jnp.int32, block.shape, 0)
    zero = jnp.zeros((), block.dtype)
    return jnp.where(row < HD, block, zero), jnp.where(row < HD, zero, block)


def attend_kernel(ends_ref, qt_ref, k_ref, vt_ref, low_ref, full_ref, total_ref, acc_ref, top_ref, *, size, length):
    start = pl.program_id(0) * size
    queries = split_heads(qt_ref[0])
    query_segment = segment_of(start + lax.broadcasted_iota(jnp.int32, (1, size), 1), ends_ref)
    first, whole_first, whole_last, last = key_blocks(ends_ref, start, size, length)
    acc_ref[...] = jnp.zeros_like(acc_ref)
    top_ref[...] = jnp.full_like(top_ref, masked_score)
    ones = jnp.ones((16, size), jnp.bfloat16)

    def step(masked):
        def run(block, carry):
            offset = pl.multiple_of(block * size, size)
            keys = k_ref[pl.ds(offset, size), :]
            scores = [dot_nn(keys, queries[head]) for head in range(2)]
            if masked:
                key_segment = segment_of(offset + lax.broadcasted_iota(jnp.int32, (size, 1), 0), ends_ref)
                same = key_segment == query_segment
                scores = [jnp.where(same, part, masked_score) for part in scores]
            old = [top_ref[head] for head in range(2)]
            new = [jnp.maximum(old[head], jnp.max(scores[head], axis=0, keepdims=True) * LOG2E) for head in range(2)]
            weights = [jnp.exp2(scores[head] * LOG2E - new[head]).astype(jnp.bfloat16) for head in range(2)]
            for head in range(2):
                values = jnp.concatenate([vt_ref[pl.ds(head * HD, HD), pl.ds(offset, size)], ones], axis=0)
                acc_ref[head] = acc_ref[head] * jnp.exp2(old[head] - new[head]) + dot_nn(values, weights[head])
                top_ref[head] = new[head]
            return carry

        return run

    lax.fori_loop(first, whole_first, step(True), 0)
    lax.fori_loop(whole_first, whole_last, step(False), 0)
    lax.fori_loop(whole_last, last, step(True), 0)
    for head in range(2):
        total = acc_ref[head, HD : HD + 1, :]
        attended = acc_ref[head, :HD, :] / total
        full_ref[0, head * HD : (head + 1) * HD, :] = attended
        low_ref[0, head * HD : (head + 1) * HD, :] = attended.astype(jnp.bfloat16)
        total_ref[0, head : head + 1, :] = jnp.log(total) * LOG2E + top_ref[head]


def attend_pair(ends, qt, k, vt):
    chunks, _, size = qt.shape
    length = k.shape[0]
    chunk = pl.BlockSpec((1, PAIR, size), lambda i, ends: (i, 0, 0))
    return pl.pallas_call(
        partial(attend_kernel, size=size, length=length),
        grid_spec=pltpu.PrefetchScalarGridSpec(
            num_scalar_prefetch=1,
            grid=(chunks,),
            in_specs=[
                chunk,
                pl.BlockSpec((length, PAIR), lambda i, ends: (0, 0)),
                pl.BlockSpec((PAIR, length), lambda i, ends: (0, 0)),
            ],
            out_specs=[chunk, chunk, pl.BlockSpec((1, 2, size), lambda i, ends: (i, 0, 0))],
            scratch_shapes=[pltpu.VMEM((2, HD + 16, size), jnp.float32), pltpu.VMEM((2, 1, size), jnp.float32)],
        ),
        out_shape=[
            jax.ShapeDtypeStruct((chunks, PAIR, size), jnp.bfloat16),
            jax.ShapeDtypeStruct((chunks, PAIR, size), jnp.float32),
            jax.ShapeDtypeStruct((chunks, 2, size), jnp.float32),
        ],
        compiler_params=pltpu.CompilerParams(vmem_limit_bytes=32 << 20),
        cost_estimate=pl.CostEstimate(
            flops=8 * length * length * HD, bytes_accessed=14 * length * PAIR, transcendentals=length * length
        ),
        name="attend_pair",
    )(ends, qt, k, vt)


def attend_back_kernel(
    ends_ref, qt_ref, gt_ref, full_ref, total_ref, k_ref, v_ref, kt_ref, cos_ref, sin_ref, out_ref,
    dk_ref, dv_ref, dq_ref, *, size, length, chunks,
):
    index = pl.program_id(0)
    start = index * size

    @pl.when(index == 0)
    def _():
        dk_ref[...] = jnp.zeros_like(dk_ref)
        dv_ref[...] = jnp.zeros_like(dv_ref)

    queries = split_heads(qt_ref[0])
    grads = split_heads(gt_ref[0])
    product = gt_ref[0].astype(jnp.float32) * full_ref[0]
    row_dot = [jnp.sum(product[head * HD : (head + 1) * HD], axis=0, keepdims=True) for head in range(2)]
    query_segment = segment_of(start + lax.broadcasted_iota(jnp.int32, (1, size), 1), ends_ref)
    first, whole_first, whole_last, last = key_blocks(ends_ref, start, size, length)
    dq_ref[...] = jnp.zeros_like(dq_ref)
    part = size // 2

    def step(masked):
        def run(block, carry):
            for piece in range(2):
                offset = pl.multiple_of(block * size + piece * part, part)
                rows = pl.ds(offset, part)
                keys, values = k_ref[rows, :], v_ref[rows, :]
                for head in range(2):
                    scores = dot_nn(keys, queries[head])
                    if masked:
                        key_segment = segment_of(offset + lax.broadcasted_iota(jnp.int32, (part, 1), 0), ends_ref)
                        scores = jnp.where(key_segment == query_segment, scores, masked_score)
                    weights = jnp.exp2(scores * LOG2E - total_ref[0, head : head + 1, :])
                    grad_weights = dot_nn(values, grads[head])
                    grad_scores = (weights * (grad_weights - row_dot[head])).astype(jnp.bfloat16)
                    dv_ref[rows, :] += dot_nt(weights.astype(jnp.bfloat16), grads[head])
                    dk_ref[rows, :] += dot_nt(grad_scores, queries[head])
                    dq_ref[head * HD : (head + 1) * HD, :] += dot_nn(
                        kt_ref[head * HD : (head + 1) * HD, rows], grad_scores
                    )
            return carry

        return run

    lax.fori_loop(first, whole_first, step(True), 0)
    lax.fori_loop(whole_first, whole_last, step(False), 0)
    lax.fori_loop(whole_last, last, step(True), 0)
    own = pl.ds(pl.multiple_of(start, size), size)
    out_ref[index, :PAIR, :] = turn(dq_ref[...] * SCALE, cos_ref[:, own], -sin_ref[:, own]).astype(jnp.bfloat16)

    @pl.when(index == chunks - 1)
    def _():
        for chunk in range(chunks):
            rows = pl.ds(chunk * size, size)
            turned = turn(dk_ref[rows, :].T, cos_ref[:, rows], -sin_ref[:, rows])
            out_ref[chunk, PAIR : 2 * PAIR, :] = turned.astype(jnp.bfloat16)
            out_ref[chunk, 2 * PAIR :, :] = dv_ref[rows, :].T.astype(jnp.bfloat16)


def attend_pair_back(ends, qt, gt, full, total, k, v, kt, cos_all, sin_all):
    chunks, _, size = qt.shape
    length = k.shape[0]
    chunk = pl.BlockSpec((1, PAIR, size), lambda i, ends: (i, 0, 0))

    def whole(shape):
        return pl.BlockSpec(shape, lambda i, ends: (0,) * len(shape))

    return pl.pallas_call(
        partial(attend_back_kernel, size=size, length=length, chunks=chunks),
        grid_spec=pltpu.PrefetchScalarGridSpec(
            num_scalar_prefetch=1,
            grid=(chunks,),
            in_specs=[
                chunk, chunk, chunk, pl.BlockSpec((1, 2, size), lambda i, ends: (i, 0, 0)),
                whole((length, PAIR)), whole((length, PAIR)), whole((PAIR, length)),
                whole((HD // 2, length)), whole((HD // 2, length)),
            ],
            out_specs=whole((chunks, 3 * PAIR, size)),
            scratch_shapes=[
                pltpu.VMEM((length, PAIR), jnp.float32),
                pltpu.VMEM((length, PAIR), jnp.float32),
                pltpu.VMEM((PAIR, size), jnp.float32),
            ],
        ),
        out_shape=jax.ShapeDtypeStruct((chunks, 3 * PAIR, size), jnp.bfloat16),
        compiler_params=pltpu.CompilerParams(vmem_limit_bytes=40 << 20),
        cost_estimate=pl.CostEstimate(
            flops=20 * length * length * HD, bytes_accessed=30 * length * PAIR, transcendentals=length * length
        ),
        name="attend_pair_back",
    )(ends, qt, gt, full, total, k, v, kt, cos_all, sin_all)


def pair_routes(count):
    routes = [[(source, (3 * source + piece) % count) for source in range(count)] for piece in range(3)]
    slots = [[0] * 3 for _ in range(count)]
    for piece in range(3):
        for source, target in routes[piece]:
            slots[target][piece] = (3 * source + piece) // count
    return routes, slots


def own_pair_columns(tile, count):
    routes, slots = pair_routes(count)
    width = tile.shape[1] // 3
    got = [lax.ppermute(tile[:, p * width : (p + 1) * width], "seq", routes[p]) for p in range(3)]
    slot_of = jnp.asarray(slots, jnp.int32)[lax.axis_index("seq")]
    columns = []
    for slot in range(3):
        columns.append(
            jnp.where(slot_of[0] == slot, got[0], jnp.where(slot_of[1] == slot, got[1], got[2]))
        )
    return jnp.concatenate(columns, axis=1)


def stored_columns(pair_tile, count):
    routes, slots = pair_routes(count)
    width = pair_tile.shape[1] // 3
    slot_of = jnp.asarray(slots, jnp.int32)[lax.axis_index("seq")]
    parts = [pair_tile[:, s * width : (s + 1) * width] for s in range(3)]
    back = []
    for piece in range(3):
        slot = slot_of[piece]
        chosen = jnp.where(slot == 0, parts[0], jnp.where(slot == 1, parts[1], parts[2]))
        back.append(lax.ppermute(chosen, "seq", [(target, source) for source, target in routes[piece]]))
    return jnp.concatenate(back, axis=1)


def chip_routes(dp, seq):
    chips = seq // 2

    def flat(move):
        return [(d * seq + s, move(d, s)) for d in range(dp) for s in range(seq)]

    def along_z(step):
        return flat(lambda d, s: d * seq + 2 * ((s // 2 + step) % chips) + s % 2)

    return {
        "x": flat(lambda d, s: (d ^ 1) * seq + s),
        "y": flat(lambda d, s: (d ^ 2) * seq + s),
        "xy": flat(lambda d, s: (d ^ 3) * seq + s),
        "core": flat(lambda d, s: d * seq + (s ^ 1)),
        "z": [along_z(step) for step in range(1, chips)],
    }


def send(value, route):
    return lax.ppermute(value, ("dp", "seq"), route)


def gather_column(tile, routes):
    return jnp.stack([tile] + [send(tile, route) for route in routes["z"]])


def gather_near(column, route):
    return jnp.stack([column, send(column, route)])


GELU_C = math.sqrt(2.0 / math.pi)


def gelu_parts(value):
    square = value * value
    slope = jnp.tanh(GELU_C * value * (1.0 + 0.044715 * square))
    low = 0.5 * (1.0 + slope)
    derivative = low + 0.5 * value * (1.0 - slope * slope) * (GELU_C * (1.0 + 3 * 0.044715 * square))
    return value * low, derivative


def lanes(parts):
    return jnp.concatenate(parts, axis=1)


def middle_kernel(
    place_ref, att_ref, stream_ref, low_ref, scale_ref, shift_ref, out_w_ref,
    up_0, up_1, up_2, up_3, down_0, down_1, down_2, down_3,
    layer_ref, hidden_ref, grad_up_ref, grad_mid_ref, grad_low_ref, grad_att_ref, sums_ref, turned_ref,
    up_w, down_w, normed_ref, middle_ref, out_acc, grad_acc, up_sem, down_sem, *, dp, seq,
):
    dp_at, chip_at, core_at = place_ref[0], place_ref[1], place_ref[2]
    chips = seq // 2
    up_rows, up_cols = up_0.shape[2], up_0.shape[3]
    down_rows, down_cols = down_0.shape[2], down_0.shape[3]

    def copies():
        made = []
        for name, pieces, masks, sems in (
            ("up", (up_0, up_1, up_2, up_3), (1, 2), up_sem),
            ("down", (down_0, down_1, down_2, down_3), (2, 1), down_sem),
        ):
            for part in range(4):
                core = core_at if part < 2 else 1 - core_at
                for step in range(2):
                    mask = (masks[1] if part % 2 else 0) ^ (masks[0] if step else 0)
                    row = jnp.bitwise_xor(dp_at, mask)
                    for back in range(chips):
                        block = 2 * lax.rem(chip_at + chips - back, chips) + core
                        if name == "up":
                            target = up_w.at[block, pl.ds(pl.multiple_of(row * up_rows, up_rows), up_rows), :]
                        else:
                            target = down_w.at[
                                pl.ds(pl.multiple_of(row * down_rows, down_rows), down_rows),
                                pl.ds(pl.multiple_of(block * down_cols, down_cols), down_cols),
                            ]
                        made.append(
                            pltpu.make_async_copy(
                                pieces[part].at[step, back], target, sems.at[(part * 2 + step) * chips + back]
                            )
                        )
        return made

    for copy in copies():
        copy.start()
    width = stream_ref.shape[1]
    tile_rows = width // dp
    middle_ref[...] = stream_ref[...]
    for row in range(dp):
        weight = lanes([out_w_ref[row * seq + s] for s in range(seq)])
        middle_ref[...] += dot_tn(att_ref[row * tile_rows : (row + 1) * tile_rows, :], weight)
    middle = middle_ref[...]
    inverse = lax.rsqrt(jnp.mean(middle * middle, axis=-1, keepdims=True) + epsilon)
    normed = middle * inverse * (1.0 + scale_ref[...]) + shift_ref[...]
    normed_ref[...] = normed.astype(jnp.bfloat16)
    turned_ref[...] = normed.T.astype(jnp.bfloat16)
    for copy in copies():
        copy.wait()
    out_acc[...] = jnp.zeros_like(out_acc)
    grad_acc[...] = jnp.zeros_like(grad_acc)

    @pl.loop(0, seq)
    def _(block):
        rows = pl.ds(pl.multiple_of(block * up_cols, up_cols), up_cols)
        up_weight, down_weight = up_w[block], down_w[rows, :]
        value, derivative = gelu_parts(dot_nn(normed_ref[...], up_weight))
        hidden = value.astype(jnp.bfloat16)
        hidden_ref[:, rows] = hidden
        out_acc[...] += dot_nn(hidden, down_weight)
        grad_up = (dot_nt(low_ref[...], down_weight) * derivative).astype(jnp.bfloat16)
        grad_up_ref[:, rows] = grad_up
        grad_acc[...] += dot_nt(grad_up, up_weight)

    middle = middle_ref[...]
    layer_ref[...] = (middle + out_acc[...]).astype(jnp.bfloat16)
    inverse = lax.rsqrt(jnp.mean(middle * middle, axis=-1, keepdims=True) + epsilon)
    unit = middle * inverse
    grad = grad_acc[...]
    lifted = grad * (1.0 + scale_ref[...])
    sums_ref[0:1, :] = jnp.sum(grad * unit, axis=0, keepdims=True)
    sums_ref[1:2, :] = jnp.sum(grad, axis=0, keepdims=True)
    grad_mid = low_ref[...].astype(jnp.float32) + inverse * (
        lifted - unit * jnp.mean(lifted * unit, axis=-1, keepdims=True)
    )
    grad_mid_ref[...] = grad_mid
    grad_low_ref[...] = grad_mid.astype(jnp.bfloat16)
    for row in range(dp):
        weight = lanes([out_w_ref[row * seq + s] for s in range(seq)])
        grad_att_ref[row * tile_rows : (row + 1) * tile_rows, :] = dot_nt(weight, grad_low_ref[...]).astype(
            jnp.bfloat16
        )


def middle_block(place, attended, stream, grad_low, scale, shift, out_tiles, up_pieces, down_pieces, dp, seq):
    frames, width = stream.shape
    hidden = up_pieces[0].shape[3] * seq
    whole = pl.BlockSpec(memory_space=pltpu.VMEM)
    anywhere = pl.BlockSpec(memory_space=pl.ANY)
    low, wide = jnp.bfloat16, jnp.float32
    return pl.pallas_call(
        partial(middle_kernel, dp=dp, seq=seq),
        in_specs=[pl.BlockSpec(memory_space=pltpu.SMEM)] + [whole] * 6 + [anywhere] * 8,
        out_specs=[whole] * 8,
        out_shape=[
            jax.ShapeDtypeStruct((frames, width), low),
            jax.ShapeDtypeStruct((frames, hidden), low),
            jax.ShapeDtypeStruct((frames, hidden), low),
            jax.ShapeDtypeStruct((frames, width), wide),
            jax.ShapeDtypeStruct((frames, width), low),
            jax.ShapeDtypeStruct((width, frames), low),
            jax.ShapeDtypeStruct((2, width), wide),
            jax.ShapeDtypeStruct((width, frames), low),
        ],
        scratch_shapes=[
            pltpu.VMEM((seq, width, hidden // seq), low),
            pltpu.VMEM((hidden, width), low),
            pltpu.VMEM((frames, width), low),
            pltpu.VMEM((frames, width), wide),
            pltpu.VMEM((frames, width), wide),
            pltpu.VMEM((frames, width), wide),
            pltpu.SemaphoreType.DMA((dp * seq,)),
            pltpu.SemaphoreType.DMA((dp * seq,)),
        ],
        compiler_params=pltpu.CompilerParams(vmem_limit_bytes=58 << 20),
        cost_estimate=pl.CostEstimate(
            flops=8 * frames * width * hidden + 4 * frames * width * width,
            bytes_accessed=4 * hidden * width + 24 * frames * width,
            transcendentals=frames * hidden,
        ),
        name="middle_block",
    )(place, attended, stream, grad_low, scale, shift, out_tiles, *up_pieces, *down_pieces)


def entry_kernel(main_ref, side_ref, weight_ref, scale_ref, shift_ref, stream_ref, normed_ref, *, dp, seq):
    row = pl.program_id(0)

    @pl.when(row == 0)
    def _():
        stream_ref[...] = jnp.zeros_like(stream_ref)

    operand = jnp.where(row < dp // 2, main_ref[...], side_ref[...])
    stream_ref[...] += dot_nn(operand, lanes([weight_ref[s] for s in range(seq)]))

    @pl.when(row == dp - 1)
    def _():
        stream = stream_ref[...]
        inverse = lax.rsqrt(jnp.mean(stream * stream, axis=-1, keepdims=True) + epsilon)
        normed_ref[...] = (stream * inverse * (1.0 + scale_ref[...]) + shift_ref[...]).astype(jnp.bfloat16)


def entry_block(main, side, skip_tiles, scale, shift, dp, seq):
    frames, width = main.shape
    rows, columns = skip_tiles.shape[1:]
    fixed = pl.BlockSpec((1, width), lambda i: (0, 0))
    return pl.pallas_call(
        partial(entry_kernel, dp=dp, seq=seq),
        grid=(dp,),
        in_specs=[
            pl.BlockSpec((frames, rows), lambda i: (0, jnp.minimum(i, dp // 2 - 1))),
            pl.BlockSpec((frames, rows), lambda i: (0, jnp.maximum(i - dp // 2, 0))),
            pl.BlockSpec((seq, rows, columns), lambda i: (i, 0, 0)),
            fixed,
            fixed,
        ],
        out_specs=[pl.BlockSpec((frames, width), lambda i: (0, 0))] * 2,
        out_shape=[
            jax.ShapeDtypeStruct((frames, width), jnp.float32),
            jax.ShapeDtypeStruct((frames, width), jnp.bfloat16),
        ],
        compiler_params=pltpu.CompilerParams(vmem_limit_bytes=32 << 20),
        cost_estimate=pl.CostEstimate(
            flops=4 * frames * width * width, bytes_accessed=14 * frames * width, transcendentals=0
        ),
        name="entry_block",
    )(main, side, skip_tiles, scale, shift)


def exit_kernel(
    projected_ref, pair_ref, stream_ref, grad_mid_ref, scale_ref, grad_ref, turned_ref, sums_ref, normed_ref,
    *, dp, seq,
):
    rows = pair_ref.shape[1]
    for row in range(dp):
        weight = lanes([pair_ref[row * seq + s] for s in range(seq)])
        normed_ref[:, row * rows : (row + 1) * rows] = dot_nn(weight, projected_ref[...]).T
    grad, stream = normed_ref[...], stream_ref[...]
    inverse = lax.rsqrt(jnp.mean(stream * stream, axis=-1, keepdims=True) + epsilon)
    unit = stream * inverse
    lifted = grad * (1.0 + scale_ref[...])
    sums_ref[0:1, :] = jnp.sum(grad * unit, axis=0, keepdims=True)
    sums_ref[1:2, :] = jnp.sum(grad, axis=0, keepdims=True)
    grad_stream = grad_mid_ref[...] + inverse * (lifted - unit * jnp.mean(lifted * unit, axis=-1, keepdims=True))
    grad_ref[...] = grad_stream.astype(jnp.bfloat16)
    turned_ref[...] = grad_stream.T.astype(jnp.bfloat16)


def exit_block(projected, pair_tiles, stream, grad_mid, scale, dp, seq):
    frames, width = stream.shape
    whole = pl.BlockSpec(memory_space=pltpu.VMEM)
    return pl.pallas_call(
        partial(exit_kernel, dp=dp, seq=seq),
        in_specs=[whole] * 5,
        out_specs=[whole] * 3,
        out_shape=[
            jax.ShapeDtypeStruct((frames, width), jnp.bfloat16),
            jax.ShapeDtypeStruct((width, frames), jnp.bfloat16),
            jax.ShapeDtypeStruct((2, width), jnp.float32),
        ],
        scratch_shapes=[pltpu.VMEM((frames, width), jnp.float32)],
        compiler_params=pltpu.CompilerParams(vmem_limit_bytes=40 << 20),
        cost_estimate=pl.CostEstimate(
            flops=6 * frames * width * width, bytes_accessed=18 * frames * width + 6 * width * width, transcendentals=0
        ),
        name="exit_block",
    )(projected, pair_tiles, stream, grad_mid, scale)


def joined_kernel(grad_ref, weight_ref, main_ref, side_ref, *, dp, seq):
    row = pl.program_id(0)
    grad = dot_nt(grad_ref[...], lanes([weight_ref[s] for s in range(seq)]))

    @pl.when(row < dp // 2)
    def _():
        main_ref[...] = grad

    @pl.when(row >= dp // 2)
    def _():
        side_ref[...] = grad


def joined_grads(grad_stream, skip_tiles, dp, seq):
    frames, width = grad_stream.shape
    rows, columns = skip_tiles.shape[1:]
    out = jax.ShapeDtypeStruct((frames, width), jnp.float32)
    return pl.pallas_call(
        partial(joined_kernel, dp=dp, seq=seq),
        grid=(dp,),
        in_specs=[
            pl.BlockSpec((frames, width), lambda i: (0, 0)),
            pl.BlockSpec((seq, rows, columns), lambda i: (i, 0, 0)),
        ],
        out_specs=[
            pl.BlockSpec((frames, rows), lambda i: (0, jnp.minimum(i, dp // 2 - 1))),
            pl.BlockSpec((frames, rows), lambda i: (0, jnp.maximum(i - dp // 2, 0))),
        ],
        out_shape=[out, out],
        compiler_params=pltpu.CompilerParams(vmem_limit_bytes=32 << 20),
        cost_estimate=pl.CostEstimate(
            flops=4 * frames * width * width, bytes_accessed=14 * frames * width, transcendentals=0
        ),
        name="joined_grads",
    )(grad_stream, skip_tiles)


def blocks_kernel(place_ref, left_ref, right_ref, *refs, kind, masks, other, chips):
    chip_at, core_at = place_ref[1], place_ref[2]
    core = 1 - core_at if other else core_at
    step = pl.program_id(0)
    out_refs = refs if other else refs[1:]
    block = out_refs[0].shape[2] if kind == "turned" else out_refs[0].shape[3]
    starts = [(2 * lax.rem(chip_at + ahead, chips) + core) * block for ahead in range(chips)]
    starts = [pl.multiple_of(start, block) for start in starts]
    if kind == "turned":
        left = jnp.concatenate([left_ref[pl.ds(start, block), :] for start in starts], axis=0)
        product = dot_nn(left, right_ref[...])
        parts = [product[ahead * block : (ahead + 1) * block] for ahead in range(chips)]
    else:
        right = lanes([right_ref[:, pl.ds(start, block)] for start in starts])
        product = dot_nn(left_ref[...], right)
        parts = [product[:, ahead * block : (ahead + 1) * block] for ahead in range(chips)]
    if other:
        for ahead in range(chips):
            out_refs[0][0, ahead] = parts[ahead].astype(jnp.bfloat16)
        return
    parts = [parts[ahead] + refs[0][0, ahead].astype(jnp.float32) for ahead in range(chips)]

    @pl.when(step < 2)
    def _():
        for ahead in range(chips):
            out_refs[0][0, ahead] = parts[ahead].astype(jnp.bfloat16)

    @pl.when(step >= 2)
    def _():
        for ahead in range(chips):
            out_refs[1][0, ahead] = parts[ahead].astype(jnp.bfloat16)


def grad_blocks(place, left, right, kind, masks, seq, arrived=None, part=(0, 1)):
    first, second = masks
    chips, dp = seq // 2, 4
    depth = left.shape[1]

    def owner(i, place):
        return jnp.bitwise_xor(place[0], (i % 2) * second + (i // 2) * first)

    if kind == "turned":
        columns = right.shape[1] // (dp * part[1])
        shape = (left.shape[0] // seq, columns)
        left_spec = pl.BlockSpec(left.shape, lambda i, place: (0, 0))
        right_spec = pl.BlockSpec((depth, columns), lambda i, place: (0, owner(i, place) * part[1] + part[0]))
    else:
        shape = (left.shape[0] // dp, right.shape[1] // seq)
        left_spec = pl.BlockSpec((shape[0], depth), lambda i, place: (owner(i, place), 0))
        right_spec = pl.BlockSpec(right.shape, lambda i, place: (0, 0))
    other = arrived is None
    one = (1, chips) + shape
    if other:
        specs, count = [pl.BlockSpec(one, lambda i, place: (i, 0, 0, 0))], 4
        extra, operands = [], (left, right)
    else:
        specs = [
            pl.BlockSpec(one, lambda i, place: (jnp.minimum(i, 1), 0, 0, 0)),
            pl.BlockSpec(one, lambda i, place: (jnp.maximum(i - 2, 0), 0, 0, 0)),
        ]
        count = 2
        extra, operands = [pl.BlockSpec(one, lambda i, place: (i, 0, 0, 0))], (left, right, arrived)
    return pl.pallas_call(
        partial(blocks_kernel, kind=kind, masks=masks, other=other, chips=chips),
        grid_spec=pltpu.PrefetchScalarGridSpec(
            num_scalar_prefetch=1, grid=(4,), in_specs=[left_spec, right_spec] + extra, out_specs=specs
        ),
        out_shape=[jax.ShapeDtypeStruct((count, chips) + shape, jnp.bfloat16)] * len(specs),
        compiler_params=pltpu.CompilerParams(vmem_limit_bytes=40 << 20),
        cost_estimate=pl.CostEstimate(
            flops=2 * dp * chips * shape[0] * shape[1] * depth,
            bytes_accessed=2 * dp * chips * shape[0] * shape[1] * (1 if other else 2) + 2 * left.size + 2 * right.size,
            transcendentals=0,
        ),
        name="grad_blocks",
    )(place, *operands)


AXIS_MASK = {"x": 1, "y": 2}


def wide(value):
    return value.astype(jnp.float32)


def scatter_first(place, left, right, kind, routes, seq, first, second, part=(0, 1)):
    masks = (AXIS_MASK[first], AXIS_MASK[second])
    (outgoing,) = grad_blocks(place, left, right, kind, masks, seq, None, part)
    arrived = send(outgoing, routes["core"])
    keep, away = grad_blocks(place, left, right, kind, masks, seq, arrived, part)
    return keep, send(away, routes[first])


def scatter_second(state, routes, second):
    keep, arrived = state
    back = send((wide(keep[1]) + wide(arrived[1])).astype(jnp.bfloat16), routes[second])
    return wide(keep[0]) + wide(arrived[0]), back


def scatter_last(state, routes):
    total = state[0] + wide(state[1])
    low = total.astype(jnp.bfloat16)
    got = [send(low[ahead + 1], route) for ahead, route in enumerate(routes["z"])]
    result = total[0]
    for piece in got:
        result = result + wide(piece)
    return result


def dp_sum(value, routes, dp):
    at = lax.axis_index("dp")
    result = wide(lax.dynamic_index_in_dim(value, at, 0, keepdims=False))
    for mask, route in ((1, routes["x"]), (2, routes["y"]), (3, routes["xy"])):
        piece = lax.dynamic_index_in_dim(value, jnp.bitwise_xor(at, mask), 0, keepdims=False)
        result = result + wide(send(piece, route))
    return result


def dp_gather(tile, routes, dp):
    at = lax.axis_index("dp")
    rows = tile.shape[0]
    full = jnp.zeros((dp * rows, tile.shape[1]), tile.dtype)
    full = lax.dynamic_update_slice_in_dim(full, tile, at * rows, 0)
    for mask, route in ((1, routes["x"]), (2, routes["y"]), (3, routes["xy"])):
        full = lax.dynamic_update_slice_in_dim(full, send(tile, route), jnp.bitwise_xor(at, mask) * rows, 0)
    return full


def local_paired(
    inputs, skip_input, time_embed, segment_ids, span_start, span_length, cotangent,
    skip_weight, ada_weight, qkv_weight, out_weight, up_weight, down_weight,
):
    seq = lax.axis_size("seq")
    dp = lax.axis_size("dp")
    frames, width = inputs.shape[1], inputs.shape[2]
    length = segment_ids.shape[1]
    segments = segment_ids[0]
    end_a = jnp.sum((segments < 1).astype(jnp.int32))
    end_b = jnp.sum((segments < 2).astype(jnp.int32))
    ends = jnp.stack([end_a, end_b])
    firsts = jnp.where(segments == 0, 0, jnp.where(segments == 1, end_a, end_b))
    position = jnp.arange(length, dtype=jnp.int32) - firsts
    half = HD // 2
    frequency = jnp.exp(-math.log(10000.0) * jnp.arange(half, dtype=jnp.float32) / half)
    angles = frequency[:, None] * position.astype(jnp.float32)[None, :]
    cos_all, sin_all = jnp.cos(angles), jnp.sin(angles)
    base = lax.axis_index("seq") * frames
    local_segments = lax.dynamic_slice_in_dim(segments, base, frames, 0)
    local_position = lax.dynamic_slice_in_dim(position, base, frames, 0)
    starts, lengths = span_start[0], span_length[0]

    def pick(table):
        return jnp.where(local_segments == 0, table[0], jnp.where(local_segments == 1, table[1], table[2]))

    span_begin = pick(starts)
    inside = jnp.logical_and(local_position >= span_begin, local_position < span_begin + pick(lengths))
    grad_low = jnp.where(inside[:, None], cotangent[0], jnp.zeros((), jnp.bfloat16))
    routes = chip_routes(dp, seq)
    seq_at = lax.axis_index("seq")
    place = jnp.stack([lax.axis_index("dp"), seq_at // 2, seq_at % 2]).astype(jnp.int32)
    up_column = gather_column(up_weight, routes)
    down_column = gather_column(down_weight, routes)
    embed_all = lax.all_gather(time_embed, "dp", axis=0, tiled=True)
    embed_rows = width // dp
    embed_part = lax.dynamic_slice_in_dim(embed_all, lax.axis_index("dp") * embed_rows, embed_rows, 1)
    modulation_part = jnp.dot(embed_part, ada_weight, preferred_element_type=jnp.float32)
    modulation_part = lax.psum_scatter(modulation_part, "dp", scatter_dimension=0, tiled=True)
    modulation = lax.all_gather(modulation_part, "seq", axis=1, tiled=True)
    scale_one = modulation[:, :width]
    shift_one = modulation[:, width : 2 * width]
    scale_two = modulation[:, 2 * width : 3 * width]
    shift_two = modulation[:, 3 * width :]

    skip_tiles = lax.all_gather(skip_weight, ("dp", "seq"), axis=0)
    pair_tile = own_pair_columns(qkv_weight, seq)
    pair_weight = dp_gather(pair_tile, routes, dp)
    skip_tiles, up_column, down_column, pair_weight, cos_all, sin_all, ends, grad_low, place = lax.optimization_barrier(
        (skip_tiles, up_column, down_column, pair_weight.T, cos_all, sin_all, ends, grad_low, place)
    )
    stream, normed_one = entry_block(inputs[0], skip_input[0], skip_tiles, scale_one, shift_one, dp, seq)
    normed_all = lax.all_gather(normed_one, "seq", axis=0)
    up_near = gather_near(up_column, routes["x"])
    down_near = gather_near(down_column, routes["y"])
    up_far, down_far = send(up_near, routes["y"]), send(down_near, routes["x"])
    up_near_core, down_near_core = send(up_near, routes["core"]), send(down_near, routes["core"])
    normed_all, up_far, down_far, up_near_core, down_near_core = lax.optimization_barrier(
        (normed_all, up_far, down_far, up_near_core, down_near_core)
    )
    up_pieces = (up_near, up_far, up_near_core, send(up_far, routes["core"]))
    down_pieces = (down_near, down_far, down_near_core, send(down_far, routes["core"]))
    qt, kt, vt, keys, values = project_pair(normed_all, pair_weight, cos_all, sin_all)
    attended_pair, attended_wide, total = attend_pair(ends, qt, keys, vt)
    attended = lax.all_to_all(attended_pair, "seq", 0, 0).reshape(width, frames)
    out_tiles = lax.all_gather(out_weight, ("dp", "seq"), axis=0)
    (
        layer_output, hidden, grad_up_act, grad_middle, grad_middle_low, grad_attended, sums_two, normed_two_turned,
    ) = middle_block(
        place, attended, stream, grad_low, scale_two, shift_two, out_tiles, up_pieces, down_pieces, dp, seq
    )
    grad_pair = lax.all_to_all(grad_attended.reshape(seq, PAIR, frames), "seq", 0, 0)
    down_sum = scatter_first(place, grad_low.T, hidden, "turned", routes, seq, "x", "y")
    up_sum = scatter_first(place, normed_two_turned, grad_up_act, "plain", routes, seq, "y", "x")
    out_sum = scatter_first(place, attended, grad_middle_low, "plain", routes, seq, "x", "y")

    grad_projected = attend_pair_back(ends, qt, grad_pair, attended_wide, total, keys, values, kt, cos_all, sin_all)
    grad_local = lax.all_to_all(grad_projected, "seq", 0, 0)
    pair_all = lax.all_gather(pair_tile, ("dp", "seq"), axis=0)
    down_sum = scatter_second(down_sum, routes, "y")
    up_sum = scatter_second(up_sum, routes, "x")
    out_sum = scatter_second(out_sum, routes, "y")
    grad_pair_weight = jnp.einsum(
        "icf,ifd->cd", grad_projected, normed_all, preferred_element_type=jnp.float32
    ).astype(jnp.bfloat16)
    grad_stream, grad_stream_turned, sums_one = exit_block(
        grad_local.reshape(3 * width, frames), pair_all, stream, grad_middle, scale_one, dp, seq
    )
    joined = jnp.concatenate([inputs[0], skip_input[0]], axis=-1)
    skip_sums = [
        scatter_first(place, grad_stream_turned, joined, "turned", routes, seq, first, second, (part, 2))
        for part, (first, second) in enumerate((("x", "y"), ("y", "x")))
    ]
    grad_main, grad_side = joined_grads(grad_stream, skip_tiles, dp, seq)
    sums_one, grad_main, grad_pair_weight = lax.optimization_barrier((sums_one, grad_main, grad_pair_weight))
    skip_sums = [scatter_second(skip_sums[0], routes, "y"), scatter_second(skip_sums[1], routes, "x")]
    skip_tile = jnp.concatenate([scatter_last(part, routes) for part in skip_sums], axis=1).T
    down_tile = scatter_last(down_sum, routes).T
    up_tile = scatter_last(up_sum, routes)
    out_tile = scatter_last(out_sum, routes)
    grad_pair_tile = dp_sum(grad_pair_weight.T.reshape(dp, width // dp, 3 * PAIR), routes, dp)
    qkv_tile = stored_columns(grad_pair_tile.astype(jnp.bfloat16), seq).astype(jnp.float32)
    grad_modulation = jnp.concatenate([sums_one[0], sums_one[1], sums_two[0], sums_two[1]])
    grad_modulation = lax.psum_scatter(grad_modulation, "seq", scatter_dimension=0, tiled=True)
    grad_modulation = lax.all_gather(grad_modulation[None], "dp", axis=0, tiled=True)
    ada_tile = lax.dot_general(
        embed_part.astype(jnp.float32), grad_modulation, (((0,), (0,)), ((), ())),
        precision=lax.Precision.HIGHEST,
    )
    return (
        layer_output[None],
        grad_main[None],
        grad_side[None],
        skip_tile,
        ada_tile,
        qkv_tile,
        out_tile,
        up_tile,
        down_tile,
    )


def solution(mesh):
    in_specs = (
        P("dp", "seq", None),
        P("dp", "seq", None),
        P("dp", None),
        P("dp", None),
        P("dp", None),
        P("dp", None),
        P("dp", "seq", None),
        P("dp", "seq"),
        P("dp", "seq"),
        P("dp", "seq"),
        P("dp", "seq"),
        P("dp", "seq"),
        P("dp", "seq"),
    )
    out_specs = (
        P("dp", "seq", None),
        P("dp", "seq", None),
        P("dp", "seq", None),
        P("dp", "seq"),
        P("dp", "seq"),
        P("dp", "seq"),
        P("dp", "seq"),
        P("dp", "seq"),
        P("dp", "seq"),
    )
    seq_size = mesh.shape["seq"]
    paired = H == 2 * seq_size and seq_size % 3 != 0 and mesh.shape["dp"] == 4
    body = local_paired if paired else local_general
    return jax.shard_map(body, mesh=mesh, in_specs=in_specs, out_specs=out_specs, check_vma=False)
```

```python
from functools import partial
import math

import jax
import jax.numpy as jnp
from jax import lax
from jax.experimental import pallas as pl
from jax.experimental.pallas import tpu as pltpu
from jax.sharding import PartitionSpec as P

H = 16
HD = 64
UTT = 3
HG = 8


epsilon = 1e-06
masked_score = -1e30


def ada_norm(stream, scale_part, shift_part):
    inverse = lax.rsqrt(jnp.mean(stream * stream, axis=-1, keepdims=True) + epsilon)
    return stream * inverse * (1.0 + scale_part) + shift_part


def rotate(tensor, cosine, sine_part):
    half_width = tensor.shape[-1] // 2
    lower_half = tensor[..., :half_width]
    upper_half = tensor[..., half_width:]
    cos_wide = cosine[..., None, :]
    sin_wide = sine_part[..., None, :]
    return jnp.concatenate(
        [
            lower_half * cos_wide - upper_half * sin_wide,
            lower_half * sin_wide + upper_half * cos_wide,
        ],
        axis=-1,
    )


def rotary_tables(position, half_width):
    frequency = jnp.exp(-math.log(10000.0) * jnp.arange(half_width, dtype=jnp.float32) / half_width)
    angles = position.astype(jnp.float32)[..., None] * frequency
    return (jnp.cos(angles), jnp.sin(angles))


def gather_weights(skip_tile, ada_tile, qkv_tile, out_tile, up_tile, down_tile):
    row_full = (
        lax.all_gather(skip_tile, "dp", axis=0, tiled=True),
        lax.all_gather(ada_tile, "dp", axis=0, tiled=True),
        lax.all_gather(qkv_tile, "dp", axis=0, tiled=True),
        lax.all_gather(out_tile, "dp", axis=0, tiled=True),
        lax.all_gather(up_tile, "dp", axis=0, tiled=True),
        lax.all_gather(down_tile, "dp", axis=0, tiled=True),
    )
    return (
        lax.all_gather(row_full[0], "seq", axis=1, tiled=True),
        lax.all_gather(row_full[1], "seq", axis=1, tiled=True),
        lax.all_gather(row_full[2], "seq", axis=1, tiled=True),
        lax.all_gather(row_full[3], "seq", axis=1, tiled=True),
        lax.all_gather(row_full[4], "seq", axis=1, tiled=True),
        lax.all_gather(row_full[5], "seq", axis=1, tiled=True),
    )


def group_scores(query_part, key_part, allowed, factor):
    scores = (
        jnp.einsum("qhd,khd->hqk", query_part, key_part, preferred_element_type=jnp.float32)
        * factor
    )
    return jnp.where(allowed[None], scores, masked_score)


def attend_row(queries, key_rows, value_rows, segment_local, segment_full):
    factor = queries.shape[2] ** (-0.5)
    allowed = segment_local[:, None] == segment_full[None, :]
    outputs = []
    totals = []
    for head_start in range(0, H, HG):
        head_end = head_start + HG
        scores = group_scores(
            queries[:, head_start:head_end], key_rows[:, head_start:head_end], allowed, factor
        )
        log_total = jax.nn.logsumexp(scores, axis=-1)
        weights = jnp.exp(scores - log_total[..., None]).astype(jnp.bfloat16)
        outputs.append(
            jnp.einsum(
                "hqk,khd->qhd",
                weights,
                value_rows[:, head_start:head_end],
                preferred_element_type=jnp.float32,
            )
        )
        totals.append(log_total)
    return (jnp.concatenate(outputs, axis=1), jnp.concatenate(totals, axis=0))


def attend_back(
    queries, key_rows, value_rows, segment_local, segment_full, log_total, grad_attended, row_dot
):
    factor = queries.shape[2] ** (-0.5)
    allowed = segment_local[:, None] == segment_full[None, :]
    query_grads = []
    key_grads = []
    value_grads = []
    for head_start in range(0, H, HG):
        head_end = head_start + HG
        key_part = key_rows[:, head_start:head_end]
        query_part = queries[:, head_start:head_end]
        grad_part = grad_attended[:, head_start:head_end]
        scores = group_scores(query_part, key_part, allowed, factor)
        weights = jnp.exp(scores - log_total[head_start:head_end][..., None])
        weights_low = weights.astype(jnp.bfloat16)
        value_grads.append(
            jnp.einsum("hqk,qhd->khd", weights_low, grad_part, preferred_element_type=jnp.float32)
        )
        grad_weights = jnp.einsum(
            "qhd,khd->hqk",
            grad_part,
            value_rows[:, head_start:head_end],
            preferred_element_type=jnp.float32,
        )
        grad_scores = (weights * (grad_weights - row_dot[head_start:head_end][..., None])).astype(
            jnp.bfloat16
        )
        query_grads.append(
            jnp.einsum("hqk,khd->qhd", grad_scores, key_part, preferred_element_type=jnp.float32)
            * factor
        )
        key_grads.append(
            jnp.einsum("hqk,qhd->khd", grad_scores, query_part, preferred_element_type=jnp.float32)
            * factor
        )
    return (
        jnp.concatenate(query_grads, axis=1),
        jnp.concatenate(key_grads, axis=1),
        jnp.concatenate(value_grads, axis=1),
    )


def local_general(
    inputs,
    skip_input,
    time_embed,
    segment_ids,
    span_start,
    span_length,
    cotangent,
    skip_weight,
    ada_weight,
    qkv_weight,
    out_weight,
    up_weight,
    down_weight,
):
    row_count = inputs.shape[0]
    frames = inputs.shape[1]
    model_width = inputs.shape[2]
    row_length = segment_ids.shape[1]
    frame_base = lax.axis_index("seq") * frames
    utterance = jnp.arange(UTT, dtype=jnp.int32)
    member = (segment_ids[:, :, None] == utterance[None, None, :]).astype(jnp.int32)
    counts = jnp.sum(member, axis=1)
    firsts = jnp.cumsum(counts, axis=1) - counts
    local_member = lax.dynamic_slice_in_dim(member, frame_base, frames, 1)
    local_segments = lax.dynamic_slice_in_dim(segment_ids, frame_base, frames, 1)
    local_frames = frame_base + jnp.arange(frames, dtype=jnp.int32)
    position = local_frames[None, :] - jnp.sum(local_member * firsts[:, None, :], axis=2)
    span_begin = jnp.sum(local_member * span_start[:, None, :], axis=2)
    span_end = span_begin + jnp.sum(local_member * span_length[:, None, :], axis=2)
    inside = jnp.logical_and(position >= span_begin, position < span_end)
    cosine, sine_part = rotary_tables(position, HD // 2)
    skip_full, ada_full, qkv_full, out_full, up_full, down_full = gather_weights(
        skip_weight, ada_weight, qkv_weight, out_weight, up_weight, down_weight
    )
    joined = jnp.concatenate([inputs, skip_input], axis=-1)
    stream = jnp.einsum("rfc,cd->rfd", joined, skip_full, preferred_element_type=jnp.float32)
    modulation = jnp.dot(time_embed, ada_full, preferred_element_type=jnp.float32)[:, None, :]
    scale_one = modulation[..., :model_width]
    shift_one = modulation[..., model_width : 2 * model_width]
    scale_two = modulation[..., 2 * model_width : 3 * model_width]
    shift_two = modulation[..., 3 * model_width :]
    normed_one = ada_norm(stream, scale_one, shift_one).astype(jnp.bfloat16)
    projected = jnp.einsum("rfd,de->rfe", normed_one, qkv_full, preferred_element_type=jnp.float32)
    queries = rotate(
        projected[..., :model_width].reshape(row_count, frames, H, HD), cosine, sine_part
    ).astype(jnp.bfloat16)
    key_rotated = rotate(
        projected[..., model_width : 2 * model_width].reshape(row_count, frames, H, HD),
        cosine,
        sine_part,
    )
    key_local = key_rotated.reshape(row_count, frames, model_width).astype(jnp.bfloat16)
    value_local = projected[..., 2 * model_width :].astype(jnp.bfloat16)
    key_all, value_all = (
        lax.all_gather(key_local, "seq", axis=1, tiled=True),
        lax.all_gather(value_local, "seq", axis=1, tiled=True),
    )

    def forward_row(row_items):
        query_row, key_row, value_row, local_row, full_row = row_items
        return attend_row(
            query_row,
            key_row.reshape(row_length, H, HD),
            value_row.reshape(row_length, H, HD),
            local_row,
            full_row,
        )

    attended, log_total = lax.map(
        forward_row, (queries, key_all, value_all, local_segments, segment_ids)
    )
    attended = attended.reshape(row_count, frames, model_width)
    attended_low = attended.astype(jnp.bfloat16)
    middle = stream + jnp.einsum(
        "rfe,ed->rfd", attended_low, out_full, preferred_element_type=jnp.float32
    )
    normed_two = ada_norm(middle, scale_two, shift_two).astype(jnp.bfloat16)
    up_proj = jnp.einsum("rfd,di->rfi", normed_two, up_full, preferred_element_type=jnp.float32)
    hidden = jax.nn.gelu(up_proj, approximate=True).astype(jnp.bfloat16)
    down_proj = jnp.einsum("rfi,id->rfd", hidden, down_full, preferred_element_type=jnp.float32)
    layer_output = (middle + down_proj).astype(jnp.bfloat16)
    skip_full, ada_full, qkv_full, out_full, up_full, down_full = gather_weights(
        skip_weight, ada_weight, qkv_weight, out_weight, up_weight, down_weight
    )
    grad_out = cotangent.astype(jnp.float32) * inside[..., None].astype(jnp.float32)
    grad_low = grad_out.astype(jnp.bfloat16)
    grad_hidden = jnp.einsum("rfd,id->rfi", grad_low, down_full, preferred_element_type=jnp.float32)
    _, gelu_pull = jax.vjp(partial(jax.nn.gelu, approximate=True), up_proj)
    grad_up_act = gelu_pull(grad_hidden)[0].astype(jnp.bfloat16)
    grad_normed_two = jnp.einsum(
        "rfi,di->rfd", grad_up_act, up_full, preferred_element_type=jnp.float32
    )
    _, norm_pull_two = jax.vjp(ada_norm, middle, scale_two, shift_two)
    grad_middle_norm, grad_scale_two, grad_shift_two = norm_pull_two(grad_normed_two)
    grad_middle = grad_out + grad_middle_norm
    grad_middle_low = grad_middle.astype(jnp.bfloat16)
    grad_attended = jnp.einsum(
        "rfd,ed->rfe", grad_middle_low, out_full, preferred_element_type=jnp.float32
    ).astype(jnp.bfloat16)
    row_dot = jnp.sum(
        (grad_attended.astype(jnp.float32) * attended).reshape(row_count, frames, H, HD), axis=-1
    )
    row_dot = jnp.swapaxes(row_dot, 1, 2)
    grad_heads = grad_attended.reshape(row_count, frames, H, HD)

    def backward_row(row_items):
        query_row, key_row, value_row, local_row, full_row, total_row, grad_row, dot_row = row_items
        return attend_back(
            query_row,
            key_row.reshape(row_length, H, HD),
            value_row.reshape(row_length, H, HD),
            local_row,
            full_row,
            total_row,
            grad_row,
            dot_row,
        )

    grad_queries, grad_keys, grad_values = lax.map(
        backward_row,
        (queries, key_all, value_all, local_segments, segment_ids, log_total, grad_heads, row_dot),
    )
    key_share, value_share = (
        lax.psum_scatter(
            grad_keys.reshape(row_count, row_length, model_width).astype(jnp.bfloat16),
            "seq",
            scatter_dimension=1,
            tiled=True,
        ).astype(jnp.float32),
        lax.psum_scatter(
            grad_values.reshape(row_count, row_length, model_width).astype(jnp.bfloat16),
            "seq",
            scatter_dimension=1,
            tiled=True,
        ).astype(jnp.float32),
    )
    _, rotate_pull = jax.vjp(
        partial(rotate, cosine=cosine, sine_part=sine_part),
        jnp.zeros((row_count, frames, H, HD), jnp.float32),
    )
    grad_query_raw = rotate_pull(grad_queries)[0].reshape(row_count, frames, model_width)
    grad_key_raw = rotate_pull(key_share.reshape(row_count, frames, H, HD))[0].reshape(
        row_count, frames, model_width
    )
    grad_projected = jnp.concatenate([grad_query_raw, grad_key_raw, value_share], axis=-1).astype(
        jnp.bfloat16
    )
    grad_normed_one = jnp.einsum(
        "rfe,de->rfd", grad_projected, qkv_full, preferred_element_type=jnp.float32
    )
    _, norm_pull_one = jax.vjp(ada_norm, stream, scale_one, shift_one)
    grad_stream_norm, grad_scale_one, grad_shift_one = norm_pull_one(grad_normed_one)
    grad_stream = (grad_middle + grad_stream_norm).astype(jnp.bfloat16)
    grad_joined = jnp.einsum(
        "rfd,cd->rfc", grad_stream, skip_full, preferred_element_type=jnp.float32
    )
    grad_modulation = jnp.concatenate(
        [grad_scale_one, grad_shift_one, grad_scale_two, grad_shift_two], axis=-1
    )[:, 0, :]
    grad_down = jnp.einsum("rfi,rfd->id", hidden, grad_low, preferred_element_type=jnp.float32)
    grad_up = jnp.einsum("rfd,rfi->di", normed_two, grad_up_act, preferred_element_type=jnp.float32)
    grad_attn_out = jnp.einsum(
        "rfe,rfd->ed", attended_low, grad_middle_low, preferred_element_type=jnp.float32
    )
    grad_qkv = jnp.einsum(
        "rfd,rfe->de", normed_one, grad_projected, preferred_element_type=jnp.float32
    )
    grad_skip_w = jnp.einsum("rfc,rfd->cd", joined, grad_stream, preferred_element_type=jnp.float32)
    grad_ada = jnp.einsum(
        "rd,re->de",
        time_embed.astype(jnp.float32),
        grad_modulation,
        precision=lax.Precision.HIGHEST,
    )
    column_parts = (
        lax.psum_scatter(
            grad_skip_w.astype(jnp.bfloat16), "seq", scatter_dimension=1, tiled=True
        ).astype(jnp.float32),
        lax.psum_scatter(
            grad_ada.astype(jnp.bfloat16), "seq", scatter_dimension=1, tiled=True
        ).astype(jnp.float32),
        lax.psum_scatter(
            grad_qkv.astype(jnp.bfloat16), "seq", scatter_dimension=1, tiled=True
        ).astype(jnp.float32),
        lax.psum_scatter(
            grad_attn_out.astype(jnp.bfloat16), "seq", scatter_dimension=1, tiled=True
        ).astype(jnp.float32),
        lax.psum_scatter(
            grad_up.astype(jnp.bfloat16), "seq", scatter_dimension=1, tiled=True
        ).astype(jnp.float32),
        lax.psum_scatter(
            grad_down.astype(jnp.bfloat16), "seq", scatter_dimension=1, tiled=True
        ).astype(jnp.float32),
    )
    weight_tiles = (
        lax.psum_scatter(
            column_parts[0].astype(jnp.bfloat16), "dp", scatter_dimension=0, tiled=True
        ).astype(jnp.float32),
        lax.psum_scatter(
            column_parts[1].astype(jnp.bfloat16), "dp", scatter_dimension=0, tiled=True
        ).astype(jnp.float32),
        lax.psum_scatter(
            column_parts[2].astype(jnp.bfloat16), "dp", scatter_dimension=0, tiled=True
        ).astype(jnp.float32),
        lax.psum_scatter(
            column_parts[3].astype(jnp.bfloat16), "dp", scatter_dimension=0, tiled=True
        ).astype(jnp.float32),
        lax.psum_scatter(
            column_parts[4].astype(jnp.bfloat16), "dp", scatter_dimension=0, tiled=True
        ).astype(jnp.float32),
        lax.psum_scatter(
            column_parts[5].astype(jnp.bfloat16), "dp", scatter_dimension=0, tiled=True
        ).astype(jnp.float32),
    )
    skip_tile, ada_tile, qkv_tile, out_tile, up_tile, down_tile = weight_tiles
    return (
        layer_output,
        grad_joined[..., :model_width],
        grad_joined[..., model_width:],
        skip_tile,
        ada_tile,
        qkv_tile,
        out_tile,
        up_tile,
        down_tile,
    )


LOG2E = 1.4426950408889634
SCALE = HD**-0.5
PAIR = 2 * HD


def dot_nn(a, b):
    return lax.dot_general(a, b, (((1,), (0,)), ((), ())), preferred_element_type=jnp.float32)


def dot_nt(a, b):
    return lax.dot_general(a, b, (((1,), (1,)), ((), ())), preferred_element_type=jnp.float32)


def dot_tn(a, b):
    return lax.dot_general(a, b, (((0,), (0,)), ((), ())), preferred_element_type=jnp.float32)


def segment_of(index, ends_ref):
    return (index >= ends_ref[0]).astype(jnp.int32) + (index >= ends_ref[1]).astype(jnp.int32)


def segment_span(ends_ref, first, last, length):
    end_a, end_b = ends_ref[0], ends_ref[1]
    low = jnp.where(first < end_a, 0, jnp.where(first < end_b, end_a, end_b))
    high = jnp.where(last < end_a, end_a, jnp.where(last < end_b, end_b, length))
    return low, high


def key_blocks(ends_ref, start, size, length):
    low, high = segment_span(ends_ref, start, start + size - 1, length)
    low_last, _ = segment_span(ends_ref, start + size - 1, start, length)
    first = low // size
    last = (high + size - 1) // size
    whole_first = jnp.where(low == low_last, (low + size - 1) // size, last)
    whole_first = jnp.minimum(whole_first, last)
    whole_last = jnp.where(low == low_last, jnp.maximum(high // size, whole_first), last)
    return first, whole_first, whole_last, last


def turn(pair, cosine, sine_part):
    half = HD // 2
    rows = []
    for head in range(2):
        lower = pair[head * HD : head * HD + half]
        upper = pair[head * HD + half : (head + 1) * HD]
        rows += [lower * cosine - upper * sine_part, lower * sine_part + upper * cosine]
    return jnp.concatenate(rows, axis=0)


def project_kernel(normed_ref, weight_ref, cos_ref, sin_ref, qt_ref, kt_ref, vt_ref, k_ref, v_ref):
    projected = dot_nt(weight_ref[...], normed_ref[0])
    cosine, sine_part = cos_ref[...], sin_ref[...]
    queries = turn(projected[:PAIR], cosine, sine_part).astype(jnp.bfloat16)
    keys = turn(projected[PAIR : 2 * PAIR], cosine, sine_part)
    values = projected[2 * PAIR :]
    qt_ref[0] = (queries.astype(jnp.float32) * SCALE).astype(jnp.bfloat16)
    kt_ref[...] = keys.astype(jnp.bfloat16)
    vt_ref[...] = values.astype(jnp.bfloat16)
    k_ref[...] = keys.T.astype(jnp.bfloat16)
    v_ref[...] = values.T.astype(jnp.bfloat16)


def project_pair(normed_all, weight_rows, cos_all, sin_all):
    chunks, frames, width = normed_all.shape
    length = chunks * frames
    return pl.pallas_call(
        project_kernel,
        grid=(chunks,),
        in_specs=[
            pl.BlockSpec((1, frames, width), lambda i: (i, 0, 0)),
            pl.BlockSpec((3 * PAIR, width), lambda i: (0, 0)),
            pl.BlockSpec((HD // 2, frames), lambda i: (0, i)),
            pl.BlockSpec((HD // 2, frames), lambda i: (0, i)),
        ],
        out_specs=[
            pl.BlockSpec((1, PAIR, frames), lambda i: (i, 0, 0)),
            pl.BlockSpec((PAIR, frames), lambda i: (0, i)),
            pl.BlockSpec((PAIR, frames), lambda i: (0, i)),
            pl.BlockSpec((frames, PAIR), lambda i: (i, 0)),
            pl.BlockSpec((frames, PAIR), lambda i: (i, 0)),
        ],
        out_shape=[
            jax.ShapeDtypeStruct((chunks, PAIR, frames), jnp.bfloat16),
            jax.ShapeDtypeStruct((PAIR, length), jnp.bfloat16),
            jax.ShapeDtypeStruct((PAIR, length), jnp.bfloat16),
            jax.ShapeDtypeStruct((length, PAIR), jnp.bfloat16),
            jax.ShapeDtypeStruct((length, PAIR), jnp.bfloat16),
        ],
        compiler_params=pltpu.CompilerParams(vmem_limit_bytes=32 << 20),
        cost_estimate=pl.CostEstimate(
            flops=6 * length * width * PAIR, bytes_accessed=2 * length * (width + 5 * PAIR), transcendentals=0
        ),
        name="project_pair",
    )(normed_all, weight_rows, cos_all, sin_all)


def split_heads(block):
    row = lax.broadcasted_iota(jnp.int32, block.shape, 0)
    zero = jnp.zeros((), block.dtype)
    return jnp.where(row < HD, block, zero), jnp.where(row < HD, zero, block)


def attend_kernel(ends_ref, qt_ref, k_ref, vt_ref, low_ref, full_ref, total_ref, acc_ref, top_ref, *, size, length):
    start = pl.program_id(0) * size
    queries = split_heads(qt_ref[0])
    query_segment = segment_of(start + lax.broadcasted_iota(jnp.int32, (1, size), 1), ends_ref)
    first, whole_first, whole_last, last = key_blocks(ends_ref, start, size, length)
    acc_ref[...] = jnp.zeros_like(acc_ref)
    top_ref[...] = jnp.full_like(top_ref, masked_score)
    ones = jnp.ones((16, size), jnp.bfloat16)

    def step(masked):
        def run(block, carry):
            offset = pl.multiple_of(block * size, size)
            keys = k_ref[pl.ds(offset, size), :]
            scores = [dot_nn(keys, queries[head]) for head in range(2)]
            if masked:
                key_segment = segment_of(offset + lax.broadcasted_iota(jnp.int32, (size, 1), 0), ends_ref)
                same = key_segment == query_segment
                scores = [jnp.where(same, part, masked_score) for part in scores]
            old = [top_ref[head] for head in range(2)]
            new = [jnp.maximum(old[head], jnp.max(scores[head], axis=0, keepdims=True) * LOG2E) for head in range(2)]
            weights = [jnp.exp2(scores[head] * LOG2E - new[head]).astype(jnp.bfloat16) for head in range(2)]
            for head in range(2):
                values = jnp.concatenate([vt_ref[pl.ds(head * HD, HD), pl.ds(offset, size)], ones], axis=0)
                acc_ref[head] = acc_ref[head] * jnp.exp2(old[head] - new[head]) + dot_nn(values, weights[head])
                top_ref[head] = new[head]
            return carry

        return run

    lax.fori_loop(first, whole_first, step(True), 0)
    lax.fori_loop(whole_first, whole_last, step(False), 0)
    lax.fori_loop(whole_last, last, step(True), 0)
    for head in range(2):
        total = acc_ref[head, HD : HD + 1, :]
        attended = acc_ref[head, :HD, :] / total
        full_ref[0, head * HD : (head + 1) * HD, :] = attended
        low_ref[0, head * HD : (head + 1) * HD, :] = attended.astype(jnp.bfloat16)
        total_ref[0, head : head + 1, :] = jnp.log(total) * LOG2E + top_ref[head]


def attend_pair(ends, qt, k, vt):
    chunks, _, size = qt.shape
    length = k.shape[0]
    chunk = pl.BlockSpec((1, PAIR, size), lambda i, ends: (i, 0, 0))
    return pl.pallas_call(
        partial(attend_kernel, size=size, length=length),
        grid_spec=pltpu.PrefetchScalarGridSpec(
            num_scalar_prefetch=1,
            grid=(chunks,),
            in_specs=[
                chunk,
                pl.BlockSpec((length, PAIR), lambda i, ends: (0, 0)),
                pl.BlockSpec((PAIR, length), lambda i, ends: (0, 0)),
            ],
            out_specs=[chunk, chunk, pl.BlockSpec((1, 2, size), lambda i, ends: (i, 0, 0))],
            scratch_shapes=[pltpu.VMEM((2, HD + 16, size), jnp.float32), pltpu.VMEM((2, 1, size), jnp.float32)],
        ),
        out_shape=[
            jax.ShapeDtypeStruct((chunks, PAIR, size), jnp.bfloat16),
            jax.ShapeDtypeStruct((chunks, PAIR, size), jnp.float32),
            jax.ShapeDtypeStruct((chunks, 2, size), jnp.float32),
        ],
        compiler_params=pltpu.CompilerParams(vmem_limit_bytes=32 << 20),
        cost_estimate=pl.CostEstimate(
            flops=8 * length * length * HD, bytes_accessed=14 * length * PAIR, transcendentals=length * length
        ),
        name="attend_pair",
    )(ends, qt, k, vt)


def attend_back_kernel(
    ends_ref, qt_ref, gt_ref, full_ref, total_ref, k_ref, v_ref, kt_ref, cos_ref, sin_ref, out_ref,
    dk_ref, dv_ref, dq_ref, *, size, length, chunks,
):
    index = pl.program_id(0)
    start = index * size

    @pl.when(index == 0)
    def _():
        dk_ref[...] = jnp.zeros_like(dk_ref)
        dv_ref[...] = jnp.zeros_like(dv_ref)

    queries = split_heads(qt_ref[0])
    grads = split_heads(gt_ref[0])
    product = gt_ref[0].astype(jnp.float32) * full_ref[0]
    row_dot = [jnp.sum(product[head * HD : (head + 1) * HD], axis=0, keepdims=True) for head in range(2)]
    query_segment = segment_of(start + lax.broadcasted_iota(jnp.int32, (1, size), 1), ends_ref)
    first, whole_first, whole_last, last = key_blocks(ends_ref, start, size, length)
    dq_ref[...] = jnp.zeros_like(dq_ref)
    part = size // 2

    def step(masked):
        def run(block, carry):
            for piece in range(2):
                offset = pl.multiple_of(block * size + piece * part, part)
                rows = pl.ds(offset, part)
                keys, values = k_ref[rows, :], v_ref[rows, :]
                for head in range(2):
                    scores = dot_nn(keys, queries[head])
                    if masked:
                        key_segment = segment_of(offset + lax.broadcasted_iota(jnp.int32, (part, 1), 0), ends_ref)
                        scores = jnp.where(key_segment == query_segment, scores, masked_score)
                    weights = jnp.exp2(scores * LOG2E - total_ref[0, head : head + 1, :])
                    grad_weights = dot_nn(values, grads[head])
                    grad_scores = (weights * (grad_weights - row_dot[head])).astype(jnp.bfloat16)
                    dv_ref[rows, :] += dot_nt(weights.astype(jnp.bfloat16), grads[head])
                    dk_ref[rows, :] += dot_nt(grad_scores, queries[head])
                    dq_ref[head * HD : (head + 1) * HD, :] += dot_nn(
                        kt_ref[head * HD : (head + 1) * HD, rows], grad_scores
                    )
            return carry

        return run

    lax.fori_loop(first, whole_first, step(True), 0)
    lax.fori_loop(whole_first, whole_last, step(False), 0)
    lax.fori_loop(whole_last, last, step(True), 0)
    own = pl.ds(pl.multiple_of(start, size), size)
    out_ref[index, :PAIR, :] = turn(dq_ref[...] * SCALE, cos_ref[:, own], -sin_ref[:, own]).astype(jnp.bfloat16)

    @pl.when(index == chunks - 1)
    def _():
        for chunk in range(chunks):
            rows = pl.ds(chunk * size, size)
            turned = turn(dk_ref[rows, :].T, cos_ref[:, rows], -sin_ref[:, rows])
            out_ref[chunk, PAIR : 2 * PAIR, :] = turned.astype(jnp.bfloat16)
            out_ref[chunk, 2 * PAIR :, :] = dv_ref[rows, :].T.astype(jnp.bfloat16)


def attend_pair_back(ends, qt, gt, full, total, k, v, kt, cos_all, sin_all):
    chunks, _, size = qt.shape
    length = k.shape[0]
    chunk = pl.BlockSpec((1, PAIR, size), lambda i, ends: (i, 0, 0))

    def whole(shape):
        return pl.BlockSpec(shape, lambda i, ends: (0,) * len(shape))

    return pl.pallas_call(
        partial(attend_back_kernel, size=size, length=length, chunks=chunks),
        grid_spec=pltpu.PrefetchScalarGridSpec(
            num_scalar_prefetch=1,
            grid=(chunks,),
            in_specs=[
                chunk, chunk, chunk, pl.BlockSpec((1, 2, size), lambda i, ends: (i, 0, 0)),
                whole((length, PAIR)), whole((length, PAIR)), whole((PAIR, length)),
                whole((HD // 2, length)), whole((HD // 2, length)),
            ],
            out_specs=whole((chunks, 3 * PAIR, size)),
            scratch_shapes=[
                pltpu.VMEM((length, PAIR), jnp.float32),
                pltpu.VMEM((length, PAIR), jnp.float32),
                pltpu.VMEM((PAIR, size), jnp.float32),
            ],
        ),
        out_shape=jax.ShapeDtypeStruct((chunks, 3 * PAIR, size), jnp.bfloat16),
        compiler_params=pltpu.CompilerParams(vmem_limit_bytes=40 << 20),
        cost_estimate=pl.CostEstimate(
            flops=20 * length * length * HD, bytes_accessed=30 * length * PAIR, transcendentals=length * length
        ),
        name="attend_pair_back",
    )(ends, qt, gt, full, total, k, v, kt, cos_all, sin_all)


def pair_routes(count):
    routes = [[(source, (3 * source + piece) % count) for source in range(count)] for piece in range(3)]
    slots = [[0] * 3 for _ in range(count)]
    for piece in range(3):
        for source, target in routes[piece]:
            slots[target][piece] = (3 * source + piece) // count
    return routes, slots


def own_pair_columns(tile, count):
    routes, slots = pair_routes(count)
    width = tile.shape[1] // 3
    got = [lax.ppermute(tile[:, p * width : (p + 1) * width], "seq", routes[p]) for p in range(3)]
    slot_of = jnp.asarray(slots, jnp.int32)[lax.axis_index("seq")]
    columns = []
    for slot in range(3):
        columns.append(
            jnp.where(slot_of[0] == slot, got[0], jnp.where(slot_of[1] == slot, got[1], got[2]))
        )
    return jnp.concatenate(columns, axis=1)


def stored_columns(pair_tile, count):
    routes, slots = pair_routes(count)
    width = pair_tile.shape[1] // 3
    slot_of = jnp.asarray(slots, jnp.int32)[lax.axis_index("seq")]
    parts = [pair_tile[:, s * width : (s + 1) * width] for s in range(3)]
    back = []
    for piece in range(3):
        slot = slot_of[piece]
        chosen = jnp.where(slot == 0, parts[0], jnp.where(slot == 1, parts[1], parts[2]))
        back.append(lax.ppermute(chosen, "seq", [(target, source) for source, target in routes[piece]]))
    return jnp.concatenate(back, axis=1)


def chip_routes(dp, seq):
    chips = seq // 2

    def flat(move):
        return [(d * seq + s, move(d, s)) for d in range(dp) for s in range(seq)]

    def along_z(step):
        return flat(lambda d, s: d * seq + 2 * ((s // 2 + step) % chips) + s % 2)

    return {
        "x": flat(lambda d, s: (d ^ 1) * seq + s),
        "y": flat(lambda d, s: (d ^ 2) * seq + s),
        "xy": flat(lambda d, s: (d ^ 3) * seq + s),
        "core": flat(lambda d, s: d * seq + (s ^ 1)),
        "z": [along_z(step) for step in range(1, chips)],
    }


def send(value, route):
    return lax.ppermute(value, ("dp", "seq"), route)


def gather_column(tile, routes):
    return jnp.stack([tile] + [send(tile, route) for route in routes["z"]])


def gather_near(column, route):
    return jnp.stack([column, send(column, route)])


GELU_C = math.sqrt(2.0 / math.pi)


def gelu_parts(value):
    square = value * value
    slope = jnp.tanh(GELU_C * value * (1.0 + 0.044715 * square))
    low = 0.5 * (1.0 + slope)
    derivative = low + 0.5 * value * (1.0 - slope * slope) * (GELU_C * (1.0 + 3 * 0.044715 * square))
    return value * low, derivative


def lanes(parts):
    return jnp.concatenate(parts, axis=1)


def stay_order(value, first, second):
    return (value // second) % 2 + 2 * ((value // first) % 2)


def middle_kernel(
    place_ref, att_ref, stream_ref, low_ref, turned_low_ref, scale_ref, shift_ref,
    up_0, up_1, up_2, up_3, down_0, down_1, down_2, down_3,
    layer_ref, grad_mid_ref, grad_att_ref, sums_ref, down_own_out, down_other_out, up_own_out, up_other_out,
    up_w, down_w, out_w, normed_ref, turned_ref, sorted_ref, middle_ref, out_acc,
    down_own, down_other, up_own, up_other, up_sem, down_sem, out_sem, send_sem, *, dp, seq,
):
    dp_at, chip_at, core_at = place_ref[0], place_ref[1], place_ref[2]
    chips = seq // 2
    up_rows, up_cols = up_0.shape[2], up_0.shape[3]
    cols = down_0.shape[3]
    width = stream_ref.shape[1]
    out_rows = width // dp
    down_rows = down_0.shape[2] - out_rows

    def copies(name):
        made = []
        pieces, masks = ((up_0, up_1, up_2, up_3), (1, 2)) if name == "up" else ((down_0, down_1, down_2, down_3), (2, 1))
        for part in range(4):
            core = core_at if part < 2 else 1 - core_at
            for step in range(2):
                mask = (masks[1] if part % 2 else 0) ^ (masks[0] if step else 0)
                row = jnp.bitwise_xor(dp_at, mask)
                for back in range(chips):
                    block = 2 * lax.rem(chip_at + chips - back, chips) + core
                    column = pl.ds(pl.multiple_of(block * cols, cols), cols)
                    source, at = pieces[part].at[step, back], (part * 2 + step) * chips + back
                    if name == "up":
                        target = up_w.at[block, pl.ds(pl.multiple_of(row * up_rows, up_rows), up_rows), :]
                        sem = up_sem.at[at]
                    elif name == "down":
                        source = source.at[pl.ds(0, down_rows), :]
                        target = down_w.at[pl.ds(pl.multiple_of(row * down_rows, down_rows), down_rows), column]
                        sem = down_sem.at[at]
                    else:
                        source = source.at[pl.ds(down_rows, out_rows), :]
                        target = out_w.at[pl.ds(pl.multiple_of(row * out_rows, out_rows), out_rows), column]
                        sem = out_sem.at[at]
                    made.append(pltpu.make_async_copy(source, target, sem))
        return made

    for name in ("out", "up", "down"):
        for copy in copies(name):
            copy.start()
    tiles = [
        2 * lax.rem(chip_at + ahead, chips) + (1 - core_at if other else core_at)
        for other in range(2)
        for ahead in range(chips)
    ]
    for at, tile in enumerate(tiles):
        rows = pl.ds(pl.multiple_of(tile * cols, cols), cols)
        sorted_ref[at * cols : (at + 1) * cols, :] = turned_low_ref[rows, :]
    for copy in copies("out"):
        copy.wait()
    middle_ref[...] = stream_ref[...] + dot_tn(att_ref[...], out_w[...])
    grad_acc = grad_mid_ref
    chunk = 128

    @pl.loop(0, stream_ref.shape[0] // chunk)
    def _(index):
        rows = pl.ds(pl.multiple_of(index * chunk, chunk), chunk)
        middle = middle_ref[rows, :]
        inverse = lax.rsqrt(jnp.mean(middle * middle, axis=-1, keepdims=True) + epsilon)
        normed = middle * inverse * (1.0 + scale_ref[...]) + shift_ref[...]
        normed_ref[rows, :] = normed.astype(jnp.bfloat16)
        turned = normed.T.astype(jnp.bfloat16)
        for row in range(dp):
            place = stay_order(jnp.bitwise_xor(dp_at, row), 2, 1)
            turned_ref[pl.ds(pl.multiple_of(place * out_rows, out_rows), out_rows), rows] = turned[
                row * out_rows : (row + 1) * out_rows
            ]
        out_acc[rows, :] = jnp.zeros_like(middle)
        grad_acc[rows, :] = jnp.zeros_like(middle)

    for name in ("up", "down"):
        for copy in copies(name):
            copy.wait()

    def hidden_block(other, up_grads):
        def run(ahead, carry):
            core = 1 - core_at if other else core_at
            block = 2 * lax.rem(chip_at + ahead, chips) + core
            rows = pl.ds(pl.multiple_of(block * up_cols, up_cols), up_cols)
            up_weight, down_weight = up_w[block], down_w[rows, :]
            value, derivative = gelu_parts(dot_nn(normed_ref[...], up_weight))
            hidden = value.astype(jnp.bfloat16)
            out_acc[...] += dot_nn(hidden, down_weight)
            grad_up = (dot_nt(low_ref[...], down_weight) * derivative).astype(jnp.bfloat16)
            grad_acc[...] += dot_nt(grad_up, up_weight)
            for owner in range(dp):
                part = dot_nn(turned_ref[owner * up_rows : (owner + 1) * up_rows, :], grad_up)
                up_grads[owner, ahead] = part.astype(jnp.bfloat16)
            per_owner = down_rows // up_cols
            owner = stay_order(jnp.bitwise_xor(dp_at, block // per_owner), 1, 2)
            at = pl.ds(pl.multiple_of(lax.rem(block, per_owner) * cols, cols), cols)
            for pair in range(chips):
                part = dot_nn(sorted_ref[2 * pair * cols : 2 * (pair + 1) * cols, :], hidden).astype(jnp.bfloat16)
                for tile in range(2):
                    target, place = (down_own, 2 * pair + tile) if pair < chips // 2 else (down_other, 2 * pair + tile - chips)
                    target[owner, place, at, :] = part[tile * cols : (tile + 1) * cols]
            return carry

        lax.fori_loop(0, chips, run, 0)

    hidden_block(1, up_other)
    send_up_other = pltpu.make_async_copy(up_other, up_other_out, send_sem.at[0])
    send_up_other.start()
    hidden_block(0, up_own)
    packed = down_rows * cols // up_cols
    sends = [
        pltpu.make_async_copy(up_own, up_own_out, send_sem.at[1]),
        pltpu.make_async_copy(
            down_other.at[:, :, pl.ds(0, packed), :], down_other_out.at[:, :, pl.ds(0, packed), :], send_sem.at[2]
        ),
        pltpu.make_async_copy(
            down_own.at[:, :, pl.ds(0, packed), :], down_own_out.at[:, :, pl.ds(0, packed), :], send_sem.at[3]
        ),
    ]
    for copy in sends:
        copy.start()
    sums_ref[...] = jnp.zeros_like(sums_ref)

    @pl.loop(0, stream_ref.shape[0] // chunk)
    def _(index):
        rows = pl.ds(pl.multiple_of(index * chunk, chunk), chunk)
        middle = middle_ref[rows, :]
        layer_ref[rows, :] = (middle + out_acc[rows, :]).astype(jnp.bfloat16)
        inverse = lax.rsqrt(jnp.mean(middle * middle, axis=-1, keepdims=True) + epsilon)
        unit = middle * inverse
        grad = grad_acc[rows, :]
        lifted = grad * (1.0 + scale_ref[...])
        sums_ref[0:1, :] += jnp.sum(grad * unit, axis=0, keepdims=True)
        sums_ref[1:2, :] += jnp.sum(grad, axis=0, keepdims=True)
        grad_mid = low_ref[rows, :].astype(jnp.float32) + inverse * (
            lifted - unit * jnp.mean(lifted * unit, axis=-1, keepdims=True)
        )
        grad_mid_ref[rows, :] = grad_mid
        normed_ref[rows, :] = grad_mid.astype(jnp.bfloat16)

    grad_att_ref[...] = dot_nt(out_w[...], normed_ref[...]).astype(jnp.bfloat16)
    grads = lanes([normed_ref[:, pl.ds(pl.multiple_of(tile * cols, cols), cols)] for tile in tiles])
    per_row = up_cols // cols
    folded = out_rows // per_row
    for row in range(dp):
        owner = stay_order(jnp.bitwise_xor(dp_at, row), 1, 2)
        product = dot_nn(att_ref[row * out_rows : (row + 1) * out_rows, :], grads).astype(jnp.bfloat16)
        for at in range(seq):
            part = product[:, at * cols : (at + 1) * cols]
            part = lanes([part[i * folded : (i + 1) * folded] for i in range(per_row)])
            target = down_own if at < chips else down_other
            target[owner, at % chips, packed : packed + folded, :] = part
    last = [
        pltpu.make_async_copy(
            down_other.at[:, :, pl.ds(packed, folded), :], down_other_out.at[:, :, pl.ds(packed, folded), :], send_sem.at[4]
        ),
        pltpu.make_async_copy(
            down_own.at[:, :, pl.ds(packed, folded), :], down_own_out.at[:, :, pl.ds(packed, folded), :], send_sem.at[5]
        ),
    ]
    for copy in last:
        copy.start()
    for copy in [send_up_other] + sends + last:
        copy.wait()


def middle_block(place, attended, stream, grad_low, scale, shift, up_pieces, down_pieces, dp, seq):
    frames, width = stream.shape
    tile_cols = up_pieces[0].shape[3]
    hidden = tile_cols * seq
    chips = seq // 2
    packed = hidden // dp * (width // seq) // tile_cols + width // dp * (width // seq) // tile_cols
    whole = pl.BlockSpec(memory_space=pltpu.VMEM)
    anywhere = pl.BlockSpec(memory_space=pl.ANY)
    half, full = jnp.bfloat16, jnp.float32
    down_shape, up_shape = (dp, chips, packed, tile_cols), (dp, chips, width // dp, tile_cols)
    return pl.pallas_call(
        partial(middle_kernel, dp=dp, seq=seq),
        in_specs=[pl.BlockSpec(memory_space=pltpu.SMEM)] + [whole] * 6 + [anywhere] * 8,
        out_specs=[whole] * 4 + [anywhere] * 4,
        out_shape=[
            jax.ShapeDtypeStruct((frames, width), half),
            jax.ShapeDtypeStruct((frames, width), full),
            jax.ShapeDtypeStruct((width, frames), half),
            jax.ShapeDtypeStruct((2, width), full),
            jax.ShapeDtypeStruct(down_shape, half),
            jax.ShapeDtypeStruct(down_shape, half),
            jax.ShapeDtypeStruct(up_shape, half),
            jax.ShapeDtypeStruct(up_shape, half),
        ],
        scratch_shapes=[
            pltpu.VMEM((seq, width, tile_cols), half),
            pltpu.VMEM((hidden, width), half),
            pltpu.VMEM((width, width), half),
            pltpu.VMEM((frames, width), half),
            pltpu.VMEM((width, frames), half),
            pltpu.VMEM((width, frames), half),
            pltpu.VMEM((frames, width), full),
            pltpu.VMEM((frames, width), full),
            pltpu.VMEM(down_shape, half),
            pltpu.VMEM(down_shape, half),
            pltpu.VMEM(up_shape, half),
            pltpu.VMEM(up_shape, half),
            pltpu.SemaphoreType.DMA((dp * seq,)),
            pltpu.SemaphoreType.DMA((dp * seq,)),
            pltpu.SemaphoreType.DMA((dp * seq,)),
            pltpu.SemaphoreType.DMA((6,)),
        ],
        compiler_params=pltpu.CompilerParams(vmem_limit_bytes=62 << 20),
        cost_estimate=pl.CostEstimate(
            flops=12 * frames * width * hidden + 6 * frames * width * width,
            bytes_accessed=8 * hidden * width + 24 * frames * width,
            transcendentals=frames * hidden,
        ),
        name="middle_block",
    )(place, attended, stream, grad_low, grad_low.T, scale, shift, *up_pieces, *down_pieces)


def entry_kernel(main_ref, side_ref, weight_ref, scale_ref, shift_ref, stream_ref, normed_ref, *, dp, seq):
    row = pl.program_id(0)

    @pl.when(row == 0)
    def _():
        stream_ref[...] = jnp.zeros_like(stream_ref)

    operand = jnp.where(row < dp // 2, main_ref[...], side_ref[...])
    stream_ref[...] += dot_nn(operand, lanes([weight_ref[s] for s in range(seq)]))

    @pl.when(row == dp - 1)
    def _():
        stream = stream_ref[...]
        inverse = lax.rsqrt(jnp.mean(stream * stream, axis=-1, keepdims=True) + epsilon)
        normed_ref[...] = (stream * inverse * (1.0 + scale_ref[...]) + shift_ref[...]).astype(jnp.bfloat16)


def entry_block(main, side, skip_tiles, scale, shift, dp, seq):
    frames, width = main.shape
    rows, columns = skip_tiles.shape[1:]
    fixed = pl.BlockSpec((1, width), lambda i: (0, 0))
    return pl.pallas_call(
        partial(entry_kernel, dp=dp, seq=seq),
        grid=(dp,),
        in_specs=[
            pl.BlockSpec((frames, rows), lambda i: (0, jnp.minimum(i, dp // 2 - 1))),
            pl.BlockSpec((frames, rows), lambda i: (0, jnp.maximum(i - dp // 2, 0))),
            pl.BlockSpec((seq, rows, columns), lambda i: (i, 0, 0)),
            fixed,
            fixed,
        ],
        out_specs=[pl.BlockSpec((frames, width), lambda i: (0, 0))] * 2,
        out_shape=[
            jax.ShapeDtypeStruct((frames, width), jnp.float32),
            jax.ShapeDtypeStruct((frames, width), jnp.bfloat16),
        ],
        compiler_params=pltpu.CompilerParams(vmem_limit_bytes=32 << 20),
        cost_estimate=pl.CostEstimate(
            flops=4 * frames * width * width, bytes_accessed=14 * frames * width, transcendentals=0
        ),
        name="entry_block",
    )(main, side, skip_tiles, scale, shift)


def exit_kernel(
    projected_ref, pair_ref, stream_ref, grad_mid_ref, scale_ref, grad_ref, turned_ref, sums_ref, normed_ref,
    *, dp, seq,
):
    rows = pair_ref.shape[1]
    for row in range(dp):
        weight = lanes([pair_ref[row * seq + s] for s in range(seq)])
        normed_ref[:, row * rows : (row + 1) * rows] = dot_nn(weight, projected_ref[...]).T
    grad, stream = normed_ref[...], stream_ref[...]
    inverse = lax.rsqrt(jnp.mean(stream * stream, axis=-1, keepdims=True) + epsilon)
    unit = stream * inverse
    lifted = grad * (1.0 + scale_ref[...])
    sums_ref[0:1, :] = jnp.sum(grad * unit, axis=0, keepdims=True)
    sums_ref[1:2, :] = jnp.sum(grad, axis=0, keepdims=True)
    grad_stream = grad_mid_ref[...] + inverse * (lifted - unit * jnp.mean(lifted * unit, axis=-1, keepdims=True))
    grad_ref[...] = grad_stream.astype(jnp.bfloat16)
    turned_ref[...] = grad_stream.T.astype(jnp.bfloat16)


def exit_block(projected, pair_tiles, stream, grad_mid, scale, dp, seq):
    frames, width = stream.shape
    whole = pl.BlockSpec(memory_space=pltpu.VMEM)
    return pl.pallas_call(
        partial(exit_kernel, dp=dp, seq=seq),
        in_specs=[whole] * 5,
        out_specs=[whole] * 3,
        out_shape=[
            jax.ShapeDtypeStruct((frames, width), jnp.bfloat16),
            jax.ShapeDtypeStruct((width, frames), jnp.bfloat16),
            jax.ShapeDtypeStruct((2, width), jnp.float32),
        ],
        scratch_shapes=[pltpu.VMEM((frames, width), jnp.float32)],
        compiler_params=pltpu.CompilerParams(vmem_limit_bytes=40 << 20),
        cost_estimate=pl.CostEstimate(
            flops=6 * frames * width * width, bytes_accessed=18 * frames * width + 6 * width * width, transcendentals=0
        ),
        name="exit_block",
    )(projected, pair_tiles, stream, grad_mid, scale)


def joined_kernel(grad_ref, weight_ref, main_ref, side_ref, *, dp, seq):
    row = pl.program_id(0)
    grad = dot_nt(grad_ref[...], lanes([weight_ref[s] for s in range(seq)]))

    @pl.when(row < dp // 2)
    def _():
        main_ref[...] = grad

    @pl.when(row >= dp // 2)
    def _():
        side_ref[...] = grad


def joined_grads(grad_stream, skip_tiles, dp, seq):
    frames, width = grad_stream.shape
    rows, columns = skip_tiles.shape[1:]
    out = jax.ShapeDtypeStruct((frames, width), jnp.float32)
    return pl.pallas_call(
        partial(joined_kernel, dp=dp, seq=seq),
        grid=(dp,),
        in_specs=[
            pl.BlockSpec((frames, width), lambda i: (0, 0)),
            pl.BlockSpec((seq, rows, columns), lambda i: (i, 0, 0)),
        ],
        out_specs=[
            pl.BlockSpec((frames, rows), lambda i: (0, jnp.minimum(i, dp // 2 - 1))),
            pl.BlockSpec((frames, rows), lambda i: (0, jnp.maximum(i - dp // 2, 0))),
        ],
        out_shape=[out, out],
        compiler_params=pltpu.CompilerParams(vmem_limit_bytes=32 << 20),
        cost_estimate=pl.CostEstimate(
            flops=4 * frames * width * width, bytes_accessed=14 * frames * width, transcendentals=0
        ),
        name="joined_grads",
    )(grad_stream, skip_tiles)


def near_first(place_ref, chips, other, block):
    core = 1 - place_ref[2] if other else place_ref[2]
    starts = [(2 * lax.rem(place_ref[1] + ahead, chips) + core) * block for ahead in range(chips)]
    return [pl.multiple_of(start, block) for start in starts]


def turned_parts(place_ref, left_ref, right_ref, chips, seq, other):
    block = left_ref.shape[0] // seq
    starts = near_first(place_ref, chips, other, block)
    left = jnp.concatenate([left_ref[pl.ds(start, block), :] for start in starts], axis=0)
    product = dot_nn(left, right_ref[...])
    return [product[ahead * block : (ahead + 1) * block] for ahead in range(chips)]


def plain_parts(place_ref, left_ref, right_ref, chips, seq, other):
    block = right_ref.shape[1] // seq
    starts = near_first(place_ref, chips, other, block)
    product = dot_nn(left_ref[...], lanes([right_ref[:, pl.ds(start, block)] for start in starts]))
    return [product[:, ahead * block : (ahead + 1) * block] for ahead in range(chips)]


def fold_columns(part, width):
    return jnp.concatenate([part[:, at : at + width] for at in range(0, part.shape[1], width)], axis=0)


def fold_rows(part, width):
    rows = part.shape[0] * part.shape[1] // width
    return lanes([part[at : at + rows] for at in range(0, part.shape[0], rows)])


def blocks_kernel(place_ref, *refs, kinds, other, seq, width):
    chips = seq // 2
    step = pl.program_id(0)
    operands, outs = refs[: 2 * len(kinds)], refs[2 * len(kinds) :]
    packed = [[] for _ in range(chips)]
    for at, kind in enumerate(kinds):
        left_ref, right_ref = operands[2 * at], operands[2 * at + 1]
        if kind == "turned":
            parts = [fold_columns(part, width) for part in turned_parts(place_ref, left_ref, right_ref, chips, seq, other)]
        else:
            parts = plain_parts(place_ref, left_ref, right_ref, chips, seq, other)
            parts = [fold_rows(part, width) if part.shape[1] < width else part for part in parts]
        for ahead in range(chips):
            packed[ahead].append(parts[ahead])
    if not other:
        arrived_ref, outs = outs[0], outs[1:]
    for ahead in range(chips):
        row = 0
        for part in packed[ahead]:
            rows = slice(row, row + part.shape[0])
            row += part.shape[0]
            if other:
                outs[0][0, ahead, rows, :] = part.astype(jnp.bfloat16)
            else:
                low = (part + arrived_ref[0, ahead, rows, :].astype(jnp.float32)).astype(jnp.bfloat16)

                @pl.when(step < 2)
                def _(low=low, ahead=ahead, rows=rows):
                    outs[0][0, ahead, rows, :] = low

                @pl.when(step >= 2)
                def _(low=low, ahead=ahead, rows=rows):
                    outs[1][0, ahead, rows, :] = low


def grad_blocks(place, products, masks, seq, width, arrived=None, part=(0, 1)):
    first, second = masks
    chips, dp = seq // 2, 4

    def owner(i, place):
        return jnp.bitwise_xor(place[0], (i % 2) * second + (i // 2) * first)

    specs, operands, kinds, rows, flops = [], [], [], 0, 0
    for kind, left, right in products:
        depth = left.shape[1]
        if kind == "turned":
            columns = right.shape[1] // (dp * part[1])
            shape = (left.shape[0] // seq, columns)
            specs += [
                pl.BlockSpec(left.shape, lambda i, place: (0, 0)),
                pl.BlockSpec((depth, columns), lambda i, place: (0, owner(i, place) * part[1] + part[0])),
            ]
        else:
            shape = (left.shape[0] // dp, right.shape[1] // seq)
            specs += [
                pl.BlockSpec((shape[0], depth), lambda i, place: (owner(i, place), 0)),
                pl.BlockSpec(right.shape, lambda i, place: (0, 0)),
            ]
        operands += [left, right]
        kinds.append(kind)
        rows += shape[0] * shape[1] // width
        flops += 2 * dp * chips * shape[0] * shape[1] * depth
    other = arrived is None
    one = (1, chips, rows, width)
    if other:
        outs, count = [pl.BlockSpec(one, lambda i, place: (i, 0, 0, 0))], 4
    else:
        outs = [
            pl.BlockSpec(one, lambda i, place: (jnp.minimum(i, 1), 0, 0, 0)),
            pl.BlockSpec(one, lambda i, place: (jnp.maximum(i - 2, 0), 0, 0, 0)),
        ]
        count = 2
        specs.append(pl.BlockSpec(one, lambda i, place: (i, 0, 0, 0)))
        operands.append(arrived)
    return pl.pallas_call(
        partial(blocks_kernel, kinds=tuple(kinds), other=other, seq=seq, width=width),
        grid_spec=pltpu.PrefetchScalarGridSpec(num_scalar_prefetch=1, grid=(4,), in_specs=specs, out_specs=outs),
        out_shape=[jax.ShapeDtypeStruct((count, chips, rows, width), jnp.bfloat16)] * len(outs),
        compiler_params=pltpu.CompilerParams(vmem_limit_bytes=48 << 20),
        cost_estimate=pl.CostEstimate(
            flops=flops, bytes_accessed=8 * rows * width * chips * (1 if other else 2) + flops // 512, transcendentals=0
        ),
        name="grad_blocks",
    )(place, *operands)


AXIS_MASK = {"x": 1, "y": 2}


def wide(value):
    return value.astype(jnp.float32)


def low(value):
    return value.astype(jnp.bfloat16)


def pair_sum(place, products, routes, seq, width, first, second, part=(0, 1)):
    masks = (AXIS_MASK[first], AXIS_MASK[second])
    (outgoing,) = grad_blocks(place, products, masks, seq, width, None, part)
    return grad_blocks(place, products, masks, seq, width, send(outgoing, routes["core"]), part)


def dp_gather(tile, routes, dp):
    at = lax.axis_index("dp")
    rows = tile.shape[0]
    full = jnp.zeros((dp * rows, tile.shape[1]), tile.dtype)
    full = lax.dynamic_update_slice_in_dim(full, tile, at * rows, 0)
    for mask, route in ((1, routes["x"]), (2, routes["y"]), (3, routes["xy"])):
        full = lax.dynamic_update_slice_in_dim(full, send(tile, route), jnp.bitwise_xor(at, mask) * rows, 0)
    return full


def local_paired(
    inputs, skip_input, time_embed, segment_ids, span_start, span_length, cotangent,
    skip_weight, ada_weight, qkv_weight, out_weight, up_weight, down_weight,
):
    seq = lax.axis_size("seq")
    dp = lax.axis_size("dp")
    frames, width = inputs.shape[1], inputs.shape[2]
    length = segment_ids.shape[1]
    segments = segment_ids[0]
    end_a = jnp.sum((segments < 1).astype(jnp.int32))
    end_b = jnp.sum((segments < 2).astype(jnp.int32))
    ends = jnp.stack([end_a, end_b])
    firsts = jnp.where(segments == 0, 0, jnp.where(segments == 1, end_a, end_b))
    position = jnp.arange(length, dtype=jnp.int32) - firsts
    half = HD // 2
    frequency = jnp.exp(-math.log(10000.0) * jnp.arange(half, dtype=jnp.float32) / half)
    angles = frequency[:, None] * position.astype(jnp.float32)[None, :]
    cos_all, sin_all = jnp.cos(angles), jnp.sin(angles)
    base = lax.axis_index("seq") * frames
    local_segments = lax.dynamic_slice_in_dim(segments, base, frames, 0)
    local_position = lax.dynamic_slice_in_dim(position, base, frames, 0)
    starts, lengths = span_start[0], span_length[0]

    def pick(table):
        return jnp.where(local_segments == 0, table[0], jnp.where(local_segments == 1, table[1], table[2]))

    span_begin = pick(starts)
    inside = jnp.logical_and(local_position >= span_begin, local_position < span_begin + pick(lengths))
    grad_low = jnp.where(inside[:, None], cotangent[0], jnp.zeros((), jnp.bfloat16))
    routes = chip_routes(dp, seq)
    seq_at = lax.axis_index("seq")
    place = jnp.stack([lax.axis_index("dp"), seq_at // 2, seq_at % 2]).astype(jnp.int32)
    up_column = gather_column(up_weight, routes)
    down_column = gather_column(jnp.concatenate([down_weight, out_weight]), routes)
    embed_all = lax.all_gather(time_embed, "dp", axis=0, tiled=True)
    embed_rows = width // dp
    embed_part = lax.dynamic_slice_in_dim(embed_all, lax.axis_index("dp") * embed_rows, embed_rows, 1)
    modulation_part = jnp.dot(embed_part, ada_weight, preferred_element_type=jnp.float32)
    modulation_part = lax.psum_scatter(modulation_part, "dp", scatter_dimension=0, tiled=True)
    modulation = lax.all_gather(modulation_part, "seq", axis=1, tiled=True)
    scale_one = modulation[:, :width]
    shift_one = modulation[:, width : 2 * width]
    scale_two = modulation[:, 2 * width : 3 * width]
    shift_two = modulation[:, 3 * width :]

    skip_tiles = lax.all_gather(skip_weight, ("dp", "seq"), axis=0)
    pair_tile = own_pair_columns(qkv_weight, seq)
    pair_weight = dp_gather(pair_tile, routes, dp)
    skip_tiles, up_column, down_column, cos_all, sin_all, ends, grad_low, place = lax.optimization_barrier(
        (skip_tiles, up_column, down_column, cos_all, sin_all, ends, grad_low, place)
    )
    stream, normed_one = entry_block(inputs[0], skip_input[0], skip_tiles, scale_one, shift_one, dp, seq)
    normed_all = lax.all_gather(normed_one, "seq", axis=0)
    up_near = gather_near(up_column, routes["x"])
    down_near = gather_near(down_column, routes["y"])
    normed_all, up_near, down_near, pair_weight = lax.optimization_barrier(
        (normed_all, up_near, down_near, pair_weight.T)
    )
    up_far, down_far = send(up_near, routes["y"]), send(down_near, routes["x"])
    up_near_core, down_near_core = send(up_near, routes["core"]), send(down_near, routes["core"])
    qt, kt, vt, keys, values = project_pair(normed_all, pair_weight, cos_all, sin_all)
    attended_pair, attended_wide, total = attend_pair(ends, qt, keys, vt)
    attended_pair, up_far, down_far = lax.optimization_barrier((attended_pair, up_far, down_far))
    up_pieces = (up_near, up_far, up_near_core, send(up_far, routes["core"]))
    down_pieces = (down_near, down_far, down_near_core, send(down_far, routes["core"]))
    attended = lax.all_to_all(attended_pair, "seq", 0, 0).reshape(width, frames)
    layer_output, grad_middle, grad_attended, sums_two, down_own, down_other, up_own, up_other = middle_block(
        place, attended, stream, grad_low, scale_two, shift_two, up_pieces, down_pieces, dp, seq
    )
    grad_pair = lax.all_to_all(grad_attended.reshape(seq, PAIR, frames), "seq", 0, 0)
    down_other, up_other = send(down_other, routes["core"]), send(up_other, routes["core"])
    down_keep, down_away = low(wide(down_own[:2]) + wide(down_other[:2])), low(wide(down_own[2:]) + wide(down_other[2:]))
    up_keep, up_away = low(wide(up_own[:2]) + wide(up_other[:2])), low(wide(up_own[2:]) + wide(up_other[2:]))
    grad_pair, down_away, up_away, down_keep, up_keep = lax.optimization_barrier(
        (grad_pair, down_away, up_away, down_keep, up_keep)
    )
    down_got, up_got = send(down_away, routes["x"]), send(up_away, routes["y"])
    grad_projected = attend_pair_back(ends, qt, grad_pair, attended_wide, total, keys, values, kt, cos_all, sin_all)
    grad_projected, down_got, up_got = lax.optimization_barrier((grad_projected, down_got, up_got))
    grad_local = lax.all_to_all(grad_projected, "seq", 0, 0)
    pair_tiles = lax.all_gather(pair_tile, ("dp", "seq"), axis=0)
    down_back = send(low(wide(down_keep[1]) + wide(down_got[1])), routes["y"])
    up_back = send(low(wide(up_keep[1]) + wide(up_got[1])), routes["x"])
    grad_pair_weight = jnp.einsum(
        "icf,ifd->cd", grad_projected, normed_all, preferred_element_type=jnp.float32
    ).astype(jnp.bfloat16)
    down_total = wide(down_keep[0]) + wide(down_got[0]) + wide(down_back)
    up_total = wide(up_keep[0]) + wide(up_got[0]) + wide(up_back)
    mlp_low = [jnp.concatenate([low(down_total[ahead]), low(up_total[ahead])]) for ahead in range(seq // 2)]
    grad_local, *mlp_low = lax.optimization_barrier((grad_local, *mlp_low))
    mlp_got = [send(mlp_low[ahead + 1], route) for ahead, route in enumerate(routes["z"])]
    mlp_own = jnp.concatenate([down_total[0], up_total[0]])

    grad_stream, grad_stream_turned, sums_one = exit_block(
        grad_local.reshape(3 * width, frames), pair_tiles, stream, grad_middle, scale_one, dp, seq
    )
    joined = jnp.concatenate([inputs[0], skip_input[0]], axis=-1)
    half_tile = skip_weight.shape[0] // 2
    at = lax.axis_index("dp")
    half_pair = 3 * PAIR // 2
    wide_tile = up_weight.shape[1]
    skip_parts = []
    for part, (first, second) in enumerate((("x", "y"), ("y", "x"))):
        keep, away = pair_sum(
            place, [("turned", grad_stream_turned, joined)], routes, seq, half_tile, first, second, (part, 2)
        )
        pair_rows = grad_pair_weight[part * half_pair : (part + 1) * half_pair]

        def pair_block(mask):
            return lax.dynamic_slice_in_dim(pair_rows, jnp.bitwise_xor(at, mask) * half_tile, half_tile, 1)

        near, far = AXIS_MASK[first], AXIS_MASK[second]
        keep = jnp.concatenate([keep.reshape(2, -1, half_tile), jnp.stack([pair_block(0), pair_block(far)])], axis=1)
        away = jnp.concatenate(
            [away.reshape(2, -1, half_tile), jnp.stack([pair_block(near), pair_block(near ^ far)])], axis=1
        )
        skip_parts.append((keep, send(away, routes[first]), routes[second]))
    grad_main, grad_side = joined_grads(grad_stream, skip_tiles, dp, seq)
    skip_own, skip_low, pair_sums = [], [], []
    skip_rows = seq // 2 * (width // seq)
    for keep, got, route in skip_parts:
        back = send(low(wide(keep[1]) + wide(got[1])), route)
        total_part = wide(keep[0]) + wide(got[0]) + wide(back)
        pair_sums.append(total_part[skip_rows:])
        blocks = total_part[:skip_rows].reshape(seq // 2, width // seq, half_tile)
        skip_own.append(blocks[0])
        skip_low.append(low(blocks))
    skip_tile = jnp.concatenate(skip_own, axis=1)
    skip_low = jnp.concatenate(skip_low, axis=2)
    for ahead, route in enumerate(routes["z"]):
        skip_tile = skip_tile + wide(send(skip_low[ahead + 1], route))
    skip_tile = skip_tile.T
    qkv_tile = wide(stored_columns(low(jnp.concatenate(pair_sums)).T, seq))

    mlp_tile = mlp_own
    for piece in mlp_got:
        mlp_tile = mlp_tile + wide(piece)
    columns = width // seq
    fold = down_weight.shape[0] // wide_tile
    down_tile = lanes([mlp_tile[i * columns : (i + 1) * columns] for i in range(fold)]).T
    out_tile = mlp_tile[fold * columns : down_total.shape[1]]
    out_tile = jnp.concatenate([out_tile[:, i * columns : (i + 1) * columns] for i in range(wide_tile // columns)])
    up_tile = mlp_tile[down_total.shape[1] :]
    sums_one, grad_main = lax.optimization_barrier((sums_one, grad_main))
    grad_modulation = jnp.concatenate([sums_one[0], sums_one[1], sums_two[0], sums_two[1]]).reshape(1, seq, -1)
    grad_modulation = jnp.broadcast_to(grad_modulation, (dp,) + grad_modulation.shape[1:]).reshape(dp * seq, -1)
    grad_modulation = lax.all_to_all(grad_modulation, ("dp", "seq"), 0, 0, tiled=True)
    grad_modulation = jnp.sum(grad_modulation.reshape(dp, seq, -1), axis=1)
    ada_tile = lax.dot_general(
        embed_part.astype(jnp.float32), grad_modulation, (((0,), (0,)), ((), ())),
        precision=lax.Precision.HIGHEST,
    )
    return (
        layer_output[None],
        grad_main[None],
        grad_side[None],
        skip_tile,
        ada_tile,
        qkv_tile,
        out_tile,
        up_tile,
        down_tile,
    )


def solution(mesh):
    in_specs = (
        P("dp", "seq", None),
        P("dp", "seq", None),
        P("dp", None),
        P("dp", None),
        P("dp", None),
        P("dp", None),
        P("dp", "seq", None),
        P("dp", "seq"),
        P("dp", "seq"),
        P("dp", "seq"),
        P("dp", "seq"),
        P("dp", "seq"),
        P("dp", "seq"),
    )
    out_specs = (
        P("dp", "seq", None),
        P("dp", "seq", None),
        P("dp", "seq", None),
        P("dp", "seq"),
        P("dp", "seq"),
        P("dp", "seq"),
        P("dp", "seq"),
        P("dp", "seq"),
        P("dp", "seq"),
    )
    seq_size = mesh.shape["seq"]
    paired = H == 2 * seq_size and seq_size % 3 != 0 and mesh.shape["dp"] == 4
    body = local_paired if paired else local_general
    return jax.shard_map(body, mesh=mesh, in_specs=in_specs, out_specs=out_specs, check_vma=False)
```

```python
from functools import partial
import math

import jax
import jax.numpy as jnp
from jax import lax
from jax.experimental import pallas as pl
from jax.experimental.pallas import tpu as pltpu
from jax.sharding import PartitionSpec as P

H = 16
HD = 64
UTT = 3
HG = 8


epsilon = 1e-06
masked_score = -1e30


def ada_norm(stream, scale_part, shift_part):
    inverse = lax.rsqrt(jnp.mean(stream * stream, axis=-1, keepdims=True) + epsilon)
    return stream * inverse * (1.0 + scale_part) + shift_part


def rotate(tensor, cosine, sine_part):
    half_width = tensor.shape[-1] // 2
    lower_half = tensor[..., :half_width]
    upper_half = tensor[..., half_width:]
    cos_wide = cosine[..., None, :]
    sin_wide = sine_part[..., None, :]
    return jnp.concatenate(
        [
            lower_half * cos_wide - upper_half * sin_wide,
            lower_half * sin_wide + upper_half * cos_wide,
        ],
        axis=-1,
    )


def rotary_tables(position, half_width):
    frequency = jnp.exp(-math.log(10000.0) * jnp.arange(half_width, dtype=jnp.float32) / half_width)
    angles = position.astype(jnp.float32)[..., None] * frequency
    return (jnp.cos(angles), jnp.sin(angles))


def gather_weights(skip_tile, ada_tile, qkv_tile, out_tile, up_tile, down_tile):
    row_full = (
        lax.all_gather(skip_tile, "dp", axis=0, tiled=True),
        lax.all_gather(ada_tile, "dp", axis=0, tiled=True),
        lax.all_gather(qkv_tile, "dp", axis=0, tiled=True),
        lax.all_gather(out_tile, "dp", axis=0, tiled=True),
        lax.all_gather(up_tile, "dp", axis=0, tiled=True),
        lax.all_gather(down_tile, "dp", axis=0, tiled=True),
    )
    return (
        lax.all_gather(row_full[0], "seq", axis=1, tiled=True),
        lax.all_gather(row_full[1], "seq", axis=1, tiled=True),
        lax.all_gather(row_full[2], "seq", axis=1, tiled=True),
        lax.all_gather(row_full[3], "seq", axis=1, tiled=True),
        lax.all_gather(row_full[4], "seq", axis=1, tiled=True),
        lax.all_gather(row_full[5], "seq", axis=1, tiled=True),
    )


def group_scores(query_part, key_part, allowed, factor):
    scores = (
        jnp.einsum("qhd,khd->hqk", query_part, key_part, preferred_element_type=jnp.float32)
        * factor
    )
    return jnp.where(allowed[None], scores, masked_score)


def attend_row(queries, key_rows, value_rows, segment_local, segment_full):
    factor = queries.shape[2] ** (-0.5)
    allowed = segment_local[:, None] == segment_full[None, :]
    outputs = []
    totals = []
    for head_start in range(0, H, HG):
        head_end = head_start + HG
        scores = group_scores(
            queries[:, head_start:head_end], key_rows[:, head_start:head_end], allowed, factor
        )
        log_total = jax.nn.logsumexp(scores, axis=-1)
        weights = jnp.exp(scores - log_total[..., None]).astype(jnp.bfloat16)
        outputs.append(
            jnp.einsum(
                "hqk,khd->qhd",
                weights,
                value_rows[:, head_start:head_end],
                preferred_element_type=jnp.float32,
            )
        )
        totals.append(log_total)
    return (jnp.concatenate(outputs, axis=1), jnp.concatenate(totals, axis=0))


def attend_back(
    queries, key_rows, value_rows, segment_local, segment_full, log_total, grad_attended, row_dot
):
    factor = queries.shape[2] ** (-0.5)
    allowed = segment_local[:, None] == segment_full[None, :]
    query_grads = []
    key_grads = []
    value_grads = []
    for head_start in range(0, H, HG):
        head_end = head_start + HG
        key_part = key_rows[:, head_start:head_end]
        query_part = queries[:, head_start:head_end]
        grad_part = grad_attended[:, head_start:head_end]
        scores = group_scores(query_part, key_part, allowed, factor)
        weights = jnp.exp(scores - log_total[head_start:head_end][..., None])
        weights_low = weights.astype(jnp.bfloat16)
        value_grads.append(
            jnp.einsum("hqk,qhd->khd", weights_low, grad_part, preferred_element_type=jnp.float32)
        )
        grad_weights = jnp.einsum(
            "qhd,khd->hqk",
            grad_part,
            value_rows[:, head_start:head_end],
            preferred_element_type=jnp.float32,
        )
        grad_scores = (weights * (grad_weights - row_dot[head_start:head_end][..., None])).astype(
            jnp.bfloat16
        )
        query_grads.append(
            jnp.einsum("hqk,khd->qhd", grad_scores, key_part, preferred_element_type=jnp.float32)
            * factor
        )
        key_grads.append(
            jnp.einsum("hqk,qhd->khd", grad_scores, query_part, preferred_element_type=jnp.float32)
            * factor
        )
    return (
        jnp.concatenate(query_grads, axis=1),
        jnp.concatenate(key_grads, axis=1),
        jnp.concatenate(value_grads, axis=1),
    )


def local_general(
    inputs,
    skip_input,
    time_embed,
    segment_ids,
    span_start,
    span_length,
    cotangent,
    skip_weight,
    ada_weight,
    qkv_weight,
    out_weight,
    up_weight,
    down_weight,
):
    row_count = inputs.shape[0]
    frames = inputs.shape[1]
    model_width = inputs.shape[2]
    row_length = segment_ids.shape[1]
    frame_base = lax.axis_index("seq") * frames
    utterance = jnp.arange(UTT, dtype=jnp.int32)
    member = (segment_ids[:, :, None] == utterance[None, None, :]).astype(jnp.int32)
    counts = jnp.sum(member, axis=1)
    firsts = jnp.cumsum(counts, axis=1) - counts
    local_member = lax.dynamic_slice_in_dim(member, frame_base, frames, 1)
    local_segments = lax.dynamic_slice_in_dim(segment_ids, frame_base, frames, 1)
    local_frames = frame_base + jnp.arange(frames, dtype=jnp.int32)
    position = local_frames[None, :] - jnp.sum(local_member * firsts[:, None, :], axis=2)
    span_begin = jnp.sum(local_member * span_start[:, None, :], axis=2)
    span_end = span_begin + jnp.sum(local_member * span_length[:, None, :], axis=2)
    inside = jnp.logical_and(position >= span_begin, position < span_end)
    cosine, sine_part = rotary_tables(position, HD // 2)
    skip_full, ada_full, qkv_full, out_full, up_full, down_full = gather_weights(
        skip_weight, ada_weight, qkv_weight, out_weight, up_weight, down_weight
    )
    joined = jnp.concatenate([inputs, skip_input], axis=-1)
    stream = jnp.einsum("rfc,cd->rfd", joined, skip_full, preferred_element_type=jnp.float32)
    modulation = jnp.dot(time_embed, ada_full, preferred_element_type=jnp.float32)[:, None, :]
    scale_one = modulation[..., :model_width]
    shift_one = modulation[..., model_width : 2 * model_width]
    scale_two = modulation[..., 2 * model_width : 3 * model_width]
    shift_two = modulation[..., 3 * model_width :]
    normed_one = ada_norm(stream, scale_one, shift_one).astype(jnp.bfloat16)
    projected = jnp.einsum("rfd,de->rfe", normed_one, qkv_full, preferred_element_type=jnp.float32)
    queries = rotate(
        projected[..., :model_width].reshape(row_count, frames, H, HD), cosine, sine_part
    ).astype(jnp.bfloat16)
    key_rotated = rotate(
        projected[..., model_width : 2 * model_width].reshape(row_count, frames, H, HD),
        cosine,
        sine_part,
    )
    key_local = key_rotated.reshape(row_count, frames, model_width).astype(jnp.bfloat16)
    value_local = projected[..., 2 * model_width :].astype(jnp.bfloat16)
    key_all, value_all = (
        lax.all_gather(key_local, "seq", axis=1, tiled=True),
        lax.all_gather(value_local, "seq", axis=1, tiled=True),
    )

    def forward_row(row_items):
        query_row, key_row, value_row, local_row, full_row = row_items
        return attend_row(
            query_row,
            key_row.reshape(row_length, H, HD),
            value_row.reshape(row_length, H, HD),
            local_row,
            full_row,
        )

    attended, log_total = lax.map(
        forward_row, (queries, key_all, value_all, local_segments, segment_ids)
    )
    attended = attended.reshape(row_count, frames, model_width)
    attended_low = attended.astype(jnp.bfloat16)
    middle = stream + jnp.einsum(
        "rfe,ed->rfd", attended_low, out_full, preferred_element_type=jnp.float32
    )
    normed_two = ada_norm(middle, scale_two, shift_two).astype(jnp.bfloat16)
    up_proj = jnp.einsum("rfd,di->rfi", normed_two, up_full, preferred_element_type=jnp.float32)
    hidden = jax.nn.gelu(up_proj, approximate=True).astype(jnp.bfloat16)
    down_proj = jnp.einsum("rfi,id->rfd", hidden, down_full, preferred_element_type=jnp.float32)
    layer_output = (middle + down_proj).astype(jnp.bfloat16)
    skip_full, ada_full, qkv_full, out_full, up_full, down_full = gather_weights(
        skip_weight, ada_weight, qkv_weight, out_weight, up_weight, down_weight
    )
    grad_out = cotangent.astype(jnp.float32) * inside[..., None].astype(jnp.float32)
    grad_low = grad_out.astype(jnp.bfloat16)
    grad_hidden = jnp.einsum("rfd,id->rfi", grad_low, down_full, preferred_element_type=jnp.float32)
    _, gelu_pull = jax.vjp(partial(jax.nn.gelu, approximate=True), up_proj)
    grad_up_act = gelu_pull(grad_hidden)[0].astype(jnp.bfloat16)
    grad_normed_two = jnp.einsum(
        "rfi,di->rfd", grad_up_act, up_full, preferred_element_type=jnp.float32
    )
    _, norm_pull_two = jax.vjp(ada_norm, middle, scale_two, shift_two)
    grad_middle_norm, grad_scale_two, grad_shift_two = norm_pull_two(grad_normed_two)
    grad_middle = grad_out + grad_middle_norm
    grad_middle_low = grad_middle.astype(jnp.bfloat16)
    grad_attended = jnp.einsum(
        "rfd,ed->rfe", grad_middle_low, out_full, preferred_element_type=jnp.float32
    ).astype(jnp.bfloat16)
    row_dot = jnp.sum(
        (grad_attended.astype(jnp.float32) * attended).reshape(row_count, frames, H, HD), axis=-1
    )
    row_dot = jnp.swapaxes(row_dot, 1, 2)
    grad_heads = grad_attended.reshape(row_count, frames, H, HD)

    def backward_row(row_items):
        query_row, key_row, value_row, local_row, full_row, total_row, grad_row, dot_row = row_items
        return attend_back(
            query_row,
            key_row.reshape(row_length, H, HD),
            value_row.reshape(row_length, H, HD),
            local_row,
            full_row,
            total_row,
            grad_row,
            dot_row,
        )

    grad_queries, grad_keys, grad_values = lax.map(
        backward_row,
        (queries, key_all, value_all, local_segments, segment_ids, log_total, grad_heads, row_dot),
    )
    key_share, value_share = (
        lax.psum_scatter(
            grad_keys.reshape(row_count, row_length, model_width).astype(jnp.bfloat16),
            "seq",
            scatter_dimension=1,
            tiled=True,
        ).astype(jnp.float32),
        lax.psum_scatter(
            grad_values.reshape(row_count, row_length, model_width).astype(jnp.bfloat16),
            "seq",
            scatter_dimension=1,
            tiled=True,
        ).astype(jnp.float32),
    )
    _, rotate_pull = jax.vjp(
        partial(rotate, cosine=cosine, sine_part=sine_part),
        jnp.zeros((row_count, frames, H, HD), jnp.float32),
    )
    grad_query_raw = rotate_pull(grad_queries)[0].reshape(row_count, frames, model_width)
    grad_key_raw = rotate_pull(key_share.reshape(row_count, frames, H, HD))[0].reshape(
        row_count, frames, model_width
    )
    grad_projected = jnp.concatenate([grad_query_raw, grad_key_raw, value_share], axis=-1).astype(
        jnp.bfloat16
    )
    grad_normed_one = jnp.einsum(
        "rfe,de->rfd", grad_projected, qkv_full, preferred_element_type=jnp.float32
    )
    _, norm_pull_one = jax.vjp(ada_norm, stream, scale_one, shift_one)
    grad_stream_norm, grad_scale_one, grad_shift_one = norm_pull_one(grad_normed_one)
    grad_stream = (grad_middle + grad_stream_norm).astype(jnp.bfloat16)
    grad_joined = jnp.einsum(
        "rfd,cd->rfc", grad_stream, skip_full, preferred_element_type=jnp.float32
    )
    grad_modulation = jnp.concatenate(
        [grad_scale_one, grad_shift_one, grad_scale_two, grad_shift_two], axis=-1
    )[:, 0, :]
    grad_down = jnp.einsum("rfi,rfd->id", hidden, grad_low, preferred_element_type=jnp.float32)
    grad_up = jnp.einsum("rfd,rfi->di", normed_two, grad_up_act, preferred_element_type=jnp.float32)
    grad_attn_out = jnp.einsum(
        "rfe,rfd->ed", attended_low, grad_middle_low, preferred_element_type=jnp.float32
    )
    grad_qkv = jnp.einsum(
        "rfd,rfe->de", normed_one, grad_projected, preferred_element_type=jnp.float32
    )
    grad_skip_w = jnp.einsum("rfc,rfd->cd", joined, grad_stream, preferred_element_type=jnp.float32)
    grad_ada = jnp.einsum(
        "rd,re->de",
        time_embed.astype(jnp.float32),
        grad_modulation,
        precision=lax.Precision.HIGHEST,
    )
    column_parts = (
        lax.psum_scatter(
            grad_skip_w.astype(jnp.bfloat16), "seq", scatter_dimension=1, tiled=True
        ).astype(jnp.float32),
        lax.psum_scatter(
            grad_ada.astype(jnp.bfloat16), "seq", scatter_dimension=1, tiled=True
        ).astype(jnp.float32),
        lax.psum_scatter(
            grad_qkv.astype(jnp.bfloat16), "seq", scatter_dimension=1, tiled=True
        ).astype(jnp.float32),
        lax.psum_scatter(
            grad_attn_out.astype(jnp.bfloat16), "seq", scatter_dimension=1, tiled=True
        ).astype(jnp.float32),
        lax.psum_scatter(
            grad_up.astype(jnp.bfloat16), "seq", scatter_dimension=1, tiled=True
        ).astype(jnp.float32),
        lax.psum_scatter(
            grad_down.astype(jnp.bfloat16), "seq", scatter_dimension=1, tiled=True
        ).astype(jnp.float32),
    )
    weight_tiles = (
        lax.psum_scatter(
            column_parts[0].astype(jnp.bfloat16), "dp", scatter_dimension=0, tiled=True
        ).astype(jnp.float32),
        lax.psum_scatter(
            column_parts[1].astype(jnp.bfloat16), "dp", scatter_dimension=0, tiled=True
        ).astype(jnp.float32),
        lax.psum_scatter(
            column_parts[2].astype(jnp.bfloat16), "dp", scatter_dimension=0, tiled=True
        ).astype(jnp.float32),
        lax.psum_scatter(
            column_parts[3].astype(jnp.bfloat16), "dp", scatter_dimension=0, tiled=True
        ).astype(jnp.float32),
        lax.psum_scatter(
            column_parts[4].astype(jnp.bfloat16), "dp", scatter_dimension=0, tiled=True
        ).astype(jnp.float32),
        lax.psum_scatter(
            column_parts[5].astype(jnp.bfloat16), "dp", scatter_dimension=0, tiled=True
        ).astype(jnp.float32),
    )
    skip_tile, ada_tile, qkv_tile, out_tile, up_tile, down_tile = weight_tiles
    return (
        layer_output,
        grad_joined[..., :model_width],
        grad_joined[..., model_width:],
        skip_tile,
        ada_tile,
        qkv_tile,
        out_tile,
        up_tile,
        down_tile,
    )


LOG2E = 1.4426950408889634
SCALE = HD**-0.5
PAIR = 2 * HD


def dot_nn(a, b):
    return lax.dot_general(a, b, (((1,), (0,)), ((), ())), preferred_element_type=jnp.float32)


def dot_nt(a, b):
    return lax.dot_general(a, b, (((1,), (1,)), ((), ())), preferred_element_type=jnp.float32)


def dot_tn(a, b):
    return lax.dot_general(a, b, (((0,), (0,)), ((), ())), preferred_element_type=jnp.float32)


def segment_of(index, ends_ref):
    return (index >= ends_ref[0]).astype(jnp.int32) + (index >= ends_ref[1]).astype(jnp.int32)


def segment_span(ends_ref, first, last, length):
    end_a, end_b = ends_ref[0], ends_ref[1]
    low = jnp.where(first < end_a, 0, jnp.where(first < end_b, end_a, end_b))
    high = jnp.where(last < end_a, end_a, jnp.where(last < end_b, end_b, length))
    return low, high


def key_blocks(ends_ref, start, size, length):
    low, high = segment_span(ends_ref, start, start + size - 1, length)
    low_last, _ = segment_span(ends_ref, start + size - 1, start, length)
    first = low // size
    last = (high + size - 1) // size
    whole_first = jnp.where(low == low_last, (low + size - 1) // size, last)
    whole_first = jnp.minimum(whole_first, last)
    whole_last = jnp.where(low == low_last, jnp.maximum(high // size, whole_first), last)
    return first, whole_first, whole_last, last


def turn(pair, cosine, sine_part):
    half = HD // 2
    rows = []
    for head in range(pair.shape[0] // HD):
        lower = pair[head * HD : head * HD + half]
        upper = pair[head * HD + half : (head + 1) * HD]
        rows += [lower * cosine - upper * sine_part, lower * sine_part + upper * cosine]
    return jnp.concatenate(rows, axis=0)


def head_norms(pair):
    square = pair * pair
    return [jnp.sum(square[head * HD : (head + 1) * HD], axis=0, keepdims=True) for head in range(2)]


def project_kernel(
    normed_ref, weight_ref, cos_ref, sin_ref, qt_ref, kt_ref, vt_ref, k_ref, v_ref, norms_ref
):
    projected = dot_nt(weight_ref[...], normed_ref[0])
    cosine, sine_part = cos_ref[...], sin_ref[...]
    queries = turn(projected[:PAIR], cosine, sine_part).astype(jnp.bfloat16)
    keys = turn(projected[PAIR : 2 * PAIR], cosine, sine_part)
    values = projected[2 * PAIR :]
    norms_ref[0] = jnp.concatenate(head_norms(queries.astype(jnp.float32) * SCALE) + head_norms(keys), axis=0)
    qt_ref[0] = (queries.astype(jnp.float32) * SCALE).astype(jnp.bfloat16)
    kt_ref[...] = keys.astype(jnp.bfloat16)
    vt_ref[...] = values.astype(jnp.bfloat16)
    k_ref[...] = keys.T.astype(jnp.bfloat16)
    v_ref[...] = values.T.astype(jnp.bfloat16)


def project_pair(normed_all, weight_rows, cos_all, sin_all):
    chunks, frames, width = normed_all.shape
    length = chunks * frames
    return pl.pallas_call(
        project_kernel,
        grid=(chunks,),
        in_specs=[
            pl.BlockSpec((1, frames, width), lambda i: (i, 0, 0)),
            pl.BlockSpec((3 * PAIR, width), lambda i: (0, 0)),
            pl.BlockSpec((HD // 2, frames), lambda i: (0, i)),
            pl.BlockSpec((HD // 2, frames), lambda i: (0, i)),
        ],
        out_specs=[
            pl.BlockSpec((1, PAIR, frames), lambda i: (i, 0, 0)),
            pl.BlockSpec((PAIR, frames), lambda i: (0, i)),
            pl.BlockSpec((PAIR, frames), lambda i: (0, i)),
            pl.BlockSpec((frames, PAIR), lambda i: (i, 0)),
            pl.BlockSpec((frames, PAIR), lambda i: (i, 0)),
            pl.BlockSpec((1, 4, frames), lambda i: (i, 0, 0)),
        ],
        out_shape=[
            jax.ShapeDtypeStruct((chunks, PAIR, frames), jnp.bfloat16),
            jax.ShapeDtypeStruct((PAIR, length), jnp.bfloat16),
            jax.ShapeDtypeStruct((PAIR, length), jnp.bfloat16),
            jax.ShapeDtypeStruct((length, PAIR), jnp.bfloat16),
            jax.ShapeDtypeStruct((length, PAIR), jnp.bfloat16),
            jax.ShapeDtypeStruct((chunks, 4, frames), jnp.float32),
        ],
        compiler_params=pltpu.CompilerParams(vmem_limit_bytes=60 << 20),
        cost_estimate=pl.CostEstimate(
            flops=6 * length * width * PAIR, bytes_accessed=2 * length * (width + 5 * PAIR), transcendentals=0
        ),
        name="project_pair",
    )(normed_all, weight_rows, cos_all, sin_all)


def split_heads(block):
    row = lax.broadcasted_iota(jnp.int32, block.shape, 0)
    zero = jnp.zeros((), block.dtype)
    return jnp.where(row < HD, block, zero), jnp.where(row < HD, zero, block)


SAFE_SCORE = 60.0


def attend_kernel(
    ends_ref, qt_ref, k_ref, vt_ref, norms_ref, low_ref, full_ref, total_ref, acc_ref, top_ref, *, size, length
):
    index = pl.program_id(0)
    start = index * size
    queries = split_heads(qt_ref[0])
    query_segment = segment_of(start + lax.broadcasted_iota(jnp.int32, (1, size), 1), ends_ref)
    first, whole_first, whole_last, last = key_blocks(ends_ref, start, size, length)
    acc_ref[...] = jnp.zeros_like(acc_ref)
    ones = jnp.ones((16, size), jnp.bfloat16)
    bound = jnp.max(norms_ref[index, :2, :]) * jnp.max(norms_ref[:, 2:, :])
    plain = bound < SAFE_SCORE * SAFE_SCORE

    def step(masked, shifted):
        def run(block, carry):
            offset = pl.multiple_of(block * size, size)
            keys = k_ref[pl.ds(offset, size), :]
            scores = [dot_nn(keys, queries[head]) for head in range(2)]
            if masked:
                key_segment = segment_of(offset + lax.broadcasted_iota(jnp.int32, (size, 1), 0), ends_ref)
                same = key_segment == query_segment
                scores = [jnp.where(same, part, masked_score) for part in scores]
            if shifted:
                old = [top_ref[head] for head in range(2)]
                new = [
                    jnp.maximum(old[head], jnp.max(scores[head], axis=0, keepdims=True) * LOG2E) for head in range(2)
                ]
                weights = [jnp.exp2(scores[head] * LOG2E - new[head]).astype(jnp.bfloat16) for head in range(2)]
            else:
                weights = [jnp.exp2(scores[head] * LOG2E).astype(jnp.bfloat16) for head in range(2)]
            for head in range(2):
                values = jnp.concatenate([vt_ref[pl.ds(head * HD, HD), pl.ds(offset, size)], ones], axis=0)
                if shifted:
                    acc_ref[head] = acc_ref[head] * jnp.exp2(old[head] - new[head]) + dot_nn(values, weights[head])
                    top_ref[head] = new[head]
                else:
                    acc_ref[head] += dot_nn(values, weights[head])
            return carry

        return run

    def loops(shifted):
        lax.fori_loop(first, whole_first, step(True, shifted), 0)
        lax.fori_loop(whole_first, whole_last, step(False, shifted), 0)
        lax.fori_loop(whole_last, last, step(True, shifted), 0)

    @pl.when(plain)
    def _():
        top_ref[...] = jnp.zeros_like(top_ref)
        loops(False)

    @pl.when(jnp.logical_not(plain))
    def _():
        top_ref[...] = jnp.full_like(top_ref, masked_score)
        loops(True)

    for head in range(2):
        total = acc_ref[head, HD : HD + 1, :]
        attended = acc_ref[head, :HD, :] / total
        full_ref[0, head * HD : (head + 1) * HD, :] = attended
        low_ref[0, head * HD : (head + 1) * HD, :] = attended.astype(jnp.bfloat16)
        total_ref[0, head : head + 1, :] = jnp.log(total) * LOG2E + top_ref[head]


def attend_pair(ends, qt, k, vt, norms):
    chunks, _, size = qt.shape
    length = k.shape[0]
    chunk = pl.BlockSpec((1, PAIR, size), lambda i, ends: (i, 0, 0))
    return pl.pallas_call(
        partial(attend_kernel, size=size, length=length),
        grid_spec=pltpu.PrefetchScalarGridSpec(
            num_scalar_prefetch=1,
            grid=(chunks,),
            in_specs=[
                chunk,
                pl.BlockSpec((length, PAIR), lambda i, ends: (0, 0)),
                pl.BlockSpec((PAIR, length), lambda i, ends: (0, 0)),
                pl.BlockSpec(norms.shape, lambda i, ends: (0, 0, 0)),
            ],
            out_specs=[chunk, chunk, pl.BlockSpec((1, 2, size), lambda i, ends: (i, 0, 0))],
            scratch_shapes=[pltpu.VMEM((2, HD + 16, size), jnp.float32), pltpu.VMEM((2, 1, size), jnp.float32)],
        ),
        out_shape=[
            jax.ShapeDtypeStruct((chunks, PAIR, size), jnp.bfloat16),
            jax.ShapeDtypeStruct((chunks, PAIR, size), jnp.float32),
            jax.ShapeDtypeStruct((chunks, 2, size), jnp.float32),
        ],
        compiler_params=pltpu.CompilerParams(vmem_limit_bytes=32 << 20),
        cost_estimate=pl.CostEstimate(
            flops=8 * length * length * HD, bytes_accessed=14 * length * PAIR, transcendentals=length * length
        ),
        name="attend_pair",
    )(ends, qt, k, vt, norms)


def attend_back_kernel(
    ends_ref, qt_ref, gt_ref, full_ref, total_ref, k_ref, v_ref, kt_ref, cos_ref, sin_ref, out_ref,
    dk_ref, dv_ref, dq_ref, *, head, size, length, chunks,
):
    index = pl.program_id(0)
    start = index * size

    @pl.when(index == 0)
    def _():
        dk_ref[...] = jnp.zeros_like(dk_ref)
        dv_ref[...] = jnp.zeros_like(dv_ref)

    mine = slice(head * HD, (head + 1) * HD)
    queries = split_heads(qt_ref[0])[head]
    blank = jnp.zeros_like(gt_ref[0])
    grads = jnp.concatenate([blank, gt_ref[0]] if head else [gt_ref[0], blank], axis=0)
    row_dot = jnp.sum(gt_ref[0].astype(jnp.float32) * full_ref[0, mine, :], axis=0, keepdims=True)
    total = total_ref[0, head : head + 1, :]
    query_segment = segment_of(start + lax.broadcasted_iota(jnp.int32, (1, size), 1), ends_ref)
    first, whole_first, whole_last, last = key_blocks(ends_ref, start, size, length)
    dq_ref[...] = jnp.zeros_like(dq_ref)
    pieces = 2
    part = size // pieces

    def step(masked):
        def run(block, carry):
            for piece in range(pieces):
                offset = pl.multiple_of(block * size + piece * part, part)
                rows = pl.ds(offset, part)
                scores = dot_nn(k_ref[rows, :], queries)
                if masked:
                    key_segment = segment_of(offset + lax.broadcasted_iota(jnp.int32, (part, 1), 0), ends_ref)
                    scores = jnp.where(key_segment == query_segment, scores, masked_score)
                weights = jnp.exp2(scores * LOG2E - total)
                grad_weights = dot_nn(v_ref[rows, :], grads)
                grad_scores = (weights * (grad_weights - row_dot)).astype(jnp.bfloat16)
                dv_ref[rows, :] += dot_nt(weights.astype(jnp.bfloat16), grads)
                dk_ref[rows, :] += dot_nt(grad_scores, queries)
                dq_ref[...] += dot_nn(kt_ref[mine, rows], grad_scores)
            return carry

        return run

    lax.fori_loop(first, whole_first, step(True), 0)
    lax.fori_loop(whole_first, whole_last, step(False), 0)
    lax.fori_loop(whole_last, last, step(True), 0)
    own = pl.ds(pl.multiple_of(start, size), size)
    out_ref[index, :HD, :] = turn(dq_ref[...] * SCALE, cos_ref[:, own], -sin_ref[:, own]).astype(jnp.bfloat16)

    @pl.when(index == chunks - 1)
    def _():
        for chunk in range(chunks):
            rows = pl.ds(chunk * size, size)
            turned = turn(dk_ref[rows, :].T[mine], cos_ref[:, rows], -sin_ref[:, rows])
            out_ref[chunk, HD : 2 * HD, :] = turned.astype(jnp.bfloat16)
            out_ref[chunk, 2 * HD :, :] = dv_ref[rows, :].T[mine].astype(jnp.bfloat16)


def attend_head_back(head, ends, qt, gt, full, total, k, v, kt, cos_all, sin_all):
    chunks, _, size = qt.shape
    length = k.shape[0]
    chunk = pl.BlockSpec((1, PAIR, size), lambda i, ends: (i, 0, 0))

    def whole(shape):
        return pl.BlockSpec(shape, lambda i, ends: (0,) * len(shape))

    return pl.pallas_call(
        partial(attend_back_kernel, head=head, size=size, length=length, chunks=chunks),
        grid_spec=pltpu.PrefetchScalarGridSpec(
            num_scalar_prefetch=1,
            grid=(chunks,),
            in_specs=[
                chunk, pl.BlockSpec((1, HD, size), lambda i, ends: (i, 0, 0)), chunk,
                pl.BlockSpec((1, 2, size), lambda i, ends: (i, 0, 0)),
                whole((length, PAIR)), whole((length, PAIR)), whole((PAIR, length)),
                whole((HD // 2, length)), whole((HD // 2, length)),
            ],
            out_specs=whole((chunks, 3 * HD, size)),
            scratch_shapes=[
                pltpu.VMEM((length, PAIR), jnp.float32),
                pltpu.VMEM((length, PAIR), jnp.float32),
                pltpu.VMEM((HD, size), jnp.float32),
            ],
        ),
        out_shape=jax.ShapeDtypeStruct((chunks, 3 * HD, size), jnp.bfloat16),
        compiler_params=pltpu.CompilerParams(vmem_limit_bytes=60 << 20),
        cost_estimate=pl.CostEstimate(
            flops=40 * length * length * HD, bytes_accessed=20 * length * PAIR, transcendentals=0
        ),
        name="attend_head_back",
    )(ends, qt, gt, full, total, k, v, kt, cos_all, sin_all)


def pair_routes(count):
    routes = [[(source, (3 * source + piece) % count) for source in range(count)] for piece in range(3)]
    slots = [[0] * 3 for _ in range(count)]
    for piece in range(3):
        for source, target in routes[piece]:
            slots[target][piece] = (3 * source + piece) // count
    return routes, slots


def own_pair_rows(tile, count):
    routes, slots = pair_routes(count)
    width = tile.shape[0] // 3
    got = [lax.ppermute(tile[p * width : (p + 1) * width], "seq", routes[p]) for p in range(3)]
    slot_of = jnp.asarray(slots, jnp.int32)[lax.axis_index("seq")]
    rows = []
    for slot in range(3):
        rows.append(jnp.where(slot_of[0] == slot, got[0], jnp.where(slot_of[1] == slot, got[1], got[2])))
    return jnp.concatenate(rows, axis=0)


def stored_rows(pair_tile, count):
    routes, slots = pair_routes(count)
    width = pair_tile.shape[0] // 3
    slot_of = jnp.asarray(slots, jnp.int32)[lax.axis_index("seq")]
    parts = [pair_tile[s * width : (s + 1) * width] for s in range(3)]
    back = []
    for piece in range(3):
        slot = slot_of[piece]
        chosen = jnp.where(slot == 0, parts[0], jnp.where(slot == 1, parts[1], parts[2]))
        back.append(lax.ppermute(chosen, "seq", [(target, source) for source, target in routes[piece]]))
    return jnp.concatenate(back, axis=0)


def chip_routes(dp, seq):
    chips = seq // 2

    def flat(move):
        return [(d * seq + s, move(d, s)) for d in range(dp) for s in range(seq)]

    def along_z(step):
        return flat(lambda d, s: d * seq + 2 * ((s // 2 + step) % chips) + s % 2)

    return {
        "x": flat(lambda d, s: (d ^ 1) * seq + s),
        "y": flat(lambda d, s: (d ^ 2) * seq + s),
        "xy": flat(lambda d, s: (d ^ 3) * seq + s),
        "core": flat(lambda d, s: d * seq + (s ^ 1)),
        "z": [along_z(step) for step in range(1, chips)],
    }


def send(value, route):
    return lax.ppermute(value, ("dp", "seq"), route)


def gather_column(tile, routes):
    return jnp.stack([tile] + [send(tile, route) for route in routes["z"]])


def gather_near(column, route):
    return jnp.stack([column, send(column, route)])


GELU_C = math.sqrt(2.0 / math.pi)


def gelu_parts(value):
    square = value * value
    slope = jnp.tanh(GELU_C * value * (1.0 + 0.044715 * square))
    low = 0.5 * (1.0 + slope)
    derivative = low + 0.5 * value * (1.0 - slope * slope) * (GELU_C * (1.0 + 3 * 0.044715 * square))
    return value * low, derivative


def lanes(parts):
    return jnp.concatenate(parts, axis=1)


def stay_order(value, first, second):
    return (value // second) % 2 + 2 * ((value // first) % 2)


def middle_kernel(
    place_ref, att_ref, stream_ref, low_ref, turned_low_ref, scale_ref, shift_ref,
    up_0, up_1, up_2, up_3, down_0, down_1, down_2, down_3,
    layer_ref, grad_mid_ref, grad_att_a_ref, grad_att_b_ref, sums_ref, down_own_out, down_other_out, up_own_out, up_other_out,
    up_w, down_w, out_w, normed_ref, turned_ref, sorted_ref, middle_ref, out_acc,
    down_own, down_other, up_own, up_other, up_sem, down_sem, out_sem, send_sem, *, dp, seq,
):
    dp_at, chip_at, core_at = place_ref[0], place_ref[1], place_ref[2]
    chips = seq // 2
    up_rows, up_cols = up_0.shape[2], up_0.shape[3]
    cols = down_0.shape[3]
    width = stream_ref.shape[1]
    out_rows = width // dp
    down_rows = down_0.shape[2] - out_rows

    def copies(name):
        made = []
        pieces, masks = ((up_0, up_1, up_2, up_3), (1, 2)) if name == "up" else ((down_0, down_1, down_2, down_3), (2, 1))
        for part in range(4):
            core = core_at if part < 2 else 1 - core_at
            for step in range(2):
                mask = (masks[1] if part % 2 else 0) ^ (masks[0] if step else 0)
                row = jnp.bitwise_xor(dp_at, mask)
                for back in range(chips):
                    block = 2 * lax.rem(chip_at + chips - back, chips) + core
                    column = pl.ds(pl.multiple_of(block * cols, cols), cols)
                    source, at = pieces[part].at[step, back], (part * 2 + step) * chips + back
                    if name == "up":
                        target = up_w.at[block, pl.ds(pl.multiple_of(row * up_rows, up_rows), up_rows), :]
                        sem = up_sem.at[at]
                    elif name == "down":
                        source = source.at[pl.ds(0, down_rows), :]
                        target = down_w.at[pl.ds(pl.multiple_of(row * down_rows, down_rows), down_rows), column]
                        sem = down_sem.at[at]
                    else:
                        source = source.at[pl.ds(down_rows, out_rows), :]
                        target = out_w.at[pl.ds(pl.multiple_of(row * out_rows, out_rows), out_rows), column]
                        sem = out_sem.at[at]
                    made.append(pltpu.make_async_copy(source, target, sem))
        return made

    for name in ("out", "up", "down"):
        for copy in copies(name):
            copy.start()
    tiles = [
        2 * lax.rem(chip_at + ahead, chips) + (1 - core_at if other else core_at)
        for other in range(2)
        for ahead in range(chips)
    ]
    for at, tile in enumerate(tiles):
        rows = pl.ds(pl.multiple_of(tile * cols, cols), cols)
        sorted_ref[at * cols : (at + 1) * cols, :] = turned_low_ref[rows, :]
    for copy in copies("out"):
        copy.wait()
    middle_ref[...] = stream_ref[...] + dot_tn(att_ref[...], out_w[...])
    grad_acc = grad_mid_ref
    chunk = 128

    @pl.loop(0, stream_ref.shape[0] // chunk)
    def _(index):
        rows = pl.ds(pl.multiple_of(index * chunk, chunk), chunk)
        middle = middle_ref[rows, :]
        inverse = lax.rsqrt(jnp.mean(middle * middle, axis=-1, keepdims=True) + epsilon)
        normed = middle * inverse * (1.0 + scale_ref[...]) + shift_ref[...]
        normed_ref[rows, :] = normed.astype(jnp.bfloat16)
        turned = normed.T.astype(jnp.bfloat16)
        for row in range(dp):
            place = stay_order(jnp.bitwise_xor(dp_at, row), 2, 1)
            turned_ref[pl.ds(pl.multiple_of(place * out_rows, out_rows), out_rows), rows] = turned[
                row * out_rows : (row + 1) * out_rows
            ]
        out_acc[rows, :] = jnp.zeros_like(middle)
        grad_acc[rows, :] = jnp.zeros_like(middle)

    for name in ("up", "down"):
        for copy in copies(name):
            copy.wait()

    def hidden_block(other, up_grads):
        def run(ahead, carry):
            core = 1 - core_at if other else core_at
            block = 2 * lax.rem(chip_at + ahead, chips) + core
            rows = pl.ds(pl.multiple_of(block * up_cols, up_cols), up_cols)
            up_weight, down_weight = up_w[block], down_w[rows, :]
            value, derivative = gelu_parts(dot_nn(normed_ref[...], up_weight))
            hidden = value.astype(jnp.bfloat16)
            out_acc[...] += dot_nn(hidden, down_weight)
            grad_up = (dot_nt(low_ref[...], down_weight) * derivative).astype(jnp.bfloat16)
            grad_acc[...] += dot_nt(grad_up, up_weight)
            for owner in range(dp):
                part = dot_nn(turned_ref[owner * up_rows : (owner + 1) * up_rows, :], grad_up)
                up_grads[owner, ahead] = part.astype(jnp.bfloat16)
            per_owner = down_rows // up_cols
            owner = stay_order(jnp.bitwise_xor(dp_at, block // per_owner), 1, 2)
            at = pl.ds(pl.multiple_of(lax.rem(block, per_owner) * cols, cols), cols)
            for pair in range(chips):
                part = dot_nn(sorted_ref[2 * pair * cols : 2 * (pair + 1) * cols, :], hidden).astype(jnp.bfloat16)
                for tile in range(2):
                    target, place = (down_own, 2 * pair + tile) if pair < chips // 2 else (down_other, 2 * pair + tile - chips)
                    target[owner, place, at, :] = part[tile * cols : (tile + 1) * cols]
            return carry

        lax.fori_loop(0, chips, run, 0)

    hidden_block(1, up_other)
    send_up_other = pltpu.make_async_copy(up_other, up_other_out, send_sem.at[0])
    send_up_other.start()
    hidden_block(0, up_own)
    packed = down_rows * cols // up_cols
    sends = [
        pltpu.make_async_copy(up_own, up_own_out, send_sem.at[1]),
        pltpu.make_async_copy(
            down_other.at[:, :, pl.ds(0, packed), :], down_other_out.at[:, :, pl.ds(0, packed), :], send_sem.at[2]
        ),
        pltpu.make_async_copy(
            down_own.at[:, :, pl.ds(0, packed), :], down_own_out.at[:, :, pl.ds(0, packed), :], send_sem.at[3]
        ),
    ]
    for copy in sends:
        copy.start()
    sums_ref[...] = jnp.zeros_like(sums_ref)

    @pl.loop(0, stream_ref.shape[0] // chunk)
    def _(index):
        rows = pl.ds(pl.multiple_of(index * chunk, chunk), chunk)
        middle = middle_ref[rows, :]
        layer_ref[rows, :] = (middle + out_acc[rows, :]).astype(jnp.bfloat16)
        inverse = lax.rsqrt(jnp.mean(middle * middle, axis=-1, keepdims=True) + epsilon)
        unit = middle * inverse
        grad = grad_acc[rows, :]
        lifted = grad * (1.0 + scale_ref[...])
        sums_ref[0:1, :] += jnp.sum(grad * unit, axis=0, keepdims=True)
        sums_ref[1:2, :] += jnp.sum(grad, axis=0, keepdims=True)
        grad_mid = low_ref[rows, :].astype(jnp.float32) + inverse * (
            lifted - unit * jnp.mean(lifted * unit, axis=-1, keepdims=True)
        )
        grad_mid_ref[rows, :] = grad_mid
        normed_ref[rows, :] = grad_mid.astype(jnp.bfloat16)

    grad_att = dot_nt(out_w[...], normed_ref[...]).astype(jnp.bfloat16)
    for target in range(seq):
        grad_att_a_ref[target] = grad_att[target * PAIR : target * PAIR + HD]
        grad_att_b_ref[target] = grad_att[target * PAIR + HD : (target + 1) * PAIR]
    grads = lanes([normed_ref[:, pl.ds(pl.multiple_of(tile * cols, cols), cols)] for tile in tiles])
    per_row = up_cols // cols
    folded = out_rows // per_row
    for row in range(dp):
        owner = stay_order(jnp.bitwise_xor(dp_at, row), 1, 2)
        product = dot_nn(att_ref[row * out_rows : (row + 1) * out_rows, :], grads).astype(jnp.bfloat16)
        for at in range(seq):
            part = product[:, at * cols : (at + 1) * cols]
            part = lanes([part[i * folded : (i + 1) * folded] for i in range(per_row)])
            target = down_own if at < chips else down_other
            target[owner, at % chips, packed : packed + folded, :] = part
    last = [
        pltpu.make_async_copy(
            down_other.at[:, :, pl.ds(packed, folded), :], down_other_out.at[:, :, pl.ds(packed, folded), :], send_sem.at[4]
        ),
        pltpu.make_async_copy(
            down_own.at[:, :, pl.ds(packed, folded), :], down_own_out.at[:, :, pl.ds(packed, folded), :], send_sem.at[5]
        ),
    ]
    for copy in last:
        copy.start()
    for copy in [send_up_other] + sends + last:
        copy.wait()


def middle_block(place, attended, stream, grad_low, scale, shift, up_pieces, down_pieces, dp, seq):
    frames, width = stream.shape
    tile_cols = up_pieces[0].shape[3]
    hidden = tile_cols * seq
    chips = seq // 2
    packed = hidden // dp * (width // seq) // tile_cols + width // dp * (width // seq) // tile_cols
    whole = pl.BlockSpec(memory_space=pltpu.VMEM)
    anywhere = pl.BlockSpec(memory_space=pl.ANY)
    half, full = jnp.bfloat16, jnp.float32
    down_shape, up_shape = (dp, chips, packed, tile_cols), (dp, chips, width // dp, tile_cols)
    return pl.pallas_call(
        partial(middle_kernel, dp=dp, seq=seq),
        in_specs=[pl.BlockSpec(memory_space=pltpu.SMEM)] + [whole] * 6 + [anywhere] * 8,
        out_specs=[whole] * 5 + [anywhere] * 4,
        out_shape=[
            jax.ShapeDtypeStruct((frames, width), half),
            jax.ShapeDtypeStruct((frames, width), full),
            jax.ShapeDtypeStruct((seq, HD, frames), half),
            jax.ShapeDtypeStruct((seq, HD, frames), half),
            jax.ShapeDtypeStruct((2, width), full),
            jax.ShapeDtypeStruct(down_shape, half),
            jax.ShapeDtypeStruct(down_shape, half),
            jax.ShapeDtypeStruct(up_shape, half),
            jax.ShapeDtypeStruct(up_shape, half),
        ],
        scratch_shapes=[
            pltpu.VMEM((seq, width, tile_cols), half),
            pltpu.VMEM((hidden, width), half),
            pltpu.VMEM((width, width), half),
            pltpu.VMEM((frames, width), half),
            pltpu.VMEM((width, frames), half),
            pltpu.VMEM((width, frames), half),
            pltpu.VMEM((frames, width), full),
            pltpu.VMEM((frames, width), full),
            pltpu.VMEM(down_shape, half),
            pltpu.VMEM(down_shape, half),
            pltpu.VMEM(up_shape, half),
            pltpu.VMEM(up_shape, half),
            pltpu.SemaphoreType.DMA((dp * seq,)),
            pltpu.SemaphoreType.DMA((dp * seq,)),
            pltpu.SemaphoreType.DMA((dp * seq,)),
            pltpu.SemaphoreType.DMA((6,)),
        ],
        compiler_params=pltpu.CompilerParams(vmem_limit_bytes=62 << 20),
        cost_estimate=pl.CostEstimate(
            flops=12 * frames * width * hidden + 6 * frames * width * width,
            bytes_accessed=8 * hidden * width + 24 * frames * width,
            transcendentals=frames * hidden,
        ),
        name="middle_block",
    )(place, attended, stream, grad_low, grad_low.T, scale, shift, *up_pieces, *down_pieces)


def entry_kernel(main_ref, side_ref, weight_ref, scale_ref, shift_ref, stream_ref, normed_ref, *, dp, seq):
    row = pl.program_id(0)

    @pl.when(row == 0)
    def _():
        stream_ref[...] = jnp.zeros_like(stream_ref)

    operand = jnp.where(row < dp // 2, main_ref[...], side_ref[...])
    stream_ref[...] += dot_nn(operand, lanes([weight_ref[s] for s in range(seq)]))

    @pl.when(row == dp - 1)
    def _():
        stream = stream_ref[...]
        inverse = lax.rsqrt(jnp.mean(stream * stream, axis=-1, keepdims=True) + epsilon)
        normed_ref[...] = (stream * inverse * (1.0 + scale_ref[...]) + shift_ref[...]).astype(jnp.bfloat16)


def entry_block(main, side, skip_tiles, scale, shift, dp, seq):
    frames, width = main.shape
    rows, columns = skip_tiles.shape[1:]
    fixed = pl.BlockSpec((1, width), lambda i: (0, 0))
    return pl.pallas_call(
        partial(entry_kernel, dp=dp, seq=seq),
        grid=(dp,),
        in_specs=[
            pl.BlockSpec((frames, rows), lambda i: (0, jnp.minimum(i, dp // 2 - 1))),
            pl.BlockSpec((frames, rows), lambda i: (0, jnp.maximum(i - dp // 2, 0))),
            pl.BlockSpec((seq, rows, columns), lambda i: (i, 0, 0)),
            fixed,
            fixed,
        ],
        out_specs=[pl.BlockSpec((frames, width), lambda i: (0, 0))] * 2,
        out_shape=[
            jax.ShapeDtypeStruct((frames, width), jnp.float32),
            jax.ShapeDtypeStruct((frames, width), jnp.bfloat16),
        ],
        compiler_params=pltpu.CompilerParams(vmem_limit_bytes=32 << 20),
        cost_estimate=pl.CostEstimate(
            flops=4 * frames * width * width, bytes_accessed=14 * frames * width, transcendentals=0
        ),
        name="entry_block",
    )(main, side, skip_tiles, scale, shift)


def exit_kernel(
    head_a_ref, head_b_ref, pair_ref, stream_ref, grad_mid_ref, scale_ref, grad_ref, turned_ref, sums_ref, normed_ref,
    *, dp, seq,
):
    rows = pair_ref.shape[2]
    parts = [
        head_ref[s, piece * HD : (piece + 1) * HD]
        for s in range(seq)
        for piece in range(3)
        for head_ref in (head_a_ref, head_b_ref)
    ]
    projected = jnp.concatenate(parts, axis=0).T
    for row in range(dp):
        weight = pair_ref[row * seq : (row + 1) * seq].reshape(projected.shape[1], rows)
        normed_ref[:, row * rows : (row + 1) * rows] = dot_nn(projected, weight)
    grad, stream = normed_ref[...], stream_ref[...]
    inverse = lax.rsqrt(jnp.mean(stream * stream, axis=-1, keepdims=True) + epsilon)
    unit = stream * inverse
    lifted = grad * (1.0 + scale_ref[...])
    sums_ref[0:1, :] = jnp.sum(grad * unit, axis=0, keepdims=True)
    sums_ref[1:2, :] = jnp.sum(grad, axis=0, keepdims=True)
    grad_stream = grad_mid_ref[...] + inverse * (lifted - unit * jnp.mean(lifted * unit, axis=-1, keepdims=True))
    grad_ref[...] = grad_stream.astype(jnp.bfloat16)
    turned_ref[...] = grad_stream.T.astype(jnp.bfloat16)


def exit_block(head_a, head_b, pair_tiles, stream, grad_mid, scale, dp, seq):
    frames, width = stream.shape
    whole = pl.BlockSpec(memory_space=pltpu.VMEM)
    return pl.pallas_call(
        partial(exit_kernel, dp=dp, seq=seq),
        in_specs=[whole] * 6,
        out_specs=[whole] * 3,
        out_shape=[
            jax.ShapeDtypeStruct((frames, width), jnp.bfloat16),
            jax.ShapeDtypeStruct((width, frames), jnp.bfloat16),
            jax.ShapeDtypeStruct((2, width), jnp.float32),
        ],
        scratch_shapes=[pltpu.VMEM((frames, width), jnp.float32)],
        compiler_params=pltpu.CompilerParams(vmem_limit_bytes=40 << 20),
        cost_estimate=pl.CostEstimate(
            flops=6 * frames * width * width, bytes_accessed=18 * frames * width + 6 * width * width, transcendentals=0
        ),
        name="exit_block",
    )(head_a, head_b, pair_tiles, stream, grad_mid, scale)


def joined_kernel(grad_ref, weight_ref, main_ref, side_ref, *, dp, seq):
    row = pl.program_id(0)
    grad = dot_nt(grad_ref[...], lanes([weight_ref[s] for s in range(seq)]))

    @pl.when(row < dp // 2)
    def _():
        main_ref[...] = grad

    @pl.when(row >= dp // 2)
    def _():
        side_ref[...] = grad


def joined_grads(grad_stream, skip_tiles, dp, seq):
    frames, width = grad_stream.shape
    rows, columns = skip_tiles.shape[1:]
    out = jax.ShapeDtypeStruct((frames, width), jnp.float32)
    return pl.pallas_call(
        partial(joined_kernel, dp=dp, seq=seq),
        grid=(dp,),
        in_specs=[
            pl.BlockSpec((frames, width), lambda i: (0, 0)),
            pl.BlockSpec((seq, rows, columns), lambda i: (i, 0, 0)),
        ],
        out_specs=[
            pl.BlockSpec((frames, rows), lambda i: (0, jnp.minimum(i, dp // 2 - 1))),
            pl.BlockSpec((frames, rows), lambda i: (0, jnp.maximum(i - dp // 2, 0))),
        ],
        out_shape=[out, out],
        compiler_params=pltpu.CompilerParams(vmem_limit_bytes=32 << 20),
        cost_estimate=pl.CostEstimate(
            flops=4 * frames * width * width, bytes_accessed=14 * frames * width, transcendentals=0
        ),
        name="joined_grads",
    )(grad_stream, skip_tiles)


def near_first(place_ref, chips, other, block):
    core = 1 - place_ref[2] if other else place_ref[2]
    starts = [(2 * lax.rem(place_ref[1] + ahead, chips) + core) * block for ahead in range(chips)]
    return [pl.multiple_of(start, block) for start in starts]


def turned_parts(place_ref, left_ref, right_ref, chips, seq, other):
    block = left_ref.shape[0] // seq
    starts = near_first(place_ref, chips, other, block)
    left = jnp.concatenate([left_ref[pl.ds(start, block), :] for start in starts], axis=0)
    product = dot_nn(left, right_ref[...])
    return [product[ahead * block : (ahead + 1) * block] for ahead in range(chips)]


def plain_parts(place_ref, left_ref, right_ref, chips, seq, other):
    block = right_ref.shape[1] // seq
    starts = near_first(place_ref, chips, other, block)
    product = dot_nn(left_ref[...], lanes([right_ref[:, pl.ds(start, block)] for start in starts]))
    return [product[:, ahead * block : (ahead + 1) * block] for ahead in range(chips)]


def fold_columns(part, width):
    return jnp.concatenate([part[:, at : at + width] for at in range(0, part.shape[1], width)], axis=0)


def fold_rows(part, width):
    rows = part.shape[0] * part.shape[1] // width
    return lanes([part[at : at + rows] for at in range(0, part.shape[0], rows)])


def blocks_kernel(place_ref, *refs, kinds, other, seq, width):
    chips = seq // 2
    step = pl.program_id(0)
    operands, outs = refs[: 2 * len(kinds)], refs[2 * len(kinds) :]
    packed = [[] for _ in range(chips)]
    for at, kind in enumerate(kinds):
        left_ref, right_ref = operands[2 * at], operands[2 * at + 1]
        if kind == "turned":
            parts = [fold_columns(part, width) for part in turned_parts(place_ref, left_ref, right_ref, chips, seq, other)]
        else:
            parts = plain_parts(place_ref, left_ref, right_ref, chips, seq, other)
            parts = [fold_rows(part, width) if part.shape[1] < width else part for part in parts]
        for ahead in range(chips):
            packed[ahead].append(parts[ahead])
    if not other:
        arrived_ref, outs = outs[0], outs[1:]
    for ahead in range(chips):
        row = 0
        for part in packed[ahead]:
            rows = slice(row, row + part.shape[0])
            row += part.shape[0]
            if other:
                outs[0][0, ahead, rows, :] = part.astype(jnp.bfloat16)
            else:
                low = (part + arrived_ref[0, ahead, rows, :].astype(jnp.float32)).astype(jnp.bfloat16)

                @pl.when(step < 2)
                def _(low=low, ahead=ahead, rows=rows):
                    outs[0][0, ahead, rows, :] = low

                @pl.when(step >= 2)
                def _(low=low, ahead=ahead, rows=rows):
                    outs[1][0, ahead, rows, :] = low


def grad_blocks(place, products, masks, seq, width, arrived=None, part=(0, 1)):
    first, second = masks
    chips, dp = seq // 2, 4

    def owner(i, place):
        return jnp.bitwise_xor(place[0], (i % 2) * second + (i // 2) * first)

    specs, operands, kinds, rows, flops = [], [], [], 0, 0
    for kind, left, right in products:
        depth = left.shape[1]
        if kind == "turned":
            columns = right.shape[1] // (dp * part[1])
            shape = (left.shape[0] // seq, columns)
            specs += [
                pl.BlockSpec(left.shape, lambda i, place: (0, 0)),
                pl.BlockSpec((depth, columns), lambda i, place: (0, owner(i, place) * part[1] + part[0])),
            ]
        else:
            shape = (left.shape[0] // dp, right.shape[1] // seq)
            specs += [
                pl.BlockSpec((shape[0], depth), lambda i, place: (owner(i, place), 0)),
                pl.BlockSpec(right.shape, lambda i, place: (0, 0)),
            ]
        operands += [left, right]
        kinds.append(kind)
        rows += shape[0] * shape[1] // width
        flops += 2 * dp * chips * shape[0] * shape[1] * depth
    other = arrived is None
    one = (1, chips, rows, width)
    if other:
        outs, count = [pl.BlockSpec(one, lambda i, place: (i, 0, 0, 0))], 4
    else:
        outs = [
            pl.BlockSpec(one, lambda i, place: (jnp.minimum(i, 1), 0, 0, 0)),
            pl.BlockSpec(one, lambda i, place: (jnp.maximum(i - 2, 0), 0, 0, 0)),
        ]
        count = 2
        specs.append(pl.BlockSpec(one, lambda i, place: (i, 0, 0, 0)))
        operands.append(arrived)
    return pl.pallas_call(
        partial(blocks_kernel, kinds=tuple(kinds), other=other, seq=seq, width=width),
        grid_spec=pltpu.PrefetchScalarGridSpec(num_scalar_prefetch=1, grid=(4,), in_specs=specs, out_specs=outs),
        out_shape=[jax.ShapeDtypeStruct((count, chips, rows, width), jnp.bfloat16)] * len(outs),
        compiler_params=pltpu.CompilerParams(vmem_limit_bytes=48 << 20),
        cost_estimate=pl.CostEstimate(
            flops=flops, bytes_accessed=8 * rows * width * chips * (1 if other else 2) + flops // 512, transcendentals=0
        ),
        name="grad_blocks",
    )(place, *operands)


AXIS_MASK = {"x": 1, "y": 2}


def wide(value):
    return value.astype(jnp.float32)


def low(value):
    return value.astype(jnp.bfloat16)


def dp_gather(tile, routes, dp):
    at = lax.axis_index("dp")
    columns = tile.shape[1]
    full = jnp.zeros((tile.shape[0], dp * columns), tile.dtype)
    full = lax.dynamic_update_slice_in_dim(full, tile, at * columns, 1)
    for mask, route in ((1, routes["x"]), (2, routes["y"]), (3, routes["xy"])):
        full = lax.dynamic_update_slice_in_dim(full, send(tile, route), jnp.bitwise_xor(at, mask) * columns, 1)
    return full


def local_paired(
    inputs, skip_input, time_embed, segment_ids, span_start, span_length, cotangent,
    skip_weight, ada_weight, qkv_weight, out_weight, up_weight, down_weight,
):
    seq = lax.axis_size("seq")
    dp = lax.axis_size("dp")
    frames, width = inputs.shape[1], inputs.shape[2]
    length = segment_ids.shape[1]
    segments = segment_ids[0]
    end_a = jnp.sum((segments < 1).astype(jnp.int32))
    end_b = jnp.sum((segments < 2).astype(jnp.int32))
    ends = jnp.stack([end_a, end_b])
    firsts = jnp.where(segments == 0, 0, jnp.where(segments == 1, end_a, end_b))
    position = jnp.arange(length, dtype=jnp.int32) - firsts
    half = HD // 2
    frequency = jnp.exp(-math.log(10000.0) * jnp.arange(half, dtype=jnp.float32) / half)
    angles = frequency[:, None] * position.astype(jnp.float32)[None, :]
    cos_all, sin_all = jnp.cos(angles), jnp.sin(angles)
    base = lax.axis_index("seq") * frames
    local_segments = lax.dynamic_slice_in_dim(segments, base, frames, 0)
    local_position = lax.dynamic_slice_in_dim(position, base, frames, 0)
    starts, lengths = span_start[0], span_length[0]

    def pick(table):
        return jnp.where(local_segments == 0, table[0], jnp.where(local_segments == 1, table[1], table[2]))

    span_begin = pick(starts)
    inside = jnp.logical_and(local_position >= span_begin, local_position < span_begin + pick(lengths))
    grad_low = jnp.where(inside[:, None], cotangent[0], jnp.zeros((), jnp.bfloat16))
    routes = chip_routes(dp, seq)
    seq_at = lax.axis_index("seq")
    place = jnp.stack([lax.axis_index("dp"), seq_at // 2, seq_at % 2]).astype(jnp.int32)
    up_column = gather_column(up_weight, routes)
    down_column = gather_column(jnp.concatenate([down_weight, out_weight]), routes)
    embed_all = lax.all_gather(time_embed, "dp", axis=0, tiled=True)
    embed_rows = width // dp
    embed_part = lax.dynamic_slice_in_dim(embed_all, lax.axis_index("dp") * embed_rows, embed_rows, 1)
    modulation_part = jnp.dot(embed_part, ada_weight, preferred_element_type=jnp.float32)
    modulation_part = lax.psum_scatter(modulation_part, "dp", scatter_dimension=0, tiled=True)
    modulation = lax.all_gather(modulation_part, "seq", axis=1, tiled=True)
    scale_one = modulation[:, :width]
    shift_one = modulation[:, width : 2 * width]
    scale_two = modulation[:, 2 * width : 3 * width]
    shift_two = modulation[:, 3 * width :]

    skip_tiles = lax.all_gather(skip_weight, ("dp", "seq"), axis=0)
    pair_tile = own_pair_rows(qkv_weight.T, seq)
    skip_tiles, up_column, down_column, cos_all, sin_all, ends, grad_low, place = lax.optimization_barrier(
        (skip_tiles, up_column, down_column, cos_all, sin_all, ends, grad_low, place)
    )
    stream, normed_one = entry_block(inputs[0], skip_input[0], skip_tiles, scale_one, shift_one, dp, seq)
    normed_all = lax.all_gather(normed_one, "seq", axis=0)
    up_near = gather_near(up_column, routes["x"])
    down_near = gather_near(down_column, routes["y"])
    pair_weight = dp_gather(pair_tile, routes, dp)
    up_near, down_near, pair_weight = lax.optimization_barrier((up_near, down_near, pair_weight))
    up_far, down_far = send(up_near, routes["y"]), send(down_near, routes["x"])
    normed_all, up_near, down_near = lax.optimization_barrier((normed_all, up_near, down_near))
    up_near_core, down_near_core = send(up_near, routes["core"]), send(down_near, routes["core"])
    qt, kt, vt, keys, values, norms = project_pair(normed_all, pair_weight, cos_all, sin_all)
    attended_pair, attended_wide, total = attend_pair(ends, qt, keys, vt, norms)
    attended_pair, up_far, down_far = lax.optimization_barrier((attended_pair, up_far, down_far))
    up_pieces = (up_near, up_far, up_near_core, send(up_far, routes["core"]))
    down_pieces = (down_near, down_far, down_near_core, send(down_far, routes["core"]))
    attended = lax.all_to_all(attended_pair, "seq", 0, 0).reshape(width, frames)
    attended, pair_tile, far_up, far_down = lax.optimization_barrier(
        (attended, pair_tile, up_pieces[3], down_pieces[3])
    )
    up_pieces, down_pieces = up_pieces[:3] + (far_up,), down_pieces[:3] + (far_down,)
    pair_tiles = lax.all_gather(pair_tile, ("dp", "seq"), axis=0)
    layer_output, grad_middle, grad_head_a, grad_head_b, sums_two, down_own, down_other, up_own, up_other = middle_block(
        place, attended, stream, grad_low, scale_two, shift_two, up_pieces, down_pieces, dp, seq
    )
    grad_head_a = lax.all_to_all(grad_head_a, "seq", 0, 0)
    down_other, up_other = send(down_other, routes["core"]), send(up_other, routes["core"])
    down_half, up_half = down_own.shape[2] // 2, up_own.shape[2] // 2

    def leaves(own, other, rows):
        return low(wide(own[2:, :, rows]) + wide(other[2:, :, rows]))

    away = (
        leaves(down_own, down_other, slice(0, down_half)),
        leaves(down_own, down_other, slice(down_half, None)),
        leaves(up_own, up_other, slice(0, up_half)),
        leaves(up_own, up_other, slice(up_half, None)),
    )
    grad_head_b, *away = lax.optimization_barrier((grad_head_b, *away))
    grad_head_b = lax.all_to_all(grad_head_b, "seq", 0, 0)
    saved = (attended_wide, total, keys, values, kt, cos_all, sin_all)
    grad_head_a, pair_tiles, *away = lax.optimization_barrier((grad_head_a, pair_tiles, *away))
    down_got = [send(away[0], routes["x"]), send(away[1], routes["x"])]
    up_got = [send(away[2], routes["y"]), send(away[3], routes["y"])]
    back_a = attend_head_back(0, ends, qt, grad_head_a, *saved)
    local_a = lax.all_to_all(back_a, "seq", 0, 0)
    back_a, grad_head_b, down_got[0], up_got[0] = lax.optimization_barrier(
        (back_a, grad_head_b, down_got[0], up_got[0])
    )
    back_b = attend_head_back(1, ends, qt, grad_head_b, *saved)
    back_b, local_a = lax.optimization_barrier((back_b, local_a))
    local_b = lax.all_to_all(back_b, "seq", 0, 0)

    def stays(own, other, got, at):
        return wide(own[at]) + wide(other[at]) + wide(got[at])

    parts = [part[:, at : at + HD] for at in range(0, 3 * HD, HD) for part in (back_a, back_b)]
    grad_projected = jnp.concatenate(parts, axis=1)
    grad_projected, down_got[1], up_got[1] = lax.optimization_barrier((grad_projected, down_got[1], up_got[1]))
    down_got, up_got = jnp.concatenate(down_got, axis=2), jnp.concatenate(up_got, axis=2)
    down_back = send(low(stays(down_own, down_other, down_got, 1)), routes["y"])
    up_back = send(low(stays(up_own, up_other, up_got, 1)), routes["x"])
    grad_pair_weight = jnp.einsum(
        "icf,ifd->cd", grad_projected, normed_all, preferred_element_type=jnp.float32
    ).astype(jnp.bfloat16)
    grad_stream, grad_stream_turned, sums_one = exit_block(
        local_a, local_b, pair_tiles, stream, grad_middle, scale_one, dp, seq
    )
    joined = jnp.concatenate([inputs[0], skip_input[0]], axis=-1)
    half_tile = skip_weight.shape[0] // 2
    at = lax.axis_index("dp")
    half_pair = 3 * PAIR // 2
    wide_tile = up_weight.shape[1]
    turned = [("turned", grad_stream_turned, joined)]
    order = (("x", "y"), ("y", "x"))

    def skip_blocks(part, arrived):
        masks = tuple(AXIS_MASK[axis] for axis in order[part])
        return grad_blocks(place, turned, masks, seq, half_tile, arrived, (part, 2))

    leaving = [skip_blocks(part, None)[0] for part in range(2)]
    *leaving, down_back, up_back = lax.optimization_barrier((*leaving, down_back, up_back))
    arrived = [send(part, routes["core"]) for part in leaving]
    down_total = stays(down_own, down_other, down_got, 0) + wide(down_back)
    up_total = stays(up_own, up_other, up_got, 0) + wide(up_back)
    mlp_low = [jnp.concatenate([low(down_total[ahead]), low(up_total[ahead])]) for ahead in range(seq // 2)]
    mlp_own = jnp.concatenate([down_total[0], up_total[0]])
    mlp_got = [send(mlp_low[1], routes["z"][0])]
    grad_main, grad_side = joined_grads(grad_stream, skip_tiles, dp, seq)
    arrived[0], arrived[1], grad_main, mlp_got[0], *mlp_low = lax.optimization_barrier(
        (*arrived, grad_main, mlp_got[0], *mlp_low)
    )
    mlp_got.append(send(mlp_low[2], routes["z"][1]))
    skip_parts = []
    for part, (first, second) in enumerate(order):
        keep, away = skip_blocks(part, arrived[part])
        pair_rows = grad_pair_weight[part * half_pair : (part + 1) * half_pair]

        def pair_block(mask):
            return lax.dynamic_slice_in_dim(pair_rows, jnp.bitwise_xor(at, mask) * half_tile, half_tile, 1)

        near, far = AXIS_MASK[first], AXIS_MASK[second]
        keep = jnp.concatenate([keep.reshape(2, -1, half_tile), jnp.stack([pair_block(0), pair_block(far)])], axis=1)
        away = jnp.concatenate(
            [away.reshape(2, -1, half_tile), jnp.stack([pair_block(near), pair_block(near ^ far)])], axis=1
        )
        skip_parts.append((keep, send(away, routes[first]), routes[second]))
    keep_a, keep_b, sums_one = lax.optimization_barrier((skip_parts[0][0], skip_parts[1][0], sums_one))
    got_a, got_b, mlp_got[1], mlp_low[3] = lax.optimization_barrier(
        (skip_parts[0][1], skip_parts[1][1], mlp_got[1], mlp_low[3])
    )
    mlp_got.append(send(mlp_low[3], routes["z"][2]))
    skip_parts = [(keep_a, got_a, skip_parts[0][2]), (keep_b, got_b, skip_parts[1][2])]
    skip_own, skip_low, pair_sums = [], [], []
    skip_rows = seq // 2 * (width // seq)
    for keep, got, route in skip_parts:
        back = send(low(wide(keep[1]) + wide(got[1])), route)
        total_part = wide(keep[0]) + wide(got[0]) + wide(back)
        pair_sums.append(total_part[skip_rows:])
        blocks = total_part[:skip_rows].reshape(seq // 2, width // seq, half_tile)
        skip_own.append(blocks[0])
        skip_low.append(low(blocks))
    skip_tile = jnp.concatenate(skip_own, axis=1)
    skip_low = jnp.concatenate(skip_low, axis=2)
    skip_low, *mlp_got = lax.optimization_barrier((skip_low, *mlp_got))
    for ahead, route in enumerate(routes["z"]):
        skip_tile = skip_tile + wide(send(skip_low[ahead + 1], route))
    skip_tile = skip_tile.T
    qkv_tile = wide(stored_rows(low(jnp.concatenate(pair_sums)), seq)).T

    mlp_tile = mlp_own
    for piece in mlp_got:
        mlp_tile = mlp_tile + wide(piece)
    columns = width // seq
    fold = down_weight.shape[0] // wide_tile
    down_tile = lanes([mlp_tile[i * columns : (i + 1) * columns] for i in range(fold)]).T
    out_tile = mlp_tile[fold * columns : down_total.shape[1]]
    out_tile = jnp.concatenate([out_tile[:, i * columns : (i + 1) * columns] for i in range(wide_tile // columns)])
    up_tile = mlp_tile[down_total.shape[1] :]
    grad_modulation = jnp.concatenate([sums_one[0], sums_one[1], sums_two[0], sums_two[1]])
    chips, chip_at, core_at = seq // 2, seq_at // 2, seq_at % 2
    grad_modulation = grad_modulation.reshape(chips, 2, -1)
    kept = lax.dynamic_index_in_dim(grad_modulation, core_at, 1, keepdims=False)
    kept = kept + send(lax.dynamic_index_in_dim(grad_modulation, 1 - core_at, 1, keepdims=False), routes["core"])
    column_sum = lax.dynamic_index_in_dim(kept, chip_at, 0)
    for ahead, route in enumerate(routes["z"]):
        piece = lax.dynamic_index_in_dim(kept, (chip_at + ahead + 1) % chips, 0)
        column_sum = column_sum + send(piece, route)
    column_sum = jnp.concatenate([column_sum, send(column_sum, routes["x"])])
    grad_modulation = jnp.concatenate([column_sum, send(column_sum, routes["y"])])
    embed_part = jnp.concatenate(
        [lax.dynamic_index_in_dim(embed_part, jnp.bitwise_xor(at, mask), 0) for mask in range(dp)]
    )
    ada_tile = lax.dot_general(
        embed_part.astype(jnp.float32), grad_modulation, (((0,), (0,)), ((), ())),
        precision=lax.Precision.HIGHEST,
    )
    return (
        layer_output[None],
        grad_main[None],
        grad_side[None],
        skip_tile,
        ada_tile,
        qkv_tile,
        out_tile,
        up_tile,
        down_tile,
    )


def solution(mesh):
    in_specs = (
        P("dp", "seq", None),
        P("dp", "seq", None),
        P("dp", None),
        P("dp", None),
        P("dp", None),
        P("dp", None),
        P("dp", "seq", None),
        P("dp", "seq"),
        P("dp", "seq"),
        P("dp", "seq"),
        P("dp", "seq"),
        P("dp", "seq"),
        P("dp", "seq"),
    )
    out_specs = (
        P("dp", "seq", None),
        P("dp", "seq", None),
        P("dp", "seq", None),
        P("dp", "seq"),
        P("dp", "seq"),
        P("dp", "seq"),
        P("dp", "seq"),
        P("dp", "seq"),
        P("dp", "seq"),
    )
    seq_size = mesh.shape["seq"]
    paired = H == 2 * seq_size and seq_size % 3 != 0 and mesh.shape["dp"] == 4
    body = local_paired if paired else local_general
    return jax.shard_map(body, mesh=mesh, in_specs=in_specs, out_specs=out_specs, check_vma=False)
```

```python
from functools import partial
import math

import jax
import jax.numpy as jnp
from jax import lax
from jax.experimental import pallas as pl
from jax.experimental.pallas import tpu as pltpu
from jax.sharding import PartitionSpec as P

H = 16
HD = 64
UTT = 3
HG = 8


epsilon = 1e-06
masked_score = -1e30


def ada_norm(stream, scale_part, shift_part):
    inverse = lax.rsqrt(jnp.mean(stream * stream, axis=-1, keepdims=True) + epsilon)
    return stream * inverse * (1.0 + scale_part) + shift_part


def rotate(tensor, cosine, sine_part):
    half_width = tensor.shape[-1] // 2
    lower_half = tensor[..., :half_width]
    upper_half = tensor[..., half_width:]
    cos_wide = cosine[..., None, :]
    sin_wide = sine_part[..., None, :]
    return jnp.concatenate(
        [
            lower_half * cos_wide - upper_half * sin_wide,
            lower_half * sin_wide + upper_half * cos_wide,
        ],
        axis=-1,
    )


def rotary_tables(position, half_width):
    frequency = jnp.exp(-math.log(10000.0) * jnp.arange(half_width, dtype=jnp.float32) / half_width)
    angles = position.astype(jnp.float32)[..., None] * frequency
    return (jnp.cos(angles), jnp.sin(angles))


def gather_weights(skip_tile, ada_tile, qkv_tile, out_tile, up_tile, down_tile):
    row_full = (
        lax.all_gather(skip_tile, "dp", axis=0, tiled=True),
        lax.all_gather(ada_tile, "dp", axis=0, tiled=True),
        lax.all_gather(qkv_tile, "dp", axis=0, tiled=True),
        lax.all_gather(out_tile, "dp", axis=0, tiled=True),
        lax.all_gather(up_tile, "dp", axis=0, tiled=True),
        lax.all_gather(down_tile, "dp", axis=0, tiled=True),
    )
    return (
        lax.all_gather(row_full[0], "seq", axis=1, tiled=True),
        lax.all_gather(row_full[1], "seq", axis=1, tiled=True),
        lax.all_gather(row_full[2], "seq", axis=1, tiled=True),
        lax.all_gather(row_full[3], "seq", axis=1, tiled=True),
        lax.all_gather(row_full[4], "seq", axis=1, tiled=True),
        lax.all_gather(row_full[5], "seq", axis=1, tiled=True),
    )


def group_scores(query_part, key_part, allowed, factor):
    scores = (
        jnp.einsum("qhd,khd->hqk", query_part, key_part, preferred_element_type=jnp.float32)
        * factor
    )
    return jnp.where(allowed[None], scores, masked_score)


def attend_row(queries, key_rows, value_rows, segment_local, segment_full):
    factor = queries.shape[2] ** (-0.5)
    allowed = segment_local[:, None] == segment_full[None, :]
    outputs = []
    totals = []
    for head_start in range(0, H, HG):
        head_end = head_start + HG
        scores = group_scores(
            queries[:, head_start:head_end], key_rows[:, head_start:head_end], allowed, factor
        )
        log_total = jax.nn.logsumexp(scores, axis=-1)
        weights = jnp.exp(scores - log_total[..., None]).astype(jnp.bfloat16)
        outputs.append(
            jnp.einsum(
                "hqk,khd->qhd",
                weights,
                value_rows[:, head_start:head_end],
                preferred_element_type=jnp.float32,
            )
        )
        totals.append(log_total)
    return (jnp.concatenate(outputs, axis=1), jnp.concatenate(totals, axis=0))


def attend_back(
    queries, key_rows, value_rows, segment_local, segment_full, log_total, grad_attended, row_dot
):
    factor = queries.shape[2] ** (-0.5)
    allowed = segment_local[:, None] == segment_full[None, :]
    query_grads = []
    key_grads = []
    value_grads = []
    for head_start in range(0, H, HG):
        head_end = head_start + HG
        key_part = key_rows[:, head_start:head_end]
        query_part = queries[:, head_start:head_end]
        grad_part = grad_attended[:, head_start:head_end]
        scores = group_scores(query_part, key_part, allowed, factor)
        weights = jnp.exp(scores - log_total[head_start:head_end][..., None])
        weights_low = weights.astype(jnp.bfloat16)
        value_grads.append(
            jnp.einsum("hqk,qhd->khd", weights_low, grad_part, preferred_element_type=jnp.float32)
        )
        grad_weights = jnp.einsum(
            "qhd,khd->hqk",
            grad_part,
            value_rows[:, head_start:head_end],
            preferred_element_type=jnp.float32,
        )
        grad_scores = (weights * (grad_weights - row_dot[head_start:head_end][..., None])).astype(
            jnp.bfloat16
        )
        query_grads.append(
            jnp.einsum("hqk,khd->qhd", grad_scores, key_part, preferred_element_type=jnp.float32)
            * factor
        )
        key_grads.append(
            jnp.einsum("hqk,qhd->khd", grad_scores, query_part, preferred_element_type=jnp.float32)
            * factor
        )
    return (
        jnp.concatenate(query_grads, axis=1),
        jnp.concatenate(key_grads, axis=1),
        jnp.concatenate(value_grads, axis=1),
    )


def local_general(
    inputs,
    skip_input,
    time_embed,
    segment_ids,
    span_start,
    span_length,
    cotangent,
    skip_weight,
    ada_weight,
    qkv_weight,
    out_weight,
    up_weight,
    down_weight,
):
    row_count = inputs.shape[0]
    frames = inputs.shape[1]
    model_width = inputs.shape[2]
    row_length = segment_ids.shape[1]
    frame_base = lax.axis_index("seq") * frames
    utterance = jnp.arange(UTT, dtype=jnp.int32)
    member = (segment_ids[:, :, None] == utterance[None, None, :]).astype(jnp.int32)
    counts = jnp.sum(member, axis=1)
    firsts = jnp.cumsum(counts, axis=1) - counts
    local_member = lax.dynamic_slice_in_dim(member, frame_base, frames, 1)
    local_segments = lax.dynamic_slice_in_dim(segment_ids, frame_base, frames, 1)
    local_frames = frame_base + jnp.arange(frames, dtype=jnp.int32)
    position = local_frames[None, :] - jnp.sum(local_member * firsts[:, None, :], axis=2)
    span_begin = jnp.sum(local_member * span_start[:, None, :], axis=2)
    span_end = span_begin + jnp.sum(local_member * span_length[:, None, :], axis=2)
    inside = jnp.logical_and(position >= span_begin, position < span_end)
    cosine, sine_part = rotary_tables(position, HD // 2)
    skip_full, ada_full, qkv_full, out_full, up_full, down_full = gather_weights(
        skip_weight, ada_weight, qkv_weight, out_weight, up_weight, down_weight
    )
    joined = jnp.concatenate([inputs, skip_input], axis=-1)
    stream = jnp.einsum("rfc,cd->rfd", joined, skip_full, preferred_element_type=jnp.float32)
    modulation = jnp.dot(time_embed, ada_full, preferred_element_type=jnp.float32)[:, None, :]
    scale_one = modulation[..., :model_width]
    shift_one = modulation[..., model_width : 2 * model_width]
    scale_two = modulation[..., 2 * model_width : 3 * model_width]
    shift_two = modulation[..., 3 * model_width :]
    normed_one = ada_norm(stream, scale_one, shift_one).astype(jnp.bfloat16)
    projected = jnp.einsum("rfd,de->rfe", normed_one, qkv_full, preferred_element_type=jnp.float32)
    queries = rotate(
        projected[..., :model_width].reshape(row_count, frames, H, HD), cosine, sine_part
    ).astype(jnp.bfloat16)
    key_rotated = rotate(
        projected[..., model_width : 2 * model_width].reshape(row_count, frames, H, HD),
        cosine,
        sine_part,
    )
    key_local = key_rotated.reshape(row_count, frames, model_width).astype(jnp.bfloat16)
    value_local = projected[..., 2 * model_width :].astype(jnp.bfloat16)
    key_all, value_all = (
        lax.all_gather(key_local, "seq", axis=1, tiled=True),
        lax.all_gather(value_local, "seq", axis=1, tiled=True),
    )

    def forward_row(row_items):
        query_row, key_row, value_row, local_row, full_row = row_items
        return attend_row(
            query_row,
            key_row.reshape(row_length, H, HD),
            value_row.reshape(row_length, H, HD),
            local_row,
            full_row,
        )

    attended, log_total = lax.map(
        forward_row, (queries, key_all, value_all, local_segments, segment_ids)
    )
    attended = attended.reshape(row_count, frames, model_width)
    attended_low = attended.astype(jnp.bfloat16)
    middle = stream + jnp.einsum(
        "rfe,ed->rfd", attended_low, out_full, preferred_element_type=jnp.float32
    )
    normed_two = ada_norm(middle, scale_two, shift_two).astype(jnp.bfloat16)
    up_proj = jnp.einsum("rfd,di->rfi", normed_two, up_full, preferred_element_type=jnp.float32)
    hidden = jax.nn.gelu(up_proj, approximate=True).astype(jnp.bfloat16)
    down_proj = jnp.einsum("rfi,id->rfd", hidden, down_full, preferred_element_type=jnp.float32)
    layer_output = (middle + down_proj).astype(jnp.bfloat16)
    skip_full, ada_full, qkv_full, out_full, up_full, down_full = gather_weights(
        skip_weight, ada_weight, qkv_weight, out_weight, up_weight, down_weight
    )
    grad_out = cotangent.astype(jnp.float32) * inside[..., None].astype(jnp.float32)
    grad_low = grad_out.astype(jnp.bfloat16)
    grad_hidden = jnp.einsum("rfd,id->rfi", grad_low, down_full, preferred_element_type=jnp.float32)
    _, gelu_pull = jax.vjp(partial(jax.nn.gelu, approximate=True), up_proj)
    grad_up_act = gelu_pull(grad_hidden)[0].astype(jnp.bfloat16)
    grad_normed_two = jnp.einsum(
        "rfi,di->rfd", grad_up_act, up_full, preferred_element_type=jnp.float32
    )
    _, norm_pull_two = jax.vjp(ada_norm, middle, scale_two, shift_two)
    grad_middle_norm, grad_scale_two, grad_shift_two = norm_pull_two(grad_normed_two)
    grad_middle = grad_out + grad_middle_norm
    grad_middle_low = grad_middle.astype(jnp.bfloat16)
    grad_attended = jnp.einsum(
        "rfd,ed->rfe", grad_middle_low, out_full, preferred_element_type=jnp.float32
    ).astype(jnp.bfloat16)
    row_dot = jnp.sum(
        (grad_attended.astype(jnp.float32) * attended).reshape(row_count, frames, H, HD), axis=-1
    )
    row_dot = jnp.swapaxes(row_dot, 1, 2)
    grad_heads = grad_attended.reshape(row_count, frames, H, HD)

    def backward_row(row_items):
        query_row, key_row, value_row, local_row, full_row, total_row, grad_row, dot_row = row_items
        return attend_back(
            query_row,
            key_row.reshape(row_length, H, HD),
            value_row.reshape(row_length, H, HD),
            local_row,
            full_row,
            total_row,
            grad_row,
            dot_row,
        )

    grad_queries, grad_keys, grad_values = lax.map(
        backward_row,
        (queries, key_all, value_all, local_segments, segment_ids, log_total, grad_heads, row_dot),
    )
    key_share, value_share = (
        lax.psum_scatter(
            grad_keys.reshape(row_count, row_length, model_width).astype(jnp.bfloat16),
            "seq",
            scatter_dimension=1,
            tiled=True,
        ).astype(jnp.float32),
        lax.psum_scatter(
            grad_values.reshape(row_count, row_length, model_width).astype(jnp.bfloat16),
            "seq",
            scatter_dimension=1,
            tiled=True,
        ).astype(jnp.float32),
    )
    _, rotate_pull = jax.vjp(
        partial(rotate, cosine=cosine, sine_part=sine_part),
        jnp.zeros((row_count, frames, H, HD), jnp.float32),
    )
    grad_query_raw = rotate_pull(grad_queries)[0].reshape(row_count, frames, model_width)
    grad_key_raw = rotate_pull(key_share.reshape(row_count, frames, H, HD))[0].reshape(
        row_count, frames, model_width
    )
    grad_projected = jnp.concatenate([grad_query_raw, grad_key_raw, value_share], axis=-1).astype(
        jnp.bfloat16
    )
    grad_normed_one = jnp.einsum(
        "rfe,de->rfd", grad_projected, qkv_full, preferred_element_type=jnp.float32
    )
    _, norm_pull_one = jax.vjp(ada_norm, stream, scale_one, shift_one)
    grad_stream_norm, grad_scale_one, grad_shift_one = norm_pull_one(grad_normed_one)
    grad_stream = (grad_middle + grad_stream_norm).astype(jnp.bfloat16)
    grad_joined = jnp.einsum(
        "rfd,cd->rfc", grad_stream, skip_full, preferred_element_type=jnp.float32
    )
    grad_modulation = jnp.concatenate(
        [grad_scale_one, grad_shift_one, grad_scale_two, grad_shift_two], axis=-1
    )[:, 0, :]
    grad_down = jnp.einsum("rfi,rfd->id", hidden, grad_low, preferred_element_type=jnp.float32)
    grad_up = jnp.einsum("rfd,rfi->di", normed_two, grad_up_act, preferred_element_type=jnp.float32)
    grad_attn_out = jnp.einsum(
        "rfe,rfd->ed", attended_low, grad_middle_low, preferred_element_type=jnp.float32
    )
    grad_qkv = jnp.einsum(
        "rfd,rfe->de", normed_one, grad_projected, preferred_element_type=jnp.float32
    )
    grad_skip_w = jnp.einsum("rfc,rfd->cd", joined, grad_stream, preferred_element_type=jnp.float32)
    grad_ada = jnp.einsum(
        "rd,re->de",
        time_embed.astype(jnp.float32),
        grad_modulation,
        precision=lax.Precision.HIGHEST,
    )
    column_parts = (
        lax.psum_scatter(
            grad_skip_w.astype(jnp.bfloat16), "seq", scatter_dimension=1, tiled=True
        ).astype(jnp.float32),
        lax.psum_scatter(
            grad_ada.astype(jnp.bfloat16), "seq", scatter_dimension=1, tiled=True
        ).astype(jnp.float32),
        lax.psum_scatter(
            grad_qkv.astype(jnp.bfloat16), "seq", scatter_dimension=1, tiled=True
        ).astype(jnp.float32),
        lax.psum_scatter(
            grad_attn_out.astype(jnp.bfloat16), "seq", scatter_dimension=1, tiled=True
        ).astype(jnp.float32),
        lax.psum_scatter(
            grad_up.astype(jnp.bfloat16), "seq", scatter_dimension=1, tiled=True
        ).astype(jnp.float32),
        lax.psum_scatter(
            grad_down.astype(jnp.bfloat16), "seq", scatter_dimension=1, tiled=True
        ).astype(jnp.float32),
    )
    weight_tiles = (
        lax.psum_scatter(
            column_parts[0].astype(jnp.bfloat16), "dp", scatter_dimension=0, tiled=True
        ).astype(jnp.float32),
        lax.psum_scatter(
            column_parts[1].astype(jnp.bfloat16), "dp", scatter_dimension=0, tiled=True
        ).astype(jnp.float32),
        lax.psum_scatter(
            column_parts[2].astype(jnp.bfloat16), "dp", scatter_dimension=0, tiled=True
        ).astype(jnp.float32),
        lax.psum_scatter(
            column_parts[3].astype(jnp.bfloat16), "dp", scatter_dimension=0, tiled=True
        ).astype(jnp.float32),
        lax.psum_scatter(
            column_parts[4].astype(jnp.bfloat16), "dp", scatter_dimension=0, tiled=True
        ).astype(jnp.float32),
        lax.psum_scatter(
            column_parts[5].astype(jnp.bfloat16), "dp", scatter_dimension=0, tiled=True
        ).astype(jnp.float32),
    )
    skip_tile, ada_tile, qkv_tile, out_tile, up_tile, down_tile = weight_tiles
    return (
        layer_output,
        grad_joined[..., :model_width],
        grad_joined[..., model_width:],
        skip_tile,
        ada_tile,
        qkv_tile,
        out_tile,
        up_tile,
        down_tile,
    )


LOG2E = 1.4426950408889634
SCALE = HD**-0.5
PAIR = 2 * HD


def dot_nn(a, b):
    return lax.dot_general(a, b, (((1,), (0,)), ((), ())), preferred_element_type=jnp.float32)


def dot_nt(a, b):
    return lax.dot_general(a, b, (((1,), (1,)), ((), ())), preferred_element_type=jnp.float32)


def dot_tn(a, b):
    return lax.dot_general(a, b, (((0,), (0,)), ((), ())), preferred_element_type=jnp.float32)


def segment_of(index, ends_ref):
    return (index >= ends_ref[0]).astype(jnp.int32) + (index >= ends_ref[1]).astype(jnp.int32)


def segment_span(ends_ref, first, last, length):
    end_a, end_b = ends_ref[0], ends_ref[1]
    low = jnp.where(first < end_a, 0, jnp.where(first < end_b, end_a, end_b))
    high = jnp.where(last < end_a, end_a, jnp.where(last < end_b, end_b, length))
    return low, high


def key_blocks(ends_ref, start, size, length):
    low, high = segment_span(ends_ref, start, start + size - 1, length)
    low_last, _ = segment_span(ends_ref, start + size - 1, start, length)
    first = low // size
    last = (high + size - 1) // size
    whole_first = jnp.where(low == low_last, (low + size - 1) // size, last)
    whole_first = jnp.minimum(whole_first, last)
    whole_last = jnp.where(low == low_last, jnp.maximum(high // size, whole_first), last)
    return first, whole_first, whole_last, last


def turn(pair, cosine, sine_part):
    half = HD // 2
    rows = []
    for head in range(pair.shape[0] // HD):
        lower = pair[head * HD : head * HD + half]
        upper = pair[head * HD + half : (head + 1) * HD]
        rows += [lower * cosine - upper * sine_part, lower * sine_part + upper * cosine]
    return jnp.concatenate(rows, axis=0)


def head_norms(pair):
    square = pair * pair
    return [jnp.sum(square[head * HD : (head + 1) * HD], axis=0, keepdims=True) for head in range(2)]


def project_kernel(
    normed_ref, weight_ref, cos_ref, sin_ref, qt_ref, kt_ref, vt_ref, k_ref, v_ref, norms_ref
):
    projected = dot_nt(weight_ref[...], normed_ref[0])
    cosine, sine_part = cos_ref[...], sin_ref[...]
    queries = turn(projected[:PAIR], cosine, sine_part).astype(jnp.bfloat16)
    keys = turn(projected[PAIR : 2 * PAIR], cosine, sine_part)
    values = projected[2 * PAIR :]
    norms_ref[0] = jnp.concatenate(head_norms(queries.astype(jnp.float32) * SCALE) + head_norms(keys), axis=0)
    qt_ref[0] = (queries.astype(jnp.float32) * SCALE).astype(jnp.bfloat16)
    kt_ref[...] = keys.astype(jnp.bfloat16)
    vt_ref[...] = values.astype(jnp.bfloat16)
    k_ref[...] = keys.T.astype(jnp.bfloat16)
    v_ref[...] = values.T.astype(jnp.bfloat16)


def project_pair(normed_all, weight_rows, cos_all, sin_all):
    chunks, frames, width = normed_all.shape
    length = chunks * frames
    return pl.pallas_call(
        project_kernel,
        grid=(chunks,),
        in_specs=[
            pl.BlockSpec((1, frames, width), lambda i: (i, 0, 0)),
            pl.BlockSpec((3 * PAIR, width), lambda i: (0, 0)),
            pl.BlockSpec((HD // 2, frames), lambda i: (0, i)),
            pl.BlockSpec((HD // 2, frames), lambda i: (0, i)),
        ],
        out_specs=[
            pl.BlockSpec((1, PAIR, frames), lambda i: (i, 0, 0)),
            pl.BlockSpec((PAIR, frames), lambda i: (0, i)),
            pl.BlockSpec((PAIR, frames), lambda i: (0, i)),
            pl.BlockSpec((frames, PAIR), lambda i: (i, 0)),
            pl.BlockSpec((frames, PAIR), lambda i: (i, 0)),
            pl.BlockSpec((1, 4, frames), lambda i: (i, 0, 0)),
        ],
        out_shape=[
            jax.ShapeDtypeStruct((chunks, PAIR, frames), jnp.bfloat16),
            jax.ShapeDtypeStruct((PAIR, length), jnp.bfloat16),
            jax.ShapeDtypeStruct((PAIR, length), jnp.bfloat16),
            jax.ShapeDtypeStruct((length, PAIR), jnp.bfloat16),
            jax.ShapeDtypeStruct((length, PAIR), jnp.bfloat16),
            jax.ShapeDtypeStruct((chunks, 4, frames), jnp.float32),
        ],
        compiler_params=pltpu.CompilerParams(vmem_limit_bytes=60 << 20),
        cost_estimate=pl.CostEstimate(
            flops=6 * length * width * PAIR, bytes_accessed=2 * length * (width + 5 * PAIR), transcendentals=0
        ),
        name="project_pair",
    )(normed_all, weight_rows, cos_all, sin_all)


def split_heads(block):
    row = lax.broadcasted_iota(jnp.int32, block.shape, 0)
    zero = jnp.zeros((), block.dtype)
    return jnp.where(row < HD, block, zero), jnp.where(row < HD, zero, block)


SAFE_SCORE = 60.0


def attend_kernel(
    ends_ref, qt_ref, k_ref, vt_ref, norms_ref, low_ref, full_ref, total_ref, acc_ref, top_ref, *, size, length
):
    index = pl.program_id(0)
    start = index * size
    queries = split_heads(qt_ref[0])
    query_segment = segment_of(start + lax.broadcasted_iota(jnp.int32, (1, size), 1), ends_ref)
    first, whole_first, whole_last, last = key_blocks(ends_ref, start, size, length)
    acc_ref[...] = jnp.zeros_like(acc_ref)
    ones = jnp.ones((16, size), jnp.bfloat16)
    bound = jnp.max(norms_ref[index, :2, :]) * jnp.max(norms_ref[:, 2:, :])
    plain = bound < SAFE_SCORE * SAFE_SCORE

    def step(masked, shifted):
        def run(block, carry):
            offset = pl.multiple_of(block * size, size)
            keys = k_ref[pl.ds(offset, size), :]
            scores = [dot_nn(keys, queries[head]) for head in range(2)]
            if masked:
                key_segment = segment_of(offset + lax.broadcasted_iota(jnp.int32, (size, 1), 0), ends_ref)
                same = key_segment == query_segment
                scores = [jnp.where(same, part, masked_score) for part in scores]
            if shifted:
                old = [top_ref[head] for head in range(2)]
                new = [
                    jnp.maximum(old[head], jnp.max(scores[head], axis=0, keepdims=True) * LOG2E) for head in range(2)
                ]
                weights = [jnp.exp2(scores[head] * LOG2E - new[head]).astype(jnp.bfloat16) for head in range(2)]
            else:
                weights = [jnp.exp2(scores[head] * LOG2E).astype(jnp.bfloat16) for head in range(2)]
            for head in range(2):
                values = jnp.concatenate([vt_ref[pl.ds(head * HD, HD), pl.ds(offset, size)], ones], axis=0)
                if shifted:
                    acc_ref[head] = acc_ref[head] * jnp.exp2(old[head] - new[head]) + dot_nn(values, weights[head])
                    top_ref[head] = new[head]
                else:
                    acc_ref[head] += dot_nn(values, weights[head])
            return carry

        return run

    def loops(shifted):
        lax.fori_loop(first, whole_first, step(True, shifted), 0)
        lax.fori_loop(whole_first, whole_last, step(False, shifted), 0)
        lax.fori_loop(whole_last, last, step(True, shifted), 0)

    @pl.when(plain)
    def _():
        top_ref[...] = jnp.zeros_like(top_ref)
        loops(False)

    @pl.when(jnp.logical_not(plain))
    def _():
        top_ref[...] = jnp.full_like(top_ref, masked_score)
        loops(True)

    for head in range(2):
        total = acc_ref[head, HD : HD + 1, :]
        attended = acc_ref[head, :HD, :] / total
        full_ref[0, head * HD : (head + 1) * HD, :] = attended
        low_ref[0, head * HD : (head + 1) * HD, :] = attended.astype(jnp.bfloat16)
        total_ref[0, head : head + 1, :] = jnp.log(total) * LOG2E + top_ref[head]


def attend_pair(ends, qt, k, vt, norms):
    chunks, _, size = qt.shape
    length = k.shape[0]
    chunk = pl.BlockSpec((1, PAIR, size), lambda i, ends: (i, 0, 0))
    return pl.pallas_call(
        partial(attend_kernel, size=size, length=length),
        grid_spec=pltpu.PrefetchScalarGridSpec(
            num_scalar_prefetch=1,
            grid=(chunks,),
            in_specs=[
                chunk,
                pl.BlockSpec((length, PAIR), lambda i, ends: (0, 0)),
                pl.BlockSpec((PAIR, length), lambda i, ends: (0, 0)),
                pl.BlockSpec(norms.shape, lambda i, ends: (0, 0, 0)),
            ],
            out_specs=[chunk, chunk, pl.BlockSpec((1, 2, size), lambda i, ends: (i, 0, 0))],
            scratch_shapes=[pltpu.VMEM((2, HD + 16, size), jnp.float32), pltpu.VMEM((2, 1, size), jnp.float32)],
        ),
        out_shape=[
            jax.ShapeDtypeStruct((chunks, PAIR, size), jnp.bfloat16),
            jax.ShapeDtypeStruct((chunks, PAIR, size), jnp.float32),
            jax.ShapeDtypeStruct((chunks, 2, size), jnp.float32),
        ],
        compiler_params=pltpu.CompilerParams(vmem_limit_bytes=32 << 20),
        cost_estimate=pl.CostEstimate(
            flops=8 * length * length * HD, bytes_accessed=14 * length * PAIR, transcendentals=length * length
        ),
        name="attend_pair",
    )(ends, qt, k, vt, norms)


def attend_back_kernel(
    ends_ref, qt_ref, gt_ref, full_ref, total_ref, k_ref, v_ref, kt_ref, cos_ref, sin_ref, out_ref,
    dk_ref, dv_ref, dq_ref, *, head, size, length, chunks,
):
    index = pl.program_id(0)
    start = index * size

    @pl.when(index == 0)
    def _():
        dk_ref[...] = jnp.zeros_like(dk_ref)
        dv_ref[...] = jnp.zeros_like(dv_ref)

    mine = slice(head * HD, (head + 1) * HD)
    queries = split_heads(qt_ref[0])[head]
    blank = jnp.zeros_like(gt_ref[0])
    grads = jnp.concatenate([blank, gt_ref[0]] if head else [gt_ref[0], blank], axis=0)
    row_dot = jnp.sum(gt_ref[0].astype(jnp.float32) * full_ref[0, mine, :], axis=0, keepdims=True)
    total = total_ref[0, head : head + 1, :]
    query_segment = segment_of(start + lax.broadcasted_iota(jnp.int32, (1, size), 1), ends_ref)
    first, whole_first, whole_last, last = key_blocks(ends_ref, start, size, length)
    dq_ref[...] = jnp.zeros_like(dq_ref)
    pieces = 2
    part = size // pieces

    def step(masked):
        def run(block, carry):
            for piece in range(pieces):
                offset = pl.multiple_of(block * size + piece * part, part)
                rows = pl.ds(offset, part)
                scores = dot_nn(k_ref[rows, :], queries)
                if masked:
                    key_segment = segment_of(offset + lax.broadcasted_iota(jnp.int32, (part, 1), 0), ends_ref)
                    scores = jnp.where(key_segment == query_segment, scores, masked_score)
                weights = jnp.exp2(scores * LOG2E - total)
                grad_weights = dot_nn(v_ref[rows, :], grads)
                grad_scores = (weights * (grad_weights - row_dot)).astype(jnp.bfloat16)
                dv_ref[rows, :] += dot_nt(weights.astype(jnp.bfloat16), grads)
                dk_ref[rows, :] += dot_nt(grad_scores, queries)
                dq_ref[...] += dot_nn(kt_ref[mine, rows], grad_scores)
            return carry

        return run

    lax.fori_loop(first, whole_first, step(True), 0)
    lax.fori_loop(whole_first, whole_last, step(False), 0)
    lax.fori_loop(whole_last, last, step(True), 0)
    own = pl.ds(pl.multiple_of(start, size), size)
    out_ref[index, :HD, :] = turn(dq_ref[...] * SCALE, cos_ref[:, own], -sin_ref[:, own]).astype(jnp.bfloat16)

    @pl.when(index == chunks - 1)
    def _():
        for chunk in range(chunks):
            rows = pl.ds(chunk * size, size)
            turned = turn(dk_ref[rows, :].T[mine], cos_ref[:, rows], -sin_ref[:, rows])
            out_ref[chunk, HD : 2 * HD, :] = turned.astype(jnp.bfloat16)
            out_ref[chunk, 2 * HD :, :] = dv_ref[rows, :].T[mine].astype(jnp.bfloat16)


def attend_head_back(head, ends, qt, gt, full, total, k, v, kt, cos_all, sin_all):
    chunks, _, size = qt.shape
    length = k.shape[0]
    chunk = pl.BlockSpec((1, PAIR, size), lambda i, ends: (i, 0, 0))

    def whole(shape):
        return pl.BlockSpec(shape, lambda i, ends: (0,) * len(shape))

    return pl.pallas_call(
        partial(attend_back_kernel, head=head, size=size, length=length, chunks=chunks),
        grid_spec=pltpu.PrefetchScalarGridSpec(
            num_scalar_prefetch=1,
            grid=(chunks,),
            in_specs=[
                chunk, pl.BlockSpec((1, HD, size), lambda i, ends: (i, 0, 0)), chunk,
                pl.BlockSpec((1, 2, size), lambda i, ends: (i, 0, 0)),
                whole((length, PAIR)), whole((length, PAIR)), whole((PAIR, length)),
                whole((HD // 2, length)), whole((HD // 2, length)),
            ],
            out_specs=whole((chunks, 3 * HD, size)),
            scratch_shapes=[
                pltpu.VMEM((length, PAIR), jnp.float32),
                pltpu.VMEM((length, PAIR), jnp.float32),
                pltpu.VMEM((HD, size), jnp.float32),
            ],
        ),
        out_shape=jax.ShapeDtypeStruct((chunks, 3 * HD, size), jnp.bfloat16),
        compiler_params=pltpu.CompilerParams(vmem_limit_bytes=60 << 20),
        cost_estimate=pl.CostEstimate(
            flops=40 * length * length * HD, bytes_accessed=20 * length * PAIR, transcendentals=0
        ),
        name="attend_head_back",
    )(ends, qt, gt, full, total, k, v, kt, cos_all, sin_all)


def pair_routes(count):
    routes = [[(source, (3 * source + piece) % count) for source in range(count)] for piece in range(3)]
    slots = [[0] * 3 for _ in range(count)]
    for piece in range(3):
        for source, target in routes[piece]:
            slots[target][piece] = (3 * source + piece) // count
    return routes, slots


def own_pair_rows(tile, count):
    routes, slots = pair_routes(count)
    width = tile.shape[0] // 3
    got = [lax.ppermute(tile[p * width : (p + 1) * width], "seq", routes[p]) for p in range(3)]
    slot_of = jnp.asarray(slots, jnp.int32)[lax.axis_index("seq")]
    rows = []
    for slot in range(3):
        rows.append(jnp.where(slot_of[0] == slot, got[0], jnp.where(slot_of[1] == slot, got[1], got[2])))
    return jnp.concatenate(rows, axis=0)


def stored_rows(pair_tile, count):
    routes, slots = pair_routes(count)
    width = pair_tile.shape[0] // 3
    slot_of = jnp.asarray(slots, jnp.int32)[lax.axis_index("seq")]
    parts = [pair_tile[s * width : (s + 1) * width] for s in range(3)]
    back = []
    for piece in range(3):
        slot = slot_of[piece]
        chosen = jnp.where(slot == 0, parts[0], jnp.where(slot == 1, parts[1], parts[2]))
        back.append(lax.ppermute(chosen, "seq", [(target, source) for source, target in routes[piece]]))
    return jnp.concatenate(back, axis=0)


def chip_routes(dp, seq):
    chips = seq // 2

    def flat(move):
        return [(d * seq + s, move(d, s)) for d in range(dp) for s in range(seq)]

    def along_z(step):
        return flat(lambda d, s: d * seq + 2 * ((s // 2 + step) % chips) + s % 2)

    return {
        "x": flat(lambda d, s: (d ^ 1) * seq + s),
        "y": flat(lambda d, s: (d ^ 2) * seq + s),
        "xy": flat(lambda d, s: (d ^ 3) * seq + s),
        "core": flat(lambda d, s: d * seq + (s ^ 1)),
        "z": [along_z(step) for step in range(1, chips)],
    }


def send(value, route):
    return lax.ppermute(value, ("dp", "seq"), route)


def gather_column(tile, routes):
    return jnp.stack([tile] + [send(tile, route) for route in routes["z"]])


def gather_near(column, route):
    return jnp.stack([column, send(column, route)])


GELU_C = math.sqrt(2.0 / math.pi)


def gelu_parts(value):
    square = value * value
    slope = jnp.tanh(GELU_C * value * (1.0 + 0.044715 * square))
    low = 0.5 * (1.0 + slope)
    derivative = low + 0.5 * value * (1.0 - slope * slope) * (GELU_C * (1.0 + 3 * 0.044715 * square))
    return value * low, derivative


def lanes(parts):
    return jnp.concatenate(parts, axis=1)


def stay_order(value, first, second):
    return (value // second) % 2 + 2 * ((value // first) % 2)


def middle_kernel(
    place_ref, att_ref, stream_ref, low_ref, turned_low_ref, scale_ref, shift_ref,
    up_0, up_1, up_2, up_3, down_0, down_1, down_2, down_3,
    layer_ref, grad_mid_ref, grad_att_a_ref, grad_att_b_ref, sums_ref, down_own_out, down_other_out, up_own_out, up_other_out,
    up_w, down_w, out_w, normed_ref, turned_ref, sorted_ref, middle_ref, out_acc,
    down_own, down_other, up_own, up_other, up_sem, down_sem, out_sem, send_sem, *, dp, seq,
):
    dp_at, chip_at, core_at = place_ref[0], place_ref[1], place_ref[2]
    chips = seq // 2
    up_rows, up_cols = up_0.shape[2], up_0.shape[3]
    cols = down_0.shape[3]
    width = stream_ref.shape[1]
    out_rows = width // dp
    down_rows = down_0.shape[2] - out_rows

    def copies(name):
        made = []
        pieces, masks = ((up_0, up_1, up_2, up_3), (1, 2)) if name == "up" else ((down_0, down_1, down_2, down_3), (2, 1))
        for part in range(4):
            core = core_at if part < 2 else 1 - core_at
            for step in range(2):
                mask = (masks[1] if part % 2 else 0) ^ (masks[0] if step else 0)
                row = jnp.bitwise_xor(dp_at, mask)
                for back in range(chips):
                    block = 2 * lax.rem(chip_at + chips - back, chips) + core
                    column = pl.ds(pl.multiple_of(block * cols, cols), cols)
                    source, at = pieces[part].at[step, back], (part * 2 + step) * chips + back
                    if name == "up":
                        target = up_w.at[block, pl.ds(pl.multiple_of(row * up_rows, up_rows), up_rows), :]
                        sem = up_sem.at[at]
                    elif name == "down":
                        source = source.at[pl.ds(0, down_rows), :]
                        target = down_w.at[pl.ds(pl.multiple_of(row * down_rows, down_rows), down_rows), column]
                        sem = down_sem.at[at]
                    else:
                        source = source.at[pl.ds(down_rows, out_rows), :]
                        target = out_w.at[pl.ds(pl.multiple_of(row * out_rows, out_rows), out_rows), column]
                        sem = out_sem.at[at]
                    made.append(pltpu.make_async_copy(source, target, sem))
        return made

    for name in ("out", "up", "down"):
        for copy in copies(name):
            copy.start()
    tiles = [
        2 * ahead + (1 - core_at if other else core_at)
        for other in range(2)
        for ahead in range(chips)
    ]
    for at, tile in enumerate(tiles):
        rows = pl.ds(pl.multiple_of(tile * cols, cols), cols)
        sorted_ref[at * cols : (at + 1) * cols, :] = turned_low_ref[rows, :]
    for copy in copies("out"):
        copy.wait()
    middle_ref[...] = stream_ref[...] + dot_tn(att_ref[...], out_w[...])
    grad_acc = grad_mid_ref
    chunk = 128

    @pl.loop(0, stream_ref.shape[0] // chunk)
    def _(index):
        rows = pl.ds(pl.multiple_of(index * chunk, chunk), chunk)
        middle = middle_ref[rows, :]
        inverse = lax.rsqrt(jnp.mean(middle * middle, axis=-1, keepdims=True) + epsilon)
        normed = middle * inverse * (1.0 + scale_ref[...]) + shift_ref[...]
        normed_ref[rows, :] = normed.astype(jnp.bfloat16)
        turned = normed.T.astype(jnp.bfloat16)
        for row in range(dp):
            place = stay_order(jnp.bitwise_xor(dp_at, row), 2, 1)
            turned_ref[pl.ds(pl.multiple_of(place * out_rows, out_rows), out_rows), rows] = turned[
                row * out_rows : (row + 1) * out_rows
            ]
        out_acc[rows, :] = jnp.zeros_like(middle)
        grad_acc[rows, :] = jnp.zeros_like(middle)

    for name in ("up", "down"):
        for copy in copies(name):
            copy.wait()

    def hidden_block(other, up_grads):
        def run(ahead, carry):
            core = 1 - core_at if other else core_at
            block = 2 * ahead + core
            rows = pl.ds(pl.multiple_of(block * up_cols, up_cols), up_cols)
            up_weight, down_weight = up_w[block], down_w[rows, :]
            value, derivative = gelu_parts(dot_nn(normed_ref[...], up_weight))
            hidden = value.astype(jnp.bfloat16)
            out_acc[...] += dot_nn(hidden, down_weight)
            grad_up = (dot_nt(low_ref[...], down_weight) * derivative).astype(jnp.bfloat16)
            grad_acc[...] += dot_nt(grad_up, up_weight)
            for owner in range(dp):
                part = dot_nn(turned_ref[owner * up_rows : (owner + 1) * up_rows, :], grad_up)
                up_grads[owner, ahead] = part.astype(jnp.bfloat16)
            per_owner = down_rows // up_cols
            owner = stay_order(jnp.bitwise_xor(dp_at, block // per_owner), 1, 2)
            at = pl.ds(pl.multiple_of(lax.rem(block, per_owner) * cols, cols), cols)
            for pair in range(chips):
                part = dot_nn(sorted_ref[2 * pair * cols : 2 * (pair + 1) * cols, :], hidden).astype(jnp.bfloat16)
                for tile in range(2):
                    target, place = (down_own, 2 * pair + tile) if pair < chips // 2 else (down_other, 2 * pair + tile - chips)
                    target[owner, place, at, :] = part[tile * cols : (tile + 1) * cols]
            return carry

        lax.fori_loop(0, chips, run, 0, unroll=2)

    hidden_block(1, up_other)
    send_up_other = pltpu.make_async_copy(up_other, up_other_out, send_sem.at[0])
    send_up_other.start()
    hidden_block(0, up_own)
    packed = down_rows * cols // up_cols
    sends = [
        pltpu.make_async_copy(up_own, up_own_out, send_sem.at[1]),
        pltpu.make_async_copy(
            down_other.at[:, :, pl.ds(0, packed), :], down_other_out.at[:, :, pl.ds(0, packed), :], send_sem.at[2]
        ),
        pltpu.make_async_copy(
            down_own.at[:, :, pl.ds(0, packed), :], down_own_out.at[:, :, pl.ds(0, packed), :], send_sem.at[3]
        ),
    ]
    for copy in sends:
        copy.start()
    sums_ref[...] = jnp.zeros_like(sums_ref)

    @pl.loop(0, stream_ref.shape[0] // chunk)
    def _(index):
        rows = pl.ds(pl.multiple_of(index * chunk, chunk), chunk)
        middle = middle_ref[rows, :]
        layer_ref[rows, :] = (middle + out_acc[rows, :]).astype(jnp.bfloat16)
        inverse = lax.rsqrt(jnp.mean(middle * middle, axis=-1, keepdims=True) + epsilon)
        unit = middle * inverse
        grad = grad_acc[rows, :]
        lifted = grad * (1.0 + scale_ref[...])
        sums_ref[0:1, :] += jnp.sum(grad * unit, axis=0, keepdims=True)
        sums_ref[1:2, :] += jnp.sum(grad, axis=0, keepdims=True)
        grad_mid = low_ref[rows, :].astype(jnp.float32) + inverse * (
            lifted - unit * jnp.mean(lifted * unit, axis=-1, keepdims=True)
        )
        grad_mid_ref[rows, :] = grad_mid
        normed_ref[rows, :] = grad_mid.astype(jnp.bfloat16)

    grad_att = dot_nt(out_w[...], normed_ref[...]).astype(jnp.bfloat16)
    for target in range(seq):
        grad_att_a_ref[target] = grad_att[target * PAIR : target * PAIR + HD]
        grad_att_b_ref[target] = grad_att[target * PAIR + HD : (target + 1) * PAIR]
    grads = lanes([normed_ref[:, pl.ds(pl.multiple_of(tile * cols, cols), cols)] for tile in tiles])
    per_row = up_cols // cols
    folded = out_rows // per_row
    for row in range(dp):
        owner = stay_order(jnp.bitwise_xor(dp_at, row), 1, 2)
        product = dot_nn(att_ref[row * out_rows : (row + 1) * out_rows, :], grads).astype(jnp.bfloat16)
        for at in range(seq):
            part = product[:, at * cols : (at + 1) * cols]
            part = lanes([part[i * folded : (i + 1) * folded] for i in range(per_row)])
            target = down_own if at < chips else down_other
            target[owner, at % chips, packed : packed + folded, :] = part
    last = [
        pltpu.make_async_copy(
            down_other.at[:, :, pl.ds(packed, folded), :], down_other_out.at[:, :, pl.ds(packed, folded), :], send_sem.at[4]
        ),
        pltpu.make_async_copy(
            down_own.at[:, :, pl.ds(packed, folded), :], down_own_out.at[:, :, pl.ds(packed, folded), :], send_sem.at[5]
        ),
    ]
    for copy in last:
        copy.start()
    for copy in [send_up_other] + sends + last:
        copy.wait()


def middle_block(place, attended, stream, grad_low, scale, shift, up_pieces, down_pieces, dp, seq):
    frames, width = stream.shape
    tile_cols = up_pieces[0].shape[3]
    hidden = tile_cols * seq
    chips = seq // 2
    packed = hidden // dp * (width // seq) // tile_cols + width // dp * (width // seq) // tile_cols
    whole = pl.BlockSpec(memory_space=pltpu.VMEM)
    anywhere = pl.BlockSpec(memory_space=pl.ANY)
    half, full = jnp.bfloat16, jnp.float32
    down_shape, up_shape = (dp, chips, packed, tile_cols), (dp, chips, width // dp, tile_cols)
    return pl.pallas_call(
        partial(middle_kernel, dp=dp, seq=seq),
        in_specs=[pl.BlockSpec(memory_space=pltpu.SMEM)] + [whole] * 6 + [anywhere] * 8,
        out_specs=[whole] * 5 + [anywhere] * 4,
        out_shape=[
            jax.ShapeDtypeStruct((frames, width), half),
            jax.ShapeDtypeStruct((frames, width), full),
            jax.ShapeDtypeStruct((seq, HD, frames), half),
            jax.ShapeDtypeStruct((seq, HD, frames), half),
            jax.ShapeDtypeStruct((2, width), full),
            jax.ShapeDtypeStruct(down_shape, half),
            jax.ShapeDtypeStruct(down_shape, half),
            jax.ShapeDtypeStruct(up_shape, half),
            jax.ShapeDtypeStruct(up_shape, half),
        ],
        scratch_shapes=[
            pltpu.VMEM((seq, width, tile_cols), half),
            pltpu.VMEM((hidden, width), half),
            pltpu.VMEM((width, width), half),
            pltpu.VMEM((frames, width), half),
            pltpu.VMEM((width, frames), half),
            pltpu.VMEM((width, frames), half),
            pltpu.VMEM((frames, width), full),
            pltpu.VMEM((frames, width), full),
            pltpu.VMEM(down_shape, half),
            pltpu.VMEM(down_shape, half),
            pltpu.VMEM(up_shape, half),
            pltpu.VMEM(up_shape, half),
            pltpu.SemaphoreType.DMA((dp * seq,)),
            pltpu.SemaphoreType.DMA((dp * seq,)),
            pltpu.SemaphoreType.DMA((dp * seq,)),
            pltpu.SemaphoreType.DMA((6,)),
        ],
        compiler_params=pltpu.CompilerParams(vmem_limit_bytes=62 << 20),
        cost_estimate=pl.CostEstimate(
            flops=12 * frames * width * hidden + 6 * frames * width * width,
            bytes_accessed=8 * hidden * width + 24 * frames * width,
            transcendentals=frames * hidden,
        ),
        name="middle_block",
    )(place, attended, stream, grad_low, grad_low.T, scale, shift, *up_pieces, *down_pieces)


def entry_kernel(main_ref, side_ref, weight_ref, scale_ref, shift_ref, stream_ref, normed_ref, *, dp, seq):
    row = pl.program_id(0)

    @pl.when(row == 0)
    def _():
        stream_ref[...] = jnp.zeros_like(stream_ref)

    operand = jnp.where(row < dp // 2, main_ref[...], side_ref[...])
    stream_ref[...] += dot_nn(operand, lanes([weight_ref[s] for s in range(seq)]))

    @pl.when(row == dp - 1)
    def _():
        stream = stream_ref[...]
        inverse = lax.rsqrt(jnp.mean(stream * stream, axis=-1, keepdims=True) + epsilon)
        normed_ref[...] = (stream * inverse * (1.0 + scale_ref[...]) + shift_ref[...]).astype(jnp.bfloat16)


def entry_block(main, side, skip_tiles, scale, shift, dp, seq):
    frames, width = main.shape
    rows, columns = skip_tiles.shape[1:]
    fixed = pl.BlockSpec((1, width), lambda i: (0, 0))
    return pl.pallas_call(
        partial(entry_kernel, dp=dp, seq=seq),
        grid=(dp,),
        in_specs=[
            pl.BlockSpec((frames, rows), lambda i: (0, jnp.minimum(i, dp // 2 - 1))),
            pl.BlockSpec((frames, rows), lambda i: (0, jnp.maximum(i - dp // 2, 0))),
            pl.BlockSpec((seq, rows, columns), lambda i: (i, 0, 0)),
            fixed,
            fixed,
        ],
        out_specs=[pl.BlockSpec((frames, width), lambda i: (0, 0))] * 2,
        out_shape=[
            jax.ShapeDtypeStruct((frames, width), jnp.float32),
            jax.ShapeDtypeStruct((frames, width), jnp.bfloat16),
        ],
        compiler_params=pltpu.CompilerParams(vmem_limit_bytes=32 << 20),
        cost_estimate=pl.CostEstimate(
            flops=4 * frames * width * width, bytes_accessed=14 * frames * width, transcendentals=0
        ),
        name="entry_block",
    )(main, side, skip_tiles, scale, shift)


def head_product(head, head_ref, pair_ref, dp, seq):
    parts = [head_ref[s, piece * HD : (piece + 1) * HD] for s in range(seq) for piece in range(3)]
    projected = jnp.concatenate(parts, axis=0).T
    for row in range(dp):
        weight = jnp.concatenate(
            [
                pair_ref[row * seq + s, piece * PAIR + head * HD : piece * PAIR + (head + 1) * HD]
                for s in range(seq)
                for piece in range(3)
            ],
            axis=0,
        )
        yield row, dot_nn(projected, weight)


def first_head_kernel(head_ref, pair_ref, out_ref, *, dp, seq):
    rows = pair_ref.shape[2]
    for row, product in head_product(0, head_ref, pair_ref, dp, seq):
        out_ref[:, row * rows : (row + 1) * rows] = product


def first_head(head_a, pair_tiles, dp, seq):
    frames, width = head_a.shape[2], pair_tiles.shape[2] * dp
    whole = pl.BlockSpec(memory_space=pltpu.VMEM)
    return pl.pallas_call(
        partial(first_head_kernel, dp=dp, seq=seq),
        in_specs=[whole] * 2,
        out_specs=whole,
        out_shape=jax.ShapeDtypeStruct((frames, width), jnp.float32),
        compiler_params=pltpu.CompilerParams(vmem_limit_bytes=32 << 20),
        cost_estimate=pl.CostEstimate(
            flops=3 * frames * width * width, bytes_accessed=7 * frames * width + 6 * width * width, transcendentals=0
        ),
        name="first_head",
    )(head_a, pair_tiles)


def exit_kernel(
    partial_ref, head_ref, pair_ref, stream_ref, grad_mid_ref, scale_ref, grad_ref, turned_ref, sums_ref, normed_ref,
    *, dp, seq,
):
    rows = pair_ref.shape[2]
    for row, product in head_product(1, head_ref, pair_ref, dp, seq):
        columns = slice(row * rows, (row + 1) * rows)
        normed_ref[:, columns] = product + partial_ref[:, columns]
    sums_ref[...] = jnp.zeros_like(sums_ref)
    chunk = 128

    @pl.loop(0, stream_ref.shape[0] // chunk)
    def _(index):
        at = pl.ds(pl.multiple_of(index * chunk, chunk), chunk)
        grad, stream = normed_ref[at, :], stream_ref[at, :]
        inverse = lax.rsqrt(jnp.mean(stream * stream, axis=-1, keepdims=True) + epsilon)
        unit = stream * inverse
        lifted = grad * (1.0 + scale_ref[...])
        sums_ref[0:1, :] += jnp.sum(grad * unit, axis=0, keepdims=True)
        sums_ref[1:2, :] += jnp.sum(grad, axis=0, keepdims=True)
        grad_stream = grad_mid_ref[at, :] + inverse * (
            lifted - unit * jnp.mean(lifted * unit, axis=-1, keepdims=True)
        )
        grad_ref[at, :] = grad_stream.astype(jnp.bfloat16)
        turned_ref[:, at] = grad_stream.T.astype(jnp.bfloat16)


def exit_block(first, head_b, pair_tiles, stream, grad_mid, scale, dp, seq):
    frames, width = stream.shape
    whole = pl.BlockSpec(memory_space=pltpu.VMEM)
    return pl.pallas_call(
        partial(exit_kernel, dp=dp, seq=seq),
        in_specs=[whole] * 6,
        out_specs=[whole] * 3,
        out_shape=[
            jax.ShapeDtypeStruct((frames, width), jnp.bfloat16),
            jax.ShapeDtypeStruct((width, frames), jnp.bfloat16),
            jax.ShapeDtypeStruct((2, width), jnp.float32),
        ],
        scratch_shapes=[pltpu.VMEM((frames, width), jnp.float32)],
        compiler_params=pltpu.CompilerParams(vmem_limit_bytes=40 << 20),
        cost_estimate=pl.CostEstimate(
            flops=3 * frames * width * width, bytes_accessed=18 * frames * width + 6 * width * width, transcendentals=0
        ),
        name="exit_block",
    )(first, head_b, pair_tiles, stream, grad_mid, scale)


def joined_kernel(grad_ref, weight_ref, main_ref, side_ref, *, dp, seq):
    row = pl.program_id(0)
    grad = dot_nt(grad_ref[...], lanes([weight_ref[s] for s in range(seq)]))

    @pl.when(row < dp // 2)
    def _():
        main_ref[...] = grad

    @pl.when(row >= dp // 2)
    def _():
        side_ref[...] = grad


def joined_grads(grad_stream, skip_tiles, dp, seq):
    frames, width = grad_stream.shape
    rows, columns = skip_tiles.shape[1:]
    out = jax.ShapeDtypeStruct((frames, width), jnp.float32)
    return pl.pallas_call(
        partial(joined_kernel, dp=dp, seq=seq),
        grid=(dp,),
        in_specs=[
            pl.BlockSpec((frames, width), lambda i: (0, 0)),
            pl.BlockSpec((seq, rows, columns), lambda i: (i, 0, 0)),
        ],
        out_specs=[
            pl.BlockSpec((frames, rows), lambda i: (0, jnp.minimum(i, dp // 2 - 1))),
            pl.BlockSpec((frames, rows), lambda i: (0, jnp.maximum(i - dp // 2, 0))),
        ],
        out_shape=[out, out],
        compiler_params=pltpu.CompilerParams(vmem_limit_bytes=32 << 20),
        cost_estimate=pl.CostEstimate(
            flops=4 * frames * width * width, bytes_accessed=14 * frames * width, transcendentals=0
        ),
        name="joined_grads",
    )(grad_stream, skip_tiles)


def along_chips(place_ref, chips, other, block):
    core = 1 - place_ref[2] if other else place_ref[2]
    return [pl.multiple_of((2 * chip + core) * block, block) for chip in range(chips)]


def turned_parts(place_ref, left_ref, right_ref, chips, seq, other):
    block = left_ref.shape[0] // seq
    starts = along_chips(place_ref, chips, other, block)
    left = jnp.concatenate([left_ref[pl.ds(start, block), :] for start in starts], axis=0)
    product = dot_nn(left, right_ref[...])
    return [product[ahead * block : (ahead + 1) * block] for ahead in range(chips)]


def plain_parts(place_ref, left_ref, right_ref, chips, seq, other):
    block = right_ref.shape[1] // seq
    starts = along_chips(place_ref, chips, other, block)
    product = dot_nn(left_ref[...], lanes([right_ref[:, pl.ds(start, block)] for start in starts]))
    return [product[:, ahead * block : (ahead + 1) * block] for ahead in range(chips)]


def fold_columns(part, width):
    return jnp.concatenate([part[:, at : at + width] for at in range(0, part.shape[1], width)], axis=0)


def fold_rows(part, width):
    rows = part.shape[0] * part.shape[1] // width
    return lanes([part[at : at + rows] for at in range(0, part.shape[0], rows)])


def blocks_kernel(place_ref, *refs, kinds, other, seq, width):
    chips = seq // 2
    step = pl.program_id(0)
    operands, outs = refs[: 2 * len(kinds)], refs[2 * len(kinds) :]
    packed = [[] for _ in range(chips)]
    for at, kind in enumerate(kinds):
        left_ref, right_ref = operands[2 * at], operands[2 * at + 1]
        if kind == "turned":
            parts = [fold_columns(part, width) for part in turned_parts(place_ref, left_ref, right_ref, chips, seq, other)]
        else:
            parts = plain_parts(place_ref, left_ref, right_ref, chips, seq, other)
            parts = [fold_rows(part, width) if part.shape[1] < width else part for part in parts]
        for ahead in range(chips):
            packed[ahead].append(parts[ahead])
    if not other:
        arrived_ref, outs = outs[0], outs[1:]
    for ahead in range(chips):
        row = 0
        for part in packed[ahead]:
            rows = slice(row, row + part.shape[0])
            row += part.shape[0]
            if other:
                outs[0][0, ahead, rows, :] = part.astype(jnp.bfloat16)
            else:
                low = (part + arrived_ref[0, ahead, rows, :].astype(jnp.float32)).astype(jnp.bfloat16)

                @pl.when(step < 2)
                def _(low=low, ahead=ahead, rows=rows):
                    outs[0][0, ahead, rows, :] = low

                @pl.when(step >= 2)
                def _(low=low, ahead=ahead, rows=rows):
                    outs[1][0, ahead, rows, :] = low


def grad_blocks(place, products, masks, seq, width, arrived=None, part=(0, 1)):
    first, second = masks
    chips, dp = seq // 2, 4

    def owner(i, place):
        return jnp.bitwise_xor(place[0], (i % 2) * second + (i // 2) * first)

    specs, operands, kinds, rows, flops = [], [], [], 0, 0
    for kind, left, right in products:
        depth = left.shape[1]
        if kind == "turned":
            columns = right.shape[1] // (dp * part[1])
            shape = (left.shape[0] // seq, columns)
            specs += [
                pl.BlockSpec(left.shape, lambda i, place: (0, 0)),
                pl.BlockSpec((depth, columns), lambda i, place: (0, owner(i, place) * part[1] + part[0])),
            ]
        else:
            shape = (left.shape[0] // dp, right.shape[1] // seq)
            specs += [
                pl.BlockSpec((shape[0], depth), lambda i, place: (owner(i, place), 0)),
                pl.BlockSpec(right.shape, lambda i, place: (0, 0)),
            ]
        operands += [left, right]
        kinds.append(kind)
        rows += shape[0] * shape[1] // width
        flops += 2 * dp * chips * shape[0] * shape[1] * depth
    other = arrived is None
    one = (1, chips, rows, width)
    if other:
        outs, count = [pl.BlockSpec(one, lambda i, place: (i, 0, 0, 0))], 4
    else:
        outs = [
            pl.BlockSpec(one, lambda i, place: (jnp.minimum(i, 1), 0, 0, 0)),
            pl.BlockSpec(one, lambda i, place: (jnp.maximum(i - 2, 0), 0, 0, 0)),
        ]
        count = 2
        specs.append(pl.BlockSpec(one, lambda i, place: (i, 0, 0, 0)))
        operands.append(arrived)
    return pl.pallas_call(
        partial(blocks_kernel, kinds=tuple(kinds), other=other, seq=seq, width=width),
        grid_spec=pltpu.PrefetchScalarGridSpec(num_scalar_prefetch=1, grid=(4,), in_specs=specs, out_specs=outs),
        out_shape=[jax.ShapeDtypeStruct((count, chips, rows, width), jnp.bfloat16)] * len(outs),
        compiler_params=pltpu.CompilerParams(vmem_limit_bytes=48 << 20),
        cost_estimate=pl.CostEstimate(
            flops=flops, bytes_accessed=8 * rows * width * chips * (1 if other else 2) + flops // 512, transcendentals=0
        ),
        name="grad_blocks",
    )(place, *operands)


AXIS_MASK = {"x": 1, "y": 2}


def wide(value):
    return value.astype(jnp.float32)


def low(value):
    return value.astype(jnp.bfloat16)


def dp_gather(tile, routes, dp):
    at = lax.axis_index("dp")
    columns = tile.shape[1]
    full = jnp.zeros((tile.shape[0], dp * columns), tile.dtype)
    full = lax.dynamic_update_slice_in_dim(full, tile, at * columns, 1)
    for mask, route in ((1, routes["x"]), (2, routes["y"]), (3, routes["xy"])):
        full = lax.dynamic_update_slice_in_dim(full, send(tile, route), jnp.bitwise_xor(at, mask) * columns, 1)
    return full


def chips_exchange(value, seq):
    groups = [[core + 2 * chip for chip in range(seq // 2)] for core in range(2)]
    return lax.all_to_all(value, "seq", 0, 0, axis_index_groups=groups)


def local_paired(
    inputs, skip_input, time_embed, segment_ids, span_start, span_length, cotangent,
    skip_weight, ada_weight, qkv_weight, out_weight, up_weight, down_weight,
):
    seq = lax.axis_size("seq")
    dp = lax.axis_size("dp")
    frames, width = inputs.shape[1], inputs.shape[2]
    length = segment_ids.shape[1]
    segments = segment_ids[0]
    end_a = jnp.sum((segments < 1).astype(jnp.int32))
    end_b = jnp.sum((segments < 2).astype(jnp.int32))
    ends = jnp.stack([end_a, end_b])
    firsts = jnp.where(segments == 0, 0, jnp.where(segments == 1, end_a, end_b))
    position = jnp.arange(length, dtype=jnp.int32) - firsts
    half = HD // 2
    frequency = jnp.exp(-math.log(10000.0) * jnp.arange(half, dtype=jnp.float32) / half)
    angles = frequency[:, None] * position.astype(jnp.float32)[None, :]
    cos_all, sin_all = jnp.cos(angles), jnp.sin(angles)
    base = lax.axis_index("seq") * frames
    local_segments = lax.dynamic_slice_in_dim(segments, base, frames, 0)
    local_position = lax.dynamic_slice_in_dim(position, base, frames, 0)
    starts, lengths = span_start[0], span_length[0]

    def pick(table):
        return jnp.where(local_segments == 0, table[0], jnp.where(local_segments == 1, table[1], table[2]))

    span_begin = pick(starts)
    inside = jnp.logical_and(local_position >= span_begin, local_position < span_begin + pick(lengths))
    grad_low = jnp.where(inside[:, None], cotangent[0], jnp.zeros((), jnp.bfloat16))
    routes = chip_routes(dp, seq)
    seq_at = lax.axis_index("seq")
    place = jnp.stack([lax.axis_index("dp"), seq_at // 2, seq_at % 2]).astype(jnp.int32)
    up_column = gather_column(up_weight, routes)
    down_column = gather_column(jnp.concatenate([down_weight, out_weight]), routes)
    embed_all = lax.all_gather(time_embed, "dp", axis=0, tiled=True)
    embed_rows = width // dp
    embed_part = lax.dynamic_slice_in_dim(embed_all, lax.axis_index("dp") * embed_rows, embed_rows, 1)
    modulation_part = jnp.dot(embed_part, ada_weight, preferred_element_type=jnp.float32)
    modulation_part = lax.psum_scatter(modulation_part, "dp", scatter_dimension=0, tiled=True)
    modulation = lax.all_gather(modulation_part, "seq", axis=1, tiled=True)
    scale_one = modulation[:, :width]
    shift_one = modulation[:, width : 2 * width]
    scale_two = modulation[:, 2 * width : 3 * width]
    shift_two = modulation[:, 3 * width :]

    skip_tiles = lax.all_gather(skip_weight, ("dp", "seq"), axis=0)
    pair_tile = own_pair_rows(qkv_weight.T, seq)
    skip_tiles, up_column, down_column, cos_all, sin_all, ends, grad_low, place = lax.optimization_barrier(
        (skip_tiles, up_column, down_column, cos_all, sin_all, ends, grad_low, place)
    )
    stream, normed_one = entry_block(inputs[0], skip_input[0], skip_tiles, scale_one, shift_one, dp, seq)
    normed_all = lax.all_gather(normed_one, "seq", axis=0)
    up_near = gather_near(up_column, routes["x"])
    down_near = gather_near(down_column, routes["y"])
    pair_weight = dp_gather(pair_tile, routes, dp)
    up_near, down_near, pair_weight = lax.optimization_barrier((up_near, down_near, pair_weight))
    up_far, down_far = send(up_near, routes["y"]), send(down_near, routes["x"])
    normed_all, up_near, down_near = lax.optimization_barrier((normed_all, up_near, down_near))
    up_near_core, down_near_core = send(up_near, routes["core"]), send(down_near, routes["core"])
    qt, kt, vt, keys, values, norms = project_pair(normed_all, pair_weight, cos_all, sin_all)
    attended_pair, attended_wide, total = attend_pair(ends, qt, keys, vt, norms)
    attended_pair, up_far, down_far = lax.optimization_barrier((attended_pair, up_far, down_far))
    up_pieces = (up_near, up_far, up_near_core, send(up_far, routes["core"]))
    down_pieces = (down_near, down_far, down_near_core, send(down_far, routes["core"]))
    attended = lax.all_to_all(attended_pair, "seq", 0, 0).reshape(width, frames)
    attended, pair_tile, far_up, far_down = lax.optimization_barrier(
        (attended, pair_tile, up_pieces[3], down_pieces[3])
    )
    up_pieces, down_pieces = up_pieces[:3] + (far_up,), down_pieces[:3] + (far_down,)
    pair_tiles = lax.all_gather(pair_tile, ("dp", "seq"), axis=0)
    layer_output, grad_middle, grad_head_a, grad_head_b, sums_two, down_own, down_other, up_own, up_other = middle_block(
        place, attended, stream, grad_low, scale_two, shift_two, up_pieces, down_pieces, dp, seq
    )
    grad_head_a = lax.all_to_all(grad_head_a, "seq", 0, 0)
    down_other, up_other = send(down_other, routes["core"]), send(up_other, routes["core"])
    down_half, up_half = down_own.shape[2] // 2, up_own.shape[2] // 2

    def leaves(own, other, rows):
        return low(wide(own[2:, :, rows]) + wide(other[2:, :, rows]))

    away = (
        leaves(down_own, down_other, slice(0, down_half)),
        leaves(down_own, down_other, slice(down_half, None)),
        leaves(up_own, up_other, slice(0, up_half)),
        leaves(up_own, up_other, slice(up_half, None)),
    )
    grad_head_b, *away = lax.optimization_barrier((grad_head_b, *away))
    grad_head_b = lax.all_to_all(grad_head_b, "seq", 0, 0)
    saved = (attended_wide, total, keys, values, kt, cos_all, sin_all)
    grad_head_a, pair_tiles, *away = lax.optimization_barrier((grad_head_a, pair_tiles, *away))
    down_got = [send(away[0], routes["x"]), send(away[1], routes["x"])]
    up_got = [send(away[2], routes["y"]), send(away[3], routes["y"])]
    back_a = attend_head_back(0, ends, qt, grad_head_a, *saved)
    local_a = lax.all_to_all(back_a, "seq", 0, 0)
    back_a, grad_head_b, down_got[0], up_got[0] = lax.optimization_barrier(
        (back_a, grad_head_b, down_got[0], up_got[0])
    )
    back_b = attend_head_back(1, ends, qt, grad_head_b, *saved)
    back_b, local_a = lax.optimization_barrier((back_b, local_a))
    local_b = lax.all_to_all(back_b, "seq", 0, 0)

    def stays(own, other, got, at):
        return wide(own[at]) + wide(other[at]) + wide(got[at])

    back_a, back_b, down_got[1], up_got[1] = lax.optimization_barrier((back_a, back_b, down_got[1], up_got[1]))
    down_got, up_got = jnp.concatenate(down_got, axis=2), jnp.concatenate(up_got, axis=2)
    down_low, up_low = low(stays(down_own, down_other, down_got, 1)), low(stays(up_own, up_other, up_got, 1))
    down_low, up_low, back_a, back_b = lax.optimization_barrier((down_low, up_low, back_a, back_b))
    down_back, up_back = send(down_low, routes["y"]), send(up_low, routes["x"])
    parts = [part[:, at : at + HD] for at in range(0, 3 * HD, HD) for part in (back_a, back_b)]
    grad_projected = jnp.concatenate(parts, axis=1)
    grad_pair_weight = jnp.einsum(
        "icf,ifd->cd", grad_projected, normed_all, preferred_element_type=jnp.float32
    ).astype(jnp.bfloat16)
    local_b, grad_pair_weight = lax.optimization_barrier((local_b, grad_pair_weight))
    grad_stream, grad_stream_turned, sums_one = exit_block(
        first_head(local_a, pair_tiles, dp, seq), local_b, pair_tiles, stream, grad_middle, scale_one, dp, seq
    )
    joined = jnp.concatenate([inputs[0], skip_input[0]], axis=-1)
    chips, chip_at, core_at = seq // 2, seq_at // 2, seq_at % 2
    grad_modulation = jnp.concatenate([sums_one[0], sums_one[1], sums_two[0], sums_two[1]]).reshape(chips, 2, -1)
    kept = lax.dynamic_index_in_dim(grad_modulation, core_at, 1, keepdims=False)
    kept = kept + send(lax.dynamic_index_in_dim(grad_modulation, 1 - core_at, 1, keepdims=False), routes["core"])
    column_sum = lax.dynamic_index_in_dim(kept, chip_at, 0)
    for ahead, route in enumerate(routes["z"]):
        piece = lax.dynamic_index_in_dim(kept, (chip_at + ahead + 1) % chips, 0)
        column_sum = column_sum + send(piece, route)
    half_tile = skip_weight.shape[0] // 2
    at = lax.axis_index("dp")
    half_pair = 3 * PAIR // 2
    wide_tile = up_weight.shape[1]
    turned = [("turned", grad_stream_turned, joined)]
    order = (("x", "y"), ("y", "x"))

    def skip_blocks(part, arrived):
        masks = tuple(AXIS_MASK[axis] for axis in order[part])
        return grad_blocks(place, turned, masks, seq, half_tile, arrived, (part, 2))

    leaving = [skip_blocks(part, None)[0] for part in range(2)]
    *leaving, down_back, up_back = lax.optimization_barrier((*leaving, down_back, up_back))
    arrived = [send(part, routes["core"]) for part in leaving]
    down_total = stays(down_own, down_other, down_got, 0) + wide(down_back)
    up_total = stays(up_own, up_other, up_got, 0) + wide(up_back)
    mlp_low = jnp.concatenate([low(down_total), low(up_total)], axis=1)
    column_sum, mlp_low = lax.optimization_barrier((column_sum, mlp_low))
    mlp_got = chips_exchange(mlp_low, seq)
    skip_parts = []
    for part, (first, second) in enumerate(order):
        keep, away = skip_blocks(part, arrived[part])
        pair_rows = grad_pair_weight[part * half_pair : (part + 1) * half_pair]

        def pair_block(mask):
            return lax.dynamic_slice_in_dim(pair_rows, jnp.bitwise_xor(at, mask) * half_tile, half_tile, 1)

        near, far = AXIS_MASK[first], AXIS_MASK[second]
        keep = jnp.concatenate([keep.reshape(2, -1, half_tile), jnp.stack([pair_block(0), pair_block(far)])], axis=1)
        away = jnp.concatenate(
            [away.reshape(2, -1, half_tile), jnp.stack([pair_block(near), pair_block(near ^ far)])], axis=1
        )
        skip_parts.append([keep, away, first, second])
    skip_parts[0][1], skip_parts[1][1], grad_stream, column_sum = lax.optimization_barrier(
        (skip_parts[0][1], skip_parts[1][1], grad_stream, column_sum)
    )
    skip_parts = [(keep, send(away, routes[first]), routes[second]) for keep, away, first, second in skip_parts]
    grad_main, grad_side = joined_grads(grad_stream, skip_tiles, dp, seq)
    got_a, got_b, grad_main, column_sum = lax.optimization_barrier(
        (skip_parts[0][1], skip_parts[1][1], grad_main, column_sum)
    )
    skip_parts = [(skip_parts[0][0], got_a, skip_parts[0][2]), (skip_parts[1][0], got_b, skip_parts[1][2])]
    grad_modulation = jnp.concatenate([column_sum, send(column_sum, routes["x"])])
    grad_modulation = jnp.concatenate([grad_modulation, send(grad_modulation, routes["y"])])
    skip_low, pair_sums = [], []
    skip_rows = chips * (width // seq)
    for keep, got, route in skip_parts:
        back = send(low(wide(keep[1]) + wide(got[1])), route)
        total_part = wide(keep[0]) + wide(got[0]) + wide(back)
        pair_sums.append(total_part[skip_rows:])
        skip_low.append(low(total_part[:skip_rows].reshape(chips, width // seq, half_tile)))
    skip_low = jnp.concatenate(skip_low, axis=2)
    skip_low, mlp_got = lax.optimization_barrier((skip_low, mlp_got))
    skip_tile = jnp.sum(wide(chips_exchange(skip_low, seq)), axis=0).T
    qkv_tile = wide(stored_rows(low(jnp.concatenate(pair_sums)), seq)).T

    mlp_tile = jnp.sum(wide(mlp_got), axis=0)
    columns = width // seq
    fold = down_weight.shape[0] // wide_tile
    down_tile = lanes([mlp_tile[i * columns : (i + 1) * columns] for i in range(fold)]).T
    out_tile = mlp_tile[fold * columns : down_total.shape[1]]
    out_tile = jnp.concatenate([out_tile[:, i * columns : (i + 1) * columns] for i in range(wide_tile // columns)])
    up_tile = mlp_tile[down_total.shape[1] :]
    embed_part = jnp.concatenate(
        [lax.dynamic_index_in_dim(embed_part, jnp.bitwise_xor(at, mask), 0) for mask in range(dp)]
    )
    ada_tile = lax.dot_general(
        embed_part.astype(jnp.float32), grad_modulation, (((0,), (0,)), ((), ())),
        precision=lax.Precision.HIGHEST,
    )
    return (
        layer_output[None],
        grad_main[None],
        grad_side[None],
        skip_tile,
        ada_tile,
        qkv_tile,
        out_tile,
        up_tile,
        down_tile,
    )


def solution(mesh):
    in_specs = (
        P("dp", "seq", None),
        P("dp", "seq", None),
        P("dp", None),
        P("dp", None),
        P("dp", None),
        P("dp", None),
        P("dp", "seq", None),
        P("dp", "seq"),
        P("dp", "seq"),
        P("dp", "seq"),
        P("dp", "seq"),
        P("dp", "seq"),
        P("dp", "seq"),
    )
    out_specs = (
        P("dp", "seq", None),
        P("dp", "seq", None),
        P("dp", "seq", None),
        P("dp", "seq"),
        P("dp", "seq"),
        P("dp", "seq"),
        P("dp", "seq"),
        P("dp", "seq"),
        P("dp", "seq"),
    )
    seq_size = mesh.shape["seq"]
    paired = H == 2 * seq_size and seq_size % 3 != 0 and mesh.shape["dp"] == 4
    body = local_paired if paired else local_general
    return jax.shard_map(body, mesh=mesh, in_specs=in_specs, out_specs=out_specs, check_vma=False)
```

```python
from functools import partial
import math

import jax
import jax.numpy as jnp
from jax import lax
from jax.experimental import pallas as pl
from jax.experimental.pallas import tpu as pltpu
from jax.sharding import PartitionSpec as P

H = 16
HD = 64
UTT = 3
HG = 8


epsilon = 1e-06
masked_score = -1e30


def ada_norm(stream, scale_part, shift_part):
    inverse = lax.rsqrt(jnp.mean(stream * stream, axis=-1, keepdims=True) + epsilon)
    return stream * inverse * (1.0 + scale_part) + shift_part


def rotate(tensor, cosine, sine_part):
    half_width = tensor.shape[-1] // 2
    lower_half = tensor[..., :half_width]
    upper_half = tensor[..., half_width:]
    cos_wide = cosine[..., None, :]
    sin_wide = sine_part[..., None, :]
    return jnp.concatenate(
        [
            lower_half * cos_wide - upper_half * sin_wide,
            lower_half * sin_wide + upper_half * cos_wide,
        ],
        axis=-1,
    )


def rotary_tables(position, half_width):
    frequency = jnp.exp(-math.log(10000.0) * jnp.arange(half_width, dtype=jnp.float32) / half_width)
    angles = position.astype(jnp.float32)[..., None] * frequency
    return (jnp.cos(angles), jnp.sin(angles))


def gather_weights(skip_tile, ada_tile, qkv_tile, out_tile, up_tile, down_tile):
    row_full = (
        lax.all_gather(skip_tile, "dp", axis=0, tiled=True),
        lax.all_gather(ada_tile, "dp", axis=0, tiled=True),
        lax.all_gather(qkv_tile, "dp", axis=0, tiled=True),
        lax.all_gather(out_tile, "dp", axis=0, tiled=True),
        lax.all_gather(up_tile, "dp", axis=0, tiled=True),
        lax.all_gather(down_tile, "dp", axis=0, tiled=True),
    )
    return (
        lax.all_gather(row_full[0], "seq", axis=1, tiled=True),
        lax.all_gather(row_full[1], "seq", axis=1, tiled=True),
        lax.all_gather(row_full[2], "seq", axis=1, tiled=True),
        lax.all_gather(row_full[3], "seq", axis=1, tiled=True),
        lax.all_gather(row_full[4], "seq", axis=1, tiled=True),
        lax.all_gather(row_full[5], "seq", axis=1, tiled=True),
    )


def group_scores(query_part, key_part, allowed, factor):
    scores = (
        jnp.einsum("qhd,khd->hqk", query_part, key_part, preferred_element_type=jnp.float32)
        * factor
    )
    return jnp.where(allowed[None], scores, masked_score)


def attend_row(queries, key_rows, value_rows, segment_local, segment_full):
    factor = queries.shape[2] ** (-0.5)
    allowed = segment_local[:, None] == segment_full[None, :]
    outputs = []
    totals = []
    for head_start in range(0, H, HG):
        head_end = head_start + HG
        scores = group_scores(
            queries[:, head_start:head_end], key_rows[:, head_start:head_end], allowed, factor
        )
        log_total = jax.nn.logsumexp(scores, axis=-1)
        weights = jnp.exp(scores - log_total[..., None]).astype(jnp.bfloat16)
        outputs.append(
            jnp.einsum(
                "hqk,khd->qhd",
                weights,
                value_rows[:, head_start:head_end],
                preferred_element_type=jnp.float32,
            )
        )
        totals.append(log_total)
    return (jnp.concatenate(outputs, axis=1), jnp.concatenate(totals, axis=0))


def attend_back(
    queries, key_rows, value_rows, segment_local, segment_full, log_total, grad_attended, row_dot
):
    factor = queries.shape[2] ** (-0.5)
    allowed = segment_local[:, None] == segment_full[None, :]
    query_grads = []
    key_grads = []
    value_grads = []
    for head_start in range(0, H, HG):
        head_end = head_start + HG
        key_part = key_rows[:, head_start:head_end]
        query_part = queries[:, head_start:head_end]
        grad_part = grad_attended[:, head_start:head_end]
        scores = group_scores(query_part, key_part, allowed, factor)
        weights = jnp.exp(scores - log_total[head_start:head_end][..., None])
        weights_low = weights.astype(jnp.bfloat16)
        value_grads.append(
            jnp.einsum("hqk,qhd->khd", weights_low, grad_part, preferred_element_type=jnp.float32)
        )
        grad_weights = jnp.einsum(
            "qhd,khd->hqk",
            grad_part,
            value_rows[:, head_start:head_end],
            preferred_element_type=jnp.float32,
        )
        grad_scores = (weights * (grad_weights - row_dot[head_start:head_end][..., None])).astype(
            jnp.bfloat16
        )
        query_grads.append(
            jnp.einsum("hqk,khd->qhd", grad_scores, key_part, preferred_element_type=jnp.float32)
            * factor
        )
        key_grads.append(
            jnp.einsum("hqk,qhd->khd", grad_scores, query_part, preferred_element_type=jnp.float32)
            * factor
        )
    return (
        jnp.concatenate(query_grads, axis=1),
        jnp.concatenate(key_grads, axis=1),
        jnp.concatenate(value_grads, axis=1),
    )


def local_general(
    inputs,
    skip_input,
    time_embed,
    segment_ids,
    span_start,
    span_length,
    cotangent,
    skip_weight,
    ada_weight,
    qkv_weight,
    out_weight,
    up_weight,
    down_weight,
):
    row_count = inputs.shape[0]
    frames = inputs.shape[1]
    model_width = inputs.shape[2]
    row_length = segment_ids.shape[1]
    frame_base = lax.axis_index("seq") * frames
    utterance = jnp.arange(UTT, dtype=jnp.int32)
    member = (segment_ids[:, :, None] == utterance[None, None, :]).astype(jnp.int32)
    counts = jnp.sum(member, axis=1)
    firsts = jnp.cumsum(counts, axis=1) - counts
    local_member = lax.dynamic_slice_in_dim(member, frame_base, frames, 1)
    local_segments = lax.dynamic_slice_in_dim(segment_ids, frame_base, frames, 1)
    local_frames = frame_base + jnp.arange(frames, dtype=jnp.int32)
    position = local_frames[None, :] - jnp.sum(local_member * firsts[:, None, :], axis=2)
    span_begin = jnp.sum(local_member * span_start[:, None, :], axis=2)
    span_end = span_begin + jnp.sum(local_member * span_length[:, None, :], axis=2)
    inside = jnp.logical_and(position >= span_begin, position < span_end)
    cosine, sine_part = rotary_tables(position, HD // 2)
    skip_full, ada_full, qkv_full, out_full, up_full, down_full = gather_weights(
        skip_weight, ada_weight, qkv_weight, out_weight, up_weight, down_weight
    )
    joined = jnp.concatenate([inputs, skip_input], axis=-1)
    stream = jnp.einsum("rfc,cd->rfd", joined, skip_full, preferred_element_type=jnp.float32)
    modulation = jnp.dot(time_embed, ada_full, preferred_element_type=jnp.float32)[:, None, :]
    scale_one = modulation[..., :model_width]
    shift_one = modulation[..., model_width : 2 * model_width]
    scale_two = modulation[..., 2 * model_width : 3 * model_width]
    shift_two = modulation[..., 3 * model_width :]
    normed_one = ada_norm(stream, scale_one, shift_one).astype(jnp.bfloat16)
    projected = jnp.einsum("rfd,de->rfe", normed_one, qkv_full, preferred_element_type=jnp.float32)
    queries = rotate(
        projected[..., :model_width].reshape(row_count, frames, H, HD), cosine, sine_part
    ).astype(jnp.bfloat16)
    key_rotated = rotate(
        projected[..., model_width : 2 * model_width].reshape(row_count, frames, H, HD),
        cosine,
        sine_part,
    )
    key_local = key_rotated.reshape(row_count, frames, model_width).astype(jnp.bfloat16)
    value_local = projected[..., 2 * model_width :].astype(jnp.bfloat16)
    key_all, value_all = (
        lax.all_gather(key_local, "seq", axis=1, tiled=True),
        lax.all_gather(value_local, "seq", axis=1, tiled=True),
    )

    def forward_row(row_items):
        query_row, key_row, value_row, local_row, full_row = row_items
        return attend_row(
            query_row,
            key_row.reshape(row_length, H, HD),
            value_row.reshape(row_length, H, HD),
            local_row,
            full_row,
        )

    attended, log_total = lax.map(
        forward_row, (queries, key_all, value_all, local_segments, segment_ids)
    )
    attended = attended.reshape(row_count, frames, model_width)
    attended_low = attended.astype(jnp.bfloat16)
    middle = stream + jnp.einsum(
        "rfe,ed->rfd", attended_low, out_full, preferred_element_type=jnp.float32
    )
    normed_two = ada_norm(middle, scale_two, shift_two).astype(jnp.bfloat16)
    up_proj = jnp.einsum("rfd,di->rfi", normed_two, up_full, preferred_element_type=jnp.float32)
    hidden = jax.nn.gelu(up_proj, approximate=True).astype(jnp.bfloat16)
    down_proj = jnp.einsum("rfi,id->rfd", hidden, down_full, preferred_element_type=jnp.float32)
    layer_output = (middle + down_proj).astype(jnp.bfloat16)
    skip_full, ada_full, qkv_full, out_full, up_full, down_full = gather_weights(
        skip_weight, ada_weight, qkv_weight, out_weight, up_weight, down_weight
    )
    grad_out = cotangent.astype(jnp.float32) * inside[..., None].astype(jnp.float32)
    grad_low = grad_out.astype(jnp.bfloat16)
    grad_hidden = jnp.einsum("rfd,id->rfi", grad_low, down_full, preferred_element_type=jnp.float32)
    _, gelu_pull = jax.vjp(partial(jax.nn.gelu, approximate=True), up_proj)
    grad_up_act = gelu_pull(grad_hidden)[0].astype(jnp.bfloat16)
    grad_normed_two = jnp.einsum(
        "rfi,di->rfd", grad_up_act, up_full, preferred_element_type=jnp.float32
    )
    _, norm_pull_two = jax.vjp(ada_norm, middle, scale_two, shift_two)
    grad_middle_norm, grad_scale_two, grad_shift_two = norm_pull_two(grad_normed_two)
    grad_middle = grad_out + grad_middle_norm
    grad_middle_low = grad_middle.astype(jnp.bfloat16)
    grad_attended = jnp.einsum(
        "rfd,ed->rfe", grad_middle_low, out_full, preferred_element_type=jnp.float32
    ).astype(jnp.bfloat16)
    row_dot = jnp.sum(
        (grad_attended.astype(jnp.float32) * attended).reshape(row_count, frames, H, HD), axis=-1
    )
    row_dot = jnp.swapaxes(row_dot, 1, 2)
    grad_heads = grad_attended.reshape(row_count, frames, H, HD)

    def backward_row(row_items):
        query_row, key_row, value_row, local_row, full_row, total_row, grad_row, dot_row = row_items
        return attend_back(
            query_row,
            key_row.reshape(row_length, H, HD),
            value_row.reshape(row_length, H, HD),
            local_row,
            full_row,
            total_row,
            grad_row,
            dot_row,
        )

    grad_queries, grad_keys, grad_values = lax.map(
        backward_row,
        (queries, key_all, value_all, local_segments, segment_ids, log_total, grad_heads, row_dot),
    )
    key_share, value_share = (
        lax.psum_scatter(
            grad_keys.reshape(row_count, row_length, model_width).astype(jnp.bfloat16),
            "seq",
            scatter_dimension=1,
            tiled=True,
        ).astype(jnp.float32),
        lax.psum_scatter(
            grad_values.reshape(row_count, row_length, model_width).astype(jnp.bfloat16),
            "seq",
            scatter_dimension=1,
            tiled=True,
        ).astype(jnp.float32),
    )
    _, rotate_pull = jax.vjp(
        partial(rotate, cosine=cosine, sine_part=sine_part),
        jnp.zeros((row_count, frames, H, HD), jnp.float32),
    )
    grad_query_raw = rotate_pull(grad_queries)[0].reshape(row_count, frames, model_width)
    grad_key_raw = rotate_pull(key_share.reshape(row_count, frames, H, HD))[0].reshape(
        row_count, frames, model_width
    )
    grad_projected = jnp.concatenate([grad_query_raw, grad_key_raw, value_share], axis=-1).astype(
        jnp.bfloat16
    )
    grad_normed_one = jnp.einsum(
        "rfe,de->rfd", grad_projected, qkv_full, preferred_element_type=jnp.float32
    )
    _, norm_pull_one = jax.vjp(ada_norm, stream, scale_one, shift_one)
    grad_stream_norm, grad_scale_one, grad_shift_one = norm_pull_one(grad_normed_one)
    grad_stream = (grad_middle + grad_stream_norm).astype(jnp.bfloat16)
    grad_joined = jnp.einsum(
        "rfd,cd->rfc", grad_stream, skip_full, preferred_element_type=jnp.float32
    )
    grad_modulation = jnp.concatenate(
        [grad_scale_one, grad_shift_one, grad_scale_two, grad_shift_two], axis=-1
    )[:, 0, :]
    grad_down = jnp.einsum("rfi,rfd->id", hidden, grad_low, preferred_element_type=jnp.float32)
    grad_up = jnp.einsum("rfd,rfi->di", normed_two, grad_up_act, preferred_element_type=jnp.float32)
    grad_attn_out = jnp.einsum(
        "rfe,rfd->ed", attended_low, grad_middle_low, preferred_element_type=jnp.float32
    )
    grad_qkv = jnp.einsum(
        "rfd,rfe->de", normed_one, grad_projected, preferred_element_type=jnp.float32
    )
    grad_skip_w = jnp.einsum("rfc,rfd->cd", joined, grad_stream, preferred_element_type=jnp.float32)
    grad_ada = jnp.einsum(
        "rd,re->de",
        time_embed.astype(jnp.float32),
        grad_modulation,
        precision=lax.Precision.HIGHEST,
    )
    column_parts = (
        lax.psum_scatter(
            grad_skip_w.astype(jnp.bfloat16), "seq", scatter_dimension=1, tiled=True
        ).astype(jnp.float32),
        lax.psum_scatter(
            grad_ada.astype(jnp.bfloat16), "seq", scatter_dimension=1, tiled=True
        ).astype(jnp.float32),
        lax.psum_scatter(
            grad_qkv.astype(jnp.bfloat16), "seq", scatter_dimension=1, tiled=True
        ).astype(jnp.float32),
        lax.psum_scatter(
            grad_attn_out.astype(jnp.bfloat16), "seq", scatter_dimension=1, tiled=True
        ).astype(jnp.float32),
        lax.psum_scatter(
            grad_up.astype(jnp.bfloat16), "seq", scatter_dimension=1, tiled=True
        ).astype(jnp.float32),
        lax.psum_scatter(
            grad_down.astype(jnp.bfloat16), "seq", scatter_dimension=1, tiled=True
        ).astype(jnp.float32),
    )
    weight_tiles = (
        lax.psum_scatter(
            column_parts[0].astype(jnp.bfloat16), "dp", scatter_dimension=0, tiled=True
        ).astype(jnp.float32),
        lax.psum_scatter(
            column_parts[1].astype(jnp.bfloat16), "dp", scatter_dimension=0, tiled=True
        ).astype(jnp.float32),
        lax.psum_scatter(
            column_parts[2].astype(jnp.bfloat16), "dp", scatter_dimension=0, tiled=True
        ).astype(jnp.float32),
        lax.psum_scatter(
            column_parts[3].astype(jnp.bfloat16), "dp", scatter_dimension=0, tiled=True
        ).astype(jnp.float32),
        lax.psum_scatter(
            column_parts[4].astype(jnp.bfloat16), "dp", scatter_dimension=0, tiled=True
        ).astype(jnp.float32),
        lax.psum_scatter(
            column_parts[5].astype(jnp.bfloat16), "dp", scatter_dimension=0, tiled=True
        ).astype(jnp.float32),
    )
    skip_tile, ada_tile, qkv_tile, out_tile, up_tile, down_tile = weight_tiles
    return (
        layer_output,
        grad_joined[..., :model_width],
        grad_joined[..., model_width:],
        skip_tile,
        ada_tile,
        qkv_tile,
        out_tile,
        up_tile,
        down_tile,
    )


LOG2E = 1.4426950408889634
SCALE = HD**-0.5
PAIR = 2 * HD


def dot_nn(a, b):
    return lax.dot_general(a, b, (((1,), (0,)), ((), ())), preferred_element_type=jnp.float32)


def dot_nt(a, b):
    return lax.dot_general(a, b, (((1,), (1,)), ((), ())), preferred_element_type=jnp.float32)


def dot_tn(a, b):
    return lax.dot_general(a, b, (((0,), (0,)), ((), ())), preferred_element_type=jnp.float32)


def segment_of(index, ends_ref):
    return (index >= ends_ref[0]).astype(jnp.int32) + (index >= ends_ref[1]).astype(jnp.int32)


def segment_span(ends_ref, first, last, length):
    end_a, end_b = ends_ref[0], ends_ref[1]
    low = jnp.where(first < end_a, 0, jnp.where(first < end_b, end_a, end_b))
    high = jnp.where(last < end_a, end_a, jnp.where(last < end_b, end_b, length))
    return low, high


def key_blocks(ends_ref, start, size, length):
    low, high = segment_span(ends_ref, start, start + size - 1, length)
    low_last, _ = segment_span(ends_ref, start + size - 1, start, length)
    first = low // size
    last = (high + size - 1) // size
    whole_first = jnp.where(low == low_last, (low + size - 1) // size, last)
    whole_first = jnp.minimum(whole_first, last)
    whole_last = jnp.where(low == low_last, jnp.maximum(high // size, whole_first), last)
    return first, whole_first, whole_last, last


def turn(pair, cosine, sine_part):
    half = HD // 2
    rows = []
    for head in range(pair.shape[0] // HD):
        lower = pair[head * HD : head * HD + half]
        upper = pair[head * HD + half : (head + 1) * HD]
        rows += [lower * cosine - upper * sine_part, lower * sine_part + upper * cosine]
    return jnp.concatenate(rows, axis=0)


def head_norms(pair):
    square = pair * pair
    return [jnp.sum(square[head * HD : (head + 1) * HD], axis=0, keepdims=True) for head in range(2)]


def project_kernel(
    normed_ref, weight_ref, cos_ref, sin_ref, qt_ref, kt_ref, vt_ref, k_ref, v_ref, norms_ref
):
    projected = dot_nt(weight_ref[...], normed_ref[0])
    cosine, sine_part = cos_ref[...], sin_ref[...]
    queries = turn(projected[:PAIR], cosine, sine_part).astype(jnp.bfloat16)
    keys = turn(projected[PAIR : 2 * PAIR], cosine, sine_part)
    values = projected[2 * PAIR :]
    norms_ref[0] = jnp.concatenate(head_norms(queries.astype(jnp.float32) * SCALE) + head_norms(keys), axis=0)
    qt_ref[0] = (queries.astype(jnp.float32) * SCALE).astype(jnp.bfloat16)
    kt_ref[...] = keys.astype(jnp.bfloat16)
    vt_ref[...] = values.astype(jnp.bfloat16)
    k_ref[...] = keys.T.astype(jnp.bfloat16)
    v_ref[...] = values.T.astype(jnp.bfloat16)


def project_pair(normed_all, weight_rows, cos_all, sin_all):
    chunks, frames, width = normed_all.shape
    length = chunks * frames
    return pl.pallas_call(
        project_kernel,
        grid=(chunks,),
        in_specs=[
            pl.BlockSpec((1, frames, width), lambda i: (i, 0, 0)),
            pl.BlockSpec((3 * PAIR, width), lambda i: (0, 0)),
            pl.BlockSpec((HD // 2, frames), lambda i: (0, i)),
            pl.BlockSpec((HD // 2, frames), lambda i: (0, i)),
        ],
        out_specs=[
            pl.BlockSpec((1, PAIR, frames), lambda i: (i, 0, 0)),
            pl.BlockSpec((PAIR, frames), lambda i: (0, i)),
            pl.BlockSpec((PAIR, frames), lambda i: (0, i)),
            pl.BlockSpec((frames, PAIR), lambda i: (i, 0)),
            pl.BlockSpec((frames, PAIR), lambda i: (i, 0)),
            pl.BlockSpec((1, 4, frames), lambda i: (i, 0, 0)),
        ],
        out_shape=[
            jax.ShapeDtypeStruct((chunks, PAIR, frames), jnp.bfloat16),
            jax.ShapeDtypeStruct((PAIR, length), jnp.bfloat16),
            jax.ShapeDtypeStruct((PAIR, length), jnp.bfloat16),
            jax.ShapeDtypeStruct((length, PAIR), jnp.bfloat16),
            jax.ShapeDtypeStruct((length, PAIR), jnp.bfloat16),
            jax.ShapeDtypeStruct((chunks, 4, frames), jnp.float32),
        ],
        compiler_params=pltpu.CompilerParams(vmem_limit_bytes=60 << 20),
        cost_estimate=pl.CostEstimate(
            flops=6 * length * width * PAIR, bytes_accessed=2 * length * (width + 5 * PAIR), transcendentals=0
        ),
        name="project_pair",
    )(normed_all, weight_rows, cos_all, sin_all)


def split_heads(block):
    row = lax.broadcasted_iota(jnp.int32, block.shape, 0)
    zero = jnp.zeros((), block.dtype)
    return jnp.where(row < HD, block, zero), jnp.where(row < HD, zero, block)


SAFE_SCORE = 60.0


def attend_kernel(
    ends_ref, qt_ref, k_ref, vt_ref, norms_ref, low_ref, full_ref, total_ref, acc_ref, top_ref, *, size, length
):
    index = pl.program_id(0)
    start = index * size
    queries = split_heads(qt_ref[0])
    query_segment = segment_of(start + lax.broadcasted_iota(jnp.int32, (1, size), 1), ends_ref)
    first, whole_first, whole_last, last = key_blocks(ends_ref, start, size, length)
    acc_ref[...] = jnp.zeros_like(acc_ref)
    ones = jnp.ones((16, size), jnp.bfloat16)
    bound = jnp.max(norms_ref[index, :2, :]) * jnp.max(norms_ref[:, 2:, :])
    plain = bound < SAFE_SCORE * SAFE_SCORE

    def step(masked, shifted):
        def run(block, carry):
            offset = pl.multiple_of(block * size, size)
            keys = k_ref[pl.ds(offset, size), :]
            scores = [dot_nn(keys, queries[head]) for head in range(2)]
            if masked:
                key_segment = segment_of(offset + lax.broadcasted_iota(jnp.int32, (size, 1), 0), ends_ref)
                same = key_segment == query_segment
                scores = [jnp.where(same, part, masked_score) for part in scores]
            if shifted:
                old = [top_ref[head] for head in range(2)]
                new = [
                    jnp.maximum(old[head], jnp.max(scores[head], axis=0, keepdims=True) * LOG2E) for head in range(2)
                ]
                weights = [jnp.exp2(scores[head] * LOG2E - new[head]).astype(jnp.bfloat16) for head in range(2)]
            else:
                weights = [jnp.exp2(scores[head] * LOG2E).astype(jnp.bfloat16) for head in range(2)]
            for head in range(2):
                values = jnp.concatenate([vt_ref[pl.ds(head * HD, HD), pl.ds(offset, size)], ones], axis=0)
                if shifted:
                    acc_ref[head] = acc_ref[head] * jnp.exp2(old[head] - new[head]) + dot_nn(values, weights[head])
                    top_ref[head] = new[head]
                else:
                    acc_ref[head] += dot_nn(values, weights[head])
            return carry

        return run

    def loops(shifted):
        lax.fori_loop(first, whole_first, step(True, shifted), 0)
        lax.fori_loop(whole_first, whole_last, step(False, shifted), 0)
        lax.fori_loop(whole_last, last, step(True, shifted), 0)

    @pl.when(plain)
    def _():
        top_ref[...] = jnp.zeros_like(top_ref)
        loops(False)

    @pl.when(jnp.logical_not(plain))
    def _():
        top_ref[...] = jnp.full_like(top_ref, masked_score)
        loops(True)

    for head in range(2):
        total = acc_ref[head, HD : HD + 1, :]
        attended = acc_ref[head, :HD, :] / total
        full_ref[0, head * HD : (head + 1) * HD, :] = attended
        low_ref[0, head * HD : (head + 1) * HD, :] = attended.astype(jnp.bfloat16)
        total_ref[0, head : head + 1, :] = jnp.log(total) * LOG2E + top_ref[head]


def attend_pair(ends, qt, k, vt, norms):
    chunks, _, size = qt.shape
    length = k.shape[0]
    chunk = pl.BlockSpec((1, PAIR, size), lambda i, ends: (i, 0, 0))
    return pl.pallas_call(
        partial(attend_kernel, size=size, length=length),
        grid_spec=pltpu.PrefetchScalarGridSpec(
            num_scalar_prefetch=1,
            grid=(chunks,),
            in_specs=[
                chunk,
                pl.BlockSpec((length, PAIR), lambda i, ends: (0, 0)),
                pl.BlockSpec((PAIR, length), lambda i, ends: (0, 0)),
                pl.BlockSpec(norms.shape, lambda i, ends: (0, 0, 0)),
            ],
            out_specs=[chunk, chunk, pl.BlockSpec((1, 2, size), lambda i, ends: (i, 0, 0))],
            scratch_shapes=[pltpu.VMEM((2, HD + 16, size), jnp.float32), pltpu.VMEM((2, 1, size), jnp.float32)],
        ),
        out_shape=[
            jax.ShapeDtypeStruct((chunks, PAIR, size), jnp.bfloat16),
            jax.ShapeDtypeStruct((chunks, PAIR, size), jnp.float32),
            jax.ShapeDtypeStruct((chunks, 2, size), jnp.float32),
        ],
        compiler_params=pltpu.CompilerParams(vmem_limit_bytes=60 << 20),
        cost_estimate=pl.CostEstimate(
            flops=8 * length * length * HD, bytes_accessed=14 * length * PAIR, transcendentals=length * length
        ),
        name="attend_pair",
    )(ends, qt, k, vt, norms)


def attend_back_kernel(
    ends_ref, qt_ref, gt_ref, full_ref, total_ref, k_ref, v_ref, kt_ref, cos_ref, sin_ref, out_ref,
    dk_ref, dv_ref, dq_ref, *, head, size, length, chunks,
):
    index = pl.program_id(0)
    start = index * size

    @pl.when(index == 0)
    def _():
        dk_ref[...] = jnp.zeros_like(dk_ref)
        dv_ref[...] = jnp.zeros_like(dv_ref)

    mine = slice(head * HD, (head + 1) * HD)
    queries = split_heads(qt_ref[0])[head]
    blank = jnp.zeros_like(gt_ref[0])
    grads = jnp.concatenate([blank, gt_ref[0]] if head else [gt_ref[0], blank], axis=0)
    row_dot = jnp.sum(gt_ref[0].astype(jnp.float32) * full_ref[0, mine, :], axis=0, keepdims=True)
    total = total_ref[0, head : head + 1, :]
    query_segment = segment_of(start + lax.broadcasted_iota(jnp.int32, (1, size), 1), ends_ref)
    first, whole_first, whole_last, last = key_blocks(ends_ref, start, size, length)
    dq_ref[...] = jnp.zeros_like(dq_ref)
    pieces = 2
    part = size // pieces

    def step(masked):
        def run(block, carry):
            for piece in range(pieces):
                offset = pl.multiple_of(block * size + piece * part, part)
                rows = pl.ds(offset, part)
                scores = dot_nn(k_ref[rows, :], queries)
                if masked:
                    key_segment = segment_of(offset + lax.broadcasted_iota(jnp.int32, (part, 1), 0), ends_ref)
                    scores = jnp.where(key_segment == query_segment, scores, masked_score)
                weights = jnp.exp2(scores * LOG2E - total)
                grad_weights = dot_nn(v_ref[rows, :], grads)
                grad_scores = (weights * (grad_weights - row_dot)).astype(jnp.bfloat16)
                dv_ref[rows, :] += dot_nt(weights.astype(jnp.bfloat16), grads)
                dk_ref[rows, :] += dot_nt(grad_scores, queries)
                dq_ref[...] += dot_nn(kt_ref[mine, rows], grad_scores)
            return carry

        return run

    lax.fori_loop(first, whole_first, step(True), 0)
    lax.fori_loop(whole_first, whole_last, step(False), 0)
    lax.fori_loop(whole_last, last, step(True), 0)
    own = pl.ds(pl.multiple_of(start, size), size)
    out_ref[index, :HD, :] = turn(dq_ref[...] * SCALE, cos_ref[:, own], -sin_ref[:, own]).astype(jnp.bfloat16)

    @pl.when(index == chunks - 1)
    def _():
        for chunk in range(chunks):
            rows = pl.ds(chunk * size, size)
            turned = turn(dk_ref[rows, :].T[mine], cos_ref[:, rows], -sin_ref[:, rows])
            out_ref[chunk, HD : 2 * HD, :] = turned.astype(jnp.bfloat16)
            out_ref[chunk, 2 * HD :, :] = dv_ref[rows, :].T[mine].astype(jnp.bfloat16)


def attend_head_back(head, ends, qt, gt, full, total, k, v, kt, cos_all, sin_all):
    chunks, _, size = qt.shape
    length = k.shape[0]
    chunk = pl.BlockSpec((1, PAIR, size), lambda i, ends: (i, 0, 0))

    def whole(shape):
        return pl.BlockSpec(shape, lambda i, ends: (0,) * len(shape))

    return pl.pallas_call(
        partial(attend_back_kernel, head=head, size=size, length=length, chunks=chunks),
        grid_spec=pltpu.PrefetchScalarGridSpec(
            num_scalar_prefetch=1,
            grid=(chunks,),
            in_specs=[
                chunk, pl.BlockSpec((1, HD, size), lambda i, ends: (i, 0, 0)), chunk,
                pl.BlockSpec((1, 2, size), lambda i, ends: (i, 0, 0)),
                whole((length, PAIR)), whole((length, PAIR)), whole((PAIR, length)),
                whole((HD // 2, length)), whole((HD // 2, length)),
            ],
            out_specs=whole((chunks, 3 * HD, size)),
            scratch_shapes=[
                pltpu.VMEM((length, PAIR), jnp.float32),
                pltpu.VMEM((length, PAIR), jnp.float32),
                pltpu.VMEM((HD, size), jnp.float32),
            ],
        ),
        out_shape=jax.ShapeDtypeStruct((chunks, 3 * HD, size), jnp.bfloat16),
        compiler_params=pltpu.CompilerParams(vmem_limit_bytes=60 << 20),
        cost_estimate=pl.CostEstimate(
            flops=40 * length * length * HD, bytes_accessed=20 * length * PAIR, transcendentals=0
        ),
        name="attend_head_back",
    )(ends, qt, gt, full, total, k, v, kt, cos_all, sin_all)


def pair_routes(count):
    routes = [[(source, (3 * source + piece) % count) for source in range(count)] for piece in range(3)]
    slots = [[0] * 3 for _ in range(count)]
    for piece in range(3):
        for source, target in routes[piece]:
            slots[target][piece] = (3 * source + piece) // count
    return routes, slots


def own_pair_rows(tile, count):
    routes, slots = pair_routes(count)
    width = tile.shape[0] // 3
    got = [lax.ppermute(tile[p * width : (p + 1) * width], "seq", routes[p]) for p in range(3)]
    slot_of = jnp.asarray(slots, jnp.int32)[lax.axis_index("seq")]
    rows = []
    for slot in range(3):
        rows.append(jnp.where(slot_of[0] == slot, got[0], jnp.where(slot_of[1] == slot, got[1], got[2])))
    return jnp.concatenate(rows, axis=0)


def stored_rows(pair_tile, count):
    routes, slots = pair_routes(count)
    width = pair_tile.shape[0] // 3
    slot_of = jnp.asarray(slots, jnp.int32)[lax.axis_index("seq")]
    parts = [pair_tile[s * width : (s + 1) * width] for s in range(3)]
    back = []
    for piece in range(3):
        slot = slot_of[piece]
        chosen = jnp.where(slot == 0, parts[0], jnp.where(slot == 1, parts[1], parts[2]))
        back.append(lax.ppermute(chosen, "seq", [(target, source) for source, target in routes[piece]]))
    return jnp.concatenate(back, axis=0)


def chip_routes(dp, seq):
    chips = seq // 2

    def flat(move):
        return [(d * seq + s, move(d, s)) for d in range(dp) for s in range(seq)]

    def along_z(step):
        return flat(lambda d, s: d * seq + 2 * ((s // 2 + step) % chips) + s % 2)

    return {
        "x": flat(lambda d, s: (d ^ 1) * seq + s),
        "y": flat(lambda d, s: (d ^ 2) * seq + s),
        "xy": flat(lambda d, s: (d ^ 3) * seq + s),
        "core": flat(lambda d, s: d * seq + (s ^ 1)),
        "z": [along_z(step) for step in range(1, chips)],
    }


def send(value, route):
    return lax.ppermute(value, ("dp", "seq"), route)


def gather_column(tile, routes):
    return jnp.stack([tile] + [send(tile, route) for route in routes["z"]])


def gather_near(column, route):
    return jnp.stack([column, send(column, route)])


GELU_C = math.sqrt(2.0 / math.pi)


def gelu_parts(value):
    square = value * value
    slope = jnp.tanh(GELU_C * value * (1.0 + 0.044715 * square))
    low = 0.5 * (1.0 + slope)
    derivative = low + 0.5 * value * (1.0 - slope * slope) * (GELU_C * (1.0 + 3 * 0.044715 * square))
    return value * low, derivative


def lanes(parts):
    return jnp.concatenate(parts, axis=1)


def stay_order(value, first, second):
    return (value // second) % 2 + 2 * ((value // first) % 2)


def middle_kernel(
    place_ref, att_ref, stream_ref, low_ref, turned_low_ref, scale_ref, shift_ref,
    up_0, up_1, up_2, up_3, down_0, down_1, down_2, down_3,
    layer_ref, grad_mid_ref, grad_att_a_ref, grad_att_b_ref, sums_ref, down_own_out, down_other_out, up_own_out, up_other_out,
    up_w, down_w, out_w, normed_ref, turned_ref, sorted_ref, middle_ref, out_acc,
    down_own, down_other, up_own, up_other, up_sem, down_sem, out_sem, send_sem, *, dp, seq,
):
    dp_at, chip_at, core_at = place_ref[0], place_ref[1], place_ref[2]
    chips = seq // 2
    up_rows, up_cols = up_0.shape[2], up_0.shape[3]
    cols = down_0.shape[3]
    width = stream_ref.shape[1]
    out_rows = width // dp
    down_rows = down_0.shape[2] - out_rows

    def copies(name):
        made = []
        pieces, masks = ((up_0, up_1, up_2, up_3), (1, 2)) if name == "up" else ((down_0, down_1, down_2, down_3), (2, 1))
        for part in range(4):
            core = core_at if part < 2 else 1 - core_at
            for step in range(2):
                mask = (masks[1] if part % 2 else 0) ^ (masks[0] if step else 0)
                row = jnp.bitwise_xor(dp_at, mask)
                for back in range(chips):
                    block = 2 * lax.rem(chip_at + chips - back, chips) + core
                    column = pl.ds(pl.multiple_of(block * cols, cols), cols)
                    source, at = pieces[part].at[step, back], (part * 2 + step) * chips + back
                    if name == "up":
                        target = up_w.at[block, pl.ds(pl.multiple_of(row * up_rows, up_rows), up_rows), :]
                        sem = up_sem.at[at]
                    elif name == "down":
                        source = source.at[pl.ds(0, down_rows), :]
                        target = down_w.at[pl.ds(pl.multiple_of(row * down_rows, down_rows), down_rows), column]
                        sem = down_sem.at[at]
                    else:
                        source = source.at[pl.ds(down_rows, out_rows), :]
                        target = out_w.at[pl.ds(pl.multiple_of(row * out_rows, out_rows), out_rows), column]
                        sem = out_sem.at[at]
                    made.append(pltpu.make_async_copy(source, target, sem))
        return made

    for name in ("out", "up", "down"):
        for copy in copies(name):
            copy.start()
    tiles = [
        2 * ahead + (1 - core_at if other else core_at)
        for other in range(2)
        for ahead in range(chips)
    ]
    for at, tile in enumerate(tiles):
        rows = pl.ds(pl.multiple_of(tile * cols, cols), cols)
        sorted_ref[at * cols : (at + 1) * cols, :] = turned_low_ref[rows, :]
    for copy in copies("out"):
        copy.wait()
    middle_ref[...] = stream_ref[...] + dot_tn(att_ref[...], out_w[...])
    grad_acc = grad_mid_ref
    chunk = 128

    @pl.loop(0, stream_ref.shape[0] // chunk)
    def _(index):
        rows = pl.ds(pl.multiple_of(index * chunk, chunk), chunk)
        middle = middle_ref[rows, :]
        inverse = lax.rsqrt(jnp.mean(middle * middle, axis=-1, keepdims=True) + epsilon)
        normed = middle * inverse * (1.0 + scale_ref[...]) + shift_ref[...]
        normed_ref[rows, :] = normed.astype(jnp.bfloat16)
        turned = normed.T.astype(jnp.bfloat16)
        for row in range(dp):
            place = stay_order(jnp.bitwise_xor(dp_at, row), 2, 1)
            turned_ref[pl.ds(pl.multiple_of(place * out_rows, out_rows), out_rows), rows] = turned[
                row * out_rows : (row + 1) * out_rows
            ]
        out_acc[rows, :] = jnp.zeros_like(middle)
        grad_acc[rows, :] = jnp.zeros_like(middle)

    for name in ("up", "down"):
        for copy in copies(name):
            copy.wait()

    def hidden_block(other, up_grads):
        def run(ahead, carry):
            core = 1 - core_at if other else core_at
            block = 2 * ahead + core
            rows = pl.ds(pl.multiple_of(block * up_cols, up_cols), up_cols)
            up_weight, down_weight = up_w[block], down_w[rows, :]
            value, derivative = gelu_parts(dot_nn(normed_ref[...], up_weight))
            hidden = value.astype(jnp.bfloat16)
            out_acc[...] += dot_nn(hidden, down_weight)
            grad_up = (dot_nt(low_ref[...], down_weight) * derivative).astype(jnp.bfloat16)
            grad_acc[...] += dot_nt(grad_up, up_weight)
            for owner in range(dp):
                part = dot_nn(turned_ref[owner * up_rows : (owner + 1) * up_rows, :], grad_up)
                up_grads[owner, ahead] = part.astype(jnp.bfloat16)
            per_owner = down_rows // up_cols
            owner = stay_order(jnp.bitwise_xor(dp_at, block // per_owner), 1, 2)
            at = pl.ds(pl.multiple_of(lax.rem(block, per_owner) * cols, cols), cols)
            for pair in range(chips):
                part = dot_nn(sorted_ref[2 * pair * cols : 2 * (pair + 1) * cols, :], hidden).astype(jnp.bfloat16)
                for tile in range(2):
                    target, place = (down_own, 2 * pair + tile) if pair < chips // 2 else (down_other, 2 * pair + tile - chips)
                    target[owner, place, at, :] = part[tile * cols : (tile + 1) * cols]
            return carry

        lax.fori_loop(0, chips, run, 0, unroll=2)

    hidden_block(1, up_other)
    send_up_other = pltpu.make_async_copy(up_other, up_other_out, send_sem.at[0])
    send_up_other.start()
    hidden_block(0, up_own)
    packed = down_rows * cols // up_cols
    sends = [
        pltpu.make_async_copy(up_own, up_own_out, send_sem.at[1]),
        pltpu.make_async_copy(
            down_other.at[:, :, pl.ds(0, packed), :], down_other_out.at[:, :, pl.ds(0, packed), :], send_sem.at[2]
        ),
        pltpu.make_async_copy(
            down_own.at[:, :, pl.ds(0, packed), :], down_own_out.at[:, :, pl.ds(0, packed), :], send_sem.at[3]
        ),
    ]
    for copy in sends:
        copy.start()
    sums_ref[...] = jnp.zeros_like(sums_ref)

    @pl.loop(0, stream_ref.shape[0] // chunk)
    def _(index):
        rows = pl.ds(pl.multiple_of(index * chunk, chunk), chunk)
        middle = middle_ref[rows, :]
        layer_ref[rows, :] = (middle + out_acc[rows, :]).astype(jnp.bfloat16)
        inverse = lax.rsqrt(jnp.mean(middle * middle, axis=-1, keepdims=True) + epsilon)
        unit = middle * inverse
        grad = grad_acc[rows, :]
        lifted = grad * (1.0 + scale_ref[...])
        sums_ref[0:1, :] += jnp.sum(grad * unit, axis=0, keepdims=True)
        sums_ref[1:2, :] += jnp.sum(grad, axis=0, keepdims=True)
        grad_mid = low_ref[rows, :].astype(jnp.float32) + inverse * (
            lifted - unit * jnp.mean(lifted * unit, axis=-1, keepdims=True)
        )
        grad_mid_ref[rows, :] = grad_mid
        normed_ref[rows, :] = grad_mid.astype(jnp.bfloat16)

    grad_att = dot_nt(out_w[...], normed_ref[...]).astype(jnp.bfloat16)
    for target in range(seq):
        grad_att_a_ref[target] = grad_att[target * PAIR : target * PAIR + HD]
        grad_att_b_ref[target] = grad_att[target * PAIR + HD : (target + 1) * PAIR]
    grads = lanes([normed_ref[:, pl.ds(pl.multiple_of(tile * cols, cols), cols)] for tile in tiles])
    per_row = up_cols // cols
    folded = out_rows // per_row
    for row in range(dp):
        owner = stay_order(jnp.bitwise_xor(dp_at, row), 1, 2)
        product = dot_nn(att_ref[row * out_rows : (row + 1) * out_rows, :], grads).astype(jnp.bfloat16)
        for at in range(seq):
            part = product[:, at * cols : (at + 1) * cols]
            part = lanes([part[i * folded : (i + 1) * folded] for i in range(per_row)])
            target = down_own if at < chips else down_other
            target[owner, at % chips, packed : packed + folded, :] = part
    last = [
        pltpu.make_async_copy(
            down_other.at[:, :, pl.ds(packed, folded), :], down_other_out.at[:, :, pl.ds(packed, folded), :], send_sem.at[4]
        ),
        pltpu.make_async_copy(
            down_own.at[:, :, pl.ds(packed, folded), :], down_own_out.at[:, :, pl.ds(packed, folded), :], send_sem.at[5]
        ),
    ]
    for copy in last:
        copy.start()
    for copy in [send_up_other] + sends + last:
        copy.wait()


def middle_block(place, attended, stream, grad_low, grad_low_turned, scale, shift, up_pieces, down_pieces, dp, seq):
    frames, width = stream.shape
    tile_cols = up_pieces[0].shape[3]
    hidden = tile_cols * seq
    chips = seq // 2
    packed = hidden // dp * (width // seq) // tile_cols + width // dp * (width // seq) // tile_cols
    whole = pl.BlockSpec(memory_space=pltpu.VMEM)
    anywhere = pl.BlockSpec(memory_space=pl.ANY)
    half, full = jnp.bfloat16, jnp.float32
    down_shape, up_shape = (dp, chips, packed, tile_cols), (dp, chips, width // dp, tile_cols)
    return pl.pallas_call(
        partial(middle_kernel, dp=dp, seq=seq),
        in_specs=[pl.BlockSpec(memory_space=pltpu.SMEM)] + [whole] * 6 + [anywhere] * 8,
        out_specs=[whole] * 5 + [anywhere] * 4,
        out_shape=[
            jax.ShapeDtypeStruct((frames, width), half),
            jax.ShapeDtypeStruct((frames, width), full),
            jax.ShapeDtypeStruct((seq, HD, frames), half),
            jax.ShapeDtypeStruct((seq, HD, frames), half),
            jax.ShapeDtypeStruct((2, width), full),
            jax.ShapeDtypeStruct(down_shape, half),
            jax.ShapeDtypeStruct(down_shape, half),
            jax.ShapeDtypeStruct(up_shape, half),
            jax.ShapeDtypeStruct(up_shape, half),
        ],
        scratch_shapes=[
            pltpu.VMEM((seq, width, tile_cols), half),
            pltpu.VMEM((hidden, width), half),
            pltpu.VMEM((width, width), half),
            pltpu.VMEM((frames, width), half),
            pltpu.VMEM((width, frames), half),
            pltpu.VMEM((width, frames), half),
            pltpu.VMEM((frames, width), full),
            pltpu.VMEM((frames, width), full),
            pltpu.VMEM(down_shape, half),
            pltpu.VMEM(down_shape, half),
            pltpu.VMEM(up_shape, half),
            pltpu.VMEM(up_shape, half),
            pltpu.SemaphoreType.DMA((dp * seq,)),
            pltpu.SemaphoreType.DMA((dp * seq,)),
            pltpu.SemaphoreType.DMA((dp * seq,)),
            pltpu.SemaphoreType.DMA((6,)),
        ],
        compiler_params=pltpu.CompilerParams(vmem_limit_bytes=62 << 20),
        cost_estimate=pl.CostEstimate(
            flops=12 * frames * width * hidden + 6 * frames * width * width,
            bytes_accessed=8 * hidden * width + 24 * frames * width,
            transcendentals=frames * hidden,
        ),
        name="middle_block",
    )(place, attended, stream, grad_low, grad_low_turned, scale, shift, *up_pieces, *down_pieces)


def entry_kernel(main_ref, side_ref, weight_ref, scale_ref, shift_ref, stream_ref, normed_ref, *, dp, seq):
    row = pl.program_id(0)

    @pl.when(row == 0)
    def _():
        stream_ref[...] = jnp.zeros_like(stream_ref)

    operand = jnp.where(row < dp // 2, main_ref[...], side_ref[...])
    stream_ref[...] += dot_nn(operand, lanes([weight_ref[s] for s in range(seq)]))

    @pl.when(row == dp - 1)
    def _():
        stream = stream_ref[...]
        inverse = lax.rsqrt(jnp.mean(stream * stream, axis=-1, keepdims=True) + epsilon)
        normed_ref[...] = (stream * inverse * (1.0 + scale_ref[...]) + shift_ref[...]).astype(jnp.bfloat16)


def entry_block(main, side, skip_tiles, scale, shift, dp, seq):
    frames, width = main.shape
    rows, columns = skip_tiles.shape[1:]
    fixed = pl.BlockSpec((1, width), lambda i: (0, 0))
    return pl.pallas_call(
        partial(entry_kernel, dp=dp, seq=seq),
        grid=(dp,),
        in_specs=[
            pl.BlockSpec((frames, rows), lambda i: (0, jnp.minimum(i, dp // 2 - 1))),
            pl.BlockSpec((frames, rows), lambda i: (0, jnp.maximum(i - dp // 2, 0))),
            pl.BlockSpec((seq, rows, columns), lambda i: (i, 0, 0)),
            fixed,
            fixed,
        ],
        out_specs=[pl.BlockSpec((frames, width), lambda i: (0, 0))] * 2,
        out_shape=[
            jax.ShapeDtypeStruct((frames, width), jnp.float32),
            jax.ShapeDtypeStruct((frames, width), jnp.bfloat16),
        ],
        compiler_params=pltpu.CompilerParams(vmem_limit_bytes=32 << 20),
        cost_estimate=pl.CostEstimate(
            flops=4 * frames * width * width, bytes_accessed=14 * frames * width, transcendentals=0
        ),
        name="entry_block",
    )(main, side, skip_tiles, scale, shift)


def head_product(head, head_ref, pair_ref, dp, seq):
    parts = [head_ref[s, piece * HD : (piece + 1) * HD] for s in range(seq) for piece in range(3)]
    projected = jnp.concatenate(parts, axis=0).T
    for row in range(dp):
        weight = jnp.concatenate(
            [
                pair_ref[row * seq + s, piece * PAIR + head * HD : piece * PAIR + (head + 1) * HD]
                for s in range(seq)
                for piece in range(3)
            ],
            axis=0,
        )
        yield row, dot_nn(projected, weight)


def first_head_kernel(head_ref, pair_ref, out_ref, *, dp, seq):
    rows = pair_ref.shape[2]
    for row, product in head_product(0, head_ref, pair_ref, dp, seq):
        out_ref[:, row * rows : (row + 1) * rows] = product


def first_head(head_a, pair_tiles, dp, seq):
    frames, width = head_a.shape[2], pair_tiles.shape[2] * dp
    whole = pl.BlockSpec(memory_space=pltpu.VMEM)
    return pl.pallas_call(
        partial(first_head_kernel, dp=dp, seq=seq),
        in_specs=[whole] * 2,
        out_specs=whole,
        out_shape=jax.ShapeDtypeStruct((frames, width), jnp.float32),
        compiler_params=pltpu.CompilerParams(vmem_limit_bytes=32 << 20),
        cost_estimate=pl.CostEstimate(
            flops=3 * frames * width * width, bytes_accessed=7 * frames * width + 6 * width * width, transcendentals=0
        ),
        name="first_head",
    )(head_a, pair_tiles)


def exit_kernel(
    partial_ref, head_ref, pair_ref, stream_ref, grad_mid_ref, scale_ref, grad_ref, turned_ref, sums_ref, normed_ref,
    *, dp, seq,
):
    rows = pair_ref.shape[2]
    for row, product in head_product(1, head_ref, pair_ref, dp, seq):
        columns = slice(row * rows, (row + 1) * rows)
        normed_ref[:, columns] = product + partial_ref[:, columns]
    sums_ref[...] = jnp.zeros_like(sums_ref)
    chunk = 128

    @pl.loop(0, stream_ref.shape[0] // chunk)
    def _(index):
        at = pl.ds(pl.multiple_of(index * chunk, chunk), chunk)
        grad, stream = normed_ref[at, :], stream_ref[at, :]
        inverse = lax.rsqrt(jnp.mean(stream * stream, axis=-1, keepdims=True) + epsilon)
        unit = stream * inverse
        lifted = grad * (1.0 + scale_ref[...])
        sums_ref[0:1, :] += jnp.sum(grad * unit, axis=0, keepdims=True)
        sums_ref[1:2, :] += jnp.sum(grad, axis=0, keepdims=True)
        grad_stream = grad_mid_ref[at, :] + inverse * (
            lifted - unit * jnp.mean(lifted * unit, axis=-1, keepdims=True)
        )
        grad_ref[at, :] = grad_stream.astype(jnp.bfloat16)
        turned_ref[:, at] = grad_stream.T.astype(jnp.bfloat16)


def exit_block(first, head_b, pair_tiles, stream, grad_mid, scale, dp, seq):
    frames, width = stream.shape
    whole = pl.BlockSpec(memory_space=pltpu.VMEM)
    return pl.pallas_call(
        partial(exit_kernel, dp=dp, seq=seq),
        in_specs=[whole] * 6,
        out_specs=[whole] * 3,
        out_shape=[
            jax.ShapeDtypeStruct((frames, width), jnp.bfloat16),
            jax.ShapeDtypeStruct((width, frames), jnp.bfloat16),
            jax.ShapeDtypeStruct((2, width), jnp.float32),
        ],
        scratch_shapes=[pltpu.VMEM((frames, width), jnp.float32)],
        compiler_params=pltpu.CompilerParams(vmem_limit_bytes=60 << 20),
        cost_estimate=pl.CostEstimate(
            flops=3 * frames * width * width, bytes_accessed=18 * frames * width + 6 * width * width, transcendentals=0
        ),
        name="exit_block",
    )(first, head_b, pair_tiles, stream, grad_mid, scale)


def joined_kernel(grad_ref, weight_ref, main_ref, side_ref, *, dp, seq):
    row = pl.program_id(0)
    grad = dot_nt(grad_ref[...], lanes([weight_ref[s] for s in range(seq)]))

    @pl.when(row < dp // 2)
    def _():
        main_ref[...] = grad

    @pl.when(row >= dp // 2)
    def _():
        side_ref[...] = grad


def joined_grads(grad_stream, skip_tiles, dp, seq):
    frames, width = grad_stream.shape
    rows, columns = skip_tiles.shape[1:]
    out = jax.ShapeDtypeStruct((frames, width), jnp.float32)
    return pl.pallas_call(
        partial(joined_kernel, dp=dp, seq=seq),
        grid=(dp,),
        in_specs=[
            pl.BlockSpec((frames, width), lambda i: (0, 0)),
            pl.BlockSpec((seq, rows, columns), lambda i: (i, 0, 0)),
        ],
        out_specs=[
            pl.BlockSpec((frames, rows), lambda i: (0, jnp.minimum(i, dp // 2 - 1))),
            pl.BlockSpec((frames, rows), lambda i: (0, jnp.maximum(i - dp // 2, 0))),
        ],
        out_shape=[out, out],
        compiler_params=pltpu.CompilerParams(vmem_limit_bytes=32 << 20),
        cost_estimate=pl.CostEstimate(
            flops=4 * frames * width * width, bytes_accessed=14 * frames * width, transcendentals=0
        ),
        name="joined_grads",
    )(grad_stream, skip_tiles)


def along_chips(place_ref, chips, other, block):
    core = 1 - place_ref[2] if other else place_ref[2]
    return [pl.multiple_of((2 * chip + core) * block, block) for chip in range(chips)]


def turned_parts(place_ref, left_ref, right_ref, chips, seq, other):
    block = left_ref.shape[0] // seq
    starts = along_chips(place_ref, chips, other, block)
    left = jnp.concatenate([left_ref[pl.ds(start, block), :] for start in starts], axis=0)
    product = dot_nn(left, right_ref[...])
    return [product[ahead * block : (ahead + 1) * block] for ahead in range(chips)]


def plain_parts(place_ref, left_ref, right_ref, chips, seq, other):
    block = right_ref.shape[1] // seq
    starts = along_chips(place_ref, chips, other, block)
    product = dot_nn(left_ref[...], lanes([right_ref[:, pl.ds(start, block)] for start in starts]))
    return [product[:, ahead * block : (ahead + 1) * block] for ahead in range(chips)]


def fold_columns(part, width):
    return jnp.concatenate([part[:, at : at + width] for at in range(0, part.shape[1], width)], axis=0)


def fold_rows(part, width):
    rows = part.shape[0] * part.shape[1] // width
    return lanes([part[at : at + rows] for at in range(0, part.shape[0], rows)])


def blocks_kernel(place_ref, *refs, kinds, other, seq, width):
    chips = seq // 2
    step = pl.program_id(0)
    operands, outs = refs[: 2 * len(kinds)], refs[2 * len(kinds) :]
    packed = [[] for _ in range(chips)]
    for at, kind in enumerate(kinds):
        left_ref, right_ref = operands[2 * at], operands[2 * at + 1]
        if kind == "turned":
            parts = [fold_columns(part, width) for part in turned_parts(place_ref, left_ref, right_ref, chips, seq, other)]
        else:
            parts = plain_parts(place_ref, left_ref, right_ref, chips, seq, other)
            parts = [fold_rows(part, width) if part.shape[1] < width else part for part in parts]
        for ahead in range(chips):
            packed[ahead].append(parts[ahead])
    if not other:
        arrived_ref, outs = outs[0], outs[1:]
    for ahead in range(chips):
        row = 0
        for part in packed[ahead]:
            rows = slice(row, row + part.shape[0])
            row += part.shape[0]
            if other:
                outs[0][0, ahead, rows, :] = part.astype(jnp.bfloat16)
            else:
                low = (part + arrived_ref[0, ahead, rows, :].astype(jnp.float32)).astype(jnp.bfloat16)

                @pl.when(step < 2)
                def _(low=low, ahead=ahead, rows=rows):
                    outs[0][0, ahead, rows, :] = low

                @pl.when(step >= 2)
                def _(low=low, ahead=ahead, rows=rows):
                    outs[1][0, ahead, rows, :] = low


def grad_blocks(place, products, masks, seq, width, arrived=None, part=(0, 1)):
    first, second = masks
    chips, dp = seq // 2, 4

    def owner(i, place):
        return jnp.bitwise_xor(place[0], (i % 2) * second + (i // 2) * first)

    specs, operands, kinds, rows, flops = [], [], [], 0, 0
    for kind, left, right in products:
        depth = left.shape[1]
        if kind == "turned":
            columns = right.shape[1] // (dp * part[1])
            shape = (left.shape[0] // seq, columns)
            specs += [
                pl.BlockSpec(left.shape, lambda i, place: (0, 0)),
                pl.BlockSpec((depth, columns), lambda i, place: (0, owner(i, place) * part[1] + part[0])),
            ]
        else:
            shape = (left.shape[0] // dp, right.shape[1] // seq)
            specs += [
                pl.BlockSpec((shape[0], depth), lambda i, place: (owner(i, place), 0)),
                pl.BlockSpec(right.shape, lambda i, place: (0, 0)),
            ]
        operands += [left, right]
        kinds.append(kind)
        rows += shape[0] * shape[1] // width
        flops += 2 * dp * chips * shape[0] * shape[1] * depth
    other = arrived is None
    one = (1, chips, rows, width)
    if other:
        outs, count = [pl.BlockSpec(one, lambda i, place: (i, 0, 0, 0))], 4
    else:
        outs = [
            pl.BlockSpec(one, lambda i, place: (jnp.minimum(i, 1), 0, 0, 0)),
            pl.BlockSpec(one, lambda i, place: (jnp.maximum(i - 2, 0), 0, 0, 0)),
        ]
        count = 2
        specs.append(pl.BlockSpec(one, lambda i, place: (i, 0, 0, 0)))
        operands.append(arrived)
    return pl.pallas_call(
        partial(blocks_kernel, kinds=tuple(kinds), other=other, seq=seq, width=width),
        grid_spec=pltpu.PrefetchScalarGridSpec(num_scalar_prefetch=1, grid=(4,), in_specs=specs, out_specs=outs),
        out_shape=[jax.ShapeDtypeStruct((count, chips, rows, width), jnp.bfloat16)] * len(outs),
        compiler_params=pltpu.CompilerParams(vmem_limit_bytes=48 << 20),
        cost_estimate=pl.CostEstimate(
            flops=flops, bytes_accessed=8 * rows * width * chips * (1 if other else 2) + flops // 512, transcendentals=0
        ),
        name="grad_blocks",
    )(place, *operands)


AXIS_MASK = {"x": 1, "y": 2}


def wide(value):
    return value.astype(jnp.float32)


def low(value):
    return value.astype(jnp.bfloat16)


def dp_gather(tile, routes, dp):
    at = lax.axis_index("dp")
    columns = tile.shape[1]
    full = jnp.zeros((tile.shape[0], dp * columns), tile.dtype)
    full = lax.dynamic_update_slice_in_dim(full, tile, at * columns, 1)
    for mask, route in ((1, routes["x"]), (2, routes["y"]), (3, routes["xy"])):
        full = lax.dynamic_update_slice_in_dim(full, send(tile, route), jnp.bitwise_xor(at, mask) * columns, 1)
    return full


def chips_exchange(value, seq):
    groups = [[core + 2 * chip for chip in range(seq // 2)] for core in range(2)]
    return lax.all_to_all(value, "seq", 0, 0, axis_index_groups=groups)


def local_paired(
    inputs, skip_input, time_embed, segment_ids, span_start, span_length, cotangent,
    skip_weight, ada_weight, qkv_weight, out_weight, up_weight, down_weight,
):
    seq = lax.axis_size("seq")
    dp = lax.axis_size("dp")
    frames, width = inputs.shape[1], inputs.shape[2]
    length = segment_ids.shape[1]
    segments = segment_ids[0]
    end_a = jnp.sum((segments < 1).astype(jnp.int32))
    end_b = jnp.sum((segments < 2).astype(jnp.int32))
    ends = jnp.stack([end_a, end_b])
    firsts = jnp.where(segments == 0, 0, jnp.where(segments == 1, end_a, end_b))
    position = jnp.arange(length, dtype=jnp.int32) - firsts
    half = HD // 2
    frequency = jnp.exp(-math.log(10000.0) * jnp.arange(half, dtype=jnp.float32) / half)
    angles = frequency[:, None] * position.astype(jnp.float32)[None, :]
    cos_all, sin_all = jnp.cos(angles), jnp.sin(angles)
    base = lax.axis_index("seq") * frames
    local_segments = lax.dynamic_slice_in_dim(segments, base, frames, 0)
    local_position = lax.dynamic_slice_in_dim(position, base, frames, 0)
    starts, lengths = span_start[0], span_length[0]

    def pick(table):
        return jnp.where(local_segments == 0, table[0], jnp.where(local_segments == 1, table[1], table[2]))

    span_begin = pick(starts)
    inside = jnp.logical_and(local_position >= span_begin, local_position < span_begin + pick(lengths))
    grad_low = jnp.where(inside[:, None], cotangent[0], jnp.zeros((), jnp.bfloat16))
    routes = chip_routes(dp, seq)
    seq_at = lax.axis_index("seq")
    place = jnp.stack([lax.axis_index("dp"), seq_at // 2, seq_at % 2]).astype(jnp.int32)
    up_column = gather_column(up_weight, routes)
    down_column = gather_column(jnp.concatenate([down_weight, out_weight]), routes)
    embed_all = lax.all_gather(time_embed, "dp", axis=0, tiled=True)
    embed_rows = width // dp
    embed_part = lax.dynamic_slice_in_dim(embed_all, lax.axis_index("dp") * embed_rows, embed_rows, 1)
    modulation_part = jnp.dot(embed_part, ada_weight, preferred_element_type=jnp.float32)
    modulation_part = lax.psum_scatter(modulation_part, "dp", scatter_dimension=0, tiled=True)
    modulation = lax.all_gather(modulation_part, "seq", axis=1, tiled=True)
    scale_one = modulation[:, :width]
    shift_one = modulation[:, width : 2 * width]
    scale_two = modulation[:, 2 * width : 3 * width]
    shift_two = modulation[:, 3 * width :]

    skip_tiles = lax.all_gather(skip_weight, ("dp", "seq"), axis=0)
    pair_tile = own_pair_rows(qkv_weight.T, seq)
    skip_tiles, up_column, down_column, cos_all, sin_all, ends, grad_low, grad_low_turned, place = lax.optimization_barrier(
        (skip_tiles, up_column, down_column, cos_all, sin_all, ends, grad_low, grad_low.T, place)
    )
    stream, normed_one = entry_block(inputs[0], skip_input[0], skip_tiles, scale_one, shift_one, dp, seq)
    normed_all = lax.all_gather(normed_one, "seq", axis=0)
    up_near = gather_near(up_column, routes["x"])
    down_near = gather_near(down_column, routes["y"])
    pair_weight = dp_gather(pair_tile, routes, dp)
    up_near, down_near, pair_weight = lax.optimization_barrier((up_near, down_near, pair_weight))
    up_far, down_far = send(up_near, routes["y"]), send(down_near, routes["x"])
    normed_all, up_near, down_near = lax.optimization_barrier((normed_all, up_near, down_near))
    up_near_core, down_near_core = send(up_near, routes["core"]), send(down_near, routes["core"])
    qt, kt, vt, keys, values, norms = project_pair(normed_all, pair_weight, cos_all, sin_all)
    attended_pair, attended_wide, total = attend_pair(ends, qt, keys, vt, norms)
    attended_pair, up_far, down_far = lax.optimization_barrier((attended_pair, up_far, down_far))
    up_pieces = (up_near, up_far, up_near_core, send(up_far, routes["core"]))
    down_pieces = (down_near, down_far, down_near_core, send(down_far, routes["core"]))
    attended = lax.all_to_all(attended_pair, "seq", 0, 0).reshape(width, frames)
    attended, pair_tile, far_up, far_down = lax.optimization_barrier(
        (attended, pair_tile, up_pieces[3], down_pieces[3])
    )
    up_pieces, down_pieces = up_pieces[:3] + (far_up,), down_pieces[:3] + (far_down,)
    pair_tiles = lax.all_gather(pair_tile, ("dp", "seq"), axis=0)
    layer_output, grad_middle, grad_head_a, grad_head_b, sums_two, down_own, down_other, up_own, up_other = middle_block(
        place, attended, stream, grad_low, grad_low_turned, scale_two, shift_two, up_pieces, down_pieces, dp, seq
    )
    grad_head_a = lax.all_to_all(grad_head_a, "seq", 0, 0)
    down_other, up_other = send(down_other, routes["core"]), send(up_other, routes["core"])
    down_half, up_half = down_own.shape[2] // 2, up_own.shape[2] // 2

    def leaves(own, other, rows):
        return low(wide(own[2:, :, rows]) + wide(other[2:, :, rows]))

    away = (
        leaves(down_own, down_other, slice(0, down_half)),
        leaves(down_own, down_other, slice(down_half, None)),
        leaves(up_own, up_other, slice(0, up_half)),
        leaves(up_own, up_other, slice(up_half, None)),
    )
    grad_head_b, *away = lax.optimization_barrier((grad_head_b, *away))
    grad_head_b = lax.all_to_all(grad_head_b, "seq", 0, 0)
    saved = (attended_wide, total, keys, values, kt, cos_all, sin_all)
    grad_head_a, pair_tiles, *away = lax.optimization_barrier((grad_head_a, pair_tiles, *away))
    down_got = [send(away[0], routes["x"]), send(away[1], routes["x"])]
    up_got = [send(away[2], routes["y"]), send(away[3], routes["y"])]
    back_a = attend_head_back(0, ends, qt, grad_head_a, *saved)
    local_a = lax.all_to_all(back_a, "seq", 0, 0)
    back_a, grad_head_b, down_got[0], up_got[0] = lax.optimization_barrier(
        (back_a, grad_head_b, down_got[0], up_got[0])
    )
    back_b = attend_head_back(1, ends, qt, grad_head_b, *saved)
    back_b, local_a = lax.optimization_barrier((back_b, local_a))
    local_b = lax.all_to_all(back_b, "seq", 0, 0)

    def stays(own, other, got, at):
        return wide(own[at]) + wide(other[at]) + wide(got[at])

    back_a, back_b, down_got[1], up_got[1] = lax.optimization_barrier((back_a, back_b, down_got[1], up_got[1]))
    down_got, up_got = jnp.concatenate(down_got, axis=2), jnp.concatenate(up_got, axis=2)
    down_low, up_low = low(stays(down_own, down_other, down_got, 1)), low(stays(up_own, up_other, up_got, 1))
    down_low, up_low, back_a, back_b = lax.optimization_barrier((down_low, up_low, back_a, back_b))
    down_back, up_back = send(down_low, routes["y"]), send(up_low, routes["x"])
    parts = [part[:, at : at + HD] for at in range(0, 3 * HD, HD) for part in (back_a, back_b)]
    grad_projected = jnp.concatenate(parts, axis=1)
    grad_pair_weight = jnp.einsum(
        "icf,ifd->cd", grad_projected, normed_all, preferred_element_type=jnp.float32
    ).astype(jnp.bfloat16)
    local_b, grad_pair_weight = lax.optimization_barrier((local_b, grad_pair_weight))
    grad_stream, grad_stream_turned, sums_one = exit_block(
        first_head(local_a, pair_tiles, dp, seq), local_b, pair_tiles, stream, grad_middle, scale_one, dp, seq
    )
    joined = jnp.concatenate([inputs[0], skip_input[0]], axis=-1)
    chips, chip_at, core_at = seq // 2, seq_at // 2, seq_at % 2
    grad_modulation = jnp.concatenate([sums_one[0], sums_one[1], sums_two[0], sums_two[1]]).reshape(chips, 2, -1)
    kept = lax.dynamic_index_in_dim(grad_modulation, core_at, 1, keepdims=False)
    kept = kept + send(lax.dynamic_index_in_dim(grad_modulation, 1 - core_at, 1, keepdims=False), routes["core"])
    column_sum = lax.dynamic_index_in_dim(kept, chip_at, 0)
    for ahead, route in enumerate(routes["z"]):
        piece = lax.dynamic_index_in_dim(kept, (chip_at + ahead + 1) % chips, 0)
        column_sum = column_sum + send(piece, route)
    half_tile = skip_weight.shape[0] // 2
    at = lax.axis_index("dp")
    half_pair = 3 * PAIR // 2
    wide_tile = up_weight.shape[1]
    turned = [("turned", grad_stream_turned, joined)]
    order = (("x", "y"), ("y", "x"))

    def skip_blocks(part, arrived):
        masks = tuple(AXIS_MASK[axis] for axis in order[part])
        return grad_blocks(place, turned, masks, seq, half_tile, arrived, (part, 2))

    leaving = [skip_blocks(part, None)[0] for part in range(2)]
    *leaving, down_back, up_back = lax.optimization_barrier((*leaving, down_back, up_back))
    arrived = [send(part, routes["core"]) for part in leaving]
    down_total = stays(down_own, down_other, down_got, 0) + wide(down_back)
    up_total = stays(up_own, up_other, up_got, 0) + wide(up_back)
    mlp_low = jnp.concatenate([low(down_total), low(up_total)], axis=1)
    column_sum, mlp_low = lax.optimization_barrier((column_sum, mlp_low))
    mlp_got = chips_exchange(mlp_low, seq)
    skip_parts = []
    for part, (first, second) in enumerate(order):
        keep, away = skip_blocks(part, arrived[part])
        pair_rows = grad_pair_weight[part * half_pair : (part + 1) * half_pair]

        def pair_block(mask):
            return lax.dynamic_slice_in_dim(pair_rows, jnp.bitwise_xor(at, mask) * half_tile, half_tile, 1)

        near, far = AXIS_MASK[first], AXIS_MASK[second]
        keep = jnp.concatenate([keep.reshape(2, -1, half_tile), jnp.stack([pair_block(0), pair_block(far)])], axis=1)
        away = jnp.concatenate(
            [away.reshape(2, -1, half_tile), jnp.stack([pair_block(near), pair_block(near ^ far)])], axis=1
        )
        skip_parts.append([keep, away, first, second])
    skip_parts[0][1], skip_parts[1][1], grad_stream, column_sum = lax.optimization_barrier(
        (skip_parts[0][1], skip_parts[1][1], grad_stream, column_sum)
    )
    skip_parts = [(keep, send(away, routes[first]), routes[second]) for keep, away, first, second in skip_parts]
    grad_main, grad_side = joined_grads(grad_stream, skip_tiles, dp, seq)
    got_a, got_b, grad_main, column_sum = lax.optimization_barrier(
        (skip_parts[0][1], skip_parts[1][1], grad_main, column_sum)
    )
    skip_parts = [(skip_parts[0][0], got_a, skip_parts[0][2]), (skip_parts[1][0], got_b, skip_parts[1][2])]
    grad_modulation = jnp.concatenate([column_sum, send(column_sum, routes["x"])])
    grad_modulation = jnp.concatenate([grad_modulation, send(grad_modulation, routes["y"])])
    skip_low, pair_sums = [], []
    skip_rows = chips * (width // seq)
    for keep, got, route in skip_parts:
        back = send(low(wide(keep[1]) + wide(got[1])), route)
        total_part = wide(keep[0]) + wide(got[0]) + wide(back)
        pair_sums.append(total_part[skip_rows:])
        skip_low.append(low(total_part[:skip_rows].reshape(chips, width // seq, half_tile)))
    skip_low = jnp.concatenate(skip_low, axis=2)
    skip_low, mlp_got = lax.optimization_barrier((skip_low, mlp_got))
    skip_tile = jnp.sum(wide(chips_exchange(skip_low, seq)), axis=0).T
    qkv_tile = wide(stored_rows(low(jnp.concatenate(pair_sums)), seq)).T

    mlp_tile = jnp.sum(wide(mlp_got), axis=0)
    columns = width // seq
    fold = down_weight.shape[0] // wide_tile
    down_tile = lanes([mlp_tile[i * columns : (i + 1) * columns] for i in range(fold)]).T
    out_tile = mlp_tile[fold * columns : down_total.shape[1]]
    out_tile = jnp.concatenate([out_tile[:, i * columns : (i + 1) * columns] for i in range(wide_tile // columns)])
    up_tile = mlp_tile[down_total.shape[1] :]
    embed_part = jnp.concatenate(
        [lax.dynamic_index_in_dim(embed_part, jnp.bitwise_xor(at, mask), 0) for mask in range(dp)]
    )
    ada_tile = lax.dot_general(
        embed_part.astype(jnp.float32), grad_modulation, (((0,), (0,)), ((), ())),
        precision=lax.Precision.HIGHEST,
    )
    return (
        layer_output[None],
        grad_main[None],
        grad_side[None],
        skip_tile,
        ada_tile,
        qkv_tile,
        out_tile,
        up_tile,
        down_tile,
    )


def solution(mesh):
    in_specs = (
        P("dp", "seq", None),
        P("dp", "seq", None),
        P("dp", None),
        P("dp", None),
        P("dp", None),
        P("dp", None),
        P("dp", "seq", None),
        P("dp", "seq"),
        P("dp", "seq"),
        P("dp", "seq"),
        P("dp", "seq"),
        P("dp", "seq"),
        P("dp", "seq"),
    )
    out_specs = (
        P("dp", "seq", None),
        P("dp", "seq", None),
        P("dp", "seq", None),
        P("dp", "seq"),
        P("dp", "seq"),
        P("dp", "seq"),
        P("dp", "seq"),
        P("dp", "seq"),
        P("dp", "seq"),
    )
    seq_size = mesh.shape["seq"]
    paired = H == 2 * seq_size and seq_size % 3 != 0 and mesh.shape["dp"] == 4
    body = local_paired if paired else local_general
    return jax.shard_map(body, mesh=mesh, in_specs=in_specs, out_specs=out_specs, check_vma=False)
```

```python
from functools import partial
import math

import jax
import jax.numpy as jnp
from jax import lax
from jax.experimental import pallas as pl
from jax.experimental.pallas import tpu as pltpu
from jax.sharding import PartitionSpec as P

H = 16
HD = 64
UTT = 3
HG = 8


epsilon = 1e-06
masked_score = -1e30


def ada_norm(stream, scale_part, shift_part):
    inverse = lax.rsqrt(jnp.mean(stream * stream, axis=-1, keepdims=True) + epsilon)
    return stream * inverse * (1.0 + scale_part) + shift_part


def rotate(tensor, cosine, sine_part):
    half_width = tensor.shape[-1] // 2
    lower_half = tensor[..., :half_width]
    upper_half = tensor[..., half_width:]
    cos_wide = cosine[..., None, :]
    sin_wide = sine_part[..., None, :]
    return jnp.concatenate(
        [
            lower_half * cos_wide - upper_half * sin_wide,
            lower_half * sin_wide + upper_half * cos_wide,
        ],
        axis=-1,
    )


def rotary_tables(position, half_width):
    frequency = jnp.exp(-math.log(10000.0) * jnp.arange(half_width, dtype=jnp.float32) / half_width)
    angles = position.astype(jnp.float32)[..., None] * frequency
    return (jnp.cos(angles), jnp.sin(angles))


def gather_weights(skip_tile, ada_tile, qkv_tile, out_tile, up_tile, down_tile):
    row_full = (
        lax.all_gather(skip_tile, "dp", axis=0, tiled=True),
        lax.all_gather(ada_tile, "dp", axis=0, tiled=True),
        lax.all_gather(qkv_tile, "dp", axis=0, tiled=True),
        lax.all_gather(out_tile, "dp", axis=0, tiled=True),
        lax.all_gather(up_tile, "dp", axis=0, tiled=True),
        lax.all_gather(down_tile, "dp", axis=0, tiled=True),
    )
    return (
        lax.all_gather(row_full[0], "seq", axis=1, tiled=True),
        lax.all_gather(row_full[1], "seq", axis=1, tiled=True),
        lax.all_gather(row_full[2], "seq", axis=1, tiled=True),
        lax.all_gather(row_full[3], "seq", axis=1, tiled=True),
        lax.all_gather(row_full[4], "seq", axis=1, tiled=True),
        lax.all_gather(row_full[5], "seq", axis=1, tiled=True),
    )


def group_scores(query_part, key_part, allowed, factor):
    scores = (
        jnp.einsum("qhd,khd->hqk", query_part, key_part, preferred_element_type=jnp.float32)
        * factor
    )
    return jnp.where(allowed[None], scores, masked_score)


def attend_row(queries, key_rows, value_rows, segment_local, segment_full):
    factor = queries.shape[2] ** (-0.5)
    allowed = segment_local[:, None] == segment_full[None, :]
    outputs = []
    totals = []
    for head_start in range(0, H, HG):
        head_end = head_start + HG
        scores = group_scores(
            queries[:, head_start:head_end], key_rows[:, head_start:head_end], allowed, factor
        )
        log_total = jax.nn.logsumexp(scores, axis=-1)
        weights = jnp.exp(scores - log_total[..., None]).astype(jnp.bfloat16)
        outputs.append(
            jnp.einsum(
                "hqk,khd->qhd",
                weights,
                value_rows[:, head_start:head_end],
                preferred_element_type=jnp.float32,
            )
        )
        totals.append(log_total)
    return (jnp.concatenate(outputs, axis=1), jnp.concatenate(totals, axis=0))


def attend_back(
    queries, key_rows, value_rows, segment_local, segment_full, log_total, grad_attended, row_dot
):
    factor = queries.shape[2] ** (-0.5)
    allowed = segment_local[:, None] == segment_full[None, :]
    query_grads = []
    key_grads = []
    value_grads = []
    for head_start in range(0, H, HG):
        head_end = head_start + HG
        key_part = key_rows[:, head_start:head_end]
        query_part = queries[:, head_start:head_end]
        grad_part = grad_attended[:, head_start:head_end]
        scores = group_scores(query_part, key_part, allowed, factor)
        weights = jnp.exp(scores - log_total[head_start:head_end][..., None])
        weights_low = weights.astype(jnp.bfloat16)
        value_grads.append(
            jnp.einsum("hqk,qhd->khd", weights_low, grad_part, preferred_element_type=jnp.float32)
        )
        grad_weights = jnp.einsum(
            "qhd,khd->hqk",
            grad_part,
            value_rows[:, head_start:head_end],
            preferred_element_type=jnp.float32,
        )
        grad_scores = (weights * (grad_weights - row_dot[head_start:head_end][..., None])).astype(
            jnp.bfloat16
        )
        query_grads.append(
            jnp.einsum("hqk,khd->qhd", grad_scores, key_part, preferred_element_type=jnp.float32)
            * factor
        )
        key_grads.append(
            jnp.einsum("hqk,qhd->khd", grad_scores, query_part, preferred_element_type=jnp.float32)
            * factor
        )
    return (
        jnp.concatenate(query_grads, axis=1),
        jnp.concatenate(key_grads, axis=1),
        jnp.concatenate(value_grads, axis=1),
    )


def local_general(
    inputs,
    skip_input,
    time_embed,
    segment_ids,
    span_start,
    span_length,
    cotangent,
    skip_weight,
    ada_weight,
    qkv_weight,
    out_weight,
    up_weight,
    down_weight,
):
    row_count = inputs.shape[0]
    frames = inputs.shape[1]
    model_width = inputs.shape[2]
    row_length = segment_ids.shape[1]
    frame_base = lax.axis_index("seq") * frames
    utterance = jnp.arange(UTT, dtype=jnp.int32)
    member = (segment_ids[:, :, None] == utterance[None, None, :]).astype(jnp.int32)
    counts = jnp.sum(member, axis=1)
    firsts = jnp.cumsum(counts, axis=1) - counts
    local_member = lax.dynamic_slice_in_dim(member, frame_base, frames, 1)
    local_segments = lax.dynamic_slice_in_dim(segment_ids, frame_base, frames, 1)
    local_frames = frame_base + jnp.arange(frames, dtype=jnp.int32)
    position = local_frames[None, :] - jnp.sum(local_member * firsts[:, None, :], axis=2)
    span_begin = jnp.sum(local_member * span_start[:, None, :], axis=2)
    span_end = span_begin + jnp.sum(local_member * span_length[:, None, :], axis=2)
    inside = jnp.logical_and(position >= span_begin, position < span_end)
    cosine, sine_part = rotary_tables(position, HD // 2)
    skip_full, ada_full, qkv_full, out_full, up_full, down_full = gather_weights(
        skip_weight, ada_weight, qkv_weight, out_weight, up_weight, down_weight
    )
    joined = jnp.concatenate([inputs, skip_input], axis=-1)
    stream = jnp.einsum("rfc,cd->rfd", joined, skip_full, preferred_element_type=jnp.float32)
    modulation = jnp.dot(time_embed, ada_full, preferred_element_type=jnp.float32)[:, None, :]
    scale_one = modulation[..., :model_width]
    shift_one = modulation[..., model_width : 2 * model_width]
    scale_two = modulation[..., 2 * model_width : 3 * model_width]
    shift_two = modulation[..., 3 * model_width :]
    normed_one = ada_norm(stream, scale_one, shift_one).astype(jnp.bfloat16)
    projected = jnp.einsum("rfd,de->rfe", normed_one, qkv_full, preferred_element_type=jnp.float32)
    queries = rotate(
        projected[..., :model_width].reshape(row_count, frames, H, HD), cosine, sine_part
    ).astype(jnp.bfloat16)
    key_rotated = rotate(
        projected[..., model_width : 2 * model_width].reshape(row_count, frames, H, HD),
        cosine,
        sine_part,
    )
    key_local = key_rotated.reshape(row_count, frames, model_width).astype(jnp.bfloat16)
    value_local = projected[..., 2 * model_width :].astype(jnp.bfloat16)
    key_all, value_all = (
        lax.all_gather(key_local, "seq", axis=1, tiled=True),
        lax.all_gather(value_local, "seq", axis=1, tiled=True),
    )

    def forward_row(row_items):
        query_row, key_row, value_row, local_row, full_row = row_items
        return attend_row(
            query_row,
            key_row.reshape(row_length, H, HD),
            value_row.reshape(row_length, H, HD),
            local_row,
            full_row,
        )

    attended, log_total = lax.map(
        forward_row, (queries, key_all, value_all, local_segments, segment_ids)
    )
    attended = attended.reshape(row_count, frames, model_width)
    attended_low = attended.astype(jnp.bfloat16)
    middle = stream + jnp.einsum(
        "rfe,ed->rfd", attended_low, out_full, preferred_element_type=jnp.float32
    )
    normed_two = ada_norm(middle, scale_two, shift_two).astype(jnp.bfloat16)
    up_proj = jnp.einsum("rfd,di->rfi", normed_two, up_full, preferred_element_type=jnp.float32)
    hidden = jax.nn.gelu(up_proj, approximate=True).astype(jnp.bfloat16)
    down_proj = jnp.einsum("rfi,id->rfd", hidden, down_full, preferred_element_type=jnp.float32)
    layer_output = (middle + down_proj).astype(jnp.bfloat16)
    skip_full, ada_full, qkv_full, out_full, up_full, down_full = gather_weights(
        skip_weight, ada_weight, qkv_weight, out_weight, up_weight, down_weight
    )
    grad_out = cotangent.astype(jnp.float32) * inside[..., None].astype(jnp.float32)
    grad_low = grad_out.astype(jnp.bfloat16)
    grad_hidden = jnp.einsum("rfd,id->rfi", grad_low, down_full, preferred_element_type=jnp.float32)
    _, gelu_pull = jax.vjp(partial(jax.nn.gelu, approximate=True), up_proj)
    grad_up_act = gelu_pull(grad_hidden)[0].astype(jnp.bfloat16)
    grad_normed_two = jnp.einsum(
        "rfi,di->rfd", grad_up_act, up_full, preferred_element_type=jnp.float32
    )
    _, norm_pull_two = jax.vjp(ada_norm, middle, scale_two, shift_two)
    grad_middle_norm, grad_scale_two, grad_shift_two = norm_pull_two(grad_normed_two)
    grad_middle = grad_out + grad_middle_norm
    grad_middle_low = grad_middle.astype(jnp.bfloat16)
    grad_attended = jnp.einsum(
        "rfd,ed->rfe", grad_middle_low, out_full, preferred_element_type=jnp.float32
    ).astype(jnp.bfloat16)
    row_dot = jnp.sum(
        (grad_attended.astype(jnp.float32) * attended).reshape(row_count, frames, H, HD), axis=-1
    )
    row_dot = jnp.swapaxes(row_dot, 1, 2)
    grad_heads = grad_attended.reshape(row_count, frames, H, HD)

    def backward_row(row_items):
        query_row, key_row, value_row, local_row, full_row, total_row, grad_row, dot_row = row_items
        return attend_back(
            query_row,
            key_row.reshape(row_length, H, HD),
            value_row.reshape(row_length, H, HD),
            local_row,
            full_row,
            total_row,
            grad_row,
            dot_row,
        )

    grad_queries, grad_keys, grad_values = lax.map(
        backward_row,
        (queries, key_all, value_all, local_segments, segment_ids, log_total, grad_heads, row_dot),
    )
    key_share, value_share = (
        lax.psum_scatter(
            grad_keys.reshape(row_count, row_length, model_width).astype(jnp.bfloat16),
            "seq",
            scatter_dimension=1,
            tiled=True,
        ).astype(jnp.float32),
        lax.psum_scatter(
            grad_values.reshape(row_count, row_length, model_width).astype(jnp.bfloat16),
            "seq",
            scatter_dimension=1,
            tiled=True,
        ).astype(jnp.float32),
    )
    _, rotate_pull = jax.vjp(
        partial(rotate, cosine=cosine, sine_part=sine_part),
        jnp.zeros((row_count, frames, H, HD), jnp.float32),
    )
    grad_query_raw = rotate_pull(grad_queries)[0].reshape(row_count, frames, model_width)
    grad_key_raw = rotate_pull(key_share.reshape(row_count, frames, H, HD))[0].reshape(
        row_count, frames, model_width
    )
    grad_projected = jnp.concatenate([grad_query_raw, grad_key_raw, value_share], axis=-1).astype(
        jnp.bfloat16
    )
    grad_normed_one = jnp.einsum(
        "rfe,de->rfd", grad_projected, qkv_full, preferred_element_type=jnp.float32
    )
    _, norm_pull_one = jax.vjp(ada_norm, stream, scale_one, shift_one)
    grad_stream_norm, grad_scale_one, grad_shift_one = norm_pull_one(grad_normed_one)
    grad_stream = (grad_middle + grad_stream_norm).astype(jnp.bfloat16)
    grad_joined = jnp.einsum(
        "rfd,cd->rfc", grad_stream, skip_full, preferred_element_type=jnp.float32
    )
    grad_modulation = jnp.concatenate(
        [grad_scale_one, grad_shift_one, grad_scale_two, grad_shift_two], axis=-1
    )[:, 0, :]
    grad_down = jnp.einsum("rfi,rfd->id", hidden, grad_low, preferred_element_type=jnp.float32)
    grad_up = jnp.einsum("rfd,rfi->di", normed_two, grad_up_act, preferred_element_type=jnp.float32)
    grad_attn_out = jnp.einsum(
        "rfe,rfd->ed", attended_low, grad_middle_low, preferred_element_type=jnp.float32
    )
    grad_qkv = jnp.einsum(
        "rfd,rfe->de", normed_one, grad_projected, preferred_element_type=jnp.float32
    )
    grad_skip_w = jnp.einsum("rfc,rfd->cd", joined, grad_stream, preferred_element_type=jnp.float32)
    grad_ada = jnp.einsum(
        "rd,re->de",
        time_embed.astype(jnp.float32),
        grad_modulation,
        precision=lax.Precision.HIGHEST,
    )
    column_parts = (
        lax.psum_scatter(
            grad_skip_w.astype(jnp.bfloat16), "seq", scatter_dimension=1, tiled=True
        ).astype(jnp.float32),
        lax.psum_scatter(
            grad_ada.astype(jnp.bfloat16), "seq", scatter_dimension=1, tiled=True
        ).astype(jnp.float32),
        lax.psum_scatter(
            grad_qkv.astype(jnp.bfloat16), "seq", scatter_dimension=1, tiled=True
        ).astype(jnp.float32),
        lax.psum_scatter(
            grad_attn_out.astype(jnp.bfloat16), "seq", scatter_dimension=1, tiled=True
        ).astype(jnp.float32),
        lax.psum_scatter(
            grad_up.astype(jnp.bfloat16), "seq", scatter_dimension=1, tiled=True
        ).astype(jnp.float32),
        lax.psum_scatter(
            grad_down.astype(jnp.bfloat16), "seq", scatter_dimension=1, tiled=True
        ).astype(jnp.float32),
    )
    weight_tiles = (
        lax.psum_scatter(
            column_parts[0].astype(jnp.bfloat16), "dp", scatter_dimension=0, tiled=True
        ).astype(jnp.float32),
        lax.psum_scatter(
            column_parts[1].astype(jnp.bfloat16), "dp", scatter_dimension=0, tiled=True
        ).astype(jnp.float32),
        lax.psum_scatter(
            column_parts[2].astype(jnp.bfloat16), "dp", scatter_dimension=0, tiled=True
        ).astype(jnp.float32),
        lax.psum_scatter(
            column_parts[3].astype(jnp.bfloat16), "dp", scatter_dimension=0, tiled=True
        ).astype(jnp.float32),
        lax.psum_scatter(
            column_parts[4].astype(jnp.bfloat16), "dp", scatter_dimension=0, tiled=True
        ).astype(jnp.float32),
        lax.psum_scatter(
            column_parts[5].astype(jnp.bfloat16), "dp", scatter_dimension=0, tiled=True
        ).astype(jnp.float32),
    )
    skip_tile, ada_tile, qkv_tile, out_tile, up_tile, down_tile = weight_tiles
    return (
        layer_output,
        grad_joined[..., :model_width],
        grad_joined[..., model_width:],
        skip_tile,
        ada_tile,
        qkv_tile,
        out_tile,
        up_tile,
        down_tile,
    )


LOG2E = 1.4426950408889634
SCALE = HD**-0.5
PAIR = 2 * HD


def dot_nn(a, b):
    return lax.dot_general(a, b, (((1,), (0,)), ((), ())), preferred_element_type=jnp.float32)


def dot_nt(a, b):
    return lax.dot_general(a, b, (((1,), (1,)), ((), ())), preferred_element_type=jnp.float32)


def dot_tn(a, b):
    return lax.dot_general(a, b, (((0,), (0,)), ((), ())), preferred_element_type=jnp.float32)


def segment_of(index, ends_ref):
    return (index >= ends_ref[0]).astype(jnp.int32) + (index >= ends_ref[1]).astype(jnp.int32)


def segment_span(ends_ref, first, last, length):
    end_a, end_b = ends_ref[0], ends_ref[1]
    low = jnp.where(first < end_a, 0, jnp.where(first < end_b, end_a, end_b))
    high = jnp.where(last < end_a, end_a, jnp.where(last < end_b, end_b, length))
    return low, high


def key_blocks(ends_ref, start, size, length):
    low, high = segment_span(ends_ref, start, start + size - 1, length)
    low_last, _ = segment_span(ends_ref, start + size - 1, start, length)
    first = low // size
    last = (high + size - 1) // size
    whole_first = jnp.where(low == low_last, (low + size - 1) // size, last)
    whole_first = jnp.minimum(whole_first, last)
    whole_last = jnp.where(low == low_last, jnp.maximum(high // size, whole_first), last)
    return first, whole_first, whole_last, last


def turn(pair, cosine, sine_part):
    half = HD // 2
    rows = []
    for head in range(pair.shape[0] // HD):
        lower = pair[head * HD : head * HD + half]
        upper = pair[head * HD + half : (head + 1) * HD]
        rows += [lower * cosine - upper * sine_part, lower * sine_part + upper * cosine]
    return jnp.concatenate(rows, axis=0)


def head_norms(pair):
    square = pair * pair
    return [jnp.sum(square[head * HD : (head + 1) * HD], axis=0, keepdims=True) for head in range(2)]


def project_kernel(
    normed_ref, weight_ref, cos_ref, sin_ref, qt_ref, kt_ref, vt_ref, k_ref, v_ref, norms_ref
):
    projected = dot_nt(weight_ref[...], normed_ref[0])
    cosine, sine_part = cos_ref[...], sin_ref[...]
    queries = turn(projected[:PAIR], cosine, sine_part).astype(jnp.bfloat16)
    keys = turn(projected[PAIR : 2 * PAIR], cosine, sine_part)
    values = projected[2 * PAIR :]
    norms_ref[0] = jnp.concatenate(head_norms(queries.astype(jnp.float32) * SCALE) + head_norms(keys), axis=0)
    qt_ref[0] = (queries.astype(jnp.float32) * SCALE).astype(jnp.bfloat16)
    kt_ref[...] = keys.astype(jnp.bfloat16)
    vt_ref[...] = values.astype(jnp.bfloat16)
    k_ref[...] = keys.T.astype(jnp.bfloat16)
    v_ref[...] = values.T.astype(jnp.bfloat16)


def project_pair(normed_all, weight_rows, cos_all, sin_all):
    chunks, frames, width = normed_all.shape
    length = chunks * frames
    return pl.pallas_call(
        project_kernel,
        grid=(chunks,),
        in_specs=[
            pl.BlockSpec((1, frames, width), lambda i: (i, 0, 0)),
            pl.BlockSpec((3 * PAIR, width), lambda i: (0, 0)),
            pl.BlockSpec((HD // 2, frames), lambda i: (0, i)),
            pl.BlockSpec((HD // 2, frames), lambda i: (0, i)),
        ],
        out_specs=[
            pl.BlockSpec((1, PAIR, frames), lambda i: (i, 0, 0)),
            pl.BlockSpec((PAIR, frames), lambda i: (0, i)),
            pl.BlockSpec((PAIR, frames), lambda i: (0, i)),
            pl.BlockSpec((frames, PAIR), lambda i: (i, 0)),
            pl.BlockSpec((frames, PAIR), lambda i: (i, 0)),
            pl.BlockSpec((1, 4, frames), lambda i: (i, 0, 0)),
        ],
        out_shape=[
            jax.ShapeDtypeStruct((chunks, PAIR, frames), jnp.bfloat16),
            jax.ShapeDtypeStruct((PAIR, length), jnp.bfloat16),
            jax.ShapeDtypeStruct((PAIR, length), jnp.bfloat16),
            jax.ShapeDtypeStruct((length, PAIR), jnp.bfloat16),
            jax.ShapeDtypeStruct((length, PAIR), jnp.bfloat16),
            jax.ShapeDtypeStruct((chunks, 4, frames), jnp.float32),
        ],
        compiler_params=pltpu.CompilerParams(vmem_limit_bytes=60 << 20),
        cost_estimate=pl.CostEstimate(
            flops=6 * length * width * PAIR, bytes_accessed=2 * length * (width + 5 * PAIR), transcendentals=0
        ),
        name="project_pair",
    )(normed_all, weight_rows, cos_all, sin_all)


def split_heads(block):
    row = lax.broadcasted_iota(jnp.int32, block.shape, 0)
    zero = jnp.zeros((), block.dtype)
    return jnp.where(row < HD, block, zero), jnp.where(row < HD, zero, block)


SAFE_SCORE = 60.0


def attend_kernel(
    ends_ref, qt_ref, k_ref, vt_ref, norms_ref, low_ref, full_ref, total_ref, acc_ref, top_ref, *, size, length
):
    index = pl.program_id(0)
    start = index * size
    queries = split_heads(qt_ref[0])
    query_segment = segment_of(start + lax.broadcasted_iota(jnp.int32, (1, size), 1), ends_ref)
    first, whole_first, whole_last, last = key_blocks(ends_ref, start, size, length)
    acc_ref[...] = jnp.zeros_like(acc_ref)
    ones = jnp.ones((16, size), jnp.bfloat16)
    bound = jnp.max(norms_ref[index, :2, :]) * jnp.max(norms_ref[:, 2:, :])
    plain = bound < SAFE_SCORE * SAFE_SCORE

    def step(masked, shifted):
        def run(block, carry):
            offset = pl.multiple_of(block * size, size)
            keys = k_ref[pl.ds(offset, size), :]
            scores = [dot_nn(keys, queries[head]) for head in range(2)]
            if masked:
                key_segment = segment_of(offset + lax.broadcasted_iota(jnp.int32, (size, 1), 0), ends_ref)
                same = key_segment == query_segment
                scores = [jnp.where(same, part, masked_score) for part in scores]
            if shifted:
                old = [top_ref[head] for head in range(2)]
                new = [
                    jnp.maximum(old[head], jnp.max(scores[head], axis=0, keepdims=True) * LOG2E) for head in range(2)
                ]
                weights = [jnp.exp2(scores[head] * LOG2E - new[head]).astype(jnp.bfloat16) for head in range(2)]
            else:
                weights = [jnp.exp2(scores[head] * LOG2E).astype(jnp.bfloat16) for head in range(2)]
            for head in range(2):
                values = jnp.concatenate([vt_ref[pl.ds(head * HD, HD), pl.ds(offset, size)], ones], axis=0)
                if shifted:
                    acc_ref[head] = acc_ref[head] * jnp.exp2(old[head] - new[head]) + dot_nn(values, weights[head])
                    top_ref[head] = new[head]
                else:
                    acc_ref[head] += dot_nn(values, weights[head])
            return carry

        return run

    def loops(shifted):
        lax.fori_loop(first, whole_first, step(True, shifted), 0)
        lax.fori_loop(whole_first, whole_last, step(False, shifted), 0)
        lax.fori_loop(whole_last, last, step(True, shifted), 0)

    @pl.when(plain)
    def _():
        top_ref[...] = jnp.zeros_like(top_ref)
        loops(False)

    @pl.when(jnp.logical_not(plain))
    def _():
        top_ref[...] = jnp.full_like(top_ref, masked_score)
        loops(True)

    for head in range(2):
        total = acc_ref[head, HD : HD + 1, :]
        attended = acc_ref[head, :HD, :] / total
        full_ref[0, head * HD : (head + 1) * HD, :] = attended
        low_ref[0, head * HD : (head + 1) * HD, :] = attended.astype(jnp.bfloat16)
        total_ref[0, head : head + 1, :] = jnp.log(total) * LOG2E + top_ref[head]


def attend_pair(ends, qt, k, vt, norms):
    chunks, _, size = qt.shape
    length = k.shape[0]
    chunk = pl.BlockSpec((1, PAIR, size), lambda i, ends: (i, 0, 0))
    return pl.pallas_call(
        partial(attend_kernel, size=size, length=length),
        grid_spec=pltpu.PrefetchScalarGridSpec(
            num_scalar_prefetch=1,
            grid=(chunks,),
            in_specs=[
                chunk,
                pl.BlockSpec((length, PAIR), lambda i, ends: (0, 0)),
                pl.BlockSpec((PAIR, length), lambda i, ends: (0, 0)),
                pl.BlockSpec(norms.shape, lambda i, ends: (0, 0, 0)),
            ],
            out_specs=[chunk, chunk, pl.BlockSpec((1, 2, size), lambda i, ends: (i, 0, 0))],
            scratch_shapes=[pltpu.VMEM((2, HD + 16, size), jnp.float32), pltpu.VMEM((2, 1, size), jnp.float32)],
        ),
        out_shape=[
            jax.ShapeDtypeStruct((chunks, PAIR, size), jnp.bfloat16),
            jax.ShapeDtypeStruct((chunks, PAIR, size), jnp.float32),
            jax.ShapeDtypeStruct((chunks, 2, size), jnp.float32),
        ],
        compiler_params=pltpu.CompilerParams(vmem_limit_bytes=60 << 20),
        cost_estimate=pl.CostEstimate(
            flops=8 * length * length * HD, bytes_accessed=14 * length * PAIR, transcendentals=length * length
        ),
        name="attend_pair",
    )(ends, qt, k, vt, norms)


def attend_back_kernel(
    ends_ref, qt_ref, gt_ref, full_ref, total_ref, k_ref, v_ref, kt_ref, cos_ref, sin_ref, out_ref,
    dk_ref, dv_ref, dq_ref, *, head, size, length, chunks,
):
    index = pl.program_id(0)
    start = index * size

    @pl.when(index == 0)
    def _():
        dk_ref[...] = jnp.zeros_like(dk_ref)
        dv_ref[...] = jnp.zeros_like(dv_ref)

    mine = slice(head * HD, (head + 1) * HD)
    queries = split_heads(qt_ref[0])[head]
    blank = jnp.zeros_like(gt_ref[0])
    grads = jnp.concatenate([blank, gt_ref[0]] if head else [gt_ref[0], blank], axis=0)
    row_dot = jnp.sum(gt_ref[0].astype(jnp.float32) * full_ref[0, mine, :], axis=0, keepdims=True)
    total = total_ref[0, head : head + 1, :]
    query_segment = segment_of(start + lax.broadcasted_iota(jnp.int32, (1, size), 1), ends_ref)
    first, whole_first, whole_last, last = key_blocks(ends_ref, start, size, length)
    dq_ref[...] = jnp.zeros_like(dq_ref)
    pieces = 2
    part = size // pieces

    def step(masked):
        def run(block, carry):
            for piece in range(pieces):
                offset = pl.multiple_of(block * size + piece * part, part)
                rows = pl.ds(offset, part)
                scores = dot_nn(k_ref[rows, :], queries)
                if masked:
                    key_segment = segment_of(offset + lax.broadcasted_iota(jnp.int32, (part, 1), 0), ends_ref)
                    scores = jnp.where(key_segment == query_segment, scores, masked_score)
                weights = jnp.exp2(scores * LOG2E - total)
                grad_weights = dot_nn(v_ref[rows, :], grads)
                grad_scores = (weights * (grad_weights - row_dot)).astype(jnp.bfloat16)
                dv_ref[rows, :] += dot_nt(weights.astype(jnp.bfloat16), grads)
                dk_ref[rows, :] += dot_nt(grad_scores, queries)
                dq_ref[...] += dot_nn(kt_ref[mine, rows], grad_scores)
            return carry

        return run

    lax.fori_loop(first, whole_first, step(True), 0)
    lax.fori_loop(whole_first, whole_last, step(False), 0)
    lax.fori_loop(whole_last, last, step(True), 0)
    own = pl.ds(pl.multiple_of(start, size), size)
    out_ref[index, :HD, :] = turn(dq_ref[...] * SCALE, cos_ref[:, own], -sin_ref[:, own]).astype(jnp.bfloat16)

    @pl.when(index == chunks - 1)
    def _():
        for chunk in range(chunks):
            rows = pl.ds(chunk * size, size)
            turned = turn(dk_ref[rows, :].T[mine], cos_ref[:, rows], -sin_ref[:, rows])
            out_ref[chunk, HD : 2 * HD, :] = turned.astype(jnp.bfloat16)
            out_ref[chunk, 2 * HD :, :] = dv_ref[rows, :].T[mine].astype(jnp.bfloat16)


def attend_head_back(head, ends, qt, gt, full, total, k, v, kt, cos_all, sin_all):
    chunks, _, size = qt.shape
    length = k.shape[0]
    chunk = pl.BlockSpec((1, PAIR, size), lambda i, ends: (i, 0, 0))

    def whole(shape):
        return pl.BlockSpec(shape, lambda i, ends: (0,) * len(shape))

    return pl.pallas_call(
        partial(attend_back_kernel, head=head, size=size, length=length, chunks=chunks),
        grid_spec=pltpu.PrefetchScalarGridSpec(
            num_scalar_prefetch=1,
            grid=(chunks,),
            in_specs=[
                chunk, pl.BlockSpec((1, HD, size), lambda i, ends: (i, 0, 0)), chunk,
                pl.BlockSpec((1, 2, size), lambda i, ends: (i, 0, 0)),
                whole((length, PAIR)), whole((length, PAIR)), whole((PAIR, length)),
                whole((HD // 2, length)), whole((HD // 2, length)),
            ],
            out_specs=whole((chunks, 3 * HD, size)),
            scratch_shapes=[
                pltpu.VMEM((length, PAIR), jnp.float32),
                pltpu.VMEM((length, PAIR), jnp.float32),
                pltpu.VMEM((HD, size), jnp.float32),
            ],
        ),
        out_shape=jax.ShapeDtypeStruct((chunks, 3 * HD, size), jnp.bfloat16),
        compiler_params=pltpu.CompilerParams(vmem_limit_bytes=60 << 20),
        cost_estimate=pl.CostEstimate(
            flops=40 * length * length * HD, bytes_accessed=20 * length * PAIR, transcendentals=0
        ),
        name="attend_head_back",
    )(ends, qt, gt, full, total, k, v, kt, cos_all, sin_all)


def pair_routes(count):
    routes = [[(source, (3 * source + piece) % count) for source in range(count)] for piece in range(3)]
    slots = [[0] * 3 for _ in range(count)]
    for piece in range(3):
        for source, target in routes[piece]:
            slots[target][piece] = (3 * source + piece) // count
    return routes, slots


def own_pair_rows(tile, count):
    routes, slots = pair_routes(count)
    width = tile.shape[0] // 3
    got = [lax.ppermute(tile[p * width : (p + 1) * width], "seq", routes[p]) for p in range(3)]
    slot_of = jnp.asarray(slots, jnp.int32)[lax.axis_index("seq")]
    rows = []
    for slot in range(3):
        rows.append(jnp.where(slot_of[0] == slot, got[0], jnp.where(slot_of[1] == slot, got[1], got[2])))
    return jnp.concatenate(rows, axis=0)


def stored_rows(pair_tile, count):
    routes, slots = pair_routes(count)
    width = pair_tile.shape[0] // 3
    slot_of = jnp.asarray(slots, jnp.int32)[lax.axis_index("seq")]
    parts = [pair_tile[s * width : (s + 1) * width] for s in range(3)]
    back = []
    for piece in range(3):
        slot = slot_of[piece]
        chosen = jnp.where(slot == 0, parts[0], jnp.where(slot == 1, parts[1], parts[2]))
        back.append(lax.ppermute(chosen, "seq", [(target, source) for source, target in routes[piece]]))
    return jnp.concatenate(back, axis=0)


def chip_routes(dp, seq):
    chips = seq // 2

    def flat(move):
        return [(d * seq + s, move(d, s)) for d in range(dp) for s in range(seq)]

    def along_z(step):
        return flat(lambda d, s: d * seq + 2 * ((s // 2 + step) % chips) + s % 2)

    return {
        "x": flat(lambda d, s: (d ^ 1) * seq + s),
        "y": flat(lambda d, s: (d ^ 2) * seq + s),
        "xy": flat(lambda d, s: (d ^ 3) * seq + s),
        "core": flat(lambda d, s: d * seq + (s ^ 1)),
        "z": [along_z(step) for step in range(1, chips)],
    }


def send(value, route):
    return lax.ppermute(value, ("dp", "seq"), route)


def gather_column(tile, routes):
    return jnp.stack([tile] + [send(tile, route) for route in routes["z"]])


def gather_near(column, route):
    return jnp.stack([column, send(column, route)])


GELU_C = math.sqrt(2.0 / math.pi)


def gelu_parts(value):
    square = value * value
    slope = jnp.tanh(GELU_C * value * (1.0 + 0.044715 * square))
    low = 0.5 * (1.0 + slope)
    derivative = low + 0.5 * value * (1.0 - slope * slope) * (GELU_C * (1.0 + 3 * 0.044715 * square))
    return value * low, derivative


def lanes(parts):
    return jnp.concatenate(parts, axis=1)


def stay_order(value, first, second):
    return (value // second) % 2 + 2 * ((value // first) % 2)


def middle_kernel(
    place_ref, att_ref, stream_ref, low_ref, turned_low_ref, scale_ref, shift_ref,
    up_0, up_1, up_2, up_3, down_0, down_1, down_2, down_3,
    layer_ref, grad_mid_ref, grad_att_a_ref, grad_att_b_ref, sums_ref, down_own_out, down_other_out, up_own_out, up_other_out,
    up_w, down_w, out_w, normed_ref, turned_ref, sorted_ref, middle_ref, out_acc,
    down_own, down_other, up_own, up_other, up_sem, down_sem, out_sem, send_sem, *, dp, seq,
):
    dp_at, chip_at, core_at = place_ref[0], place_ref[1], place_ref[2]
    chips = seq // 2
    up_rows, up_cols = up_0.shape[2], up_0.shape[3]
    cols = down_0.shape[3]
    width = stream_ref.shape[1]
    out_rows = width // dp
    down_rows = down_0.shape[2] - out_rows

    def copies(name):
        made = []
        pieces, masks = ((up_0, up_1, up_2, up_3), (1, 2)) if name == "up" else ((down_0, down_1, down_2, down_3), (2, 1))
        for part in range(4):
            core = core_at if part < 2 else 1 - core_at
            for step in range(2):
                mask = (masks[1] if part % 2 else 0) ^ (masks[0] if step else 0)
                row = jnp.bitwise_xor(dp_at, mask)
                for back in range(chips):
                    block = 2 * lax.rem(chip_at + chips - back, chips) + core
                    column = pl.ds(pl.multiple_of(block * cols, cols), cols)
                    source, at = pieces[part].at[step, back], (part * 2 + step) * chips + back
                    if name == "up":
                        target = up_w.at[block, pl.ds(pl.multiple_of(row * up_rows, up_rows), up_rows), :]
                        sem = up_sem.at[at]
                    elif name == "down":
                        source = source.at[pl.ds(0, down_rows), :]
                        target = down_w.at[pl.ds(pl.multiple_of(row * down_rows, down_rows), down_rows), column]
                        sem = down_sem.at[at]
                    else:
                        source = source.at[pl.ds(down_rows, out_rows), :]
                        target = out_w.at[pl.ds(pl.multiple_of(row * out_rows, out_rows), out_rows), column]
                        sem = out_sem.at[at]
                    made.append(pltpu.make_async_copy(source, target, sem))
        return made

    for name in ("out", "up", "down"):
        for copy in copies(name):
            copy.start()
    tiles = [
        2 * ahead + (1 - core_at if other else core_at)
        for other in range(2)
        for ahead in range(chips)
    ]
    for at, tile in enumerate(tiles):
        rows = pl.ds(pl.multiple_of(tile * cols, cols), cols)
        sorted_ref[at * cols : (at + 1) * cols, :] = turned_low_ref[rows, :]
    for copy in copies("out"):
        copy.wait()
    middle_ref[...] = stream_ref[...] + dot_tn(att_ref[...], out_w[...])
    grad_acc = grad_mid_ref
    chunk = 128

    @pl.loop(0, stream_ref.shape[0] // chunk)
    def _(index):
        rows = pl.ds(pl.multiple_of(index * chunk, chunk), chunk)
        middle = middle_ref[rows, :]
        inverse = lax.rsqrt(jnp.mean(middle * middle, axis=-1, keepdims=True) + epsilon)
        normed = middle * inverse * (1.0 + scale_ref[...]) + shift_ref[...]
        normed_ref[rows, :] = normed.astype(jnp.bfloat16)
        turned = normed.T.astype(jnp.bfloat16)
        for row in range(dp):
            place = stay_order(jnp.bitwise_xor(dp_at, row), 2, 1)
            turned_ref[pl.ds(pl.multiple_of(place * out_rows, out_rows), out_rows), rows] = turned[
                row * out_rows : (row + 1) * out_rows
            ]
        out_acc[rows, :] = jnp.zeros_like(middle)
        grad_acc[rows, :] = jnp.zeros_like(middle)

    for name in ("up", "down"):
        for copy in copies(name):
            copy.wait()

    def hidden_block(other, up_grads):
        def run(ahead, carry):
            core = 1 - core_at if other else core_at
            block = 2 * ahead + core
            rows = pl.ds(pl.multiple_of(block * up_cols, up_cols), up_cols)
            up_weight, down_weight = up_w[block], down_w[rows, :]
            value, derivative = gelu_parts(dot_nn(normed_ref[...], up_weight))
            hidden = value.astype(jnp.bfloat16)
            out_acc[...] += dot_nn(hidden, down_weight)
            grad_up = (dot_nt(low_ref[...], down_weight) * derivative).astype(jnp.bfloat16)
            grad_acc[...] += dot_nt(grad_up, up_weight)
            for owner in range(dp):
                part = dot_nn(turned_ref[owner * up_rows : (owner + 1) * up_rows, :], grad_up)
                up_grads[owner, ahead] = part.astype(jnp.bfloat16)
            per_owner = down_rows // up_cols
            owner = stay_order(jnp.bitwise_xor(dp_at, block // per_owner), 1, 2)
            at = pl.ds(pl.multiple_of(lax.rem(block, per_owner) * cols, cols), cols)
            for pair in range(chips):
                part = dot_nn(sorted_ref[2 * pair * cols : 2 * (pair + 1) * cols, :], hidden).astype(jnp.bfloat16)
                for tile in range(2):
                    target, place = (down_own, 2 * pair + tile) if pair < chips // 2 else (down_other, 2 * pair + tile - chips)
                    target[owner, place, at, :] = part[tile * cols : (tile + 1) * cols]
            return carry

        lax.fori_loop(0, chips, run, 0, unroll=2)

    hidden_block(1, up_other)
    send_up_other = pltpu.make_async_copy(up_other, up_other_out, send_sem.at[0])
    send_up_other.start()
    hidden_block(0, up_own)
    packed = down_rows * cols // up_cols
    sends = [
        pltpu.make_async_copy(up_own, up_own_out, send_sem.at[1]),
        pltpu.make_async_copy(
            down_other.at[:, :, pl.ds(0, packed), :], down_other_out.at[:, :, pl.ds(0, packed), :], send_sem.at[2]
        ),
        pltpu.make_async_copy(
            down_own.at[:, :, pl.ds(0, packed), :], down_own_out.at[:, :, pl.ds(0, packed), :], send_sem.at[3]
        ),
    ]
    for copy in sends:
        copy.start()
    sums_ref[...] = jnp.zeros_like(sums_ref)

    @pl.loop(0, stream_ref.shape[0] // chunk)
    def _(index):
        rows = pl.ds(pl.multiple_of(index * chunk, chunk), chunk)
        middle = middle_ref[rows, :]
        layer_ref[rows, :] = (middle + out_acc[rows, :]).astype(jnp.bfloat16)
        inverse = lax.rsqrt(jnp.mean(middle * middle, axis=-1, keepdims=True) + epsilon)
        unit = middle * inverse
        grad = grad_acc[rows, :]
        lifted = grad * (1.0 + scale_ref[...])
        sums_ref[0:1, :] += jnp.sum(grad * unit, axis=0, keepdims=True)
        sums_ref[1:2, :] += jnp.sum(grad, axis=0, keepdims=True)
        grad_mid = low_ref[rows, :].astype(jnp.float32) + inverse * (
            lifted - unit * jnp.mean(lifted * unit, axis=-1, keepdims=True)
        )
        grad_mid_ref[rows, :] = grad_mid
        normed_ref[rows, :] = grad_mid.astype(jnp.bfloat16)

    grad_att = dot_nt(out_w[...], normed_ref[...]).astype(jnp.bfloat16)
    for target in range(seq):
        grad_att_a_ref[target] = grad_att[target * PAIR : target * PAIR + HD]
        grad_att_b_ref[target] = grad_att[target * PAIR + HD : (target + 1) * PAIR]
    grads = lanes([normed_ref[:, pl.ds(pl.multiple_of(tile * cols, cols), cols)] for tile in tiles])
    per_row = up_cols // cols
    folded = out_rows // per_row
    for row in range(dp):
        owner = stay_order(jnp.bitwise_xor(dp_at, row), 1, 2)
        product = dot_nn(att_ref[row * out_rows : (row + 1) * out_rows, :], grads).astype(jnp.bfloat16)
        for at in range(seq):
            part = product[:, at * cols : (at + 1) * cols]
            part = lanes([part[i * folded : (i + 1) * folded] for i in range(per_row)])
            target = down_own if at < chips else down_other
            target[owner, at % chips, packed : packed + folded, :] = part
    last = [
        pltpu.make_async_copy(
            down_other.at[:, :, pl.ds(packed, folded), :], down_other_out.at[:, :, pl.ds(packed, folded), :], send_sem.at[4]
        ),
        pltpu.make_async_copy(
            down_own.at[:, :, pl.ds(packed, folded), :], down_own_out.at[:, :, pl.ds(packed, folded), :], send_sem.at[5]
        ),
    ]
    for copy in last:
        copy.start()
    for copy in [send_up_other] + sends + last:
        copy.wait()


def middle_block(place, attended, stream, grad_low, grad_low_turned, scale, shift, up_pieces, down_pieces, dp, seq):
    frames, width = stream.shape
    tile_cols = up_pieces[0].shape[3]
    hidden = tile_cols * seq
    chips = seq // 2
    packed = hidden // dp * (width // seq) // tile_cols + width // dp * (width // seq) // tile_cols
    whole = pl.BlockSpec(memory_space=pltpu.VMEM)
    anywhere = pl.BlockSpec(memory_space=pl.ANY)
    half, full = jnp.bfloat16, jnp.float32
    down_shape, up_shape = (dp, chips, packed, tile_cols), (dp, chips, width // dp, tile_cols)
    return pl.pallas_call(
        partial(middle_kernel, dp=dp, seq=seq),
        in_specs=[pl.BlockSpec(memory_space=pltpu.SMEM)] + [whole] * 6 + [anywhere] * 8,
        out_specs=[whole] * 5 + [anywhere] * 4,
        out_shape=[
            jax.ShapeDtypeStruct((frames, width), half),
            jax.ShapeDtypeStruct((frames, width), full),
            jax.ShapeDtypeStruct((seq, HD, frames), half),
            jax.ShapeDtypeStruct((seq, HD, frames), half),
            jax.ShapeDtypeStruct((2, width), full),
            jax.ShapeDtypeStruct(down_shape, half),
            jax.ShapeDtypeStruct(down_shape, half),
            jax.ShapeDtypeStruct(up_shape, half),
            jax.ShapeDtypeStruct(up_shape, half),
        ],
        scratch_shapes=[
            pltpu.VMEM((seq, width, tile_cols), half),
            pltpu.VMEM((hidden, width), half),
            pltpu.VMEM((width, width), half),
            pltpu.VMEM((frames, width), half),
            pltpu.VMEM((width, frames), half),
            pltpu.VMEM((width, frames), half),
            pltpu.VMEM((frames, width), full),
            pltpu.VMEM((frames, width), full),
            pltpu.VMEM(down_shape, half),
            pltpu.VMEM(down_shape, half),
            pltpu.VMEM(up_shape, half),
            pltpu.VMEM(up_shape, half),
            pltpu.SemaphoreType.DMA((dp * seq,)),
            pltpu.SemaphoreType.DMA((dp * seq,)),
            pltpu.SemaphoreType.DMA((dp * seq,)),
            pltpu.SemaphoreType.DMA((6,)),
        ],
        compiler_params=pltpu.CompilerParams(vmem_limit_bytes=62 << 20),
        cost_estimate=pl.CostEstimate(
            flops=12 * frames * width * hidden + 6 * frames * width * width,
            bytes_accessed=8 * hidden * width + 24 * frames * width,
            transcendentals=frames * hidden,
        ),
        name="middle_block",
    )(place, attended, stream, grad_low, grad_low_turned, scale, shift, *up_pieces, *down_pieces)


def entry_kernel(main_ref, side_ref, weight_ref, scale_ref, shift_ref, stream_ref, normed_ref, *, dp, seq):
    row = pl.program_id(0)

    @pl.when(row == 0)
    def _():
        stream_ref[...] = jnp.zeros_like(stream_ref)

    operand = jnp.where(row < dp // 2, main_ref[...], side_ref[...])
    stream_ref[...] += dot_nn(operand, lanes([weight_ref[s] for s in range(seq)]))

    @pl.when(row == dp - 1)
    def _():
        stream = stream_ref[...]
        inverse = lax.rsqrt(jnp.mean(stream * stream, axis=-1, keepdims=True) + epsilon)
        normed_ref[...] = (stream * inverse * (1.0 + scale_ref[...]) + shift_ref[...]).astype(jnp.bfloat16)


def entry_block(main, side, skip_tiles, scale, shift, dp, seq):
    frames, width = main.shape
    rows, columns = skip_tiles.shape[1:]
    fixed = pl.BlockSpec((1, width), lambda i: (0, 0))
    return pl.pallas_call(
        partial(entry_kernel, dp=dp, seq=seq),
        grid=(dp,),
        in_specs=[
            pl.BlockSpec((frames, rows), lambda i: (0, jnp.minimum(i, dp // 2 - 1))),
            pl.BlockSpec((frames, rows), lambda i: (0, jnp.maximum(i - dp // 2, 0))),
            pl.BlockSpec((seq, rows, columns), lambda i: (i, 0, 0)),
            fixed,
            fixed,
        ],
        out_specs=[pl.BlockSpec((frames, width), lambda i: (0, 0))] * 2,
        out_shape=[
            jax.ShapeDtypeStruct((frames, width), jnp.float32),
            jax.ShapeDtypeStruct((frames, width), jnp.bfloat16),
        ],
        compiler_params=pltpu.CompilerParams(vmem_limit_bytes=32 << 20),
        cost_estimate=pl.CostEstimate(
            flops=4 * frames * width * width, bytes_accessed=14 * frames * width, transcendentals=0
        ),
        name="entry_block",
    )(main, side, skip_tiles, scale, shift)


def head_product(head, head_ref, pair_ref, dp, seq):
    parts = [head_ref[s, piece * HD : (piece + 1) * HD] for s in range(seq) for piece in range(3)]
    projected = jnp.concatenate(parts, axis=0).T
    for row in range(dp):
        weight = jnp.concatenate(
            [
                pair_ref[row * seq + s, piece * PAIR + head * HD : piece * PAIR + (head + 1) * HD]
                for s in range(seq)
                for piece in range(3)
            ],
            axis=0,
        )
        yield row, dot_nn(projected, weight)


def first_head_kernel(head_ref, pair_ref, out_ref, *, dp, seq):
    rows = pair_ref.shape[2]
    for row, product in head_product(0, head_ref, pair_ref, dp, seq):
        out_ref[:, row * rows : (row + 1) * rows] = product


def first_head(head_a, pair_tiles, dp, seq):
    frames, width = head_a.shape[2], pair_tiles.shape[2] * dp
    whole = pl.BlockSpec(memory_space=pltpu.VMEM)
    return pl.pallas_call(
        partial(first_head_kernel, dp=dp, seq=seq),
        in_specs=[whole] * 2,
        out_specs=whole,
        out_shape=jax.ShapeDtypeStruct((frames, width), jnp.float32),
        compiler_params=pltpu.CompilerParams(vmem_limit_bytes=60 << 20),
        cost_estimate=pl.CostEstimate(
            flops=3 * frames * width * width, bytes_accessed=7 * frames * width + 6 * width * width, transcendentals=0
        ),
        name="first_head",
    )(head_a, pair_tiles)


def exit_kernel(
    partial_ref, head_ref, pair_ref, stream_ref, grad_mid_ref, scale_ref, grad_ref, turned_ref, sums_ref, normed_ref,
    *, dp, seq,
):
    rows = pair_ref.shape[2]
    for row, product in head_product(1, head_ref, pair_ref, dp, seq):
        columns = slice(row * rows, (row + 1) * rows)
        normed_ref[:, columns] = product + partial_ref[:, columns]
    sums_ref[...] = jnp.zeros_like(sums_ref)
    chunk = 128

    @pl.loop(0, stream_ref.shape[0] // chunk)
    def _(index):
        at = pl.ds(pl.multiple_of(index * chunk, chunk), chunk)
        grad, stream = normed_ref[at, :], stream_ref[at, :]
        inverse = lax.rsqrt(jnp.mean(stream * stream, axis=-1, keepdims=True) + epsilon)
        unit = stream * inverse
        lifted = grad * (1.0 + scale_ref[...])
        sums_ref[0:1, :] += jnp.sum(grad * unit, axis=0, keepdims=True)
        sums_ref[1:2, :] += jnp.sum(grad, axis=0, keepdims=True)
        grad_stream = grad_mid_ref[at, :] + inverse * (
            lifted - unit * jnp.mean(lifted * unit, axis=-1, keepdims=True)
        )
        grad_ref[at, :] = grad_stream.astype(jnp.bfloat16)
        turned_ref[:, at] = grad_stream.T.astype(jnp.bfloat16)


def exit_block(first, head_b, pair_tiles, stream, grad_mid, scale, dp, seq):
    frames, width = stream.shape
    whole = pl.BlockSpec(memory_space=pltpu.VMEM)
    return pl.pallas_call(
        partial(exit_kernel, dp=dp, seq=seq),
        in_specs=[whole] * 6,
        out_specs=[whole] * 3,
        out_shape=[
            jax.ShapeDtypeStruct((frames, width), jnp.bfloat16),
            jax.ShapeDtypeStruct((width, frames), jnp.bfloat16),
            jax.ShapeDtypeStruct((2, width), jnp.float32),
        ],
        scratch_shapes=[pltpu.VMEM((frames, width), jnp.float32)],
        compiler_params=pltpu.CompilerParams(vmem_limit_bytes=60 << 20),
        cost_estimate=pl.CostEstimate(
            flops=3 * frames * width * width, bytes_accessed=18 * frames * width + 6 * width * width, transcendentals=0
        ),
        name="exit_block",
    )(first, head_b, pair_tiles, stream, grad_mid, scale)


def joined_kernel(grad_ref, weight_ref, main_ref, side_ref, *, dp, seq):
    row = pl.program_id(0)
    grad = dot_nt(grad_ref[...], lanes([weight_ref[s] for s in range(seq)]))

    @pl.when(row < dp // 2)
    def _():
        main_ref[...] = grad

    @pl.when(row >= dp // 2)
    def _():
        side_ref[...] = grad


def joined_grads(grad_stream, skip_tiles, dp, seq):
    frames, width = grad_stream.shape
    rows, columns = skip_tiles.shape[1:]
    out = jax.ShapeDtypeStruct((frames, width), jnp.float32)
    return pl.pallas_call(
        partial(joined_kernel, dp=dp, seq=seq),
        grid=(dp,),
        in_specs=[
            pl.BlockSpec((frames, width), lambda i: (0, 0)),
            pl.BlockSpec((seq, rows, columns), lambda i: (i, 0, 0)),
        ],
        out_specs=[
            pl.BlockSpec((frames, rows), lambda i: (0, jnp.minimum(i, dp // 2 - 1))),
            pl.BlockSpec((frames, rows), lambda i: (0, jnp.maximum(i - dp // 2, 0))),
        ],
        out_shape=[out, out],
        compiler_params=pltpu.CompilerParams(vmem_limit_bytes=32 << 20),
        cost_estimate=pl.CostEstimate(
            flops=4 * frames * width * width, bytes_accessed=14 * frames * width, transcendentals=0
        ),
        name="joined_grads",
    )(grad_stream, skip_tiles)


def along_chips(place_ref, chips, other, block):
    core = 1 - place_ref[2] if other else place_ref[2]
    return [pl.multiple_of((2 * chip + core) * block, block) for chip in range(chips)]


def turned_parts(place_ref, left_ref, right_ref, chips, seq, other):
    block = left_ref.shape[0] // seq
    starts = along_chips(place_ref, chips, other, block)
    left = jnp.concatenate([left_ref[pl.ds(start, block), :] for start in starts], axis=0)
    product = dot_nn(left, right_ref[...])
    return [product[ahead * block : (ahead + 1) * block] for ahead in range(chips)]


def plain_parts(place_ref, left_ref, right_ref, chips, seq, other):
    block = right_ref.shape[1] // seq
    starts = along_chips(place_ref, chips, other, block)
    product = dot_nn(left_ref[...], lanes([right_ref[:, pl.ds(start, block)] for start in starts]))
    return [product[:, ahead * block : (ahead + 1) * block] for ahead in range(chips)]


def fold_columns(part, width):
    return jnp.concatenate([part[:, at : at + width] for at in range(0, part.shape[1], width)], axis=0)


def fold_rows(part, width):
    rows = part.shape[0] * part.shape[1] // width
    return lanes([part[at : at + rows] for at in range(0, part.shape[0], rows)])


def blocks_kernel(place_ref, *refs, kinds, other, seq, width):
    chips = seq // 2
    step = pl.program_id(0)
    operands, outs = refs[: 2 * len(kinds)], refs[2 * len(kinds) :]
    packed = [[] for _ in range(chips)]
    for at, kind in enumerate(kinds):
        left_ref, right_ref = operands[2 * at], operands[2 * at + 1]
        if kind == "turned":
            parts = [fold_columns(part, width) for part in turned_parts(place_ref, left_ref, right_ref, chips, seq, other)]
        else:
            parts = plain_parts(place_ref, left_ref, right_ref, chips, seq, other)
            parts = [fold_rows(part, width) if part.shape[1] < width else part for part in parts]
        for ahead in range(chips):
            packed[ahead].append(parts[ahead])
    if not other:
        arrived_ref, outs = outs[0], outs[1:]
    for ahead in range(chips):
        row = 0
        for part in packed[ahead]:
            rows = slice(row, row + part.shape[0])
            row += part.shape[0]
            if other:
                outs[0][0, ahead, rows, :] = part.astype(jnp.bfloat16)
            else:
                low = (part + arrived_ref[0, ahead, rows, :].astype(jnp.float32)).astype(jnp.bfloat16)

                @pl.when(step < 2)
                def _(low=low, ahead=ahead, rows=rows):
                    outs[0][0, ahead, rows, :] = low

                @pl.when(step >= 2)
                def _(low=low, ahead=ahead, rows=rows):
                    outs[1][0, ahead, rows, :] = low


def grad_blocks(place, products, masks, seq, width, arrived=None, part=(0, 1)):
    first, second = masks
    chips, dp = seq // 2, 4

    def owner(i, place):
        return jnp.bitwise_xor(place[0], (i % 2) * second + (i // 2) * first)

    specs, operands, kinds, rows, flops = [], [], [], 0, 0
    for kind, left, right in products:
        depth = left.shape[1]
        if kind == "turned":
            columns = right.shape[1] // (dp * part[1])
            shape = (left.shape[0] // seq, columns)
            specs += [
                pl.BlockSpec(left.shape, lambda i, place: (0, 0)),
                pl.BlockSpec((depth, columns), lambda i, place: (0, owner(i, place) * part[1] + part[0])),
            ]
        else:
            shape = (left.shape[0] // dp, right.shape[1] // seq)
            specs += [
                pl.BlockSpec((shape[0], depth), lambda i, place: (owner(i, place), 0)),
                pl.BlockSpec(right.shape, lambda i, place: (0, 0)),
            ]
        operands += [left, right]
        kinds.append(kind)
        rows += shape[0] * shape[1] // width
        flops += 2 * dp * chips * shape[0] * shape[1] * depth
    other = arrived is None
    one = (1, chips, rows, width)
    if other:
        outs, count = [pl.BlockSpec(one, lambda i, place: (i, 0, 0, 0))], 4
    else:
        outs = [
            pl.BlockSpec(one, lambda i, place: (jnp.minimum(i, 1), 0, 0, 0)),
            pl.BlockSpec(one, lambda i, place: (jnp.maximum(i - 2, 0), 0, 0, 0)),
        ]
        count = 2
        specs.append(pl.BlockSpec(one, lambda i, place: (i, 0, 0, 0)))
        operands.append(arrived)
    return pl.pallas_call(
        partial(blocks_kernel, kinds=tuple(kinds), other=other, seq=seq, width=width),
        grid_spec=pltpu.PrefetchScalarGridSpec(num_scalar_prefetch=1, grid=(4,), in_specs=specs, out_specs=outs),
        out_shape=[jax.ShapeDtypeStruct((count, chips, rows, width), jnp.bfloat16)] * len(outs),
        compiler_params=pltpu.CompilerParams(vmem_limit_bytes=48 << 20),
        cost_estimate=pl.CostEstimate(
            flops=flops, bytes_accessed=8 * rows * width * chips * (1 if other else 2) + flops // 512, transcendentals=0
        ),
        name="grad_blocks",
    )(place, *operands)


AXIS_MASK = {"x": 1, "y": 2}


def wide(value):
    return value.astype(jnp.float32)


def low(value):
    return value.astype(jnp.bfloat16)


def dp_gather(tile, routes, dp):
    at = lax.axis_index("dp")
    columns = tile.shape[1]
    full = jnp.zeros((tile.shape[0], dp * columns), tile.dtype)
    full = lax.dynamic_update_slice_in_dim(full, tile, at * columns, 1)
    for mask, route in ((1, routes["x"]), (2, routes["y"]), (3, routes["xy"])):
        full = lax.dynamic_update_slice_in_dim(full, send(tile, route), jnp.bitwise_xor(at, mask) * columns, 1)
    return full


def chips_exchange(value, seq):
    groups = [[core + 2 * chip for chip in range(seq // 2)] for core in range(2)]
    return lax.all_to_all(value, "seq", 0, 0, axis_index_groups=groups)


def local_paired(
    inputs, skip_input, time_embed, segment_ids, span_start, span_length, cotangent,
    skip_weight, ada_weight, qkv_weight, out_weight, up_weight, down_weight,
):
    seq = lax.axis_size("seq")
    dp = lax.axis_size("dp")
    frames, width = inputs.shape[1], inputs.shape[2]
    length = segment_ids.shape[1]
    segments = segment_ids[0]
    end_a = jnp.sum((segments < 1).astype(jnp.int32))
    end_b = jnp.sum((segments < 2).astype(jnp.int32))
    ends = jnp.stack([end_a, end_b])
    firsts = jnp.where(segments == 0, 0, jnp.where(segments == 1, end_a, end_b))
    position = jnp.arange(length, dtype=jnp.int32) - firsts
    half = HD // 2
    frequency = jnp.exp(-math.log(10000.0) * jnp.arange(half, dtype=jnp.float32) / half)
    angles = frequency[:, None] * position.astype(jnp.float32)[None, :]
    cos_all, sin_all = jnp.cos(angles), jnp.sin(angles)
    base = lax.axis_index("seq") * frames
    local_segments = lax.dynamic_slice_in_dim(segments, base, frames, 0)
    local_position = lax.dynamic_slice_in_dim(position, base, frames, 0)
    starts, lengths = span_start[0], span_length[0]

    def pick(table):
        return jnp.where(local_segments == 0, table[0], jnp.where(local_segments == 1, table[1], table[2]))

    span_begin = pick(starts)
    inside = jnp.logical_and(local_position >= span_begin, local_position < span_begin + pick(lengths))
    grad_low = jnp.where(inside[:, None], cotangent[0], jnp.zeros((), jnp.bfloat16))
    routes = chip_routes(dp, seq)
    seq_at = lax.axis_index("seq")
    place = jnp.stack([lax.axis_index("dp"), seq_at // 2, seq_at % 2]).astype(jnp.int32)
    up_column = gather_column(up_weight, routes)
    down_column = gather_column(jnp.concatenate([down_weight, out_weight]), routes)
    embed_all = lax.all_gather(time_embed, "dp", axis=0, tiled=True)
    embed_rows = width // dp
    embed_part = lax.dynamic_slice_in_dim(embed_all, lax.axis_index("dp") * embed_rows, embed_rows, 1)
    modulation_part = jnp.dot(embed_part, ada_weight, preferred_element_type=jnp.float32)
    modulation_part = lax.psum_scatter(modulation_part, "dp", scatter_dimension=0, tiled=True)
    modulation = lax.all_gather(modulation_part, "seq", axis=1, tiled=True)
    scale_one = modulation[:, :width]
    shift_one = modulation[:, width : 2 * width]
    scale_two = modulation[:, 2 * width : 3 * width]
    shift_two = modulation[:, 3 * width :]

    skip_tiles = lax.all_gather(skip_weight, ("dp", "seq"), axis=0)
    pair_tile = own_pair_rows(qkv_weight.T, seq)
    skip_tiles, up_column, down_column, cos_all, sin_all, ends, grad_low, grad_low_turned, place = lax.optimization_barrier(
        (skip_tiles, up_column, down_column, cos_all, sin_all, ends, grad_low, grad_low.T, place)
    )
    stream, normed_one = entry_block(inputs[0], skip_input[0], skip_tiles, scale_one, shift_one, dp, seq)
    normed_all = lax.all_gather(normed_one, "seq", axis=0)
    up_near = gather_near(up_column, routes["x"])
    down_near = gather_near(down_column, routes["y"])
    pair_weight = dp_gather(pair_tile, routes, dp)
    up_near, down_near, pair_weight = lax.optimization_barrier((up_near, down_near, pair_weight))
    up_far, down_far = send(up_near, routes["y"]), send(down_near, routes["x"])
    normed_all, up_near, down_near = lax.optimization_barrier((normed_all, up_near, down_near))
    up_near_core, down_near_core = send(up_near, routes["core"]), send(down_near, routes["core"])
    qt, kt, vt, keys, values, norms = project_pair(normed_all, pair_weight, cos_all, sin_all)
    attended_pair, attended_wide, total = attend_pair(ends, qt, keys, vt, norms)
    attended_pair, up_far, down_far = lax.optimization_barrier((attended_pair, up_far, down_far))
    up_pieces = (up_near, up_far, up_near_core, send(up_far, routes["core"]))
    down_pieces = (down_near, down_far, down_near_core, send(down_far, routes["core"]))
    attended = lax.all_to_all(attended_pair, "seq", 0, 0).reshape(width, frames)
    attended, pair_tile, far_up, far_down = lax.optimization_barrier(
        (attended, pair_tile, up_pieces[3], down_pieces[3])
    )
    up_pieces, down_pieces = up_pieces[:3] + (far_up,), down_pieces[:3] + (far_down,)
    pair_tiles = lax.all_gather(pair_tile, ("dp", "seq"), axis=0)
    layer_output, grad_middle, grad_head_a, grad_head_b, sums_two, down_own, down_other, up_own, up_other = middle_block(
        place, attended, stream, grad_low, grad_low_turned, scale_two, shift_two, up_pieces, down_pieces, dp, seq
    )
    grad_head_a = lax.all_to_all(grad_head_a, "seq", 0, 0)
    down_other, up_other = send(down_other, routes["core"]), send(up_other, routes["core"])
    down_half, up_half = down_own.shape[2] // 2, up_own.shape[2] // 2

    def leaves(own, other, rows):
        return low(wide(own[2:, :, rows]) + wide(other[2:, :, rows]))

    away = (
        leaves(down_own, down_other, slice(0, down_half)),
        leaves(down_own, down_other, slice(down_half, None)),
        leaves(up_own, up_other, slice(0, up_half)),
        leaves(up_own, up_other, slice(up_half, None)),
    )
    grad_head_b, *away = lax.optimization_barrier((grad_head_b, *away))
    grad_head_b = lax.all_to_all(grad_head_b, "seq", 0, 0)
    saved = (attended_wide, total, keys, values, kt, cos_all, sin_all)
    grad_head_a, pair_tiles, *away = lax.optimization_barrier((grad_head_a, pair_tiles, *away))
    down_got = [send(away[0], routes["x"]), send(away[1], routes["x"])]
    up_got = [send(away[2], routes["y"]), send(away[3], routes["y"])]
    back_a = attend_head_back(0, ends, qt, grad_head_a, *saved)
    local_a = lax.all_to_all(back_a, "seq", 0, 0)
    back_a, grad_head_b, down_got[0], up_got[0] = lax.optimization_barrier(
        (back_a, grad_head_b, down_got[0], up_got[0])
    )
    back_b = attend_head_back(1, ends, qt, grad_head_b, *saved)
    back_b, local_a = lax.optimization_barrier((back_b, local_a))
    local_b = lax.all_to_all(back_b, "seq", 0, 0)

    def stays(own, other, got, at):
        return wide(own[at]) + wide(other[at]) + wide(got[at])

    back_a, back_b, down_got[1], up_got[1] = lax.optimization_barrier((back_a, back_b, down_got[1], up_got[1]))
    down_got, up_got = jnp.concatenate(down_got, axis=2), jnp.concatenate(up_got, axis=2)
    down_low, up_low = low(stays(down_own, down_other, down_got, 1)), low(stays(up_own, up_other, up_got, 1))
    down_low, up_low, back_a, back_b = lax.optimization_barrier((down_low, up_low, back_a, back_b))
    down_back, up_back = send(down_low, routes["y"]), send(up_low, routes["x"])
    parts = [part[:, at : at + HD] for at in range(0, 3 * HD, HD) for part in (back_a, back_b)]
    grad_projected = jnp.concatenate(parts, axis=1)
    grad_pair_weight = jnp.einsum(
        "icf,ifd->cd", grad_projected, normed_all, preferred_element_type=jnp.float32
    ).astype(jnp.bfloat16)
    local_b, grad_pair_weight = lax.optimization_barrier((local_b, grad_pair_weight))
    grad_stream, grad_stream_turned, sums_one = exit_block(
        first_head(local_a, pair_tiles, dp, seq), local_b, pair_tiles, stream, grad_middle, scale_one, dp, seq
    )
    joined = jnp.concatenate([inputs[0], skip_input[0]], axis=-1)
    chips, chip_at, core_at = seq // 2, seq_at // 2, seq_at % 2
    grad_modulation = jnp.concatenate([sums_one[0], sums_one[1], sums_two[0], sums_two[1]]).reshape(chips, 2, -1)
    kept = lax.dynamic_index_in_dim(grad_modulation, core_at, 1, keepdims=False)
    kept = kept + send(lax.dynamic_index_in_dim(grad_modulation, 1 - core_at, 1, keepdims=False), routes["core"])
    column_sum = lax.dynamic_index_in_dim(kept, chip_at, 0)
    for ahead, route in enumerate(routes["z"]):
        piece = lax.dynamic_index_in_dim(kept, (chip_at + ahead + 1) % chips, 0)
        column_sum = column_sum + send(piece, route)
    half_tile = skip_weight.shape[0] // 2
    at = lax.axis_index("dp")
    half_pair = 3 * PAIR // 2
    wide_tile = up_weight.shape[1]
    turned = [("turned", grad_stream_turned, joined)]
    order = (("x", "y"), ("y", "x"))

    def skip_blocks(part, arrived):
        masks = tuple(AXIS_MASK[axis] for axis in order[part])
        return grad_blocks(place, turned, masks, seq, half_tile, arrived, (part, 2))

    leaving = [skip_blocks(part, None)[0] for part in range(2)]
    *leaving, down_back, up_back = lax.optimization_barrier((*leaving, down_back, up_back))
    arrived = [send(part, routes["core"]) for part in leaving]
    down_total = stays(down_own, down_other, down_got, 0) + wide(down_back)
    up_total = stays(up_own, up_other, up_got, 0) + wide(up_back)
    mlp_low = jnp.concatenate([low(down_total), low(up_total)], axis=1)
    column_sum, mlp_low = lax.optimization_barrier((column_sum, mlp_low))
    mlp_got = chips_exchange(mlp_low, seq)
    skip_parts = []
    for part, (first, second) in enumerate(order):
        keep, away = skip_blocks(part, arrived[part])
        pair_rows = grad_pair_weight[part * half_pair : (part + 1) * half_pair]

        def pair_block(mask):
            return lax.dynamic_slice_in_dim(pair_rows, jnp.bitwise_xor(at, mask) * half_tile, half_tile, 1)

        near, far = AXIS_MASK[first], AXIS_MASK[second]
        keep = jnp.concatenate([keep.reshape(2, -1, half_tile), jnp.stack([pair_block(0), pair_block(far)])], axis=1)
        away = jnp.concatenate(
            [away.reshape(2, -1, half_tile), jnp.stack([pair_block(near), pair_block(near ^ far)])], axis=1
        )
        skip_parts.append([keep, away, first, second])
    skip_parts[0][1], skip_parts[1][1], grad_stream, column_sum = lax.optimization_barrier(
        (skip_parts[0][1], skip_parts[1][1], grad_stream, column_sum)
    )
    skip_parts = [(keep, send(away, routes[first]), routes[second]) for keep, away, first, second in skip_parts]
    grad_main, grad_side = joined_grads(grad_stream, skip_tiles, dp, seq)
    got_a, got_b, grad_main, column_sum = lax.optimization_barrier(
        (skip_parts[0][1], skip_parts[1][1], grad_main, column_sum)
    )
    skip_parts = [(skip_parts[0][0], got_a, skip_parts[0][2]), (skip_parts[1][0], got_b, skip_parts[1][2])]
    grad_modulation = jnp.concatenate([column_sum, send(column_sum, routes["x"])])
    grad_modulation = jnp.concatenate([grad_modulation, send(grad_modulation, routes["y"])])
    skip_low, pair_sums = [], []
    skip_rows = chips * (width // seq)
    for keep, got, route in skip_parts:
        back = send(low(wide(keep[1]) + wide(got[1])), route)
        total_part = wide(keep[0]) + wide(got[0]) + wide(back)
        pair_sums.append(total_part[skip_rows:])
        skip_low.append(low(total_part[:skip_rows].reshape(chips, width // seq, half_tile)))
    skip_low = jnp.concatenate(skip_low, axis=2)
    skip_low, mlp_got = lax.optimization_barrier((skip_low, mlp_got))
    skip_tile = jnp.sum(wide(chips_exchange(skip_low, seq)), axis=0).T
    qkv_tile = wide(stored_rows(low(jnp.concatenate(pair_sums)), seq)).T

    mlp_tile = jnp.sum(wide(mlp_got), axis=0)
    columns = width // seq
    fold = down_weight.shape[0] // wide_tile
    down_tile = lanes([mlp_tile[i * columns : (i + 1) * columns] for i in range(fold)]).T
    out_tile = mlp_tile[fold * columns : down_total.shape[1]]
    out_tile = jnp.concatenate([out_tile[:, i * columns : (i + 1) * columns] for i in range(wide_tile // columns)])
    up_tile = mlp_tile[down_total.shape[1] :]
    embed_part = jnp.concatenate(
        [lax.dynamic_index_in_dim(embed_part, jnp.bitwise_xor(at, mask), 0) for mask in range(dp)]
    )
    ada_tile = lax.dot_general(
        embed_part.astype(jnp.float32), grad_modulation, (((0,), (0,)), ((), ())),
        precision=lax.Precision.HIGHEST,
    )
    return (
        layer_output[None],
        grad_main[None],
        grad_side[None],
        skip_tile,
        ada_tile,
        qkv_tile,
        out_tile,
        up_tile,
        down_tile,
    )


def solution(mesh):
    in_specs = (
        P("dp", "seq", None),
        P("dp", "seq", None),
        P("dp", None),
        P("dp", None),
        P("dp", None),
        P("dp", None),
        P("dp", "seq", None),
        P("dp", "seq"),
        P("dp", "seq"),
        P("dp", "seq"),
        P("dp", "seq"),
        P("dp", "seq"),
        P("dp", "seq"),
    )
    out_specs = (
        P("dp", "seq", None),
        P("dp", "seq", None),
        P("dp", "seq", None),
        P("dp", "seq"),
        P("dp", "seq"),
        P("dp", "seq"),
        P("dp", "seq"),
        P("dp", "seq"),
        P("dp", "seq"),
    )
    seq_size = mesh.shape["seq"]
    paired = H == 2 * seq_size and seq_size % 3 != 0 and mesh.shape["dp"] == 4
    body = local_paired if paired else local_general
    return jax.shard_map(body, mesh=mesh, in_specs=in_specs, out_specs=out_specs, check_vma=False)
```
